32 devices in a mesh: group: 2 (over x), ctx: 16 (over z, y, core).
Axes of the slice: x: 2, y: 2, z: 4, core: 2. Of those that a mesh axis runs over, the one named last changes fastest.
Arguments:
- hyena_qkv: bfloat16 [4096, 3, 2048], P(('group', 'ctx')), parts along dimension 0, may hold values from -6 to 6
- short_weight: float32 [3, 3, 2048], replicated, may hold values from -3.5 to 3.5
- filter_rate: float32 [128, 16], replicated, as said below
- filter_residue: float32 [128, 16], replicated, may hold values from -4 to 4
- attn_qkv: bfloat16 [4096, 3, 2048], P(('group', 'ctx')), parts along dimension 0, may hold values from -6 to 6
- doc_lengths: int32 [8], P('group'), parts along dimension 0, may hold values from 1 to 897, 2048 in all
Outputs:
- hyena_out: bfloat16 [4096, 2048], P(('group', 'ctx')), parts along dimension 0
- attn_out: bfloat16 [4096, 2048], P(('group', 'ctx')), parts along dimension 0
The draws below stay inside these ranges and needn't reach their ends.
There are 2 independent parts, one for each index of `group`. The reference program is written for one: setup_inputs(seed, part) draws one part's arguments, and reference() takes and returns one part's arrays. A program takes and returns all parts, laid end to end along the dimension named above; an argument that names none is the same for every part. Nothing has to cross between parts.
Inputs may be any that keep to these rules, and one draw needn't show every extreme that they name: `filter_rate`: every rate is positive and at most 1/30. `doc_lengths`: the lengths sum to 2048 and the longest is exactly 897.
All inputs are finite; a program needn't handle non-finite values.
Results may differ from the reference program's by a relative error of at most 0.0054.
Values may be sent and summed in bfloat16 or wider, within the bound.
No kernel may reach another device: no remote copies, remote signals or barrier semaphores. Data moves between devices by JAX's collectives and lax.ppermute only.
A program may use at most 128 MiB of HBM per device.

```python
import math
import jax
import jax.numpy as jnp
import numpy as np
from jax import lax

TOK_DEV = 128
HEAD = 128
MODES = 16
SPAN = 8
CHAN = 2048
FILTERS = 128
TOKENS = 2048
MOST = 897
DOCS = 4


def draw_filter_rate(key, part):
    key_slow, key_fast, key_pick = jax.random.split(key, 3)
    shape = (FILTERS, MODES)
    rate_slow = jnp.exp(jax.random.uniform(key_slow, shape, jnp.float32, math.log(0.2), 0.0)) * (math.log(10.0) / TOKENS)
    rate_fast = jax.random.uniform(key_fast, shape, jnp.float32, 1.0 / 50.0, 1.0 / 30.0)
    share_fast = 0.5
    picked = jax.random.uniform(key_pick, shape, jnp.float32) < share_fast
    return jnp.where(picked, rate_fast, rate_slow)


def draw_attn_qkv(key, part):
    drawn = jnp.clip(jax.random.normal(key, (TOKENS, 3, CHAN), jnp.float32), -4.0, 4.0)
    return drawn.astype(jnp.bfloat16)


def level_of(own_key, extent, shards, low, high):
    def one(axis_at, shards_of):
        steps = jax.random.uniform(jax.random.fold_in(jax.random.fold_in(own_key, 6), axis_at), (shards_of,), jnp.float32, low / len(shards), high / len(shards))
        return jnp.repeat(jnp.exp(steps), extent[axis_at] // shards_of).reshape((-1,) + (1,) * (len(extent) - axis_at - 1))

    loudness = one(*shards[0])
    for cut in shards[1:]:
        loudness = loudness * one(*cut)
    return loudness


def profile(amount, total, most, slope):
    weights = [(1 << 20) // math.isqrt(standing ** slope) + 1 for standing in range(2, amount + 1)]
    spare, given = total - most - (amount - 1), [1] * (amount - 1)
    while spare > 0:
        movable = [i for i in range(amount - 1) if given[i] < most]
        pool, budget = sum([weights[i] for i in movable]), spare
        for i in movable:
            addition = min(most - given[i], max(1, budget * weights[i] // pool), spare)
            given[i] = given[i] + addition
            spare = spare - addition
    return np.array([most] + given)


def ragged_sizes(own_key, amount, total, bound, slope):
    if amount == 2:
        one = jax.random.randint(own_key, (), max(1, total - bound), min(bound, total - 1) + 1)
        return jnp.stack([one, total - one])
    lengths = jnp.asarray(profile(amount, total, bound, slope), jnp.int32)
    twos = (amount - 1) // 2
    donor, taker = lengths[1:1 + 2 * twos:2], lengths[2:2 + 2 * twos:2]
    slack = jnp.minimum(donor - 1, bound - taker)
    passed = jax.random.randint(jax.random.fold_in(own_key, 1), (twos,), 0, 1 << 20) % (slack + 1)
    lengths = lengths.at[1:1 + 2 * twos:2].set(donor - passed).at[2:2 + 2 * twos:2].set(taker + passed)
    return lengths[jax.random.permutation(jax.random.fold_in(own_key, 2), amount)]


def bell_draw(stream_key, shape, scale, limit, pieces=(), held_as=jnp.bfloat16):
    factor_of = level_of(stream_key, shape, pieces, -0.22, 0.18) if pieces else 1.0
    entries = jax.random.normal(stream_key, shape, jnp.float32) * scale * factor_of
    return jnp.minimum(jnp.maximum(entries, -limit), limit).astype(held_as)


def setup_inputs(seed: int = 0, part: int = 0) -> dict:
    arg_keys = jax.random.split(jax.random.key(seed), 7)
    part_keys = jax.random.split(jax.random.fold_in(arg_keys[6], part), 7)
    return {
        "hyena_qkv": bell_draw(part_keys[0], (TOKENS, 3, CHAN), 1.0, 6.0, ((0, 16),)),
        "short_weight": bell_draw(arg_keys[1], (3, 3, CHAN), 3 ** -0.5, 3.5, (), jnp.float32),
        "filter_rate": draw_filter_rate(jax.random.fold_in(arg_keys[6], 71), part),
        "filter_residue": bell_draw(arg_keys[3], (FILTERS, MODES), 1.0, 4.0, (), jnp.float32),
        "attn_qkv": draw_attn_qkv(jax.random.fold_in(jax.random.fold_in(arg_keys[6], part), 71), part),
        "doc_lengths": ragged_sizes(part_keys[5], DOCS, TOKENS, MOST, 2).astype(jnp.int32),
    }


precise = lax.Precision.HIGHEST

def featurize(token_rows, before, short_weight):
    row_count = token_rows.shape[0]
    padded = jnp.concatenate([before, token_rows], axis=0).astype(jnp.float32)
    return short_weight[0] * padded[2:] + short_weight[1] * padded[1:row_count + 1] + short_weight[2] * padded[:row_count]

def filter_terms(filter_rate, filter_residue, row_count):
    mode_coeff = filter_residue * jnp.sqrt(2.0 * filter_rate / filter_rate.shape[1])
    lag_values = jnp.arange(row_count).astype(jnp.float32)
    powers = jnp.exp(-filter_rate[:, :, None] * lag_values)
    filter_taps = jnp.einsum('gm,gmk->gk', mode_coeff, powers, precision=precise)
    return (mode_coeff, filter_taps.astype(jnp.bfloat16))

def toeplitz(filter_taps):
    row_count = filter_taps.shape[1]
    lag_index = jnp.arange(row_count, dtype=jnp.int32)[:, None] - jnp.arange(row_count, dtype=jnp.int32)[None, :]
    lag_table = jnp.take(filter_taps, jnp.clip(lag_index, 0, row_count - 1), axis=1)
    return jnp.where(lag_index[None] >= 0, lag_table, jnp.zeros((), filter_taps.dtype))

def block_ends(mixed_in, filter_rate):
    row_count, channels = mixed_in.shape
    groups = filter_rate.shape[0]
    lag_values = (row_count - 1 - jnp.arange(row_count)).astype(jnp.float32)
    powers = jnp.exp(-filter_rate[:, :, None] * lag_values)
    grouped = mixed_in.astype(jnp.float32).reshape(row_count, groups, channels // groups)
    return jnp.einsum('gms,sgc->gmc', powers, grouped, precision=precise)

def block_far(carried, filter_rate, mode_coeff, row_count):
    lag_values = jnp.arange(1, row_count + 1).astype(jnp.float32)
    powers = mode_coeff[:, :, None] * jnp.exp(-filter_rate[:, :, None] * lag_values)
    return jnp.einsum('gmt,gmc->tgc', powers, carried, precision=precise)

def visible(query_pos, key_pos, doc_lengths):
    bounds = jnp.cumsum(doc_lengths, dtype=jnp.int32)
    query_doc = lax.optimization_barrier(jnp.sum((query_pos[:, None] >= bounds[None, :]).astype(jnp.int32), axis=1))
    key_doc = lax.optimization_barrier(jnp.sum((key_pos[:, None] >= bounds[None, :]).astype(jnp.int32), axis=1))
    causal = (key_pos[None, :] <= query_pos[:, None]) & (key_pos[None, :] >= 0)
    return causal & (key_doc[None, :] == query_doc[:, None])

def attend(queries, keys, values, allowed):
    row_count, channels = queries.shape
    heads = channels // HEAD

    def split_heads(matrix):
        return matrix.reshape(matrix.shape[0], heads, HEAD).transpose(1, 0, 2)

    def one_head(head_parts):
        query_rows, key_rows, value_rows = head_parts
        scores = jnp.dot(query_rows, key_rows.T, preferred_element_type=jnp.float32) * (1.0 / math.sqrt(HEAD))
        scores = jnp.where(allowed, scores, -jnp.inf)
        row_max = lax.optimization_barrier(jnp.max(scores, axis=1, keepdims=True))
        exp_scores = jnp.exp(scores - row_max)
        weight = (exp_scores / lax.optimization_barrier(jnp.sum(exp_scores, axis=1, keepdims=True))).astype(jnp.bfloat16)
        return jnp.dot(weight, value_rows, preferred_element_type=jnp.float32).astype(jnp.bfloat16)
    head_out = lax.map(one_head, (split_heads(queries), split_heads(keys), split_heads(values)))
    return head_out.transpose(1, 0, 2).reshape(row_count, channels)

def reference(hyena_qkv, short_weight, filter_rate, filter_residue, attn_qkv, doc_lengths):
    block_count = TOKENS // TOK_DEV
    groups = filter_rate.shape[0]
    mode_coeff, filter_taps = filter_terms(filter_rate, filter_residue, TOK_DEV)
    toeplitz_taps = toeplitz(filter_taps).astype(jnp.float32)
    block_decay = jnp.exp(-filter_rate * TOK_DEV)

    def advance(state, token_rows):
        carried, before = state
        featured = featurize(token_rows, before, short_weight)
        mixed_in = (featured[:, 1] * featured[:, 2]).astype(jnp.bfloat16)
        grouped = mixed_in.astype(jnp.float32).reshape(TOK_DEV, groups, CHAN // groups)
        near_part = jnp.einsum('gts,sgc->tgc', toeplitz_taps, grouped, precision=precise)
        far_part = block_far(carried, filter_rate, mode_coeff, TOK_DEV)
        mixed_out = (featured[:, 0] * (near_part + far_part).reshape(TOK_DEV, CHAN)).astype(jnp.bfloat16)
        carried = block_decay[:, :, None] * carried + block_ends(mixed_in, filter_rate)
        return ((carried, token_rows[TOK_DEV - 2:]), mixed_out)
    zero_state = jnp.zeros((groups, MODES, CHAN // groups), jnp.float32)
    opening = jnp.zeros((2, 3, CHAN), jnp.bfloat16)
    _, block_outs = lax.scan(advance, (zero_state, opening), hyena_qkv.reshape(block_count, TOK_DEV, 3, CHAN))
    hyena_out = block_outs.reshape(TOKENS, CHAN)
    all_queries = attn_qkv[:, 0]
    padding = jnp.zeros(((SPAN - 1) * TOK_DEV, 2, CHAN), jnp.bfloat16)
    padded = jnp.concatenate([padding, attn_qkv[:, 1:]], axis=0)

    def one_block(block_id):
        first_row = block_id * TOK_DEV
        queries = lax.dynamic_slice_in_dim(all_queries, first_row, TOK_DEV, 0)
        window = lax.dynamic_slice_in_dim(padded, first_row, SPAN * TOK_DEV, 0)
        query_pos = first_row + jnp.arange(TOK_DEV, dtype=jnp.int32)
        key_pos = first_row - (SPAN - 1) * TOK_DEV + jnp.arange(SPAN * TOK_DEV, dtype=jnp.int32)
        allowed = visible(query_pos, key_pos, doc_lengths)
        return attend(queries, window[:, 0], window[:, 1], allowed)
    attn_out = lax.map(one_block, jnp.arange(block_count, dtype=jnp.int32)).reshape(TOKENS, CHAN)
    return (hyena_out, attn_out)
```

```python
import functools
import math

import jax
import jax.numpy as jnp
from jax import lax
from jax.experimental import pallas as pl
from jax.experimental.pallas import tpu as pltpu
from jax.sharding import PartitionSpec as P

HEAD = 128
LANES = 128
ROW = 4

F32 = jnp.float32
BF16 = jnp.bfloat16


def flip(value, axis, bit):
    count = lax.axis_size(axis)
    return lax.ppermute(value, axis, [(at, at ^ bit) for at in range(count)])


def ahead(value, axis, steps, bit=0):
    count = lax.axis_size(axis)
    pairs = [(at, (at + steps) ^ bit) for at in range(count - steps)]
    return lax.ppermute(value, axis, pairs)


def cost(flops, moved, exps=0):
    return pl.CostEstimate(flops=flops, bytes_accessed=moved, transcendentals=exps)


VMEM = pl.BlockSpec(memory_space=pltpu.VMEM)
SMEM = pl.BlockSpec(memory_space=pltpu.SMEM)
ANY = pl.BlockSpec(memory_space=pl.ANY)


def table(rate_row, lags_down):
    return jnp.exp(-rate_row * lags_down)


def hyena_main_body(modes, x_ref, halo_ref, w_ref, rate_ref, res_ref, near_ref, q_ref, ends_ref, taps_s, u_s):
    rows, lanes = x_ref.shape[1:]
    terms = rate_ref.shape[2]
    filters = terms // modes
    width = lanes // filters
    row_at = lax.broadcasted_iota(jnp.int32, (rows, lanes), 0)
    lane_at = lax.broadcasted_iota(jnp.int32, (rows, lanes), 1)

    def feature(stream):
        here = x_ref[stream].astype(F32)
        halo = halo_ref[stream].astype(F32)
        one = jnp.where(row_at == 0, halo[1:2], pltpu.roll(here, 1, 0))
        two = pltpu.roll(here, 2, 0)
        two = jnp.where(row_at == 0, halo[0:1], jnp.where(row_at == 1, halo[1:2], two))
        tap = [w_ref[n, stream : stream + 1, :] for n in range(3)]
        return tap[0] * here + tap[1] * one + tap[2] * two

    q_ref[...] = feature(0)
    mixed = (feature(1) * feature(2)).astype(BF16)

    rate = jnp.broadcast_to(rate_ref[0], (rows, terms)).T
    residue = jnp.broadcast_to(res_ref[0], (rows, terms)).T
    coeff = residue * jnp.sqrt(2.0 * rate / modes)
    lag = (rows - 1 - lax.broadcasted_iota(jnp.int32, (terms, rows), 1)).astype(F32)
    powers = jnp.exp(-rate * lag)
    backward = jnp.sum((coeff * powers).reshape(filters, modes, rows), axis=1)
    zero = jnp.zeros((rows, lanes), BF16)
    for g in range(filters):
        spread = jnp.broadcast_to(backward[g : g + 1], (rows, rows))
        shifted = pltpu.roll(spread, 1, 1, stride=1, stride_axis=0)
        kept = jnp.where(lane_at <= row_at, shifted, 0.0)
        taps_s[:, g * rows : (g + 1) * rows] = kept.astype(BF16)
        mine = (lane_at // width) == g
        u_s[g * rows : (g + 1) * rows, :] = jnp.where(mine, mixed, zero)
    near_ref[...] = jnp.dot(taps_s[...], u_s[...], preferred_element_type=F32)

    high = powers.astype(BF16)
    low = (powers - high.astype(F32)).astype(BF16)
    ends = jnp.dot(high, mixed, preferred_element_type=F32) + jnp.dot(
        low, mixed, preferred_element_type=F32
    )
    own = (
        lax.broadcasted_iota(jnp.int32, (terms, lanes), 0) // modes
        == lax.broadcasted_iota(jnp.int32, (terms, lanes), 1) // width
    )
    ends_ref[...] = jnp.sum(jnp.where(own, ends, 0.0).reshape(filters, modes, lanes), axis=0)


def hyena_main(streams, halo, short_weight, rate_rows, res_rows, modes):
    _, rows, channels = streams.shape
    blocks, _, terms = rate_rows.shape
    lanes = channels // blocks
    filters = terms // modes
    by_block = lambda n: (0, n)
    lead = lambda n: (0, 0, n)
    whole = lambda n: (n, 0, 0)
    return pl.pallas_call(
        functools.partial(hyena_main_body, modes),
        grid=(blocks,),
        in_specs=[
            pl.BlockSpec((3, rows, lanes), lead),
            pl.BlockSpec((3, 2, lanes), lead),
            pl.BlockSpec((3, 3, lanes), lead),
            pl.BlockSpec((1, 1, terms), whole),
            pl.BlockSpec((1, 1, terms), whole),
        ],
        out_specs=[
            pl.BlockSpec((rows, lanes), by_block),
            pl.BlockSpec((rows, lanes), by_block),
            pl.BlockSpec((modes, lanes), by_block),
        ],
        out_shape=[
            jax.ShapeDtypeStruct((rows, channels), F32),
            jax.ShapeDtypeStruct((rows, channels), F32),
            jax.ShapeDtypeStruct((modes, channels), F32),
        ],
        scratch_shapes=[
            pltpu.VMEM((rows, filters * rows), BF16),
            pltpu.VMEM((filters * rows, lanes), BF16),
        ],
        cost_estimate=cost(2 * rows * rows * filters * channels, 8 * rows * channels),
        name="hyena_main",
    )(streams, halo, short_weight, rate_rows, res_rows)


def hyena_out_body(modes, near_ref, q_ref, carried_ref, rate_ref, res_ref, out_ref):
    rows, lanes = near_ref.shape
    terms = rate_ref.shape[2]
    filters = terms // modes
    width = lanes // filters
    rate = rate_ref[0]
    coeff = res_ref[0] * jnp.sqrt(2.0 * rate / modes)
    lag = (1 + lax.broadcasted_iota(jnp.int32, (rows, terms), 0)).astype(F32)
    powers = coeff * jnp.exp(-rate * lag)
    p_high = powers.astype(BF16)
    p_low = (powers - p_high.astype(F32)).astype(BF16)
    own = (
        lax.broadcasted_iota(jnp.int32, (terms, lanes), 0) // modes
        == lax.broadcasted_iota(jnp.int32, (terms, lanes), 1) // width
    )
    carried = jnp.where(own, jnp.concatenate([carried_ref[...]] * filters, axis=0), 0.0)
    c_high = carried.astype(BF16)
    c_low = (carried - c_high.astype(F32)).astype(BF16)
    far = (
        jnp.dot(p_high, c_high, preferred_element_type=F32)
        + jnp.dot(p_low, c_high, preferred_element_type=F32)
        + jnp.dot(p_high, c_low, preferred_element_type=F32)
    )
    out_ref[...] = (q_ref[...] * (near_ref[...] + far)).astype(BF16)


def hyena_finish(near, query, carried, rate_rows, res_rows, modes):
    rows, channels = near.shape
    blocks, _, terms = rate_rows.shape
    lanes = channels // blocks
    by_block = lambda n: (0, n)
    whole = lambda n: (n, 0, 0)
    return pl.pallas_call(
        functools.partial(hyena_out_body, modes),
        grid=(blocks,),
        in_specs=[
            pl.BlockSpec((rows, lanes), by_block),
            pl.BlockSpec((rows, lanes), by_block),
            pl.BlockSpec((modes, lanes), by_block),
            pl.BlockSpec((1, 1, terms), whole),
            pl.BlockSpec((1, 1, terms), whole),
        ],
        out_specs=pl.BlockSpec((rows, lanes), by_block),
        out_shape=jax.ShapeDtypeStruct((rows, channels), BF16),
        cost_estimate=cost(6 * rows * terms * channels, 10 * rows * channels),
        name="hyena_finish",
    )(near, query, carried, rate_rows, res_rows)


def scan_states(ends, filter_rate, rows):
    modes, channels = ends.shape
    half = channels // 2
    width = channels // filter_rate.shape[0]
    index = lax.axis_index("ctx")
    chips = lax.axis_size("ctx") // 2
    core = index % 2
    rate = jnp.repeat(filter_rate.T, width, axis=1)
    take = lambda matrix, which: lax.dynamic_slice_in_dim(matrix, which * half, half, 1)
    rate = take(rate, core)
    decay = lambda blocks: jnp.exp(-rate * float(rows * blocks))
    mine = take(ends, core)
    theirs = flip(take(ends, 1 - core), "ctx", 1)
    even = jnp.where(core == 0, mine, theirs)
    odd = jnp.where(core == 0, theirs, mine)
    total = decay(1) * even + odd
    before = ahead(total, "ctx", 2)
    reach = 2
    while reach < chips:
        upto = total + decay(2) * before
        before = before + decay(2 * (reach - 1)) * ahead(upto, "ctx", 2 * reach)
        reach *= 2
    second = decay(1) * before + even
    keep = jnp.where(core == 0, before, second)
    back = flip(jnp.where(core == 0, second, before), "ctx", 1)
    return jnp.concatenate(
        [jnp.where(core == 0, keep, back), jnp.where(core == 0, back, keep)], axis=1
    )


def pack_body(at_ref, mine_ref, theirs_ref, own_ref, cross_ref, local_ref, swap_ref):
    side = at_ref[0]
    quarter = own_ref.shape[3]
    here = pl.ds(pl.multiple_of(side * quarter, quarter), quarter)
    there = pl.ds(pl.multiple_of((1 - side) * quarter, quarter), quarter)
    for slot, source in enumerate((mine_ref, theirs_ref)):
        for stream in range(3):
            local_ref[slot, stream] = source[stream, :, here]
            swap_ref[slot, stream] = source[stream, :, there]
        for stream in range(2):
            own_ref[slot, stream] = source[stream + 1, :, here]
            cross_ref[slot, stream] = source[stream + 1, :, there]


def pack(side, mine, theirs):
    _, rows, half = mine.shape
    quarter = half // 2
    pairs = jax.ShapeDtypeStruct((2, 2, rows, quarter), BF16)
    full = jax.ShapeDtypeStruct((2, 3, rows, quarter), BF16)
    return pl.pallas_call(
        pack_body,
        in_specs=[SMEM, VMEM, VMEM],
        out_specs=[VMEM] * 4,
        out_shape=[pairs, pairs, full, full],
        cost_estimate=cost(0, 16 * rows * half),
        name="pack",
    )(side, mine, theirs)


def onward_body(at_ref, own_ref, cross_ref, out_ref):
    place = at_ref[0]
    for block in range(1, ROW):
        slot = place ^ block

        @pl.when(slot < 2)
        def _():
            out_ref[block - 1] = own_ref[slot]

        @pl.when(slot >= 2)
        def _():
            out_ref[block - 1] = cross_ref[slot - 2]


def onward(place, own, cross):
    return pl.pallas_call(
        onward_body,
        in_specs=[SMEM, VMEM, VMEM],
        out_specs=VMEM,
        out_shape=jax.ShapeDtypeStruct((ROW - 1,) + own.shape[1:], BF16),
        cost_estimate=cost(0, 4 * own.size),
        name="onward",
    )(place, own, cross)


def contig_start(info_ref, docs, position):
    first = jnp.zeros_like(position)
    bound = jnp.int32(0)
    for n in range(docs):
        bound = bound + info_ref[2 + n]
        first = jnp.where(position >= bound, bound, first)
    return first


def attend_body(docs, info_ref, local, swap, own, cross, acc_ref, m_ref, l_ref, q_s, k_s, v_s, sems):
    place, base = info_ref[0], info_ref[1]
    rows, quarter = q_s.shape[1:]
    copies = []

    def bring(source, target):
        copies.append(pltpu.make_async_copy(source, target, sems.at[len(copies)]))
        copies[-1].start()

    for slot in range(ROW):
        row = local.at[slot] if slot < 2 else swap.at[slot - 2]
        old = own.at[slot] if slot < 2 else cross.at[slot - 2]
        block = place ^ slot
        older = pl.ds(pl.multiple_of(block * rows, rows), rows)
        newer = pl.ds(pl.multiple_of((ROW + block) * rows, rows), rows)
        bring(row.at[0], q_s.at[block])
        bring(row.at[1], k_s.at[newer])
        bring(row.at[2], v_s.at[newer])
        bring(old.at[0], k_s.at[older])
        bring(old.at[1], v_s.at[older])
    for copy in copies:
        copy.wait()

    scale = 1.0 / math.sqrt(HEAD)
    for block in range(ROW):
        width = (ROW + 1 + block) * rows
        position = base + block * rows + lax.broadcasted_iota(jnp.int32, (rows, 1), 0)
        first = contig_start(info_ref, docs, position)
        at = base - ROW * rows + lax.broadcasted_iota(jnp.int32, (rows, width), 1)
        allowed = (at >= first) & (at <= position)
        for head in range(quarter // HEAD):
            lanes = slice(head * HEAD, (head + 1) * HEAD)
            scores = lax.dot_general(
                q_s[block, :, lanes],
                k_s[0:width, lanes],
                (((1,), (1,)), ((), ())),
                preferred_element_type=F32,
            )
            scores = jnp.where(allowed, scores * scale, -jnp.inf)
            top = jnp.max(scores, axis=1, keepdims=True)
            weight = jnp.exp(scores - top)
            m_ref[block, :, head : head + 1] = top
            l_ref[block, :, head : head + 1] = jnp.sum(weight, axis=1, keepdims=True)
            acc_ref[block, :, lanes] = jnp.dot(
                weight.astype(BF16), v_s[0:width, lanes], preferred_element_type=F32
            )


def attend(info, docs, local, swap, own, cross):
    _, _, rows, quarter = local.shape
    heads = quarter // HEAD
    return pl.pallas_call(
        functools.partial(attend_body, docs),
        in_specs=[SMEM, ANY, ANY, ANY, ANY],
        out_specs=[VMEM] * 3,
        out_shape=[
            jax.ShapeDtypeStruct((ROW, rows, quarter), F32),
            jax.ShapeDtypeStruct((ROW, rows, heads), F32),
            jax.ShapeDtypeStruct((ROW, rows, heads), F32),
        ],
        scratch_shapes=[
            pltpu.VMEM((ROW, rows, quarter), BF16),
            pltpu.VMEM((2 * ROW * rows, quarter), BF16),
            pltpu.VMEM((2 * ROW * rows, quarter), BF16),
            pltpu.SemaphoreType.DMA((5 * ROW,)),
        ],
        cost_estimate=cost(26 * 4 * rows * rows * quarter, 14 * ROW * rows * quarter, 26 * heads * rows * rows),
        name="attend",
    )(info, local, swap, own, cross)


def attend_last_body(docs, info_ref, local, swap, oldest, acc_ref, m_ref, l_ref, out_ref, q_s, sems):
    place, base = info_ref[0], info_ref[1]
    rows, quarter = q_s.shape[1:]
    copies = []
    for slot in range(ROW):
        row = local.at[slot] if slot < 2 else swap.at[slot - 2]
        copies.append(pltpu.make_async_copy(row.at[0], q_s.at[place ^ slot], sems.at[slot]))
        copies[-1].start()
    for copy in copies:
        copy.wait()
    scale = 1.0 / math.sqrt(HEAD)
    for block in range(ROW):
        slot = place ^ block
        seen = ROW - 1 - block
        width = seen * rows
        if seen:
            position = base + block * rows + lax.broadcasted_iota(jnp.int32, (rows, 1), 0)
            first = contig_start(info_ref, docs, position)
            at = base - (ROW + seen) * rows + lax.broadcasted_iota(jnp.int32, (rows, width), 1)
            allowed = at >= first
        for head in range(quarter // HEAD):
            lanes = slice(head * HEAD, (head + 1) * HEAD)
            total = acc_ref[block, :, lanes]
            below = l_ref[block, :, head : head + 1]
            if seen:
                keys = oldest[block : ROW - 1, 0, :, lanes].reshape(width, HEAD)
                values = oldest[block : ROW - 1, 1, :, lanes].reshape(width, HEAD)
                scores = lax.dot_general(
                    q_s[block, :, lanes],
                    keys,
                    (((1,), (1,)), ((), ())),
                    preferred_element_type=F32,
                )
                scores = jnp.where(allowed, scores * scale, -jnp.inf)
                past = m_ref[block, :, head : head + 1]
                top = jnp.maximum(past, jnp.max(scores, axis=1, keepdims=True))
                fade = jnp.exp(past - top)
                weight = jnp.exp(scores - top)
                below = below * fade + jnp.sum(weight, axis=1, keepdims=True)
                total = total * fade + jnp.dot(
                    weight.astype(BF16), values, preferred_element_type=F32
                )
            out_ref[slot, :, lanes] = (total / below).astype(BF16)


def attend_last(info, docs, local, swap, oldest, acc, top, below):
    _, _, rows, quarter = local.shape
    heads = quarter // HEAD
    return pl.pallas_call(
        functools.partial(attend_last_body, docs),
        in_specs=[SMEM, ANY, ANY, VMEM, VMEM, VMEM, VMEM],
        out_specs=VMEM,
        out_shape=jax.ShapeDtypeStruct((ROW, rows, quarter), BF16),
        scratch_shapes=[pltpu.VMEM((ROW, rows, quarter), BF16), pltpu.SemaphoreType.DMA((ROW,))],
        cost_estimate=cost(6 * 4 * rows * rows * quarter, 12 * ROW * rows * quarter, 6 * heads * rows * rows),
        name="attend_last",
    )(info, local, swap, oldest, acc, top, below)


def assemble_body(at_ref, kept, paired, swapped, out_ref):
    place = at_ref[0]
    quarter = kept.shape[2]
    pieces = (kept.at[0], paired.at[0], swapped.at[0], swapped.at[1])
    for slot, piece in enumerate(pieces):
        maker = place ^ slot
        which = 2 * (maker % 2) + maker // 2
        out_ref[:, pl.ds(pl.multiple_of(which * quarter, quarter), quarter)] = piece[...]


def assemble(place, kept, paired, swapped):
    _, rows, quarter = kept.shape
    return pl.pallas_call(
        assemble_body,
        in_specs=[SMEM, VMEM, VMEM, VMEM],
        out_specs=VMEM,
        out_shape=jax.ShapeDtypeStruct((rows, ROW * quarter), BF16),
        cost_estimate=cost(0, 16 * rows * quarter),
        name="assemble",
    )(place, kept, paired, swapped)


def on_device(hyena_qkv, short_weight, filter_rate, filter_residue, attn_qkv, doc_lengths):
    rows, _, channels = attn_qkv.shape
    groups, modes = filter_rate.shape
    docs = doc_lengths.shape[0]
    index = lax.axis_index("ctx")
    place = index % ROW
    core, side = place % 2, place // 2
    half = channels // 2
    spot = place.reshape(1).astype(jnp.int32)
    info = jnp.concatenate(
        [spot, ((index - place) * rows).reshape(1).astype(jnp.int32), doc_lengths]
    )

    take = lambda which: lax.dynamic_slice_in_dim(attn_qkv, which * half, half, 2).transpose(1, 0, 2)
    mine = take(core)
    theirs = flip(take(1 - core), "ctx", 1)
    own, cross, local, swap = pack(side.reshape(1).astype(jnp.int32), mine, theirs)
    own = ahead(own, "ctx", ROW)
    cross = ahead(cross, "ctx", ROW, 2)
    swap = flip(swap, "ctx", 2)
    oldest = ahead(onward(spot, own, cross), "ctx", ROW)

    halo = ahead(hyena_qkv[rows - 2 :], "ctx", 1)
    blocks = channels // LANES
    rate_rows = filter_rate.reshape(blocks, 1, -1)
    res_rows = filter_residue.reshape(blocks, 1, -1)
    near, query, ends = hyena_main(
        hyena_qkv.transpose(1, 0, 2), halo.transpose(1, 0, 2), short_weight, rate_rows, res_rows, modes
    )
    carried = scan_states(ends, filter_rate, rows)
    hyena_out = hyena_finish(near, query, carried, rate_rows, res_rows, modes)

    acc, top, below = attend(info, docs, local, swap, own, cross)
    made = attend_last(info, docs, local, swap, oldest, acc, top, below)
    paired = flip(made[1::2], "ctx", 1)
    swapped = flip(jnp.stack([made[2], paired[1]]), "ctx", 2)
    attn_out = assemble(spot, made, paired, swapped)
    return (hyena_out, attn_out)


def solution(mesh):
    in_specs = (
        P(("group", "ctx"), None, None),
        P(),
        P(),
        P(),
        P(("group", "ctx"), None, None),
        P("group"),
    )
    out_specs = (P(("group", "ctx"), None), P(("group", "ctx"), None))
    return jax.shard_map(
        on_device, mesh=mesh, in_specs=in_specs, out_specs=out_specs, check_vma=False
    )
```

```python
import functools
import math

import jax
import jax.numpy as jnp
from jax import lax
from jax.experimental import pallas as pl
from jax.experimental.pallas import tpu as pltpu
from jax.sharding import PartitionSpec as P


HEAD = 128
LANES = 128
ROW = 4

F32 = jnp.float32
BF16 = jnp.bfloat16


def flip(value, axis, bit):
    count = lax.axis_size(axis)
    return lax.ppermute(value, axis, [(at, at ^ bit) for at in range(count)])


def ahead(value, axis, steps, bit=0):
    count = lax.axis_size(axis)
    pairs = [(at, (at + steps) ^ bit) for at in range(count - steps)]
    return lax.ppermute(value, axis, pairs)


def limits(mib):
    return pltpu.CompilerParams(vmem_limit_bytes=mib << 20)


def cost(flops, moved, exps=0):
    return pl.CostEstimate(flops=flops, bytes_accessed=moved, transcendentals=exps)


VMEM = pl.BlockSpec(memory_space=pltpu.VMEM)
SMEM = pl.BlockSpec(memory_space=pltpu.SMEM)
ANY = pl.BlockSpec(memory_space=pl.ANY)


def same_filter(modes, width, terms, lanes):
    row_at = lax.broadcasted_iota(jnp.int32, (terms, lanes), 0)
    lane_at = lax.broadcasted_iota(jnp.int32, (terms, lanes), 1)
    kept = None
    for g in range(terms // modes):
        both = (
            (row_at >= g * modes)
            & (row_at < (g + 1) * modes)
            & (lane_at >= g * width)
            & (lane_at < (g + 1) * width)
        )
        kept = both if kept is None else kept | both
    return kept


def hyena_main_body(modes, x_ref, halo_ref, w_ref, rate_ref, res_ref, near_ref, q_ref, ends_ref, taps_s, u_s):
    rows = x_ref.shape[1]
    parts, _, terms = rate_ref.shape
    lanes = x_ref.shape[2] // parts
    filters = terms // modes
    width = lanes // filters
    row_at = lax.broadcasted_iota(jnp.int32, (rows, lanes), 0)
    lane_at = lax.broadcasted_iota(jnp.int32, (rows, lanes), 1)
    lag = (rows - 1 - lax.broadcasted_iota(jnp.int32, (terms, rows), 1)).astype(F32)
    own = same_filter(modes, width, terms, lanes)
    zero = jnp.zeros((rows, lanes), BF16)

    for part in range(parts):
        at = slice(part * lanes, (part + 1) * lanes)

        def feature(stream):
            here = x_ref[stream, :, at].astype(F32)
            halo = halo_ref[stream, :, at].astype(F32)
            one = jnp.where(row_at == 0, halo[1:2], pltpu.roll(here, 1, 0))
            two = pltpu.roll(here, 2, 0)
            two = jnp.where(row_at == 0, halo[0:1], jnp.where(row_at == 1, halo[1:2], two))
            tap = [w_ref[n, stream : stream + 1, at] for n in range(3)]
            return tap[0] * here + tap[1] * one + tap[2] * two

        q_ref[:, at] = feature(0)
        mixed = (feature(1) * feature(2)).astype(BF16)

        coeff = res_ref[part] * jnp.sqrt(2.0 * rate_ref[part] / modes)
        rate = jnp.broadcast_to(rate_ref[part], (rows, terms)).T
        coeff = jnp.broadcast_to(coeff, (rows, terms)).T
        powers = jnp.exp(-rate * lag)
        backward = jnp.sum((coeff * powers).reshape(filters, modes, rows), axis=1)
        for g in range(filters):
            spread = jnp.broadcast_to(backward[g : g + 1], (rows, rows))
            shifted = pltpu.roll(spread, 1, 1, stride=1, stride_axis=0)
            kept = jnp.where(lane_at <= row_at, shifted, 0.0)
            taps_s[part, :, g * rows : (g + 1) * rows] = kept.astype(BF16)
            mine = (lane_at >= g * width) & (lane_at < (g + 1) * width)
            u_s[part, g * rows : (g + 1) * rows, :] = jnp.where(mine, mixed, zero)
        near_ref[:, at] = jnp.dot(taps_s[part], u_s[part], preferred_element_type=F32)

        high = powers.astype(BF16)
        low = (powers - high.astype(F32)).astype(BF16)
        ends = jnp.dot(high, mixed, preferred_element_type=F32) + jnp.dot(
            low, mixed, preferred_element_type=F32
        )
        ends_ref[:, at] = jnp.sum(jnp.where(own, ends, 0.0).reshape(filters, modes, lanes), axis=0)


STEPS = 4


def hyena_main(streams, halo, short_weight, rate_rows, res_rows, modes):
    _, rows, channels = streams.shape
    blocks, _, terms = rate_rows.shape
    parts = blocks // STEPS
    wide = channels // STEPS
    lanes = channels // blocks
    filters = terms // modes
    by_block = lambda n: (0, n)
    lead = lambda n: (0, 0, n)
    whole = lambda n: (n, 0, 0)
    return pl.pallas_call(
        functools.partial(hyena_main_body, modes),
        grid=(STEPS,),
        in_specs=[
            pl.BlockSpec((3, rows, wide), lead),
            pl.BlockSpec((3, 2, wide), lead),
            pl.BlockSpec((3, 3, wide), lead),
            pl.BlockSpec((parts, 1, terms), whole),
            pl.BlockSpec((parts, 1, terms), whole),
        ],
        out_specs=[
            pl.BlockSpec((rows, wide), by_block),
            pl.BlockSpec((rows, wide), by_block),
            pl.BlockSpec((modes, wide), by_block),
        ],
        out_shape=[
            jax.ShapeDtypeStruct((rows, channels), F32),
            jax.ShapeDtypeStruct((rows, channels), F32),
            jax.ShapeDtypeStruct((modes, channels), F32),
        ],
        scratch_shapes=[
            pltpu.VMEM((parts, rows, filters * rows), BF16),
            pltpu.VMEM((parts, filters * rows, lanes), BF16),
        ],
        compiler_params=limits(24),
        cost_estimate=cost(2 * rows * rows * filters * channels, 8 * rows * channels),
        name="hyena_main",
    )(streams, halo, short_weight, rate_rows, res_rows)


def hyena_out_body(modes, near_ref, q_ref, carried_ref, rate_ref, res_ref, out_ref):
    rows = near_ref.shape[0]
    parts, _, terms = rate_ref.shape
    lanes = near_ref.shape[1] // parts
    filters = terms // modes
    width = lanes // filters
    lag = (1 + lax.broadcasted_iota(jnp.int32, (rows, terms), 0)).astype(F32)
    own = same_filter(modes, width, terms, lanes)
    for part in range(parts):
        at = slice(part * lanes, (part + 1) * lanes)
        rate = rate_ref[part]
        coeff = res_ref[part] * jnp.sqrt(2.0 * rate / modes)
        powers = coeff * jnp.exp(-rate * lag)
        p_high = powers.astype(BF16)
        p_low = (powers - p_high.astype(F32)).astype(BF16)
        carried = jnp.where(own, jnp.concatenate([carried_ref[:, at]] * filters, axis=0), 0.0)
        c_high = carried.astype(BF16)
        c_low = (carried - c_high.astype(F32)).astype(BF16)
        far = (
            jnp.dot(p_high, c_high, preferred_element_type=F32)
            + jnp.dot(p_low, c_high, preferred_element_type=F32)
            + jnp.dot(p_high, c_low, preferred_element_type=F32)
        )
        out_ref[:, at] = (q_ref[:, at] * (near_ref[:, at] + far)).astype(BF16)


def hyena_finish(near, query, carried, rate_rows, res_rows, modes):
    rows, channels = near.shape
    blocks, _, terms = rate_rows.shape
    parts = blocks // STEPS
    wide = channels // STEPS
    by_block = lambda n: (0, n)
    whole = lambda n: (n, 0, 0)
    return pl.pallas_call(
        functools.partial(hyena_out_body, modes),
        grid=(STEPS,),
        in_specs=[
            pl.BlockSpec((rows, wide), by_block),
            pl.BlockSpec((rows, wide), by_block),
            pl.BlockSpec((modes, wide), by_block),
            pl.BlockSpec((parts, 1, terms), whole),
            pl.BlockSpec((parts, 1, terms), whole),
        ],
        out_specs=pl.BlockSpec((rows, wide), by_block),
        out_shape=jax.ShapeDtypeStruct((rows, channels), BF16),
        compiler_params=limits(16),
        cost_estimate=cost(6 * rows * terms * channels, 10 * rows * channels),
        name="hyena_finish",
    )(near, query, carried, rate_rows, res_rows)


def scan_states(ends, filter_rate, rows):
    _, channels = ends.shape
    half = channels // 2
    width = channels // filter_rate.shape[0]
    index = lax.axis_index("ctx")
    count = lax.axis_size("ctx") // ROW
    core, side = index % 2, index // 2 % 2
    rate = jnp.repeat(filter_rate.T, width, axis=1)
    take = lambda matrix, which: lax.dynamic_slice_in_dim(matrix, which * half, half, 1)
    rate = take(rate, core)
    decay = lambda blocks: jnp.exp(-rate * float(rows * blocks))
    mine = take(ends, core)
    theirs = flip(take(ends, 1 - core), "ctx", 1)
    even = jnp.where(core == 0, mine, theirs)
    odd = jnp.where(core == 0, theirs, mine)
    chip = decay(1) * even + odd
    other = flip(chip, "ctx", 2)
    left = jnp.where(side == 0, chip, other)
    total = decay(2) * left + jnp.where(side == 0, other, chip)
    before = ahead(total, "ctx", ROW)
    reach = 2
    while reach < count:
        upto = total + decay(ROW) * before
        earlier = ahead(upto, "ctx", ROW * reach)
        before = before + decay(ROW * (reach - 1)) * earlier
        reach *= 2
    before = jnp.where(side == 0, before, decay(2) * before + left)
    second = decay(1) * before + even
    keep = jnp.where(core == 0, before, second)
    back = flip(jnp.where(core == 0, second, before), "ctx", 1)
    return jnp.concatenate(
        [jnp.where(core == 0, keep, back), jnp.where(core == 0, back, keep)], axis=1
    )


def lanes_from(start, size):
    return pl.ds(pl.multiple_of(start * size, size), size)


def halve_body(at_ref, streams_ref, out_ref):
    del at_ref
    out_ref[...] = streams_ref[...]


def halve(which, streams):
    count, rows, channels = streams.shape
    half = channels // 2
    return pl.pallas_call(
        halve_body,
        grid_spec=pltpu.PrefetchScalarGridSpec(
            num_scalar_prefetch=1,
            grid=(1,),
            in_specs=[pl.BlockSpec((count, rows, half), lambda n, at: (0, 0, at[0]))],
            out_specs=pl.BlockSpec((count, rows, half), lambda n, at: (0, 0, 0)),
        ),
        out_shape=jax.ShapeDtypeStruct((count, rows, half), streams.dtype),
        compiler_params=limits(8),
        cost_estimate=cost(0, 4 * count * rows * half),
        name="halve",
    )(which, streams)


def pack_body(first, at_ref, streams_ref, theirs_ref, *outs):
    core, side = at_ref[0], at_ref[1]
    quarter = theirs_ref.shape[2] // 2
    for out, away in zip(outs, (0, 1)[-len(outs) :]):
        to = 1 - side if away else side
        for stream in range(first, 3):
            out[0, stream - first] = streams_ref[stream, :, lanes_from(2 * core + to, quarter)]
            out[1, stream - first] = theirs_ref[stream, :, lanes_from(to, quarter)]


def pack(where, streams, theirs, first, amount):
    _, rows, half = theirs.shape
    shape = jax.ShapeDtypeStruct((2, 3 - first, rows, half // 2), BF16)
    return pl.pallas_call(
        functools.partial(pack_body, first),
        in_specs=[SMEM, VMEM, VMEM],
        out_specs=[VMEM] * amount,
        out_shape=[shape] * amount,
        compiler_params=limits(10),
        cost_estimate=cost(0, 8 * amount * rows * half),
        name="pack",
    )(where, streams, theirs)


def onward_body(at_ref, own_ref, cross_ref, out_ref):
    place = at_ref[2]
    for block in range(1, ROW):
        slot = place ^ block

        @pl.when(slot < 2)
        def _():
            out_ref[block - 1] = own_ref[slot]

        @pl.when(slot >= 2)
        def _():
            out_ref[block - 1] = cross_ref[slot - 2]


def onward(where, own, cross):
    return pl.pallas_call(
        onward_body,
        in_specs=[SMEM, VMEM, VMEM],
        out_specs=VMEM,
        out_shape=jax.ShapeDtypeStruct((ROW - 1,) + own.shape[1:], BF16),
        compiler_params=limits(6),
        cost_estimate=cost(0, 4 * own.size),
        name="onward",
    )(where, own, cross)


FIXED = 4


def contig_start(info_ref, docs, position):
    first = jnp.zeros_like(position)
    bound = jnp.int32(0)
    for n in range(docs):
        bound = bound + info_ref[FIXED + n]
        first = jnp.where(position >= bound, bound, first)
    return first


def row_part(info_ref, streams, theirs, swap, slot, stream, quarter):
    core, side = info_ref[0], info_ref[1]
    if slot == 0:
        return streams.at[stream, :, lanes_from(2 * core + side, quarter)]
    if slot == 1:
        return theirs.at[stream, :, lanes_from(side, quarter)]
    return swap.at[slot - 2, stream]


SCALE = math.log2(math.e) / math.sqrt(HEAD)


def attend_body(docs, info_ref, streams, theirs, swap, own, cross, acc_ref, m_ref, l_ref, q_s, k_s, v_s, sems):
    place, base = info_ref[2], info_ref[3]
    rows, quarter = q_s.shape[1:]
    copies = []

    def bring(source, target):
        copies.append(pltpu.make_async_copy(source, target, sems.at[len(copies)]))
        copies[-1].start()

    for slot in range(ROW):
        part = lambda stream: row_part(info_ref, streams, theirs, swap, slot, stream, quarter)
        old = own.at[slot] if slot < 2 else cross.at[slot - 2]
        block = place ^ slot
        older = lanes_from(block, rows)
        newer = lanes_from(ROW + block, rows)
        bring(part(0), q_s.at[block])
        bring(part(1), k_s.at[newer])
        bring(part(2), v_s.at[newer])
        bring(old.at[0], k_s.at[older])
        bring(old.at[1], v_s.at[older])
    for copy in copies:
        copy.wait()

    for block in range(ROW):
        width = (ROW + 1 + block) * rows
        position = base + block * rows + lax.broadcasted_iota(jnp.int32, (rows, 1), 0)
        first = contig_start(info_ref, docs, position)
        at = base - ROW * rows + lax.broadcasted_iota(jnp.int32, (rows, width), 1)
        allowed = (at >= first) & (at <= position)
        for head in range(quarter // HEAD):
            lanes = slice(head * HEAD, (head + 1) * HEAD)
            scores = lax.dot_general(
                q_s[block, :, lanes],
                k_s[0:width, lanes],
                (((1,), (1,)), ((), ())),
                preferred_element_type=F32,
            )
            scores = jnp.where(allowed, scores, -jnp.inf)
            top = jnp.max(scores, axis=1, keepdims=True)
            weight = jnp.exp2((scores - top) * SCALE)
            m_ref[block, :, head : head + 1] = top
            l_ref[block, :, head : head + 1] = jnp.sum(weight, axis=1, keepdims=True)
            acc_ref[block, :, lanes] = jnp.dot(
                weight.astype(BF16), v_s[0:width, lanes], preferred_element_type=F32
            )


def attend(info, docs, streams, theirs, swap, own, cross):
    _, _, rows, quarter = own.shape
    heads = quarter // HEAD
    return pl.pallas_call(
        functools.partial(attend_body, docs),
        in_specs=[SMEM] + [ANY] * 5,
        out_specs=[VMEM] * 3,
        out_shape=[
            jax.ShapeDtypeStruct((ROW, rows, quarter), F32),
            jax.ShapeDtypeStruct((ROW, rows, heads), F32),
            jax.ShapeDtypeStruct((ROW, rows, heads), F32),
        ],
        scratch_shapes=[
            pltpu.VMEM((ROW, rows, quarter), BF16),
            pltpu.VMEM((2 * ROW * rows, quarter), BF16),
            pltpu.VMEM((2 * ROW * rows, quarter), BF16),
            pltpu.SemaphoreType.DMA((5 * ROW,)),
        ],
        compiler_params=limits(20),
        cost_estimate=cost(26 * 4 * rows * rows * quarter, 14 * ROW * rows * quarter, 26 * heads * rows * rows),
        name="attend",
    )(info, streams, theirs, swap, own, cross)


def attend_last_body(
    docs, info_ref, streams, theirs, swap, oldest, acc_ref, m_ref, l_ref, out0, out1, out2, out3, q_s, o_s, sems
):
    place, base = info_ref[2], info_ref[3]
    rows, quarter = q_s.shape[1:]
    copies = []
    for slot in range(ROW):
        part = row_part(info_ref, streams, theirs, swap, slot, 0, quarter)
        copies.append(pltpu.make_async_copy(part, q_s.at[place ^ slot], sems.at[slot]))
        copies[-1].start()
    for copy in copies:
        copy.wait()
    for block in range(ROW):
        slot = place ^ block
        seen = ROW - 1 - block
        width = seen * rows
        if seen:
            position = base + block * rows + lax.broadcasted_iota(jnp.int32, (rows, 1), 0)
            first = contig_start(info_ref, docs, position)
            at = base - (ROW + seen) * rows + lax.broadcasted_iota(jnp.int32, (rows, width), 1)
            allowed = at >= first
        for head in range(quarter // HEAD):
            lanes = slice(head * HEAD, (head + 1) * HEAD)
            total = acc_ref[block, :, lanes]
            below = l_ref[block, :, head : head + 1]
            if seen:
                keys = oldest[block : ROW - 1, 0, :, lanes].reshape(width, HEAD)
                values = oldest[block : ROW - 1, 1, :, lanes].reshape(width, HEAD)
                scores = lax.dot_general(
                    q_s[block, :, lanes],
                    keys,
                    (((1,), (1,)), ((), ())),
                    preferred_element_type=F32,
                )
                scores = jnp.where(allowed, scores, -jnp.inf)
                past = m_ref[block, :, head : head + 1]
                top = jnp.maximum(past, jnp.max(scores, axis=1, keepdims=True))
                fade = jnp.exp2((past - top) * SCALE)
                weight = jnp.exp2((scores - top) * SCALE)
                share = 1.0 / (below * fade + jnp.sum(weight, axis=1, keepdims=True))
                total = total * (fade * share) + share * jnp.dot(
                    weight.astype(BF16), values, preferred_element_type=F32
                )
            else:
                total = total * (1.0 / below)
            o_s[slot, :, lanes] = total.astype(BF16)
    for slot, out in enumerate((out0, out1, out2, out3)):
        out[...] = o_s[slot]


def attend_last(info, docs, streams, theirs, swap, oldest, acc, top, below):
    _, rows, quarter = acc.shape
    heads = quarter // HEAD
    return pl.pallas_call(
        functools.partial(attend_last_body, docs),
        in_specs=[SMEM] + [ANY] * 3 + [VMEM] * 4,
        out_specs=[VMEM] * ROW,
        out_shape=[jax.ShapeDtypeStruct((rows, quarter), BF16)] * ROW,
        scratch_shapes=[
            pltpu.VMEM((ROW, rows, quarter), BF16),
            pltpu.VMEM((ROW, rows, quarter), BF16),
            pltpu.SemaphoreType.DMA((ROW,)),
        ],
        compiler_params=limits(16),
        cost_estimate=cost(6 * 4 * rows * rows * quarter, 12 * ROW * rows * quarter, 6 * heads * rows * rows),
        name="attend_last",
    )(info, streams, theirs, swap, oldest, acc, top, below)


def assemble_body(at_ref, *refs):
    place = at_ref[2]
    *pieces, out_ref = refs
    quarter = pieces[0].shape[1]
    for slot, piece in enumerate(pieces):
        maker = place ^ slot
        which = 2 * (maker & 1) + lax.shift_right_logical(maker, 1)
        out_ref[:, lanes_from(which, quarter)] = piece[...]


def assemble(where, pieces):
    rows, quarter = pieces[0].shape
    return pl.pallas_call(
        assemble_body,
        in_specs=[SMEM] + [VMEM] * ROW,
        out_specs=VMEM,
        out_shape=jax.ShapeDtypeStruct((rows, ROW * quarter), BF16),
        compiler_params=limits(6),
        cost_estimate=cost(0, 16 * rows * quarter),
        name="assemble",
    )(where, *pieces)


def on_device(hyena_qkv, short_weight, filter_rate, filter_residue, attn_qkv, doc_lengths):
    rows, _, channels = attn_qkv.shape
    _, modes = filter_rate.shape
    docs = doc_lengths.shape[0]
    index = lax.axis_index("ctx")
    place = index % ROW
    core, side = place % 2, place // 2
    fixed = jnp.stack([core, side, place, (index - place) * rows]).astype(jnp.int32)
    info = jnp.concatenate([fixed, doc_lengths])

    halo = ahead(hyena_qkv[rows - 2 :], "ctx", 1)

    streams = attn_qkv.transpose(1, 0, 2)
    theirs = flip(halve((1 - core).reshape(1).astype(jnp.int32), streams), "ctx", 1)
    own, cross = pack(fixed, streams, theirs, 1, 2)
    own = ahead(own, "ctx", ROW)
    cross = ahead(cross, "ctx", ROW, 2)
    (swap,) = pack(fixed, streams, theirs, 0, 1)
    swap = flip(swap, "ctx", 2)
    oldest = ahead(onward(fixed, own, cross), "ctx", ROW)

    blocks = channels // LANES
    rate_rows = filter_rate.reshape(blocks, 1, -1)
    res_rows = filter_residue.reshape(blocks, 1, -1)
    near, query, ends = hyena_main(
        hyena_qkv.transpose(1, 0, 2), halo.transpose(1, 0, 2), short_weight, rate_rows, res_rows, modes
    )
    carried = scan_states(ends, filter_rate, rows)
    hyena_out = hyena_finish(near, query, carried, rate_rows, res_rows, modes)

    acc, top, below = attend(info, docs, streams, theirs, swap, own, cross)
    made = attend_last(info, docs, streams, theirs, swap, oldest, acc, top, below)
    pieces = [made[0]] + [flip(made[n], "ctx", n) for n in range(1, ROW)]
    attn_out = assemble(fixed, pieces)
    return (hyena_out, attn_out)


def solution(mesh):
    in_specs = (
        P(("group", "ctx"), None, None),
        P(),
        P(),
        P(),
        P(("group", "ctx"), None, None),
        P("group"),
    )
    out_specs = (P(("group", "ctx"), None), P(("group", "ctx"), None))
    return jax.shard_map(
        on_device, mesh=mesh, in_specs=in_specs, out_specs=out_specs, check_vma=False
    )
```

```python
import functools
import math

import jax
import jax.numpy as jnp
from jax import lax
from jax.experimental import pallas as pl
from jax.experimental.pallas import tpu as pltpu
from jax.sharding import PartitionSpec as P


HEAD = 128
LANES = 128
EDGE = 8
ROW = 4

F32 = jnp.float32
BF16 = jnp.bfloat16


def flip(value, axis, bit):
    count = lax.axis_size(axis)
    return lax.ppermute(value, axis, [(at, at ^ bit) for at in range(count)])


def ahead(value, axis, steps, bit=0):
    count = lax.axis_size(axis)
    pairs = [(at, (at + steps) ^ bit) for at in range(count - steps)]
    return lax.ppermute(value, axis, pairs)


def limits(mib):
    return pltpu.CompilerParams(vmem_limit_bytes=mib << 20)


def cost(flops, moved, exps=0):
    return pl.CostEstimate(flops=flops, bytes_accessed=moved, transcendentals=exps)


VMEM = pl.BlockSpec(memory_space=pltpu.VMEM)
SMEM = pl.BlockSpec(memory_space=pltpu.SMEM)
ANY = pl.BlockSpec(memory_space=pl.ANY)


def same_filter(modes, width, terms, lanes):
    row_at = lax.broadcasted_iota(jnp.int32, (terms, lanes), 0)
    lane_at = lax.broadcasted_iota(jnp.int32, (terms, lanes), 1)
    kept = None
    for g in range(terms // modes):
        both = (
            (row_at >= g * modes)
            & (row_at < (g + 1) * modes)
            & (lane_at >= g * width)
            & (lane_at < (g + 1) * width)
        )
        kept = both if kept is None else kept | both
    return kept


def feature(x, halo, w_ref, stream, at):
    here = x.astype(F32)
    halo = halo.astype(F32)
    edge = halo.shape[0]
    row_at = lax.broadcasted_iota(jnp.int32, here.shape, 0)
    one = jnp.where(row_at == 0, halo[edge - 1 :], pltpu.roll(here, 1, 0))
    two = jnp.where(row_at == 1, halo[edge - 1 :], pltpu.roll(here, 2, 0))
    two = jnp.where(row_at == 0, halo[edge - 2 : edge - 1], two)
    tap = [w_ref[n, stream : stream + 1, at] for n in range(3)]
    return tap[0] * here + tap[1] * one + tap[2] * two


def hyena_ends_body(modes, x_ref, halo_ref, w_ref, rate_ref, mixed_ref, ends_ref, wide_ref):
    rows = x_ref.shape[1]
    parts, _, terms = rate_ref.shape
    lanes = x_ref.shape[2] // parts
    filters = terms // modes
    width = lanes // filters
    lag = (rows - 1 - lax.broadcasted_iota(jnp.int32, (terms, rows), 1)).astype(F32)
    own = same_filter(modes, width, terms, lanes)
    pick = lambda matrix: jnp.sum(jnp.where(own, matrix, 0.0).reshape(filters, modes, lanes), axis=0)
    for part in range(parts):
        at = slice(part * lanes, (part + 1) * lanes)
        key, value = (feature(x_ref[n, :, at], halo_ref[n, :, at], w_ref, n, at) for n in (1, 2))
        mixed = (key * value).astype(BF16)
        mixed_ref[:, at] = mixed
        rate = jnp.broadcast_to(rate_ref[part], (rows, terms)).T
        powers = jnp.exp(-rate * lag)
        high = powers.astype(BF16)
        low = (powers - high.astype(F32)).astype(BF16)
        ends = jnp.dot(high, mixed, preferred_element_type=F32) + jnp.dot(
            low, mixed, preferred_element_type=F32
        )
        ends_ref[:, at] = pick(ends)
        wide_ref[:, at] = pick(rate)


STEPS = 4


def hyena_ends(streams, halo, short_weight, rate_rows, modes):
    _, rows, channels = streams.shape
    edge = halo.shape[1]
    blocks, _, terms = rate_rows.shape
    parts = blocks // STEPS
    wide = channels // STEPS
    by_block = lambda n: (0, n)
    lead = lambda n: (0, 0, n)
    return pl.pallas_call(
        functools.partial(hyena_ends_body, modes),
        grid=(STEPS,),
        in_specs=[
            pl.BlockSpec((3, rows, wide), lead),
            pl.BlockSpec((3, edge, wide), lead),
            pl.BlockSpec((3, 3, wide), lead),
            pl.BlockSpec((parts, 1, terms), lambda n: (n, 0, 0)),
        ],
        out_specs=[
            pl.BlockSpec((rows, wide), by_block),
            pl.BlockSpec((modes, wide), by_block),
            pl.BlockSpec((modes, wide), by_block),
        ],
        out_shape=[
            jax.ShapeDtypeStruct((rows, channels), BF16),
            jax.ShapeDtypeStruct((modes, channels), F32),
            jax.ShapeDtypeStruct((modes, channels), F32),
        ],
        compiler_params=limits(16),
        cost_estimate=cost(4 * rows * terms * channels, 8 * rows * channels),
        name="hyena_ends",
    )(streams, halo, short_weight, rate_rows)


def hyena_near_body(modes, x_ref, halo_ref, w_ref, mixed_ref, rate_ref, res_ref, near_ref, q_ref, taps_s, u_s):
    rows = x_ref.shape[1]
    parts, _, terms = rate_ref.shape
    lanes = x_ref.shape[2] // parts
    filters = terms // modes
    width = lanes // filters
    row_at = lax.broadcasted_iota(jnp.int32, (rows, lanes), 0)
    lane_at = lax.broadcasted_iota(jnp.int32, (rows, lanes), 1)
    lag = (rows - 1 - lax.broadcasted_iota(jnp.int32, (terms, rows), 1)).astype(F32)
    zero = jnp.zeros((rows, lanes), BF16)
    for part in range(parts):
        at = slice(part * lanes, (part + 1) * lanes)
        q_ref[:, at] = feature(x_ref[0, :, at], halo_ref[0, :, at], w_ref, 0, at)
        mixed = mixed_ref[:, at]
        coeff = res_ref[part] * jnp.sqrt(2.0 * rate_ref[part] / modes)
        rate = jnp.broadcast_to(rate_ref[part], (rows, terms)).T
        coeff = jnp.broadcast_to(coeff, (rows, terms)).T
        powers = coeff * jnp.exp(-rate * lag)
        backward = jnp.sum(powers.reshape(filters, modes, rows), axis=1)
        for g in range(filters):
            spread = jnp.broadcast_to(backward[g : g + 1], (rows, rows))
            shifted = pltpu.roll(spread, 1, 1, stride=1, stride_axis=0)
            kept = jnp.where(lane_at <= row_at, shifted, 0.0)
            taps_s[part, :, g * rows : (g + 1) * rows] = kept.astype(BF16)
            mine = (lane_at >= g * width) & (lane_at < (g + 1) * width)
            u_s[part, g * rows : (g + 1) * rows, :] = jnp.where(mine, mixed, zero)
        near_ref[:, at] = jnp.dot(taps_s[part], u_s[part], preferred_element_type=F32)


def hyena_near(streams, halo, short_weight, mixed, rate_rows, res_rows, modes):
    _, rows, channels = streams.shape
    edge = halo.shape[1]
    blocks, _, terms = rate_rows.shape
    parts = blocks // STEPS
    wide = channels // STEPS
    lanes = channels // blocks
    filters = terms // modes
    by_block = lambda n: (0, n)
    lead = lambda n: (0, 0, n)
    whole = lambda n: (n, 0, 0)
    return pl.pallas_call(
        functools.partial(hyena_near_body, modes),
        grid=(STEPS,),
        in_specs=[
            pl.BlockSpec((1, rows, wide), lead),
            pl.BlockSpec((1, edge, wide), lead),
            pl.BlockSpec((3, 3, wide), lead),
            pl.BlockSpec((rows, wide), by_block),
            pl.BlockSpec((parts, 1, terms), whole),
            pl.BlockSpec((parts, 1, terms), whole),
        ],
        out_specs=[
            pl.BlockSpec((rows, wide), by_block),
            pl.BlockSpec((rows, wide), by_block),
        ],
        out_shape=[
            jax.ShapeDtypeStruct((rows, channels), F32),
            jax.ShapeDtypeStruct((rows, channels), F32),
        ],
        scratch_shapes=[
            pltpu.VMEM((parts, rows, filters * rows), BF16),
            pltpu.VMEM((parts, filters * rows, lanes), BF16),
        ],
        compiler_params=limits(16),
        cost_estimate=cost(2 * rows * rows * filters * channels, 12 * rows * channels),
        name="hyena_near",
    )(streams, halo, short_weight, mixed, rate_rows, res_rows)


def hyena_out_body(modes, near_ref, q_ref, carried_ref, rate_ref, res_ref, out_ref):
    rows = near_ref.shape[0]
    parts, _, terms = rate_ref.shape
    lanes = near_ref.shape[1] // parts
    filters = terms // modes
    width = lanes // filters
    lag = (1 + lax.broadcasted_iota(jnp.int32, (rows, terms), 0)).astype(F32)
    own = same_filter(modes, width, terms, lanes)
    for part in range(parts):
        at = slice(part * lanes, (part + 1) * lanes)
        rate = rate_ref[part]
        coeff = res_ref[part] * jnp.sqrt(2.0 * rate / modes)
        powers = coeff * jnp.exp(-rate * lag)
        p_high = powers.astype(BF16)
        p_low = (powers - p_high.astype(F32)).astype(BF16)
        carried = jnp.where(own, jnp.concatenate([carried_ref[:, at]] * filters, axis=0), 0.0)
        c_high = carried.astype(BF16)
        c_low = (carried - c_high.astype(F32)).astype(BF16)
        far = (
            jnp.dot(p_high, c_high, preferred_element_type=F32)
            + jnp.dot(p_low, c_high, preferred_element_type=F32)
            + jnp.dot(p_high, c_low, preferred_element_type=F32)
        )
        out_ref[:, at] = (q_ref[:, at] * (near_ref[:, at] + far)).astype(BF16)


def hyena_finish(near, query, carried, rate_rows, res_rows, modes):
    rows, channels = near.shape
    blocks, _, terms = rate_rows.shape
    parts = blocks // STEPS
    wide = channels // STEPS
    by_block = lambda n: (0, n)
    whole = lambda n: (n, 0, 0)
    return pl.pallas_call(
        functools.partial(hyena_out_body, modes),
        grid=(STEPS,),
        in_specs=[
            pl.BlockSpec((rows, wide), by_block),
            pl.BlockSpec((rows, wide), by_block),
            pl.BlockSpec((modes, wide), by_block),
            pl.BlockSpec((parts, 1, terms), whole),
            pl.BlockSpec((parts, 1, terms), whole),
        ],
        out_specs=pl.BlockSpec((rows, wide), by_block),
        out_shape=jax.ShapeDtypeStruct((rows, channels), BF16),
        compiler_params=limits(16),
        cost_estimate=cost(6 * rows * terms * channels, 10 * rows * channels),
        name="hyena_finish",
    )(near, query, carried, rate_rows, res_rows)


def scan_states(ends, rate, rows):
    half = ends.shape[1] // 2
    index = lax.axis_index("ctx")
    count = lax.axis_size("ctx") // ROW
    core, side = index % 2, index // 2 % 2
    take = lambda matrix, which: lax.dynamic_slice_in_dim(matrix, which * half, half, 1)
    rate = take(rate, core)
    decay = lambda blocks: jnp.exp(-rate * float(rows * blocks))
    mine = take(ends, core)
    theirs = flip(take(ends, 1 - core), "ctx", 1)
    even = jnp.where(core == 0, mine, theirs)
    odd = jnp.where(core == 0, theirs, mine)
    chip = decay(1) * even + odd
    other = flip(chip, "ctx", 2)
    left = jnp.where(side == 0, chip, other)
    total = decay(2) * left + jnp.where(side == 0, other, chip)
    before = ahead(total, "ctx", ROW)
    reach = 2
    while reach < count:
        upto = total + decay(ROW) * before
        earlier = ahead(upto, "ctx", ROW * reach)
        before = before + decay(ROW * (reach - 1)) * earlier
        reach *= 2
    before = jnp.where(side == 0, before, decay(2) * before + left)
    second = decay(1) * before + even
    keep = jnp.where(core == 0, before, second)
    back = flip(jnp.where(core == 0, second, before), "ctx", 1)
    return jnp.concatenate(
        [jnp.where(core == 0, keep, back), jnp.where(core == 0, back, keep)], axis=1
    )


def lanes_from(start, size):
    return pl.ds(pl.multiple_of(start * size, size), size)


def halve_body(at_ref, streams_ref, out_ref):
    del at_ref
    out_ref[...] = streams_ref[...]


def halve(which, streams):
    count, rows, channels = streams.shape
    half = channels // 2
    return pl.pallas_call(
        halve_body,
        grid_spec=pltpu.PrefetchScalarGridSpec(
            num_scalar_prefetch=1,
            grid=(1,),
            in_specs=[pl.BlockSpec((count, rows, half), lambda n, at: (0, 0, at[0]))],
            out_specs=pl.BlockSpec((count, rows, half), lambda n, at: (0, 0, 0)),
        ),
        out_shape=jax.ShapeDtypeStruct((count, rows, half), streams.dtype),
        compiler_params=limits(8),
        cost_estimate=cost(0, 4 * count * rows * half),
        name="halve",
    )(which, streams)


def pack_body(first, at_ref, streams_ref, theirs_ref, *outs):
    core, side = at_ref[0], at_ref[1]
    quarter = theirs_ref.shape[2] // 2
    for out, away in zip(outs, (0, 1)[-len(outs) :]):
        to = 1 - side if away else side
        for stream in range(first, 3):
            out[0, stream - first] = streams_ref[stream, :, lanes_from(2 * core + to, quarter)]
            out[1, stream - first] = theirs_ref[stream, :, lanes_from(to, quarter)]


def pack(where, streams, theirs, first, amount):
    _, rows, half = theirs.shape
    shape = jax.ShapeDtypeStruct((2, 3 - first, rows, half // 2), BF16)
    return pl.pallas_call(
        functools.partial(pack_body, first),
        in_specs=[SMEM, VMEM, VMEM],
        out_specs=[VMEM] * amount,
        out_shape=[shape] * amount,
        compiler_params=limits(10),
        cost_estimate=cost(0, 8 * amount * rows * half),
        name="pack",
    )(where, streams, theirs)


def onward_body(at_ref, own_ref, cross_ref, out_ref):
    place = at_ref[2]
    for block in range(1, ROW):
        slot = place ^ block

        @pl.when(slot < 2)
        def _():
            out_ref[block - 1] = own_ref[slot]

        @pl.when(slot >= 2)
        def _():
            out_ref[block - 1] = cross_ref[slot - 2]


def onward(where, own, cross):
    return pl.pallas_call(
        onward_body,
        in_specs=[SMEM, VMEM, VMEM],
        out_specs=VMEM,
        out_shape=jax.ShapeDtypeStruct((ROW - 1,) + own.shape[1:], BF16),
        compiler_params=limits(6),
        cost_estimate=cost(0, 4 * own.size),
        name="onward",
    )(where, own, cross)


FIXED = 4


def contig_start(info_ref, docs, position):
    first = jnp.zeros_like(position)
    bound = jnp.int32(0)
    for n in range(docs):
        bound = bound + info_ref[FIXED + n]
        first = jnp.where(position >= bound, bound, first)
    return first


def row_part(info_ref, streams, theirs, swap, slot, stream, quarter):
    core, side = info_ref[0], info_ref[1]
    if slot == 0:
        return streams.at[stream, :, lanes_from(2 * core + side, quarter)]
    if slot == 1:
        return theirs.at[stream, :, lanes_from(side, quarter)]
    return swap.at[slot - 2, stream]


SCALE = math.log2(math.e) / math.sqrt(HEAD)


def attend_body(docs, info_ref, streams, theirs, swap, own, cross, acc_ref, m_ref, l_ref, q_s, k_s, v_s, sems):
    place, base = info_ref[2], info_ref[3]
    rows, quarter = q_s.shape[1:]
    copies = []

    def bring(source, target):
        copies.append(pltpu.make_async_copy(source, target, sems.at[len(copies)]))
        copies[-1].start()

    for slot in range(ROW):
        part = lambda stream: row_part(info_ref, streams, theirs, swap, slot, stream, quarter)
        old = own.at[slot] if slot < 2 else cross.at[slot - 2]
        block = place ^ slot
        older = lanes_from(block, rows)
        newer = lanes_from(ROW + block, rows)
        bring(part(0), q_s.at[block])
        bring(part(1), k_s.at[newer])
        bring(part(2), v_s.at[newer])
        bring(old.at[0], k_s.at[older])
        bring(old.at[1], v_s.at[older])
    for copy in copies:
        copy.wait()

    for block in range(ROW):
        width = (ROW + 1 + block) * rows
        position = base + block * rows + lax.broadcasted_iota(jnp.int32, (rows, 1), 0)
        first = contig_start(info_ref, docs, position)
        at = base - ROW * rows + lax.broadcasted_iota(jnp.int32, (rows, width), 1)
        allowed = (at >= first) & (at <= position)
        for head in range(quarter // HEAD):
            lanes = slice(head * HEAD, (head + 1) * HEAD)
            scores = lax.dot_general(
                q_s[block, :, lanes],
                k_s[0:width, lanes],
                (((1,), (1,)), ((), ())),
                preferred_element_type=F32,
            )
            scores = jnp.where(allowed, scores, -jnp.inf)
            top = jnp.max(scores, axis=1, keepdims=True)
            weight = jnp.exp2((scores - top) * SCALE)
            m_ref[block, :, head : head + 1] = top
            l_ref[block, :, head : head + 1] = jnp.sum(weight, axis=1, keepdims=True)
            acc_ref[block, :, lanes] = jnp.dot(
                weight.astype(BF16), v_s[0:width, lanes], preferred_element_type=F32
            )


def attend(info, docs, streams, theirs, swap, own, cross):
    _, _, rows, quarter = own.shape
    heads = quarter // HEAD
    return pl.pallas_call(
        functools.partial(attend_body, docs),
        in_specs=[SMEM] + [ANY] * 5,
        out_specs=[VMEM] * 3,
        out_shape=[
            jax.ShapeDtypeStruct((ROW, rows, quarter), F32),
            jax.ShapeDtypeStruct((ROW, rows, heads), F32),
            jax.ShapeDtypeStruct((ROW, rows, heads), F32),
        ],
        scratch_shapes=[
            pltpu.VMEM((ROW, rows, quarter), BF16),
            pltpu.VMEM((2 * ROW * rows, quarter), BF16),
            pltpu.VMEM((2 * ROW * rows, quarter), BF16),
            pltpu.SemaphoreType.DMA((5 * ROW,)),
        ],
        compiler_params=limits(20),
        cost_estimate=cost(26 * 4 * rows * rows * quarter, 14 * ROW * rows * quarter, 26 * heads * rows * rows),
        name="attend",
    )(info, streams, theirs, swap, own, cross)


def attend_last_body(
    docs, info_ref, streams, theirs, swap, oldest, acc_ref, m_ref, l_ref, out0, out1, out2, out3, q_s, o_s, sems
):
    place, base = info_ref[2], info_ref[3]
    rows, quarter = q_s.shape[1:]
    copies = []
    for slot in range(ROW):
        part = row_part(info_ref, streams, theirs, swap, slot, 0, quarter)
        copies.append(pltpu.make_async_copy(part, q_s.at[place ^ slot], sems.at[slot]))
        copies[-1].start()
    for copy in copies:
        copy.wait()
    for block in range(ROW):
        slot = place ^ block
        seen = ROW - 1 - block
        width = seen * rows
        if seen:
            position = base + block * rows + lax.broadcasted_iota(jnp.int32, (rows, 1), 0)
            first = contig_start(info_ref, docs, position)
            at = base - (ROW + seen) * rows + lax.broadcasted_iota(jnp.int32, (rows, width), 1)
            allowed = at >= first
        for head in range(quarter // HEAD):
            lanes = slice(head * HEAD, (head + 1) * HEAD)
            total = acc_ref[block, :, lanes]
            below = l_ref[block, :, head : head + 1]
            if seen:
                keys = oldest[block : ROW - 1, 0, :, lanes].reshape(width, HEAD)
                values = oldest[block : ROW - 1, 1, :, lanes].reshape(width, HEAD)
                scores = lax.dot_general(
                    q_s[block, :, lanes],
                    keys,
                    (((1,), (1,)), ((), ())),
                    preferred_element_type=F32,
                )
                scores = jnp.where(allowed, scores, -jnp.inf)
                past = m_ref[block, :, head : head + 1]
                top = jnp.maximum(past, jnp.max(scores, axis=1, keepdims=True))
                fade = jnp.exp2((past - top) * SCALE)
                weight = jnp.exp2((scores - top) * SCALE)
                share = 1.0 / (below * fade + jnp.sum(weight, axis=1, keepdims=True))
                total = total * (fade * share) + share * jnp.dot(
                    weight.astype(BF16), values, preferred_element_type=F32
                )
            else:
                total = total * (1.0 / below)
            o_s[slot, :, lanes] = total.astype(BF16)
    for slot, out in enumerate((out0, out1, out2, out3)):
        out[...] = o_s[slot]


def attend_last(info, docs, streams, theirs, swap, oldest, acc, top, below):
    _, rows, quarter = acc.shape
    heads = quarter // HEAD
    return pl.pallas_call(
        functools.partial(attend_last_body, docs),
        in_specs=[SMEM] + [ANY] * 3 + [VMEM] * 4,
        out_specs=[VMEM] * ROW,
        out_shape=[jax.ShapeDtypeStruct((rows, quarter), BF16)] * ROW,
        scratch_shapes=[
            pltpu.VMEM((ROW, rows, quarter), BF16),
            pltpu.VMEM((ROW, rows, quarter), BF16),
            pltpu.SemaphoreType.DMA((ROW,)),
        ],
        compiler_params=limits(16),
        cost_estimate=cost(6 * 4 * rows * rows * quarter, 12 * ROW * rows * quarter, 6 * heads * rows * rows),
        name="attend_last",
    )(info, streams, theirs, swap, oldest, acc, top, below)


def assemble_body(at_ref, *refs):
    place = at_ref[2]
    *pieces, out_ref = refs
    quarter = pieces[0].shape[1]
    for slot, piece in enumerate(pieces):
        maker = place ^ slot
        which = 2 * (maker & 1) + lax.shift_right_logical(maker, 1)
        out_ref[:, lanes_from(which, quarter)] = piece[...]


def assemble(where, pieces):
    rows, quarter = pieces[0].shape
    return pl.pallas_call(
        assemble_body,
        in_specs=[SMEM] + [VMEM] * ROW,
        out_specs=VMEM,
        out_shape=jax.ShapeDtypeStruct((rows, ROW * quarter), BF16),
        compiler_params=limits(6),
        cost_estimate=cost(0, 16 * rows * quarter),
        name="assemble",
    )(where, *pieces)


def on_device(hyena_qkv, short_weight, filter_rate, filter_residue, attn_qkv, doc_lengths):
    rows, _, channels = attn_qkv.shape
    modes = filter_rate.shape[1]
    docs = doc_lengths.shape[0]
    index = lax.axis_index("ctx")
    place = index % ROW
    core, side = place % 2, place // 2
    fixed = jnp.stack([core, side, place, (index - place) * rows]).astype(jnp.int32)
    info = jnp.concatenate([fixed, doc_lengths])

    edge = ahead(hyena_qkv[rows - EDGE :], "ctx", 1)

    streams = attn_qkv.transpose(1, 0, 2)
    theirs = flip(halve((1 - core).reshape(1).astype(jnp.int32), streams), "ctx", 1)
    own, cross = pack(fixed, streams, theirs, 1, 2)
    own = ahead(own, "ctx", ROW)
    cross = ahead(cross, "ctx", ROW, 2)
    (swap,) = pack(fixed, streams, theirs, 0, 1)
    swap = flip(swap, "ctx", 2)
    oldest = ahead(onward(fixed, own, cross), "ctx", ROW)

    blocks = channels // LANES
    rate_rows = filter_rate.reshape(blocks, 1, -1)
    res_rows = filter_residue.reshape(blocks, 1, -1)
    inner, edge = hyena_qkv.transpose(1, 0, 2), edge.transpose(1, 0, 2)
    mixed, ends, wide = hyena_ends(inner, edge, short_weight, rate_rows, modes)
    near, query = hyena_near(inner, edge, short_weight, mixed, rate_rows, res_rows, modes)
    carried = scan_states(ends, wide, rows)
    hyena_out = hyena_finish(near, query, carried, rate_rows, res_rows, modes)

    acc, top, below = attend(info, docs, streams, theirs, swap, own, cross)
    made = attend_last(info, docs, streams, theirs, swap, oldest, acc, top, below)
    pieces = [made[0]] + [flip(made[n], "ctx", n) for n in range(1, ROW)]
    attn_out = assemble(fixed, pieces)
    return (hyena_out, attn_out)


def solution(mesh):
    in_specs = (
        P(("group", "ctx"), None, None),
        P(),
        P(),
        P(),
        P(("group", "ctx"), None, None),
        P("group"),
    )
    out_specs = (P(("group", "ctx"), None), P(("group", "ctx"), None))
    return jax.shard_map(
        on_device, mesh=mesh, in_specs=in_specs, out_specs=out_specs, check_vma=False
    )
```

```python
import functools
import math

import jax
import jax.numpy as jnp
from jax import lax
from jax.experimental import pallas as pl
from jax.experimental.pallas import tpu as pltpu
from jax.sharding import PartitionSpec as P


HEAD = 128
LANES = 128
EDGE = 8
ROW = 4

F32 = jnp.float32
BF16 = jnp.bfloat16


def flip(value, axis, bit):
    count = lax.axis_size(axis)
    return lax.ppermute(value, axis, [(at, at ^ bit) for at in range(count)])


def ahead(value, axis, steps, bit=0):
    count = lax.axis_size(axis)
    pairs = [(at, (at + steps) ^ bit) for at in range(count - steps)]
    return lax.ppermute(value, axis, pairs)


def limits(mib):
    return pltpu.CompilerParams(vmem_limit_bytes=mib << 20)


def cost(flops, moved, exps=0):
    return pl.CostEstimate(flops=flops, bytes_accessed=moved, transcendentals=exps)


VMEM = pl.BlockSpec(memory_space=pltpu.VMEM)
SMEM = pl.BlockSpec(memory_space=pltpu.SMEM)
ANY = pl.BlockSpec(memory_space=pl.ANY)


def same_filter(modes, width, terms, lanes):
    row_at = lax.broadcasted_iota(jnp.int32, (terms, lanes), 0)
    lane_at = lax.broadcasted_iota(jnp.int32, (terms, lanes), 1)
    kept = None
    for g in range(terms // modes):
        both = (
            (row_at >= g * modes)
            & (row_at < (g + 1) * modes)
            & (lane_at >= g * width)
            & (lane_at < (g + 1) * width)
        )
        kept = both if kept is None else kept | both
    return kept


def feature(x, halo, w_ref, stream, at):
    here = x.astype(F32)
    halo = halo.astype(F32)
    edge = halo.shape[0]
    row_at = lax.broadcasted_iota(jnp.int32, here.shape, 0)
    one = jnp.where(row_at == 0, halo[edge - 1 :], pltpu.roll(here, 1, 0))
    two = jnp.where(row_at == 1, halo[edge - 1 :], pltpu.roll(here, 2, 0))
    two = jnp.where(row_at == 0, halo[edge - 2 : edge - 1], two)
    tap = [w_ref[n, stream : stream + 1, at] for n in range(3)]
    return tap[0] * here + tap[1] * one + tap[2] * two


def hyena_ends_body(modes, x_ref, halo_ref, w_ref, rate_ref, mixed_ref, ends_ref, wide_ref):
    rows = x_ref.shape[1]
    parts, _, terms = rate_ref.shape
    lanes = x_ref.shape[2] // parts
    filters = terms // modes
    width = lanes // filters
    lag = (rows - 1 - lax.broadcasted_iota(jnp.int32, (terms, rows), 1)).astype(F32)
    own = same_filter(modes, width, terms, lanes)
    pick = lambda matrix: jnp.sum(jnp.where(own, matrix, 0.0).reshape(filters, modes, lanes), axis=0)
    for part in range(parts):
        at = slice(part * lanes, (part + 1) * lanes)
        key, value = (feature(x_ref[n, :, at], halo_ref[n, :, at], w_ref, n, at) for n in (1, 2))
        mixed = (key * value).astype(BF16)
        mixed_ref[:, at] = mixed
        rate = jnp.broadcast_to(rate_ref[part], (rows, terms)).T
        powers = jnp.exp(-rate * lag)
        high = powers.astype(BF16)
        low = (powers - high.astype(F32)).astype(BF16)
        ends = jnp.dot(high, mixed, preferred_element_type=F32) + jnp.dot(
            low, mixed, preferred_element_type=F32
        )
        ends_ref[:, at] = pick(ends)
        wide_ref[:, at] = pick(rate)


STEPS = 4


def hyena_ends(streams, halo, short_weight, rate_rows, modes):
    _, rows, channels = streams.shape
    edge = halo.shape[1]
    blocks, _, terms = rate_rows.shape
    parts = blocks // STEPS
    wide = channels // STEPS
    by_block = lambda n: (0, n)
    lead = lambda n: (0, 0, n)
    return pl.pallas_call(
        functools.partial(hyena_ends_body, modes),
        grid=(STEPS,),
        in_specs=[
            pl.BlockSpec((3, rows, wide), lead),
            pl.BlockSpec((3, edge, wide), lead),
            pl.BlockSpec((3, 3, wide), lead),
            pl.BlockSpec((parts, 1, terms), lambda n: (n, 0, 0)),
        ],
        out_specs=[
            pl.BlockSpec((rows, wide), by_block),
            pl.BlockSpec((modes, wide), by_block),
            pl.BlockSpec((modes, wide), by_block),
        ],
        out_shape=[
            jax.ShapeDtypeStruct((rows, channels), BF16),
            jax.ShapeDtypeStruct((modes, channels), F32),
            jax.ShapeDtypeStruct((modes, channels), F32),
        ],
        compiler_params=limits(58),
        cost_estimate=cost(4 * rows * terms * channels, 8 * rows * channels),
        name="hyena_ends",
    )(streams, halo, short_weight, rate_rows)


def hyena_near_body(modes, x_ref, halo_ref, w_ref, mixed_ref, rate_ref, res_ref, near_ref, q_ref, taps_s, u_s):
    rows = x_ref.shape[1]
    parts, _, terms = rate_ref.shape
    lanes = x_ref.shape[2] // parts
    filters = terms // modes
    width = lanes // filters
    row_at = lax.broadcasted_iota(jnp.int32, (rows, lanes), 0)
    lane_at = lax.broadcasted_iota(jnp.int32, (rows, lanes), 1)
    lag = (rows - 1 - lax.broadcasted_iota(jnp.int32, (terms, rows), 1)).astype(F32)
    zero = jnp.zeros((rows, lanes), BF16)
    for part in range(parts):
        at = slice(part * lanes, (part + 1) * lanes)
        q_ref[:, at] = feature(x_ref[0, :, at], halo_ref[0, :, at], w_ref, 0, at)
        mixed = mixed_ref[:, at]
        coeff = res_ref[part] * jnp.sqrt(2.0 * rate_ref[part] / modes)
        rate = jnp.broadcast_to(rate_ref[part], (rows, terms)).T
        coeff = jnp.broadcast_to(coeff, (rows, terms)).T
        powers = coeff * jnp.exp(-rate * lag)
        backward = jnp.sum(powers.reshape(filters, modes, rows), axis=1)
        for g in range(filters):
            spread = jnp.broadcast_to(backward[g : g + 1], (rows, rows))
            shifted = pltpu.roll(spread, 1, 1, stride=1, stride_axis=0)
            kept = jnp.where(lane_at <= row_at, shifted, 0.0)
            taps_s[part, :, g * rows : (g + 1) * rows] = kept.astype(BF16)
            mine = (lane_at >= g * width) & (lane_at < (g + 1) * width)
            u_s[part, g * rows : (g + 1) * rows, :] = jnp.where(mine, mixed, zero)
        near_ref[:, at] = jnp.dot(taps_s[part], u_s[part], preferred_element_type=F32)


def hyena_near(streams, halo, short_weight, mixed, rate_rows, res_rows, modes):
    _, rows, channels = streams.shape
    edge = halo.shape[1]
    blocks, _, terms = rate_rows.shape
    parts = blocks // STEPS
    wide = channels // STEPS
    lanes = channels // blocks
    filters = terms // modes
    by_block = lambda n: (0, n)
    lead = lambda n: (0, 0, n)
    whole = lambda n: (n, 0, 0)
    return pl.pallas_call(
        functools.partial(hyena_near_body, modes),
        grid=(STEPS,),
        in_specs=[
            pl.BlockSpec((1, rows, wide), lead),
            pl.BlockSpec((1, edge, wide), lead),
            pl.BlockSpec((3, 3, wide), lead),
            pl.BlockSpec((rows, wide), by_block),
            pl.BlockSpec((parts, 1, terms), whole),
            pl.BlockSpec((parts, 1, terms), whole),
        ],
        out_specs=[
            pl.BlockSpec((rows, wide), by_block),
            pl.BlockSpec((rows, wide), by_block),
        ],
        out_shape=[
            jax.ShapeDtypeStruct((rows, channels), F32),
            jax.ShapeDtypeStruct((rows, channels), F32),
        ],
        scratch_shapes=[
            pltpu.VMEM((parts, rows, filters * rows), BF16),
            pltpu.VMEM((parts, filters * rows, lanes), BF16),
        ],
        compiler_params=limits(58),
        cost_estimate=cost(2 * rows * rows * filters * channels, 12 * rows * channels),
        name="hyena_near",
    )(streams, halo, short_weight, mixed, rate_rows, res_rows)


def hyena_out_body(modes, near_ref, q_ref, carried_ref, rate_ref, res_ref, out_ref):
    rows = near_ref.shape[0]
    parts, _, terms = rate_ref.shape
    lanes = near_ref.shape[1] // parts
    filters = terms // modes
    width = lanes // filters
    lag = (1 + lax.broadcasted_iota(jnp.int32, (rows, terms), 0)).astype(F32)
    own = same_filter(modes, width, terms, lanes)
    for part in range(parts):
        at = slice(part * lanes, (part + 1) * lanes)
        rate = rate_ref[part]
        coeff = res_ref[part] * jnp.sqrt(2.0 * rate / modes)
        powers = coeff * jnp.exp(-rate * lag)
        p_high = powers.astype(BF16)
        p_low = (powers - p_high.astype(F32)).astype(BF16)
        carried = jnp.where(own, jnp.concatenate([carried_ref[:, at]] * filters, axis=0), 0.0)
        c_high = carried.astype(BF16)
        c_low = (carried - c_high.astype(F32)).astype(BF16)
        far = (
            jnp.dot(p_high, c_high, preferred_element_type=F32)
            + jnp.dot(p_low, c_high, preferred_element_type=F32)
            + jnp.dot(p_high, c_low, preferred_element_type=F32)
        )
        out_ref[:, at] = (q_ref[:, at] * (near_ref[:, at] + far)).astype(BF16)


def hyena_finish(near, query, carried, rate_rows, res_rows, modes):
    rows, channels = near.shape
    blocks, _, terms = rate_rows.shape
    parts = blocks // STEPS
    wide = channels // STEPS
    by_block = lambda n: (0, n)
    whole = lambda n: (n, 0, 0)
    return pl.pallas_call(
        functools.partial(hyena_out_body, modes),
        grid=(STEPS,),
        in_specs=[
            pl.BlockSpec((rows, wide), by_block),
            pl.BlockSpec((rows, wide), by_block),
            pl.BlockSpec((modes, wide), by_block),
            pl.BlockSpec((parts, 1, terms), whole),
            pl.BlockSpec((parts, 1, terms), whole),
        ],
        out_specs=pl.BlockSpec((rows, wide), by_block),
        out_shape=jax.ShapeDtypeStruct((rows, channels), BF16),
        compiler_params=limits(58),
        cost_estimate=cost(6 * rows * terms * channels, 10 * rows * channels),
        name="hyena_finish",
    )(near, query, carried, rate_rows, res_rows)


def scan_states(ends, rate, rows):
    half = ends.shape[1] // 2
    index = lax.axis_index("ctx")
    count = lax.axis_size("ctx") // ROW
    core, side = index % 2, index // 2 % 2
    take = lambda matrix, which: lax.dynamic_slice_in_dim(matrix, which * half, half, 1)
    rate = take(rate, core)
    decay = lambda blocks: jnp.exp(-rate * float(rows * blocks))
    mine = take(ends, core)
    theirs = flip(take(ends, 1 - core), "ctx", 1)
    even = jnp.where(core == 0, mine, theirs)
    odd = jnp.where(core == 0, theirs, mine)
    chip = decay(1) * even + odd
    other = flip(chip, "ctx", 2)
    left = jnp.where(side == 0, chip, other)
    total = decay(2) * left + jnp.where(side == 0, other, chip)
    before = ahead(total, "ctx", ROW)
    reach = 2
    while reach < count:
        upto = total + decay(ROW) * before
        earlier = ahead(upto, "ctx", ROW * reach)
        before = before + decay(ROW * (reach - 1)) * earlier
        reach *= 2
    before = jnp.where(side == 0, before, decay(2) * before + left)
    second = decay(1) * before + even
    keep = jnp.where(core == 0, before, second)
    back = flip(jnp.where(core == 0, second, before), "ctx", 1)
    return jnp.concatenate(
        [jnp.where(core == 0, keep, back), jnp.where(core == 0, back, keep)], axis=1
    )


def lanes_from(start, size):
    return pl.ds(pl.multiple_of(start * size, size), size)


def halve_body(at_ref, streams_ref, out_ref):
    del at_ref
    out_ref[...] = streams_ref[...]


def halve(which, streams):
    count, rows, channels = streams.shape
    half = channels // 2
    return pl.pallas_call(
        halve_body,
        grid_spec=pltpu.PrefetchScalarGridSpec(
            num_scalar_prefetch=1,
            grid=(1,),
            in_specs=[pl.BlockSpec((count, rows, half), lambda n, at: (0, 0, at[0]))],
            out_specs=pl.BlockSpec((count, rows, half), lambda n, at: (0, 0, 0)),
        ),
        out_shape=jax.ShapeDtypeStruct((count, rows, half), streams.dtype),
        compiler_params=limits(8),
        cost_estimate=cost(0, 4 * count * rows * half),
        name="halve",
    )(which, streams)


def last_rows(streams):
    count, rows, channels = streams.shape
    return pl.pallas_call(
        lambda rows_ref, out_ref: out_ref.__setitem__(..., rows_ref[:, EDGE:]),
        grid=(1,),
        in_specs=[pl.BlockSpec((count, 2 * EDGE, channels), lambda n: (0, rows // (2 * EDGE) - 1, 0))],
        out_specs=pl.BlockSpec((count, EDGE, channels), lambda n: (0, 0, 0)),
        out_shape=jax.ShapeDtypeStruct((count, EDGE, channels), streams.dtype),
        compiler_params=limits(58),
        cost_estimate=cost(0, 4 * count * EDGE * channels),
        name="last_rows",
    )(streams)


def pack_body(first, at_ref, streams_ref, theirs_ref, *outs):
    core, side = at_ref[0], at_ref[1]
    quarter = theirs_ref.shape[2] // 2
    for out, away in zip(outs, (0, 1)[-len(outs) :]):
        to = 1 - side if away else side
        for stream in range(first, 3):
            out[0, stream - first] = streams_ref[stream, :, lanes_from(2 * core + to, quarter)]
            out[1, stream - first] = theirs_ref[stream, :, lanes_from(to, quarter)]


def pack(where, streams, theirs, first, amount):
    _, rows, half = theirs.shape
    shape = jax.ShapeDtypeStruct((2, 3 - first, rows, half // 2), BF16)
    return pl.pallas_call(
        functools.partial(pack_body, first),
        in_specs=[SMEM, VMEM, VMEM],
        out_specs=[VMEM] * amount,
        out_shape=[shape] * amount,
        compiler_params=limits(10),
        cost_estimate=cost(0, 8 * amount * rows * half),
        name="pack",
    )(where, streams, theirs)


def onward_body(at_ref, own, cross, out, held, sems):
    place = at_ref[2]
    for block in range(1, ROW):
        slot = place ^ block
        into = held.at[block - 1]

        @pl.when(slot < 2)
        def _():
            pltpu.make_async_copy(own.at[slot], into, sems.at[block - 1]).start()

        @pl.when(slot >= 2)
        def _():
            pltpu.make_async_copy(cross.at[slot - 2], into, sems.at[block - 1]).start()

    leave = []
    for block in range(1, ROW):
        into = held.at[block - 1]
        pltpu.make_async_copy(own.at[0], into, sems.at[block - 1]).wait()
        leave.append(pltpu.make_async_copy(into, out.at[block - 1], sems.at[ROW + block - 2]))
        leave[-1].start()
    for copy in leave:
        copy.wait()


def onward(where, own, cross):
    shape = (ROW - 1,) + own.shape[1:]
    return pl.pallas_call(
        onward_body,
        in_specs=[SMEM, ANY, ANY],
        out_specs=ANY,
        out_shape=jax.ShapeDtypeStruct(shape, BF16),
        scratch_shapes=[pltpu.VMEM(shape, BF16), pltpu.SemaphoreType.DMA((2 * ROW - 2,))],
        compiler_params=limits(8),
        cost_estimate=cost(0, 4 * own.size),
        name="onward",
    )(where, own, cross)


FIXED = 4


def contig_start(info_ref, docs, position):
    first = jnp.zeros_like(position)
    bound = jnp.int32(0)
    for n in range(docs):
        bound = bound + info_ref[FIXED + n]
        first = jnp.where(position >= bound, bound, first)
    return first


def row_part(info_ref, streams, theirs, swap, slot, stream, quarter):
    core, side = info_ref[0], info_ref[1]
    if slot == 0:
        return streams.at[stream, :, lanes_from(2 * core + side, quarter)]
    if slot == 1:
        return theirs.at[stream, :, lanes_from(side, quarter)]
    return swap.at[slot - 2, stream]


SCALE = math.log2(math.e) / math.sqrt(HEAD)


def attend_body(docs, info_ref, streams, theirs, swap, own, cross, acc_ref, m_ref, l_ref, q_s, k_s, v_s, sems):
    place, base = info_ref[2], info_ref[3]
    rows, quarter = q_s.shape[1:]
    copies = []

    def bring(source, target):
        copies.append(pltpu.make_async_copy(source, target, sems.at[len(copies)]))
        copies[-1].start()

    for slot in range(ROW):
        part = lambda stream: row_part(info_ref, streams, theirs, swap, slot, stream, quarter)
        old = own.at[slot] if slot < 2 else cross.at[slot - 2]
        block = place ^ slot
        older = lanes_from(block, rows)
        newer = lanes_from(ROW + block, rows)
        bring(part(0), q_s.at[block])
        bring(part(1), k_s.at[newer])
        bring(part(2), v_s.at[newer])
        bring(old.at[0], k_s.at[older])
        bring(old.at[1], v_s.at[older])
    for copy in copies:
        copy.wait()

    for block in range(ROW):
        width = (ROW + 1 + block) * rows
        position = base + block * rows + lax.broadcasted_iota(jnp.int32, (rows, 1), 0)
        first = contig_start(info_ref, docs, position)
        at = base - ROW * rows + lax.broadcasted_iota(jnp.int32, (rows, width), 1)
        allowed = (at >= first) & (at <= position)
        for head in range(quarter // HEAD):
            lanes = slice(head * HEAD, (head + 1) * HEAD)
            scores = lax.dot_general(
                q_s[block, :, lanes],
                k_s[0:width, lanes],
                (((1,), (1,)), ((), ())),
                preferred_element_type=F32,
            )
            scores = jnp.where(allowed, scores, -jnp.inf)
            top = jnp.max(scores, axis=1, keepdims=True)
            weight = jnp.exp2((scores - top) * SCALE)
            m_ref[block, :, lanes] = jnp.broadcast_to(top, (rows, HEAD))
            l_ref[block, :, lanes] = jnp.broadcast_to(jnp.sum(weight, axis=1, keepdims=True), (rows, HEAD))
            acc_ref[block, :, lanes] = jnp.dot(
                weight.astype(BF16), v_s[0:width, lanes], preferred_element_type=F32
            )


def attend(info, docs, streams, theirs, swap, own, cross):
    _, _, rows, quarter = own.shape
    heads = quarter // HEAD
    return pl.pallas_call(
        functools.partial(attend_body, docs),
        in_specs=[SMEM] + [ANY] * 5,
        out_specs=[VMEM] * 3,
        out_shape=[
            jax.ShapeDtypeStruct((ROW, rows, quarter), F32),
        ]
        * 3,
        scratch_shapes=[
            pltpu.VMEM((ROW, rows, quarter), BF16),
            pltpu.VMEM((2 * ROW * rows, quarter), BF16),
            pltpu.VMEM((2 * ROW * rows, quarter), BF16),
            pltpu.SemaphoreType.DMA((5 * ROW,)),
        ],
        compiler_params=limits(20),
        cost_estimate=cost(26 * 4 * rows * rows * quarter, 14 * ROW * rows * quarter, 26 * heads * rows * rows),
        name="attend",
    )(info, streams, theirs, swap, own, cross)


def attend_last_body(
    docs, info_ref, streams, theirs, swap, oldest, acc_ref, m_ref, l_ref, out0, out1, out2, out3, q_s, o_s, sems
):
    place, base = info_ref[2], info_ref[3]
    rows, quarter = q_s.shape[1:]
    copies = []
    for slot in range(ROW):
        part = row_part(info_ref, streams, theirs, swap, slot, 0, quarter)
        copies.append(pltpu.make_async_copy(part, q_s.at[place ^ slot], sems.at[slot]))
        copies[-1].start()
    for copy in copies:
        copy.wait()
    for block in range(ROW):
        slot = place ^ block
        seen = ROW - 1 - block
        width = seen * rows
        if seen:
            position = base + block * rows + lax.broadcasted_iota(jnp.int32, (rows, 1), 0)
            first = contig_start(info_ref, docs, position)
            at = base - (ROW + seen) * rows + lax.broadcasted_iota(jnp.int32, (rows, width), 1)
            allowed = at >= first
        for head in range(quarter // HEAD):
            lanes = slice(head * HEAD, (head + 1) * HEAD)
            total = acc_ref[block, :, lanes]
            below = l_ref[block, :, lanes]
            if seen:
                keys = oldest[block : ROW - 1, 0, :, lanes].reshape(width, HEAD)
                values = oldest[block : ROW - 1, 1, :, lanes].reshape(width, HEAD)
                scores = lax.dot_general(
                    q_s[block, :, lanes],
                    keys,
                    (((1,), (1,)), ((), ())),
                    preferred_element_type=F32,
                )
                scores = jnp.where(allowed, scores, -jnp.inf)
                past = m_ref[block, :, lanes]
                top = jnp.maximum(past, jnp.max(scores, axis=1, keepdims=True))
                fade = jnp.exp2((past - top) * SCALE)
                weight = jnp.exp2((scores - jnp.concatenate([top] * seen, axis=1)) * SCALE)
                share = 1.0 / (below * fade + jnp.sum(weight, axis=1, keepdims=True))
                total = total * (fade * share) + share * jnp.dot(
                    weight.astype(BF16), values, preferred_element_type=F32
                )
            else:
                total = total * (1.0 / below)
            o_s[slot, :, lanes] = total.astype(BF16)
    for slot, out in enumerate((out0, out1, out2, out3)):
        out[...] = o_s[slot]


def attend_last(info, docs, streams, theirs, swap, oldest, acc, top, below):
    _, rows, quarter = acc.shape
    heads = quarter // HEAD
    return pl.pallas_call(
        functools.partial(attend_last_body, docs),
        in_specs=[SMEM] + [ANY] * 3 + [VMEM] * 4,
        out_specs=[VMEM] * ROW,
        out_shape=[jax.ShapeDtypeStruct((rows, quarter), BF16)] * ROW,
        scratch_shapes=[
            pltpu.VMEM((ROW, rows, quarter), BF16),
            pltpu.VMEM((ROW, rows, quarter), BF16),
            pltpu.SemaphoreType.DMA((ROW,)),
        ],
        compiler_params=limits(16),
        cost_estimate=cost(6 * 4 * rows * rows * quarter, 12 * ROW * rows * quarter, 6 * heads * rows * rows),
        name="attend_last",
    )(info, streams, theirs, swap, oldest, acc, top, below)


def assemble_body(at_ref, *refs):
    place = at_ref[2]
    *pieces, out_ref = refs
    quarter = pieces[0].shape[1]
    for slot, piece in enumerate(pieces):
        maker = place ^ slot
        which = 2 * (maker & 1) + lax.shift_right_logical(maker, 1)
        out_ref[:, lanes_from(which, quarter)] = piece[...]


def assemble(where, pieces):
    rows, quarter = pieces[0].shape
    return pl.pallas_call(
        assemble_body,
        in_specs=[SMEM] + [VMEM] * ROW,
        out_specs=VMEM,
        out_shape=jax.ShapeDtypeStruct((rows, ROW * quarter), BF16),
        compiler_params=limits(6),
        cost_estimate=cost(0, 16 * rows * quarter),
        name="assemble",
    )(where, *pieces)


def on_device(hyena_qkv, short_weight, filter_rate, filter_residue, attn_qkv, doc_lengths):
    rows, _, channels = attn_qkv.shape
    modes = filter_rate.shape[1]
    docs = doc_lengths.shape[0]
    index = lax.axis_index("ctx")
    place = index % ROW
    core, side = place % 2, place // 2
    fixed = jnp.stack([core, side, place, (index - place) * rows]).astype(jnp.int32)
    info = jnp.concatenate([fixed, doc_lengths])

    inner = hyena_qkv.transpose(1, 0, 2)
    edge = ahead(last_rows(inner), "ctx", 1)

    streams = attn_qkv.transpose(1, 0, 2)
    theirs = flip(halve((1 - core).reshape(1).astype(jnp.int32), streams), "ctx", 1)
    own, cross = pack(fixed, streams, theirs, 1, 2)
    own = ahead(own, "ctx", ROW)
    cross = ahead(cross, "ctx", ROW, 2)
    (swap,) = pack(fixed, streams, theirs, 0, 1)
    swap = flip(swap, "ctx", 2)
    oldest = ahead(onward(fixed, own, cross), "ctx", ROW)

    blocks = channels // LANES
    rate_rows = filter_rate.reshape(blocks, 1, -1)
    res_rows = filter_residue.reshape(blocks, 1, -1)
    mixed, ends, wide = hyena_ends(inner, edge, short_weight, rate_rows, modes)
    near, query = hyena_near(inner, edge, short_weight, mixed, rate_rows, res_rows, modes)
    carried = scan_states(ends, wide, rows)
    hyena_out = hyena_finish(near, query, carried, rate_rows, res_rows, modes)

    acc, top, below = attend(info, docs, streams, theirs, swap, own, cross)
    made = attend_last(info, docs, streams, theirs, swap, oldest, acc, top, below)
    pieces = [made[0]] + [flip(made[n], "ctx", n) for n in range(1, ROW)]
    attn_out = assemble(fixed, pieces)
    return (hyena_out, attn_out)


def solution(mesh):
    in_specs = (
        P(("group", "ctx"), None, None),
        P(),
        P(),
        P(),
        P(("group", "ctx"), None, None),
        P("group"),
    )
    out_specs = (P(("group", "ctx"), None), P(("group", "ctx"), None))
    return jax.shard_map(
        on_device, mesh=mesh, in_specs=in_specs, out_specs=out_specs, check_vma=False
    )
```

```python
import functools
import math

import jax
import jax.numpy as jnp
from jax import lax
from jax.experimental import pallas as pl
from jax.experimental.pallas import tpu as pltpu
from jax.sharding import PartitionSpec as P


HEAD = 128
LANES = 128
EDGE = 8
ROW = 4

F32 = jnp.float32
BF16 = jnp.bfloat16


def flip(value, axis, bit):
    count = lax.axis_size(axis)
    return lax.ppermute(value, axis, [(at, at ^ bit) for at in range(count)])


def ahead(value, axis, steps, bit=0, first=0):
    count = lax.axis_size(axis)
    pairs = [(at, (at + steps) ^ bit) for at in range(first, count - steps)]
    return lax.ppermute(value, axis, pairs)


def limits(mib):
    return pltpu.CompilerParams(vmem_limit_bytes=mib << 20)


def cost(flops, moved, exps=0):
    return pl.CostEstimate(flops=flops, bytes_accessed=moved, transcendentals=exps)


VMEM = pl.BlockSpec(memory_space=pltpu.VMEM)
SMEM = pl.BlockSpec(memory_space=pltpu.SMEM)
ANY = pl.BlockSpec(memory_space=pl.ANY)


def same_filter(modes, width, terms, lanes):
    row_at = lax.broadcasted_iota(jnp.int32, (terms, lanes), 0)
    lane_at = lax.broadcasted_iota(jnp.int32, (terms, lanes), 1)
    kept = None
    for g in range(terms // modes):
        both = (
            (row_at >= g * modes)
            & (row_at < (g + 1) * modes)
            & (lane_at >= g * width)
            & (lane_at < (g + 1) * width)
        )
        kept = both if kept is None else kept | both
    return kept


def feature(x, halo, w_ref, stream, at):
    here = x.astype(F32)
    halo = halo.astype(F32)
    edge = halo.shape[0]
    row_at = lax.broadcasted_iota(jnp.int32, here.shape, 0)
    one = jnp.where(row_at == 0, halo[edge - 1 :], pltpu.roll(here, 1, 0))
    two = jnp.where(row_at == 1, halo[edge - 1 :], pltpu.roll(here, 2, 0))
    two = jnp.where(row_at == 0, halo[edge - 2 : edge - 1], two)
    tap = [w_ref[n, stream : stream + 1, at] for n in range(3)]
    return tap[0] * here + tap[1] * one + tap[2] * two


def hyena_ends_body(modes, x_ref, halo_ref, w_ref, rate_ref, mixed_ref, ends_ref, wide_ref):
    rows = x_ref.shape[1]
    parts, _, terms = rate_ref.shape
    lanes = x_ref.shape[2] // parts
    filters = terms // modes
    width = lanes // filters
    lag = (rows - 1 - lax.broadcasted_iota(jnp.int32, (terms, rows), 1)).astype(F32)
    own = same_filter(modes, width, terms, lanes)
    pick = lambda matrix: jnp.sum(jnp.where(own, matrix, 0.0).reshape(filters, modes, lanes), axis=0)
    for part in range(parts):
        at = slice(part * lanes, (part + 1) * lanes)
        key, value = (feature(x_ref[n, :, at], halo_ref[n, :, at], w_ref, n, at) for n in (1, 2))
        mixed = (key * value).astype(BF16)
        mixed_ref[:, at] = mixed
        rate = jnp.broadcast_to(rate_ref[part], (rows, terms)).T
        powers = jnp.exp(-rate * lag)
        high = powers.astype(BF16)
        low = (powers - high.astype(F32)).astype(BF16)
        ends = jnp.dot(high, mixed, preferred_element_type=F32) + jnp.dot(
            low, mixed, preferred_element_type=F32
        )
        ends_ref[:, at] = pick(ends)
        wide_ref[:, at] = pick(rate)


STEPS = 4


def hyena_ends(streams, halo, short_weight, rate_rows, modes):
    _, rows, channels = streams.shape
    edge = halo.shape[1]
    blocks, _, terms = rate_rows.shape
    parts = blocks // STEPS
    wide = channels // STEPS
    by_block = lambda n: (0, n)
    lead = lambda n: (0, 0, n)
    return pl.pallas_call(
        functools.partial(hyena_ends_body, modes),
        grid=(STEPS,),
        in_specs=[
            pl.BlockSpec((3, rows, wide), lead),
            pl.BlockSpec((3, edge, wide), lead),
            pl.BlockSpec((3, 3, wide), lead),
            pl.BlockSpec((parts, 1, terms), lambda n: (n, 0, 0)),
        ],
        out_specs=[
            pl.BlockSpec((rows, wide), by_block),
            pl.BlockSpec((modes, wide), by_block),
            pl.BlockSpec((modes, wide), by_block),
        ],
        out_shape=[
            jax.ShapeDtypeStruct((rows, channels), BF16),
            jax.ShapeDtypeStruct((modes, channels), F32),
            jax.ShapeDtypeStruct((modes, channels), F32),
        ],
        compiler_params=limits(16),
        cost_estimate=cost(4 * rows * terms * channels, 8 * rows * channels),
        name="hyena_ends",
    )(streams, halo, short_weight, rate_rows)


def hyena_near_body(modes, x_ref, halo_ref, w_ref, mixed_ref, rate_ref, res_ref, near_ref, q_ref, taps_s, u_s):
    rows = x_ref.shape[1]
    parts, _, terms = rate_ref.shape
    lanes = x_ref.shape[2] // parts
    filters = terms // modes
    width = lanes // filters
    row_at = lax.broadcasted_iota(jnp.int32, (rows, lanes), 0)
    lane_at = lax.broadcasted_iota(jnp.int32, (rows, lanes), 1)
    lag = (rows - 1 - lax.broadcasted_iota(jnp.int32, (terms, rows), 1)).astype(F32)
    zero = jnp.zeros((rows, lanes), BF16)
    for part in range(parts):
        at = slice(part * lanes, (part + 1) * lanes)
        q_ref[:, at] = feature(x_ref[0, :, at], halo_ref[0, :, at], w_ref, 0, at)
        mixed = mixed_ref[:, at]
        coeff = res_ref[part] * jnp.sqrt(2.0 * rate_ref[part] / modes)
        rate = jnp.broadcast_to(rate_ref[part], (rows, terms)).T
        coeff = jnp.broadcast_to(coeff, (rows, terms)).T
        powers = coeff * jnp.exp(-rate * lag)
        backward = jnp.sum(powers.reshape(filters, modes, rows), axis=1)
        for g in range(filters):
            spread = jnp.broadcast_to(backward[g : g + 1], (rows, rows))
            shifted = pltpu.roll(spread, 1, 1, stride=1, stride_axis=0)
            kept = jnp.where(lane_at <= row_at, shifted, 0.0)
            taps_s[part, :, g * rows : (g + 1) * rows] = kept.astype(BF16)
            mine = (lane_at >= g * width) & (lane_at < (g + 1) * width)
            u_s[part, g * rows : (g + 1) * rows, :] = jnp.where(mine, mixed, zero)
        near_ref[:, at] = jnp.dot(taps_s[part], u_s[part], preferred_element_type=F32)


def hyena_near(streams, halo, short_weight, mixed, rate_rows, res_rows, modes):
    _, rows, channels = streams.shape
    edge = halo.shape[1]
    blocks, _, terms = rate_rows.shape
    parts = blocks // STEPS
    wide = channels // STEPS
    lanes = channels // blocks
    filters = terms // modes
    by_block = lambda n: (0, n)
    lead = lambda n: (0, 0, n)
    whole = lambda n: (n, 0, 0)
    return pl.pallas_call(
        functools.partial(hyena_near_body, modes),
        grid=(STEPS,),
        in_specs=[
            pl.BlockSpec((1, rows, wide), lead),
            pl.BlockSpec((1, edge, wide), lead),
            pl.BlockSpec((3, 3, wide), lead),
            pl.BlockSpec((rows, wide), by_block),
            pl.BlockSpec((parts, 1, terms), whole),
            pl.BlockSpec((parts, 1, terms), whole),
        ],
        out_specs=[
            pl.BlockSpec((rows, wide), by_block),
            pl.BlockSpec((rows, wide), by_block),
        ],
        out_shape=[
            jax.ShapeDtypeStruct((rows, channels), F32),
            jax.ShapeDtypeStruct((rows, channels), F32),
        ],
        scratch_shapes=[
            pltpu.VMEM((parts, rows, filters * rows), BF16),
            pltpu.VMEM((parts, filters * rows, lanes), BF16),
        ],
        compiler_params=limits(58),
        cost_estimate=cost(2 * rows * rows * filters * channels, 12 * rows * channels),
        name="hyena_near",
    )(streams, halo, short_weight, mixed, rate_rows, res_rows)


def hyena_out_body(modes, near_ref, q_ref, carried_ref, rate_ref, res_ref, out_ref):
    rows = near_ref.shape[0]
    parts, _, terms = rate_ref.shape
    lanes = near_ref.shape[1] // parts
    filters = terms // modes
    width = lanes // filters
    lag = (1 + lax.broadcasted_iota(jnp.int32, (rows, terms), 0)).astype(F32)
    own = same_filter(modes, width, terms, lanes)
    for part in range(parts):
        at = slice(part * lanes, (part + 1) * lanes)
        rate = rate_ref[part]
        coeff = res_ref[part] * jnp.sqrt(2.0 * rate / modes)
        powers = coeff * jnp.exp(-rate * lag)
        p_high = powers.astype(BF16)
        p_low = (powers - p_high.astype(F32)).astype(BF16)
        carried = jnp.where(own, jnp.concatenate([carried_ref[:, at]] * filters, axis=0), 0.0)
        c_high = carried.astype(BF16)
        c_low = (carried - c_high.astype(F32)).astype(BF16)
        far = (
            jnp.dot(p_high, c_high, preferred_element_type=F32)
            + jnp.dot(p_low, c_high, preferred_element_type=F32)
            + jnp.dot(p_high, c_low, preferred_element_type=F32)
        )
        out_ref[:, at] = (q_ref[:, at] * (near_ref[:, at] + far)).astype(BF16)


def hyena_finish(near, query, carried, rate_rows, res_rows, modes):
    rows, channels = near.shape
    blocks, _, terms = rate_rows.shape
    parts = blocks // STEPS
    wide = channels // STEPS
    by_block = lambda n: (0, n)
    whole = lambda n: (n, 0, 0)
    return pl.pallas_call(
        functools.partial(hyena_out_body, modes),
        grid=(STEPS,),
        in_specs=[
            pl.BlockSpec((rows, wide), by_block),
            pl.BlockSpec((rows, wide), by_block),
            pl.BlockSpec((modes, wide), by_block),
            pl.BlockSpec((parts, 1, terms), whole),
            pl.BlockSpec((parts, 1, terms), whole),
        ],
        out_specs=pl.BlockSpec((rows, wide), by_block),
        out_shape=jax.ShapeDtypeStruct((rows, channels), BF16),
        compiler_params=limits(58),
        cost_estimate=cost(6 * rows * terms * channels, 10 * rows * channels),
        name="hyena_finish",
    )(near, query, carried, rate_rows, res_rows)


def scan_states(ends, rate, rows):
    half = ends.shape[1] // 2
    index = lax.axis_index("ctx")
    count = lax.axis_size("ctx") // ROW
    core, side = index % 2, index // 2 % 2
    take = lambda matrix, which: lax.dynamic_slice_in_dim(matrix, which * half, half, 1)
    rate = take(rate, core)
    decay = lambda blocks: jnp.exp(-rate * float(rows * blocks))
    mine = take(ends, core)
    theirs = flip(take(ends, 1 - core), "ctx", 1)
    even = jnp.where(core == 0, mine, theirs)
    odd = jnp.where(core == 0, theirs, mine)
    chip = decay(1) * even + odd
    other = flip(chip, "ctx", 2)
    left = jnp.where(side == 0, chip, other)
    total = decay(2) * left + jnp.where(side == 0, other, chip)
    before = ahead(total, "ctx", ROW)
    reach = 2
    while reach < count:
        upto = total + decay(ROW) * before
        earlier = ahead(upto, "ctx", ROW * reach)
        before = before + decay(ROW * (reach - 1)) * earlier
        reach *= 2
    before = jnp.where(side == 0, before, decay(2) * before + left)
    second = decay(1) * before + even
    keep = jnp.where(core == 0, before, second)
    back = flip(jnp.where(core == 0, second, before), "ctx", 1)
    return jnp.concatenate(
        [jnp.where(core == 0, keep, back), jnp.where(core == 0, back, keep)], axis=1
    )


def lanes_from(start, size):
    return pl.ds(pl.multiple_of(start * size, size), size)


def front_body(at_ref, attn, hyena, theirs_ref, edge_ref, sems):
    rows, half = theirs_ref.shape[1:]
    away = attn.at[:, :, lanes_from(1 - at_ref[0], half)]
    edge = hyena.at[:, rows - EDGE : rows, :]
    copies = [
        pltpu.make_async_copy(away, theirs_ref, sems.at[0]),
        pltpu.make_async_copy(edge, edge_ref, sems.at[1]),
    ]
    for copy in copies:
        copy.start()
    for copy in copies:
        copy.wait()


def front(where, attn, hyena):
    count, rows, channels = attn.shape
    return pl.pallas_call(
        front_body,
        in_specs=[SMEM, ANY, ANY],
        out_specs=[VMEM, VMEM],
        out_shape=[
            jax.ShapeDtypeStruct((count, rows, channels // 2), attn.dtype),
            jax.ShapeDtypeStruct((count, EDGE, channels), hyena.dtype),
        ],
        scratch_shapes=[pltpu.SemaphoreType.DMA((2,))],
        compiler_params=limits(58),
        cost_estimate=cost(0, 4 * count * rows * channels // 2),
        name="front",
    )(where, attn, hyena)


def pack_body(first, at_ref, streams_ref, theirs_ref, *outs):
    core, side = at_ref[0], at_ref[1]
    quarter = theirs_ref.shape[2] // 2
    for out, away in zip(outs, (0, 1)[-len(outs) :]):
        to = 1 - side if away else side
        for stream in range(first, 3):
            out[0, stream - first] = streams_ref[stream, :, lanes_from(2 * core + to, quarter)]
            out[1, stream - first] = theirs_ref[stream, :, lanes_from(to, quarter)]


def pack(where, streams, theirs, first, amount):
    _, rows, half = theirs.shape
    shape = jax.ShapeDtypeStruct((2, 3 - first, rows, half // 2), BF16)
    return pl.pallas_call(
        functools.partial(pack_body, first),
        in_specs=[SMEM, VMEM, VMEM],
        out_specs=[VMEM] * amount,
        out_shape=[shape] * amount,
        compiler_params=limits(10),
        cost_estimate=cost(0, 8 * amount * rows * half),
        name="pack",
    )(where, streams, theirs)


FIXED = 4


def contig_start(info_ref, docs, position):
    first = jnp.zeros_like(position)
    bound = jnp.int32(0)
    for n in range(docs):
        bound = bound + info_ref[FIXED + n]
        first = jnp.where(position >= bound, bound, first)
    return first


def row_part(info_ref, streams, theirs, swap, slot, stream, quarter):
    core, side = info_ref[0], info_ref[1]
    if slot == 0:
        return streams.at[stream, :, lanes_from(2 * core + side, quarter)]
    if slot == 1:
        return theirs.at[stream, :, lanes_from(side, quarter)]
    return swap.at[slot - 2, stream]


SCALE = math.log2(math.e) / math.sqrt(HEAD)


def attend_body(docs, info_ref, streams, theirs, swap, own, cross, acc_ref, m_ref, l_ref, q_s, k_s, v_s, sems):
    place, base = info_ref[2], info_ref[3]
    rows, quarter = q_s.shape[1:]
    copies = []

    def bring(source, target):
        copies.append(pltpu.make_async_copy(source, target, sems.at[len(copies)]))
        copies[-1].start()

    for slot in range(ROW):
        part = lambda stream: row_part(info_ref, streams, theirs, swap, slot, stream, quarter)
        old = own.at[slot] if slot < 2 else cross.at[slot - 2]
        block = place ^ slot
        older = lanes_from(block, rows)
        newer = lanes_from(ROW + block, rows)
        bring(part(0), q_s.at[block])
        bring(part(1), k_s.at[newer])
        bring(part(2), v_s.at[newer])
        bring(old.at[0], k_s.at[older])
        bring(old.at[1], v_s.at[older])
    for copy in copies:
        copy.wait()

    for block in range(ROW):
        width = (ROW + 1 + block) * rows
        position = base + block * rows + lax.broadcasted_iota(jnp.int32, (rows, 1), 0)
        first = contig_start(info_ref, docs, position)
        at = base - ROW * rows + lax.broadcasted_iota(jnp.int32, (rows, width), 1)
        allowed = (at >= first) & (at <= position)
        for head in range(quarter // HEAD):
            lanes = slice(head * HEAD, (head + 1) * HEAD)
            scores = lax.dot_general(
                q_s[block, :, lanes],
                k_s[0:width, lanes],
                (((1,), (1,)), ((), ())),
                preferred_element_type=F32,
            )
            scores = jnp.where(allowed, scores, -jnp.inf)
            top = jnp.max(scores, axis=1, keepdims=True)
            weight = jnp.exp2((scores - top) * SCALE)
            m_ref[block, :, lanes] = jnp.broadcast_to(top, (rows, HEAD))
            l_ref[block, :, lanes] = jnp.broadcast_to(jnp.sum(weight, axis=1, keepdims=True), (rows, HEAD))
            acc_ref[block, :, lanes] = jnp.dot(
                weight.astype(BF16), v_s[0:width, lanes], preferred_element_type=F32
            )


def attend(info, docs, streams, theirs, swap, own, cross):
    _, _, rows, quarter = own.shape
    heads = quarter // HEAD
    return pl.pallas_call(
        functools.partial(attend_body, docs),
        in_specs=[SMEM] + [ANY] * 5,
        out_specs=[VMEM] * 3,
        out_shape=[
            jax.ShapeDtypeStruct((ROW, rows, quarter), F32),
        ]
        * 3,
        scratch_shapes=[
            pltpu.VMEM((ROW, rows, quarter), BF16),
            pltpu.VMEM((2 * ROW * rows, quarter), BF16),
            pltpu.VMEM((2 * ROW * rows, quarter), BF16),
            pltpu.SemaphoreType.DMA((5 * ROW,)),
        ],
        compiler_params=limits(20),
        cost_estimate=cost(26 * 4 * rows * rows * quarter, 14 * ROW * rows * quarter, 26 * heads * rows * rows),
        name="attend",
    )(info, streams, theirs, swap, own, cross)


def attend_last_body(
    docs, info_ref, streams, theirs, swap, own, cross, acc_ref, m_ref, l_ref, out0, out1, out2, out3, q_s, kv_s, o_s, sems
):
    place, base = info_ref[2], info_ref[3]
    rows, quarter = q_s.shape[1:]
    copies = []

    def bring(source, target):
        copies.append(pltpu.make_async_copy(source, target, sems.at[len(copies)]))
        copies[-1].start()

    for slot in range(ROW):
        block = place ^ slot
        bring(row_part(info_ref, streams, theirs, swap, slot, 0, quarter), q_s.at[block])
        bring(own.at[slot] if slot < 2 else cross.at[slot - 2], kv_s.at[block])
    for copy in copies:
        copy.wait()
    for block in range(ROW):
        slot = place ^ block
        seen = ROW - 1 - block
        width = seen * rows
        if seen:
            position = base + block * rows + lax.broadcasted_iota(jnp.int32, (rows, 1), 0)
            first = contig_start(info_ref, docs, position)
            at = base - (ROW + seen) * rows + lax.broadcasted_iota(jnp.int32, (rows, width), 1)
            allowed = at >= first
        for head in range(quarter // HEAD):
            lanes = slice(head * HEAD, (head + 1) * HEAD)
            total = acc_ref[block, :, lanes]
            below = l_ref[block, :, lanes]
            if seen:
                keys = kv_s[block + 1 : ROW, 0, :, lanes].reshape(width, HEAD)
                values = kv_s[block + 1 : ROW, 1, :, lanes].reshape(width, HEAD)
                scores = lax.dot_general(
                    q_s[block, :, lanes],
                    keys,
                    (((1,), (1,)), ((), ())),
                    preferred_element_type=F32,
                )
                scores = jnp.where(allowed, scores, -jnp.inf)
                past = m_ref[block, :, lanes]
                top = jnp.maximum(past, jnp.max(scores, axis=1, keepdims=True))
                fade = jnp.exp2((past - top) * SCALE)
                weight = jnp.exp2((scores - jnp.concatenate([top] * seen, axis=1)) * SCALE)
                share = 1.0 / (below * fade + jnp.sum(weight, axis=1, keepdims=True))
                total = total * (fade * share) + share * jnp.dot(
                    weight.astype(BF16), values, preferred_element_type=F32
                )
            else:
                total = total * (1.0 / below)
            o_s[slot, :, lanes] = total.astype(BF16)
    for slot, out in enumerate((out0, out1, out2, out3)):
        out[...] = o_s[slot]


def attend_last(info, docs, streams, theirs, swap, own, cross, acc, top, below):
    _, rows, quarter = acc.shape
    heads = quarter // HEAD
    return pl.pallas_call(
        functools.partial(attend_last_body, docs),
        in_specs=[SMEM] + [ANY] * 5 + [VMEM] * 3,
        out_specs=[VMEM] * ROW,
        out_shape=[jax.ShapeDtypeStruct((rows, quarter), BF16)] * ROW,
        scratch_shapes=[
            pltpu.VMEM((ROW, rows, quarter), BF16),
            pltpu.VMEM((ROW, 2, rows, quarter), BF16),
            pltpu.VMEM((ROW, rows, quarter), BF16),
            pltpu.SemaphoreType.DMA((2 * ROW,)),
        ],
        compiler_params=limits(16),
        cost_estimate=cost(6 * 4 * rows * rows * quarter, 12 * ROW * rows * quarter, 6 * heads * rows * rows),
        name="attend_last",
    )(info, streams, theirs, swap, own, cross, acc, top, below)


def assemble_body(at_ref, *refs):
    place = at_ref[2]
    *pieces, out_ref = refs
    quarter = pieces[0].shape[1]
    for slot, piece in enumerate(pieces):
        maker = place ^ slot
        which = 2 * (maker & 1) + lax.shift_right_logical(maker, 1)
        out_ref[:, lanes_from(which, quarter)] = piece[...]


def assemble(where, pieces):
    rows, quarter = pieces[0].shape
    return pl.pallas_call(
        assemble_body,
        in_specs=[SMEM] + [VMEM] * ROW,
        out_specs=VMEM,
        out_shape=jax.ShapeDtypeStruct((rows, ROW * quarter), BF16),
        compiler_params=limits(6),
        cost_estimate=cost(0, 16 * rows * quarter),
        name="assemble",
    )(where, *pieces)


def on_device(hyena_qkv, short_weight, filter_rate, filter_residue, attn_qkv, doc_lengths):
    rows, _, channels = attn_qkv.shape
    modes = filter_rate.shape[1]
    docs = doc_lengths.shape[0]
    index = lax.axis_index("ctx")
    place = index % ROW
    core, side = place % 2, place // 2
    fixed = jnp.stack([core, side, place, (index - place) * rows]).astype(jnp.int32)
    info = jnp.concatenate([fixed, doc_lengths])

    inner = hyena_qkv.transpose(1, 0, 2)
    streams = attn_qkv.transpose(1, 0, 2)
    theirs, edge = front(fixed, streams, inner)

    theirs = flip(theirs, "ctx", 1)
    edge = ahead(edge, "ctx", 1)
    own, cross = pack(fixed, streams, theirs, 1, 2)
    cross = ahead(cross, "ctx", ROW, 2)
    own = ahead(own, "ctx", ROW)
    (swap,) = pack(fixed, streams, theirs, 0, 1)
    swap = flip(swap, "ctx", 2)
    older_cross = ahead(cross, "ctx", ROW, 0, ROW)
    older_own = ahead(own, "ctx", ROW, 0, ROW)

    blocks = channels // LANES
    edge, filter_rate, filter_residue = lax.optimization_barrier((edge, filter_rate, filter_residue))
    rate_rows = filter_rate.reshape(blocks, 1, -1)
    res_rows = filter_residue.reshape(blocks, 1, -1)
    mixed, ends, wide = hyena_ends(inner, edge, short_weight, rate_rows, modes)
    near, query = hyena_near(inner, edge, short_weight, mixed, rate_rows, res_rows, modes)
    carried = scan_states(ends, wide, rows)
    hyena_out = hyena_finish(near, query, carried, rate_rows, res_rows, modes)

    acc, top, below = attend(info, docs, streams, theirs, swap, own, cross)
    made = attend_last(info, docs, streams, theirs, swap, older_own, older_cross, acc, top, below)
    pieces = [made[0]] + [flip(made[n], "ctx", n) for n in range(1, ROW)]
    attn_out = assemble(fixed, pieces)
    return (hyena_out, attn_out)


def solution(mesh):
    in_specs = (
        P(("group", "ctx"), None, None),
        P(),
        P(),
        P(),
        P(("group", "ctx"), None, None),
        P("group"),
    )
    out_specs = (P(("group", "ctx"), None), P(("group", "ctx"), None))
    return jax.shard_map(
        on_device, mesh=mesh, in_specs=in_specs, out_specs=out_specs, check_vma=False
    )
```

```python
import functools
import math

import jax
import jax.numpy as jnp
from jax import lax
from jax.experimental import pallas as pl
from jax.experimental.pallas import tpu as pltpu
from jax.sharding import PartitionSpec as P


HEAD = 128
LANES = 128
EDGE = 8
ROW = 4

F32 = jnp.float32
BF16 = jnp.bfloat16


def flip(value, axis, bit):
    count = lax.axis_size(axis)
    return lax.ppermute(value, axis, [(at, at ^ bit) for at in range(count)])


def side_of(at):
    return at // 2 % 2


def ahead(value, axis, steps, bit=0, first=0, side=None):
    count = lax.axis_size(axis)
    pairs = [
        (at, (at + steps) ^ bit)
        for at in range(first, count - steps)
        if side is None or side_of(at) == side
    ]
    return lax.ppermute(value, axis, pairs)


def spot():
    index = lax.axis_index("ctx")
    return index & 1, lax.shift_right_logical(index, 1) & 1, index & (ROW - 1), index // ROW


ALL_VMEM = 67043328


def limits(mib):
    return pltpu.CompilerParams(vmem_limit_bytes=mib << 20)


def cost(flops, moved, exps=0):
    return pl.CostEstimate(flops=flops, bytes_accessed=moved, transcendentals=exps)


VMEM = pl.BlockSpec(memory_space=pltpu.VMEM)
SMEM = pl.BlockSpec(memory_space=pltpu.SMEM)
ANY = pl.BlockSpec(memory_space=pl.ANY)
HBM = pl.BlockSpec(memory_space=pltpu.HBM)


def same_filter(modes, width, terms, lanes):
    row_at = lax.broadcasted_iota(jnp.int32, (terms, lanes), 0)
    lane_at = lax.broadcasted_iota(jnp.int32, (terms, lanes), 1)
    kept = None
    for g in range(terms // modes):
        both = (
            (row_at >= g * modes)
            & (row_at < (g + 1) * modes)
            & (lane_at >= g * width)
            & (lane_at < (g + 1) * width)
        )
        kept = both if kept is None else kept | both
    return kept


def feature(x, halo, w_ref, stream, at):
    here = x.astype(F32)
    halo = halo.astype(F32)
    edge = halo.shape[0]
    row_at = lax.broadcasted_iota(jnp.int32, here.shape, 0)
    one = jnp.where(row_at == 0, halo[edge - 1 :], pltpu.roll(here, 1, 0))
    two = jnp.where(row_at == 1, halo[edge - 1 :], pltpu.roll(here, 2, 0))
    two = jnp.where(row_at == 0, halo[edge - 2 : edge - 1], two)
    tap = [w_ref[n, stream : stream + 1, at] for n in range(3)]
    return tap[0] * here + tap[1] * one + tap[2] * two


def of_step(table_ref):
    groups = table_ref.shape[1]
    return pltpu.roll(table_ref[...], groups - pl.program_id(0) * (groups // STEPS), 1)


def down(table, part, filters, lanes):
    columns = [table[:, part * filters + g : part * filters + g + 1] for g in range(filters)]
    return jnp.concatenate([jnp.broadcast_to(c, (c.shape[0], lanes)) for c in columns], axis=0)


def hyena_ends_body(filters, x_ref, halo_ref, w_ref, rate_ref, mixed_ref, ends_ref, wide_ref):
    rows = x_ref.shape[1]
    modes, groups = rate_ref.shape
    parts = groups // STEPS // filters
    terms = filters * modes
    lanes = x_ref.shape[2] // parts
    width = lanes // filters
    rates = of_step(rate_ref)
    lag = (rows - 1 - lax.broadcasted_iota(jnp.int32, (terms, rows), 1)).astype(F32)
    own = same_filter(modes, width, terms, lanes)
    pick = lambda matrix: jnp.sum(jnp.where(own, matrix, 0.0).reshape(filters, modes, lanes), axis=0)
    for part in range(parts):
        at = slice(part * lanes, (part + 1) * lanes)
        key, value = (feature(x_ref[n, :, at], halo_ref[n, :, at], w_ref, n, at) for n in (1, 2))
        mixed = (key * value).astype(BF16)
        mixed_ref[:, at] = mixed
        rate = down(rates, part, filters, rows)
        powers = jnp.exp(-rate * lag)
        high = powers.astype(BF16)
        low = (powers - high.astype(F32)).astype(BF16)
        ends = jnp.dot(high, mixed, preferred_element_type=F32) + jnp.dot(
            low, mixed, preferred_element_type=F32
        )
        ends_ref[:, at] = pick(ends)
        wide_ref[:, at] = pick(rate)


STEPS = 4


def hyena_ends(streams, halo, short_weight, rates):
    _, rows, channels = streams.shape
    edge = halo.shape[1]
    modes, groups = rates.shape
    filters = groups * LANES // channels
    terms = filters * modes
    wide = channels // STEPS
    by_block = lambda n: (0, n)
    lead = lambda n: (0, 0, n)
    return pl.pallas_call(
        functools.partial(hyena_ends_body, filters),
        grid=(STEPS,),
        in_specs=[
            pl.BlockSpec((3, rows, wide), lead),
            pl.BlockSpec((3, edge, wide), lead),
            pl.BlockSpec((3, 3, wide), lead),
            pl.BlockSpec((modes, groups), lambda n: (0, 0)),
        ],
        out_specs=[
            pl.BlockSpec((rows, wide), by_block),
            pl.BlockSpec((modes, wide), by_block),
            pl.BlockSpec((modes, wide), by_block),
        ],
        out_shape=[
            jax.ShapeDtypeStruct((rows, channels), BF16),
            jax.ShapeDtypeStruct((modes, channels), F32),
            jax.ShapeDtypeStruct((modes, channels), F32),
        ],
        compiler_params=limits(16),
        cost_estimate=cost(4 * rows * terms * channels, 8 * rows * channels),
        name="hyena_ends",
    )(streams, halo, short_weight, rates)


def hyena_near_body(filters, x_ref, halo_ref, w_ref, mixed_ref, rate_ref, res_ref, near_ref, q_ref, taps_s, u_s):
    rows = x_ref.shape[1]
    modes, groups = rate_ref.shape
    parts = groups // STEPS // filters
    terms = filters * modes
    lanes = x_ref.shape[2] // parts
    width = lanes // filters
    rates = of_step(rate_ref)
    coeffs = of_step(res_ref) * jnp.sqrt(2.0 * rates / modes)
    row_at = lax.broadcasted_iota(jnp.int32, (rows, lanes), 0)
    lane_at = lax.broadcasted_iota(jnp.int32, (rows, lanes), 1)
    lag = (rows - 1 - lax.broadcasted_iota(jnp.int32, (terms, rows), 1)).astype(F32)
    zero = jnp.zeros((rows, lanes), BF16)
    for part in range(parts):
        at = slice(part * lanes, (part + 1) * lanes)
        q_ref[:, at] = feature(x_ref[0, :, at], halo_ref[0, :, at], w_ref, 0, at)
        mixed = mixed_ref[:, at]
        rate = down(rates, part, filters, rows)
        powers = down(coeffs, part, filters, rows) * jnp.exp(-rate * lag)
        backward = jnp.sum(powers.reshape(filters, modes, rows), axis=1)
        for g in range(filters):
            spread = jnp.broadcast_to(backward[g : g + 1], (rows, rows))
            shifted = pltpu.roll(spread, 1, 1, stride=1, stride_axis=0)
            kept = jnp.where(lane_at <= row_at, shifted, 0.0)
            taps_s[part, :, g * rows : (g + 1) * rows] = kept.astype(BF16)
            mine = (lane_at >= g * width) & (lane_at < (g + 1) * width)
            u_s[part, g * rows : (g + 1) * rows, :] = jnp.where(mine, mixed, zero)
        near_ref[:, at] = jnp.dot(taps_s[part], u_s[part], preferred_element_type=F32)


def hyena_near(streams, halo, short_weight, mixed, rates, residues):
    _, rows, channels = streams.shape
    edge = halo.shape[1]
    modes, groups = rates.shape
    lanes = LANES
    filters = groups * lanes // channels
    parts = groups // STEPS // filters
    wide = channels // STEPS
    by_block = lambda n: (0, n)
    lead = lambda n: (0, 0, n)
    whole = lambda n: (0, 0)
    return pl.pallas_call(
        functools.partial(hyena_near_body, filters),
        grid=(STEPS,),
        in_specs=[
            pl.BlockSpec((1, rows, wide), lead),
            pl.BlockSpec((1, edge, wide), lead),
            pl.BlockSpec((3, 3, wide), lead),
            pl.BlockSpec((rows, wide), by_block),
            pl.BlockSpec((modes, groups), whole),
            pl.BlockSpec((modes, groups), whole),
        ],
        out_specs=[
            pl.BlockSpec((rows, wide), by_block),
            pl.BlockSpec((rows, wide), by_block),
        ],
        out_shape=[
            jax.ShapeDtypeStruct((rows, channels), F32),
            jax.ShapeDtypeStruct((rows, channels), F32),
        ],
        scratch_shapes=[
            pltpu.VMEM((parts, rows, filters * rows), BF16),
            pltpu.VMEM((parts, filters * rows, lanes), BF16),
        ],
        compiler_params=limits(58),
        cost_estimate=cost(2 * rows * rows * filters * channels, 12 * rows * channels),
        name="hyena_near",
    )(streams, halo, short_weight, mixed, rates, residues)


def hyena_out_body(filters, near_ref, q_ref, carried_ref, rate_ref, res_ref, out_ref):
    rows = near_ref.shape[0]
    modes, groups = rate_ref.shape
    parts = groups // STEPS // filters
    terms = filters * modes
    lanes = near_ref.shape[1] // parts
    width = lanes // filters
    rates = of_step(rate_ref)
    coeffs = of_step(res_ref) * jnp.sqrt(2.0 * rates / modes)
    lag = (1 + lax.broadcasted_iota(jnp.int32, (terms, rows), 1)).astype(F32)
    own = same_filter(modes, width, terms, lanes)
    for part in range(parts):
        at = slice(part * lanes, (part + 1) * lanes)
        rate = down(rates, part, filters, rows)
        powers = (down(coeffs, part, filters, rows) * jnp.exp(-rate * lag)).T
        p_high = powers.astype(BF16)
        p_low = (powers - p_high.astype(F32)).astype(BF16)
        carried = jnp.where(own, jnp.concatenate([carried_ref[:, at]] * filters, axis=0), 0.0)
        c_high = carried.astype(BF16)
        c_low = (carried - c_high.astype(F32)).astype(BF16)
        far = (
            jnp.dot(p_high, c_high, preferred_element_type=F32)
            + jnp.dot(p_low, c_high, preferred_element_type=F32)
            + jnp.dot(p_high, c_low, preferred_element_type=F32)
        )
        out_ref[:, at] = (q_ref[:, at] * (near_ref[:, at] + far)).astype(BF16)


def hyena_finish(near, query, carried, rates, residues):
    rows, channels = near.shape
    modes, groups = rates.shape
    filters = groups * LANES // channels
    terms = filters * modes
    wide = channels // STEPS
    by_block = lambda n: (0, n)
    whole = lambda n: (0, 0)
    return pl.pallas_call(
        functools.partial(hyena_out_body, filters),
        grid=(STEPS,),
        in_specs=[
            pl.BlockSpec((rows, wide), by_block),
            pl.BlockSpec((rows, wide), by_block),
            pl.BlockSpec((modes, wide), by_block),
            pl.BlockSpec((modes, groups), whole),
            pl.BlockSpec((modes, groups), whole),
        ],
        out_specs=pl.BlockSpec((rows, wide), by_block),
        out_shape=jax.ShapeDtypeStruct((rows, channels), BF16),
        compiler_params=limits(16),
        cost_estimate=cost(6 * rows * terms * channels, 10 * rows * channels),
        name="hyena_finish",
    )(near, query, carried, rates, residues)


def scan_states(ends, rate, rows):
    half = ends.shape[1] // 2
    index = lax.axis_index("ctx")
    count = lax.axis_size("ctx") // ROW
    core, side = index % 2, index // 2 % 2
    take = lambda matrix, which: lax.dynamic_slice_in_dim(matrix, which * half, half, 1)
    rate = take(rate, core)
    decay = lambda blocks: jnp.exp(-rate * float(rows * blocks))
    mine = take(ends, core)
    theirs = flip(take(ends, 1 - core), "ctx", 1)
    even = jnp.where(core == 0, mine, theirs)
    odd = jnp.where(core == 0, theirs, mine)
    chip = decay(1) * even + odd
    other = flip(chip, "ctx", 2)
    left = jnp.where(side == 0, chip, other)
    total = decay(2) * left + jnp.where(side == 0, other, chip)
    before = ahead(total, "ctx", ROW)
    reach = 2
    while reach < count:
        upto = total + decay(ROW) * before
        earlier = ahead(upto, "ctx", ROW * reach)
        before = before + decay(ROW * (reach - 1)) * earlier
        reach *= 2
    before = jnp.where(side == 0, before, decay(2) * before + left)
    second = decay(1) * before + even
    keep = jnp.where(core == 0, before, second)
    back = flip(jnp.where(core == 0, second, before), "ctx", 1)
    return jnp.concatenate(
        [jnp.where(core == 0, keep, back), jnp.where(core == 0, back, keep)], axis=1
    )


def lanes_from(start, size):
    return pl.ds(pl.multiple_of(start * size, size), size)


def front_body(attn, hyena, theirs_ref, edge_ref, sems):
    rows, half = theirs_ref.shape[1:]
    away = attn.at[:, :, lanes_from(1 - spot()[0], half)]
    edge = hyena.at[:, rows - EDGE : rows, :]
    copies = [
        pltpu.make_async_copy(away, theirs_ref, sems.at[0]),
        pltpu.make_async_copy(edge, edge_ref, sems.at[1]),
    ]
    for copy in copies:
        copy.start()
    for copy in copies:
        copy.wait()


def front(attn, hyena):
    count, rows, channels = attn.shape
    return pl.pallas_call(
        front_body,
        in_specs=[HBM, HBM],
        out_specs=[VMEM, VMEM],
        out_shape=[
            jax.ShapeDtypeStruct((count, rows, channels // 2), attn.dtype),
            jax.ShapeDtypeStruct((count, EDGE, channels), hyena.dtype),
        ],
        scratch_shapes=[pltpu.SemaphoreType.DMA((2,))],
        compiler_params=pltpu.CompilerParams(vmem_limit_bytes=ALL_VMEM - (5 << 18)),
        cost_estimate=cost(0, 4 * count * rows * channels // 2),
        name="front",
    )(attn, hyena)


def pack_body(first, streams_ref, theirs_ref, *outs):
    core, side, _, _ = spot()
    slots = (0, 1) if first == 0 else (1 - core, core)
    quarter = theirs_ref.shape[2] // 2
    for out, away in zip(outs, (0, 1)[-len(outs) :]):
        to = 1 - side if away else side
        for stream in range(first, 3):
            out[slots[0], stream - first] = streams_ref[stream, :, lanes_from(2 * core + to, quarter)]
            out[slots[1], stream - first] = theirs_ref[stream, :, lanes_from(to, quarter)]


def pack(streams, theirs, first, amount):
    _, rows, half = theirs.shape
    shape = jax.ShapeDtypeStruct((2, 3 - first, rows, half // 2), BF16)
    return pl.pallas_call(
        functools.partial(pack_body, first),
        in_specs=[VMEM, VMEM],
        out_specs=[VMEM] * amount,
        out_shape=[shape] * amount,
        compiler_params=limits(10),
        cost_estimate=cost(0, 8 * amount * rows * half),
        name="pack",
    )(streams, theirs)


def contig_start(docs_ref, position):
    first = jnp.zeros_like(position)
    bound = jnp.int32(0)
    for n in range(docs_ref.shape[0]):
        bound = bound + docs_ref[n]
        first = jnp.where(position >= bound, bound, first)
    return first


def row_part(streams, theirs, swap, slot, stream, quarter):
    core, side, _, _ = spot()
    if slot == 0:
        return streams.at[stream, :, lanes_from(2 * core + side, quarter)]
    if slot == 1:
        return theirs.at[stream, :, lanes_from(side, quarter)]
    return swap.at[slot - 2, stream]


SCALE = math.log2(math.e) / math.sqrt(HEAD)


KEYS = 256


def attend_body(docs_ref, streams, theirs, swap, own, cross, acc_ref, m_ref, l_ref, q_s, k_s, v_s, bias_s, s_s, sems):
    _, side, place, row = spot()
    rows, quarter = q_s.shape[1:]
    base = row * (ROW * rows)
    copies = []

    def bring(source, target):
        copies.append(pltpu.make_async_copy(source, target, sems.at[len(copies)]))
        copies[-1].start()

    for n in range(2):
        for old, which in ((own, side), (cross, 1 - side)):
            older = lanes_from(2 * which + 1 - n, rows)
            bring(old.at[n, 0], k_s.at[older])
            bring(old.at[n, 1], v_s.at[older])
    for slot in range(ROW):
        part = lambda stream: row_part(streams, theirs, swap, slot, stream, quarter)
        block = place ^ slot
        newer = lanes_from(ROW + block, rows)
        bring(part(0), q_s.at[block])
        bring(part(1), k_s.at[newer])
        bring(part(2), v_s.at[newer])
    for copy in copies:
        copy.wait()

    for block in range(ROW):
        width = (ROW + 1 + block) * rows
        position = base + block * rows + lax.broadcasted_iota(jnp.int32, (rows, 1), 0)
        first = contig_start(docs_ref, position)
        at = base - ROW * rows + lax.broadcasted_iota(jnp.int32, (rows, width), 1)
        bias_s[:, 0:width] = jnp.where((at >= first) & (at <= position), 0.0, -jnp.inf)
        tiles = [slice(n, min(n + KEYS, width)) for n in range(0, width, KEYS)]
        for head in range(quarter // HEAD):
            lanes = slice(head * HEAD, (head + 1) * HEAD)
            turn = head % 2
            top = None
            for tile in tiles:
                scores = lax.dot_general(
                    q_s[block, :, lanes],
                    k_s[tile, lanes],
                    (((1,), (1,)), ((), ())),
                    preferred_element_type=F32,
                )
                scores = scores + bias_s[:, tile]
                s_s[turn, :, tile] = scores
                for n in range(0, tile.stop - tile.start, LANES):
                    some = scores[:, n : n + LANES]
                    top = some if top is None else jnp.maximum(top, some)
            top = jnp.broadcast_to(jnp.max(top, axis=1, keepdims=True), (rows, LANES))
            m_ref[block, :, lanes] = top
            total = jnp.zeros((rows, HEAD), F32)
            below = jnp.zeros((rows, LANES), F32)
            for tile in tiles:
                count = (tile.stop - tile.start) // LANES
                weight = jnp.exp2((s_s[turn, :, tile] - jnp.concatenate([top] * count, axis=1)) * SCALE)
                for n in range(count):
                    below = below + weight[:, n * LANES : (n + 1) * LANES]
                total = total + jnp.dot(weight.astype(BF16), v_s[tile, lanes], preferred_element_type=F32)
            l_ref[block, :, lanes] = jnp.broadcast_to(
                jnp.sum(below, axis=1, keepdims=True), (rows, LANES)
            )
            acc_ref[block, :, lanes] = total


def attend(doc_lengths, streams, theirs, swap, own, cross):
    _, _, rows, quarter = own.shape
    heads = quarter // HEAD
    return pl.pallas_call(
        attend_body,
        in_specs=[SMEM] + [ANY] * 5,
        out_specs=[VMEM] * 3,
        out_shape=[
            jax.ShapeDtypeStruct((ROW, rows, quarter), F32),
        ]
        * 3,
        scratch_shapes=[
            pltpu.VMEM((ROW, rows, quarter), BF16),
            pltpu.VMEM((2 * ROW * rows, quarter), BF16),
            pltpu.VMEM((2 * ROW * rows, quarter), BF16),
            pltpu.VMEM((rows, 2 * ROW * rows), F32),
            pltpu.VMEM((2, rows, 2 * ROW * rows), F32),
            pltpu.SemaphoreType.DMA((5 * ROW,)),
        ],
        compiler_params=limits(20),
        cost_estimate=cost(26 * 4 * rows * rows * quarter, 14 * ROW * rows * quarter, 26 * heads * rows * rows),
        name="attend",
    )(doc_lengths, streams, theirs, swap, own, cross)


def attend_last_body(docs_ref, streams, theirs, swap, *refs):
    olds, (acc_ref, m_ref, l_ref), outs, (q_s, kv_s, o_s, sems) = refs[:4], refs[4:7], refs[7:11], refs[11:]
    _, side, place, row = spot()
    rows, quarter = q_s.shape[1:]
    base = row * (ROW * rows)
    copies = []

    def copy_of(source, target, n):
        return pltpu.make_async_copy(source, target, sems.at[n])

    for slot in range(ROW):
        copies.append(copy_of(row_part(streams, theirs, swap, slot, 0, quarter), q_s.at[place ^ slot], slot))
        copies[-1].start()
    for which in range(2):
        large, small = olds[2 * which : 2 * which + 2]
        arrived = [
            copy_of(small.at[0], kv_s.at[0], ROW),
            copy_of(large.at[1], kv_s.at[1], ROW + 1),
            copy_of(large.at[0], kv_s.at[2], ROW + 2),
        ]

        @pl.when(side == which)
        def _():
            for copy in arrived:
                copy.start()

    for copy in copies + arrived:
        copy.wait()
    for block in range(ROW):
        slot = place ^ block
        seen = ROW - 1 - block
        width = seen * rows
        if seen:
            position = base + block * rows + lax.broadcasted_iota(jnp.int32, (rows, 1), 0)
            first = contig_start(docs_ref, position)
            at = base - (ROW + seen) * rows + lax.broadcasted_iota(jnp.int32, (rows, width), 1)
            allowed = at >= first
        for head in range(quarter // HEAD):
            lanes = slice(head * HEAD, (head + 1) * HEAD)
            total = acc_ref[block, :, lanes]
            below = l_ref[block, :, lanes]
            if seen:
                keys = kv_s[block : ROW - 1, 0, :, lanes].reshape(width, HEAD)
                values = kv_s[block : ROW - 1, 1, :, lanes].reshape(width, HEAD)
                scores = lax.dot_general(
                    q_s[block, :, lanes],
                    keys,
                    (((1,), (1,)), ((), ())),
                    preferred_element_type=F32,
                )
                scores = jnp.where(allowed, scores, -jnp.inf)
                past = m_ref[block, :, lanes]
                top = jnp.maximum(past, jnp.max(scores, axis=1, keepdims=True))
                fade = jnp.exp2((past - top) * SCALE)
                weight = jnp.exp2((scores - jnp.concatenate([top] * seen, axis=1)) * SCALE)
                share = 1.0 / (below * fade + jnp.sum(weight, axis=1, keepdims=True))
                total = total * (fade * share) + share * jnp.dot(
                    weight.astype(BF16), values, preferred_element_type=F32
                )
            else:
                total = total * (1.0 / below)
            o_s[slot, :, lanes] = total.astype(BF16)
    for slot, out in enumerate(outs):
        out[...] = o_s[slot]


def attend_last(doc_lengths, streams, theirs, swap, olds, acc, top, below):
    _, rows, quarter = acc.shape
    heads = quarter // HEAD
    return pl.pallas_call(
        attend_last_body,
        in_specs=[SMEM] + [ANY] * 7 + [VMEM] * 3,
        out_specs=[VMEM] * ROW,
        out_shape=[jax.ShapeDtypeStruct((rows, quarter), BF16)] * ROW,
        scratch_shapes=[
            pltpu.VMEM((ROW, rows, quarter), BF16),
            pltpu.VMEM((ROW - 1, 2, rows, quarter), BF16),
            pltpu.VMEM((ROW, rows, quarter), BF16),
            pltpu.SemaphoreType.DMA((2 * ROW,)),
        ],
        compiler_params=limits(16),
        cost_estimate=cost(6 * 4 * rows * rows * quarter, 12 * ROW * rows * quarter, 6 * heads * rows * rows),
        name="attend_last",
    )(doc_lengths, streams, theirs, swap, *olds, acc, top, below)


def assemble_body(*refs):
    place = spot()[2]
    *pieces, out_ref = refs
    quarter = pieces[0].shape[1]
    for slot, piece in enumerate(pieces):
        maker = place ^ slot
        which = 2 * (maker & 1) + lax.shift_right_logical(maker, 1)
        out_ref[:, lanes_from(which, quarter)] = piece[...]


def assemble(pieces):
    rows, quarter = pieces[0].shape
    return pl.pallas_call(
        assemble_body,
        in_specs=[VMEM] * ROW,
        out_specs=VMEM,
        out_shape=jax.ShapeDtypeStruct((rows, ROW * quarter), BF16),
        compiler_params=limits(6),
        cost_estimate=cost(0, 16 * rows * quarter),
        name="assemble",
    )(*pieces)


def on_device(hyena_qkv, short_weight, filter_rate, filter_residue, attn_qkv, doc_lengths):
    rows = attn_qkv.shape[0]
    inner = hyena_qkv.transpose(1, 0, 2)
    streams = attn_qkv.transpose(1, 0, 2)
    rates, residues = filter_rate.T, filter_residue.T
    theirs, edge = front(streams, inner)

    theirs = flip(theirs, "ctx", 1)
    edge = ahead(edge, "ctx", 1)
    own, cross = pack(streams, theirs, 1, 2)
    cross = ahead(cross, "ctx", ROW, 2)
    own = ahead(own, "ctx", ROW)
    (swap,) = pack(streams, theirs, 0, 1)
    swap = flip(swap, "ctx", 2)
    olds = (
        ahead(cross, "ctx", ROW, 0, ROW, 0),
        ahead(own[:1], "ctx", ROW, 0, ROW, 0),
        ahead(own, "ctx", ROW, 0, ROW, 1),
        ahead(cross[:1], "ctx", ROW, 0, ROW, 1),
    )

    mixed, ends, wide = hyena_ends(inner, edge, short_weight, rates)
    near, query = hyena_near(inner, edge, short_weight, mixed, rates, residues)
    carried = scan_states(ends, wide, rows)
    hyena_out = hyena_finish(near, query, carried, rates, residues)

    acc, top, below = attend(doc_lengths, streams, theirs, swap, own, cross)
    made = attend_last(doc_lengths, streams, theirs, swap, olds, acc, top, below)
    pieces = [made[0]] + [flip(made[n], "ctx", n) for n in range(1, ROW)]
    attn_out = assemble(pieces)
    return (hyena_out, attn_out)


def solution(mesh):
    in_specs = (
        P(("group", "ctx"), None, None),
        P(),
        P(),
        P(),
        P(("group", "ctx"), None, None),
        P("group"),
    )
    out_specs = (P(("group", "ctx"), None), P(("group", "ctx"), None))
    return jax.shard_map(
        on_device, mesh=mesh, in_specs=in_specs, out_specs=out_specs, check_vma=False
    )
```

```python
import functools
import math

import jax
import jax.numpy as jnp
from jax import lax
from jax.experimental import pallas as pl
from jax.experimental.pallas import tpu as pltpu
from jax.sharding import PartitionSpec as P


HEAD = 128
LANES = 128
EDGE = 8
ROW = 4

F32 = jnp.float32
BF16 = jnp.bfloat16


def flip(value, axis, bit):
    count = lax.axis_size(axis)
    return lax.ppermute(value, axis, [(at, at ^ bit) for at in range(count)])


def side_of(at):
    return at // 2 % 2


def ahead(value, axis, steps, bit=0, first=0, side=None):
    count = lax.axis_size(axis)
    pairs = [
        (at, (at + steps) ^ bit)
        for at in range(first, count - steps)
        if side is None or side_of(at) == side
    ]
    return lax.ppermute(value, axis, pairs)


def spot():
    index = lax.axis_index("ctx")
    return index & 1, lax.shift_right_logical(index, 1) & 1, index & (ROW - 1), index // ROW


ALL_VMEM = 67043328


def limits(mib):
    return pltpu.CompilerParams(vmem_limit_bytes=mib << 20)


def cost(flops, moved, exps=0):
    return pl.CostEstimate(flops=flops, bytes_accessed=moved, transcendentals=exps)


VMEM = pl.BlockSpec(memory_space=pltpu.VMEM)
SMEM = pl.BlockSpec(memory_space=pltpu.SMEM)
ANY = pl.BlockSpec(memory_space=pl.ANY)
HBM = pl.BlockSpec(memory_space=pltpu.HBM)


def same_filter(modes, width, terms, lanes):
    row_at = lax.broadcasted_iota(jnp.int32, (terms, lanes), 0)
    lane_at = lax.broadcasted_iota(jnp.int32, (terms, lanes), 1)
    kept = None
    for g in range(terms // modes):
        both = (
            (row_at >= g * modes)
            & (row_at < (g + 1) * modes)
            & (lane_at >= g * width)
            & (lane_at < (g + 1) * width)
        )
        kept = both if kept is None else kept | both
    return kept


def feature(x, halo, w_ref, stream, at):
    here = x.astype(F32)
    halo = halo.astype(F32)
    edge = halo.shape[0]
    row_at = lax.broadcasted_iota(jnp.int32, here.shape, 0)
    one = jnp.where(row_at == 0, halo[edge - 1 :], pltpu.roll(here, 1, 0))
    two = jnp.where(row_at == 1, halo[edge - 1 :], pltpu.roll(here, 2, 0))
    two = jnp.where(row_at == 0, halo[edge - 2 : edge - 1], two)
    tap = [w_ref[n, stream : stream + 1, at] for n in range(3)]
    return tap[0] * here + tap[1] * one + tap[2] * two


def of_step(table_ref):
    groups = table_ref.shape[1]
    return pltpu.roll(table_ref[...], groups - pl.program_id(0) * (groups // STEPS), 1)


def down(table, part, filters, lanes):
    columns = [table[:, part * filters + g : part * filters + g + 1] for g in range(filters)]
    return jnp.concatenate([jnp.broadcast_to(c, (c.shape[0], lanes)) for c in columns], axis=0)


def hyena_ends_body(filters, x_ref, halo_ref, w_ref, rate_ref, mixed_ref, ends_ref, wide_ref):
    rows = x_ref.shape[1]
    modes, groups = rate_ref.shape
    parts = groups // STEPS // filters
    terms = filters * modes
    lanes = x_ref.shape[2] // parts
    width = lanes // filters
    rates = of_step(rate_ref)
    lag = (rows - 1 - lax.broadcasted_iota(jnp.int32, (terms, rows), 1)).astype(F32)
    own = same_filter(modes, width, terms, lanes)
    pick = lambda matrix: jnp.sum(jnp.where(own, matrix, 0.0).reshape(filters, modes, lanes), axis=0)
    for part in range(parts):
        at = slice(part * lanes, (part + 1) * lanes)
        key, value = (feature(x_ref[n, :, at], halo_ref[n, :, at], w_ref, n, at) for n in (1, 2))
        mixed = (key * value).astype(BF16)
        mixed_ref[:, at] = mixed
        rate = down(rates, part, filters, rows)
        powers = jnp.exp(-rate * lag)
        high = powers.astype(BF16)
        low = (powers - high.astype(F32)).astype(BF16)
        ends = jnp.dot(high, mixed, preferred_element_type=F32) + jnp.dot(
            low, mixed, preferred_element_type=F32
        )
        ends_ref[:, at] = pick(ends)
        wide_ref[:, at] = pick(rate)


STEPS = 4


def hyena_ends(streams, halo, short_weight, rates):
    _, rows, channels = streams.shape
    edge = halo.shape[1]
    modes, groups = rates.shape
    filters = groups * LANES // channels
    terms = filters * modes
    wide = channels // STEPS
    by_block = lambda n: (0, n)
    lead = lambda n: (0, 0, n)
    return pl.pallas_call(
        functools.partial(hyena_ends_body, filters),
        grid=(STEPS,),
        in_specs=[
            pl.BlockSpec((3, rows, wide), lead),
            pl.BlockSpec((3, edge, wide), lead),
            pl.BlockSpec((3, 3, wide), lead),
            pl.BlockSpec((modes, groups), lambda n: (0, 0)),
        ],
        out_specs=[
            pl.BlockSpec((rows, wide), by_block),
            pl.BlockSpec((modes, wide), by_block),
            pl.BlockSpec((modes, wide), by_block),
        ],
        out_shape=[
            jax.ShapeDtypeStruct((rows, channels), BF16),
            jax.ShapeDtypeStruct((modes, channels), F32),
            jax.ShapeDtypeStruct((modes, channels), F32),
        ],
        compiler_params=limits(16),
        cost_estimate=cost(4 * rows * terms * channels, 8 * rows * channels),
        name="hyena_ends",
    )(streams, halo, short_weight, rates)


def hyena_near_body(filters, mixed_ref, rate_ref, res_ref, near_ref, taps_s, u_s):
    rows = mixed_ref.shape[0]
    modes, groups = rate_ref.shape
    parts = groups // STEPS // filters
    terms = filters * modes
    lanes = mixed_ref.shape[1] // parts
    width = lanes // filters
    rates = of_step(rate_ref)
    coeffs = of_step(res_ref) * jnp.sqrt(2.0 * rates / modes)
    row_at = lax.broadcasted_iota(jnp.int32, (rows, lanes), 0)
    lane_at = lax.broadcasted_iota(jnp.int32, (rows, lanes), 1)
    lag = (rows - 1 - lax.broadcasted_iota(jnp.int32, (terms, rows), 1)).astype(F32)
    zero = jnp.zeros((rows, lanes), BF16)
    for part in range(parts):
        at = slice(part * lanes, (part + 1) * lanes)
        mixed = mixed_ref[:, at]
        rate = down(rates, part, filters, rows)
        powers = down(coeffs, part, filters, rows) * jnp.exp(-rate * lag)
        backward = jnp.sum(powers.reshape(filters, modes, rows), axis=1)
        for g in range(filters):
            spread = jnp.broadcast_to(backward[g : g + 1], (rows, rows))
            shifted = pltpu.roll(spread, 1, 1, stride=1, stride_axis=0)
            kept = jnp.where(lane_at <= row_at, shifted, 0.0)
            taps_s[part, :, g * rows : (g + 1) * rows] = kept.astype(BF16)
            mine = (lane_at >= g * width) & (lane_at < (g + 1) * width)
            u_s[part, g * rows : (g + 1) * rows, :] = jnp.where(mine, mixed, zero)
        near_ref[:, at] = jnp.dot(taps_s[part], u_s[part], preferred_element_type=F32)


def hyena_near(mixed, rates, residues):
    rows, channels = mixed.shape
    modes, groups = rates.shape
    lanes = LANES
    filters = groups * lanes // channels
    parts = groups // STEPS // filters
    wide = channels // STEPS
    by_block = lambda n: (0, n)
    whole = lambda n: (0, 0)
    return pl.pallas_call(
        functools.partial(hyena_near_body, filters),
        grid=(STEPS,),
        in_specs=[
            pl.BlockSpec((rows, wide), by_block),
            pl.BlockSpec((modes, groups), whole),
            pl.BlockSpec((modes, groups), whole),
        ],
        out_specs=pl.BlockSpec((rows, wide), by_block),
        out_shape=jax.ShapeDtypeStruct((rows, channels), F32),
        scratch_shapes=[
            pltpu.VMEM((parts, rows, filters * rows), BF16),
            pltpu.VMEM((parts, filters * rows, lanes), BF16),
        ],
        compiler_params=limits(16),
        cost_estimate=cost(2 * rows * rows * filters * channels, 12 * rows * channels),
        name="hyena_near",
    )(mixed, rates, residues)


def hyena_out_body(filters, near_ref, x_ref, halo_ref, w_ref, carried_ref, rate_ref, res_ref, out_ref):
    rows = near_ref.shape[0]
    modes, groups = rate_ref.shape
    parts = groups // STEPS // filters
    terms = filters * modes
    lanes = near_ref.shape[1] // parts
    width = lanes // filters
    rates = of_step(rate_ref)
    coeffs = of_step(res_ref) * jnp.sqrt(2.0 * rates / modes)
    lag = (1 + lax.broadcasted_iota(jnp.int32, (terms, rows), 1)).astype(F32)
    own = same_filter(modes, width, terms, lanes)
    for part in range(parts):
        at = slice(part * lanes, (part + 1) * lanes)
        rate = down(rates, part, filters, rows)
        powers = (down(coeffs, part, filters, rows) * jnp.exp(-rate * lag)).T
        p_high = powers.astype(BF16)
        p_low = (powers - p_high.astype(F32)).astype(BF16)
        carried = jnp.where(own, jnp.concatenate([carried_ref[:, at]] * filters, axis=0), 0.0)
        c_high = carried.astype(BF16)
        c_low = (carried - c_high.astype(F32)).astype(BF16)
        far = (
            jnp.dot(p_high, c_high, preferred_element_type=F32)
            + jnp.dot(p_low, c_high, preferred_element_type=F32)
            + jnp.dot(p_high, c_low, preferred_element_type=F32)
        )
        query = feature(x_ref[0, :, at], halo_ref[0, :, at], w_ref, 0, at)
        out_ref[:, at] = (query * (near_ref[:, at] + far)).astype(BF16)


def hyena_finish(near, streams, halo, short_weight, carried, rates, residues):
    rows, channels = near.shape
    edge = halo.shape[1]
    modes, groups = rates.shape
    filters = groups * LANES // channels
    terms = filters * modes
    wide = channels // STEPS
    by_block = lambda n: (0, n)
    lead = lambda n: (0, 0, n)
    whole = lambda n: (0, 0)
    return pl.pallas_call(
        functools.partial(hyena_out_body, filters),
        grid=(STEPS,),
        in_specs=[
            pl.BlockSpec((rows, wide), by_block),
            pl.BlockSpec((1, rows, wide), lead),
            pl.BlockSpec((1, edge, wide), lead),
            pl.BlockSpec((3, 3, wide), lead),
            pl.BlockSpec((modes, wide), by_block),
            pl.BlockSpec((modes, groups), whole),
            pl.BlockSpec((modes, groups), whole),
        ],
        out_specs=pl.BlockSpec((rows, wide), by_block),
        out_shape=jax.ShapeDtypeStruct((rows, channels), BF16),
        compiler_params=limits(16),
        cost_estimate=cost(6 * rows * terms * channels, 10 * rows * channels),
        name="hyena_finish",
    )(near, streams, halo, short_weight, carried, rates, residues)


def scan_states(ends, rate, rows):
    half = ends.shape[1] // 2
    index = lax.axis_index("ctx")
    count = lax.axis_size("ctx") // ROW
    core, side = index % 2, index // 2 % 2
    take = lambda matrix, which: lax.dynamic_slice_in_dim(matrix, which * half, half, 1)
    rate = take(rate, core)
    decay = lambda blocks: jnp.exp(-rate * float(rows * blocks))
    mine = take(ends, core)
    theirs = flip(take(ends, 1 - core), "ctx", 1)
    even = jnp.where(core == 0, mine, theirs)
    odd = jnp.where(core == 0, theirs, mine)
    chip = decay(1) * even + odd
    other = flip(chip, "ctx", 2)
    left = jnp.where(side == 0, chip, other)
    total = decay(2) * left + jnp.where(side == 0, other, chip)
    before = ahead(total, "ctx", ROW)
    reach = 2
    while reach < count:
        upto = total + decay(ROW) * before
        earlier = ahead(upto, "ctx", ROW * reach)
        before = before + decay(ROW * (reach - 1)) * earlier
        reach *= 2
    before = jnp.where(side == 0, before, decay(2) * before + left)
    second = decay(1) * before + even
    keep = jnp.where(core == 0, before, second)
    back = flip(jnp.where(core == 0, second, before), "ctx", 1)
    return jnp.concatenate(
        [jnp.where(core == 0, keep, back), jnp.where(core == 0, back, keep)], axis=1
    )


def lanes_from(start, size):
    return pl.ds(pl.multiple_of(start * size, size), size)


def front_body(attn, hyena, theirs_ref, edge_ref, sems):
    rows, half = theirs_ref.shape[1:]
    away = attn.at[:, :, lanes_from(1 - spot()[0], half)]
    edge = hyena.at[:, rows - EDGE : rows, :]
    copies = [
        pltpu.make_async_copy(away, theirs_ref, sems.at[0]),
        pltpu.make_async_copy(edge, edge_ref, sems.at[1]),
    ]
    for copy in copies:
        copy.start()
    for copy in copies:
        copy.wait()


def front(attn, hyena):
    count, rows, channels = attn.shape
    return pl.pallas_call(
        front_body,
        in_specs=[HBM, HBM],
        out_specs=[VMEM, VMEM],
        out_shape=[
            jax.ShapeDtypeStruct((count, rows, channels // 2), attn.dtype),
            jax.ShapeDtypeStruct((count, EDGE, channels), hyena.dtype),
        ],
        scratch_shapes=[pltpu.SemaphoreType.DMA((2,))],
        compiler_params=pltpu.CompilerParams(vmem_limit_bytes=ALL_VMEM - (18 << 17)),
        cost_estimate=cost(0, 4 * count * rows * channels // 2),
        name="front",
    )(attn, hyena)


def pack_body(first, streams_ref, theirs_ref, *outs):
    core, side, _, _ = spot()
    slots = (0, 1) if first == 0 else (1 - core, core)
    quarter = theirs_ref.shape[2] // 2
    for out, away in zip(outs, (0, 1)[-len(outs) :]):
        to = 1 - side if away else side
        for stream in range(first, 3):
            out[slots[0], stream - first] = streams_ref[stream, :, lanes_from(2 * core + to, quarter)]
            out[slots[1], stream - first] = theirs_ref[stream, :, lanes_from(to, quarter)]


def pack(streams, theirs, first, amount):
    _, rows, half = theirs.shape
    shape = jax.ShapeDtypeStruct((2, 3 - first, rows, half // 2), BF16)
    return pl.pallas_call(
        functools.partial(pack_body, first),
        in_specs=[VMEM, VMEM],
        out_specs=[VMEM] * amount,
        out_shape=[shape] * amount,
        compiler_params=limits(10),
        cost_estimate=cost(0, 8 * amount * rows * half),
        name="pack",
    )(streams, theirs)


def contig_start(docs_ref, position):
    first = jnp.zeros_like(position)
    bound = jnp.int32(0)
    for n in range(docs_ref.shape[0]):
        bound = bound + docs_ref[n]
        first = jnp.where(position >= bound, bound, first)
    return first


def row_part(streams, theirs, swap, slot, stream, quarter):
    core, side, _, _ = spot()
    if slot == 0:
        return streams.at[stream, :, lanes_from(2 * core + side, quarter)]
    if slot == 1:
        return theirs.at[stream, :, lanes_from(side, quarter)]
    return swap.at[slot - 2, stream]


SCALE = math.log2(math.e) / math.sqrt(HEAD)


KEYS = 256
GROUP = 2
CHUNK = 32


def attend_body(docs_ref, streams, theirs, swap, own, cross, acc_ref, m_ref, l_ref, q_s, k_s, v_s, bias_s, s_s, p_s, sems):
    _, side, place, row = spot()
    rows, quarter = q_s.shape[0] // ROW, q_s.shape[1]
    base = row * (ROW * rows)
    copies = []

    def bring(source, target):
        copies.append(pltpu.make_async_copy(source, target, sems.at[len(copies)]))
        copies[-1].start()

    for n in range(2):
        for old, which in ((own, side), (cross, 1 - side)):
            older = lanes_from(2 * which + 1 - n, rows)
            bring(old.at[n, 0], k_s.at[older])
            bring(old.at[n, 1], v_s.at[older])
    for slot in range(ROW):
        part = lambda stream: row_part(streams, theirs, swap, slot, stream, quarter)
        block = place ^ slot
        newer = lanes_from(ROW + block, rows)
        bring(part(0), q_s.at[lanes_from(block, rows)])
        bring(part(1), k_s.at[newer])
        bring(part(2), v_s.at[newer])
    for copy in copies:
        copy.wait()

    for group in range(ROW // GROUP):
        tall = GROUP * rows
        width = (ROW + GROUP * (group + 1)) * rows
        here = slice(group * tall, (group + 1) * tall)
        for block in range(GROUP):
            position = base + (group * GROUP + block) * rows + lax.broadcasted_iota(jnp.int32, (rows, 1), 0)
            first = contig_start(docs_ref, position)
            at = base - ROW * rows + lax.broadcasted_iota(jnp.int32, (rows, width), 1)
            bias_s[block * rows : (block + 1) * rows, 0:width] = jnp.where(
                (at >= first) & (at <= position), 0.0, -jnp.inf
            )
        for head in range(quarter // HEAD):
            lanes = slice(head * HEAD, (head + 1) * HEAD)
            turn = head % 2
            for n in range(0, width, KEYS):
                tile = slice(n, n + KEYS)
                s_s[turn, :, tile] = lax.dot_general(
                    q_s[here, lanes],
                    k_s[tile, lanes],
                    (((1,), (1,)), ((), ())),
                    preferred_element_type=F32,
                )
            for m in range(0, tall, CHUNK):
                some = slice(m, m + CHUNK)
                out = slice(group * tall + m, group * tall + m + CHUNK)
                top = None
                parts = []
                for n in range(0, width, LANES):
                    part = s_s[turn, some, n : n + LANES] + bias_s[some, n : n + LANES]
                    parts.append(part)
                    top = part if top is None else jnp.maximum(top, part)
                top = jnp.broadcast_to(jnp.max(top, axis=1, keepdims=True), (CHUNK, LANES))
                m_ref[out, lanes] = top
                below = jnp.zeros((CHUNK, LANES), F32)
                for n, part in enumerate(parts):
                    weight = jnp.exp2((part - top) * SCALE)
                    below = below + weight
                    p_s[turn, some, n * LANES : (n + 1) * LANES] = weight.astype(BF16)
                l_ref[out, lanes] = jnp.broadcast_to(jnp.sum(below, axis=1, keepdims=True), (CHUNK, LANES))
            acc_ref[here, lanes] = jnp.dot(
                p_s[turn, :, 0:width], v_s[0:width, lanes], preferred_element_type=F32
            )


def attend(doc_lengths, streams, theirs, swap, own, cross):
    _, _, rows, quarter = own.shape
    heads = quarter // HEAD
    return pl.pallas_call(
        attend_body,
        in_specs=[SMEM] + [ANY] * 5,
        out_specs=[VMEM] * 3,
        out_shape=[
            jax.ShapeDtypeStruct((ROW * rows, quarter), F32),
        ]
        * 3,
        scratch_shapes=[
            pltpu.VMEM((ROW * rows, quarter), BF16),
            pltpu.VMEM((2 * ROW * rows, quarter), BF16),
            pltpu.VMEM((2 * ROW * rows, quarter), BF16),
            pltpu.VMEM((GROUP * rows, 2 * ROW * rows), F32),
            pltpu.VMEM((2, GROUP * rows, 2 * ROW * rows), F32),
            pltpu.VMEM((2, GROUP * rows, 2 * ROW * rows), BF16),
            pltpu.SemaphoreType.DMA((5 * ROW,)),
        ],
        compiler_params=limits(20),
        cost_estimate=cost(26 * 4 * rows * rows * quarter, 14 * ROW * rows * quarter, 26 * heads * rows * rows),
        name="attend",
    )(doc_lengths, streams, theirs, swap, own, cross)


def attend_last_body(docs_ref, streams, theirs, swap, *refs):
    olds, (acc_ref, m_ref, l_ref), outs, (q_s, kv_s, o_s, sems) = refs[:4], refs[4:7], refs[7:11], refs[11:]
    _, side, place, row = spot()
    rows, quarter = q_s.shape[1:]
    base = row * (ROW * rows)
    copies = []

    def copy_of(source, target, n):
        return pltpu.make_async_copy(source, target, sems.at[n])

    for slot in range(ROW):
        copies.append(copy_of(row_part(streams, theirs, swap, slot, 0, quarter), q_s.at[place ^ slot], slot))
        copies[-1].start()
    for which in range(2):
        large, small = olds[2 * which : 2 * which + 2]
        arrived = [
            copy_of(small.at[0], kv_s.at[0], ROW),
            copy_of(large.at[1], kv_s.at[1], ROW + 1),
            copy_of(large.at[0], kv_s.at[2], ROW + 2),
        ]

        @pl.when(side == which)
        def _():
            for copy in arrived:
                copy.start()

    for copy in copies + arrived:
        copy.wait()
    heads = [slice(n, n + HEAD) for n in range(0, quarter, HEAD)]
    for block in range(ROW):
        slot = place ^ block
        here = slice(block * rows, (block + 1) * rows)
        seen = ROW - 1 - block
        width = seen * rows
        if not seen:
            for lanes in heads:
                o_s[slot, :, lanes] = (acc_ref[here, lanes] * (1.0 / l_ref[here, lanes])).astype(BF16)
            continue
        position = base + block * rows + lax.broadcasted_iota(jnp.int32, (rows, 1), 0)
        first = contig_start(docs_ref, position)
        at = base - (ROW + seen) * rows + lax.broadcasted_iota(jnp.int32, (rows, width), 1)
        allowed = at >= first
        scores = [
            lax.dot_general(
                q_s[block, :, lanes],
                kv_s[block : ROW - 1, 0, :, lanes].reshape(width, HEAD),
                (((1,), (1,)), ((), ())),
                preferred_element_type=F32,
            )
            for lanes in heads
        ]
        scores = [jnp.where(allowed, score, -jnp.inf) for score in scores]
        tops = [
            jnp.maximum(m_ref[here, lanes], jnp.max(score, axis=1, keepdims=True))
            for lanes, score in zip(heads, scores)
        ]
        weights = [
            jnp.exp2((score - jnp.concatenate([top] * seen, axis=1)) * SCALE)
            for score, top in zip(scores, tops)
        ]
        for lanes, top, weight in zip(heads, tops, weights):
            fade = jnp.exp2((m_ref[here, lanes] - top) * SCALE)
            share = 1.0 / (l_ref[here, lanes] * fade + jnp.sum(weight, axis=1, keepdims=True))
            more = jnp.dot(
                weight.astype(BF16),
                kv_s[block : ROW - 1, 1, :, lanes].reshape(width, HEAD),
                preferred_element_type=F32,
            )
            o_s[slot, :, lanes] = ((acc_ref[here, lanes] * fade + more) * share).astype(BF16)
    for slot, out in enumerate(outs):
        out[...] = o_s[slot]


def attend_last(doc_lengths, streams, theirs, swap, olds, acc, top, below):
    rows, quarter = acc.shape[0] // ROW, acc.shape[1]
    heads = quarter // HEAD
    return pl.pallas_call(
        attend_last_body,
        in_specs=[SMEM] + [ANY] * 7 + [VMEM] * 3,
        out_specs=[VMEM] * ROW,
        out_shape=[jax.ShapeDtypeStruct((rows, quarter), BF16)] * ROW,
        scratch_shapes=[
            pltpu.VMEM((ROW, rows, quarter), BF16),
            pltpu.VMEM((ROW - 1, 2, rows, quarter), BF16),
            pltpu.VMEM((ROW, rows, quarter), BF16),
            pltpu.SemaphoreType.DMA((2 * ROW,)),
        ],
        compiler_params=limits(16),
        cost_estimate=cost(6 * 4 * rows * rows * quarter, 12 * ROW * rows * quarter, 6 * heads * rows * rows),
        name="attend_last",
    )(doc_lengths, streams, theirs, swap, *olds, acc, top, below)


def assemble_body(*refs):
    place = spot()[2]
    *pieces, out_ref = refs
    quarter = pieces[0].shape[1]
    for slot, piece in enumerate(pieces):
        maker = place ^ slot
        which = 2 * (maker & 1) + lax.shift_right_logical(maker, 1)
        out_ref[:, lanes_from(which, quarter)] = piece[...]


def assemble(pieces):
    rows, quarter = pieces[0].shape
    return pl.pallas_call(
        assemble_body,
        in_specs=[VMEM] * ROW,
        out_specs=VMEM,
        out_shape=jax.ShapeDtypeStruct((rows, ROW * quarter), BF16),
        compiler_params=limits(6),
        cost_estimate=cost(0, 16 * rows * quarter),
        name="assemble",
    )(*pieces)


def on_device(hyena_qkv, short_weight, filter_rate, filter_residue, attn_qkv, doc_lengths):
    rows = attn_qkv.shape[0]
    inner = hyena_qkv.transpose(1, 0, 2)
    streams = attn_qkv.transpose(1, 0, 2)
    rates, residues = filter_rate.T, filter_residue.T
    theirs, edge = front(streams, inner)

    theirs = flip(theirs, "ctx", 1)
    edge = ahead(edge, "ctx", 1)
    own, cross = pack(streams, theirs, 1, 2)
    cross = ahead(cross, "ctx", ROW, 2)
    own = ahead(own, "ctx", ROW)
    (swap,) = pack(streams, theirs, 0, 1)
    swap = flip(swap, "ctx", 2)
    olds = (
        ahead(cross, "ctx", ROW, 0, ROW, 0),
        ahead(own[:1], "ctx", ROW, 0, ROW, 0),
        ahead(own, "ctx", ROW, 0, ROW, 1),
        ahead(cross[:1], "ctx", ROW, 0, ROW, 1),
    )

    mixed, ends, wide = hyena_ends(inner, edge, short_weight, rates)
    near = hyena_near(mixed, rates, residues)
    carried = scan_states(ends, wide, rows)
    hyena_out = hyena_finish(near, inner, edge, short_weight, carried, rates, residues)

    acc, top, below = attend(doc_lengths, streams, theirs, swap, own, cross)
    made = attend_last(doc_lengths, streams, theirs, swap, olds, acc, top, below)
    pieces = [made[0]] + [flip(made[n], "ctx", n) for n in range(1, ROW)]
    attn_out = assemble(pieces)
    return (hyena_out, attn_out)


def solution(mesh):
    in_specs = (
        P(("group", "ctx"), None, None),
        P(),
        P(),
        P(),
        P(("group", "ctx"), None, None),
        P("group"),
    )
    out_specs = (P(("group", "ctx"), None), P(("group", "ctx"), None))
    return jax.shard_map(on_device, mesh=mesh, in_specs=in_specs, out_specs=out_specs, check_vma=False)
```

```python
import functools
import math

import jax
import jax.numpy as jnp
from jax import lax
from jax.experimental import pallas as pl
from jax.experimental.pallas import tpu as pltpu
from jax.sharding import PartitionSpec as P


HEAD = 128
LANES = 128
EDGE = 8
ROW = 4

F32 = jnp.float32
BF16 = jnp.bfloat16


def flip(value, axis, bit):
    count = lax.axis_size(axis)
    return lax.ppermute(value, axis, [(at, at ^ bit) for at in range(count)])


def side_of(at):
    return at // 2 % 2


def ahead(value, axis, steps, bit=0, first=0, side=None):
    count = lax.axis_size(axis)
    pairs = [
        (at, (at + steps) ^ bit)
        for at in range(first, count - steps)
        if side is None or side_of(at) == side
    ]
    return lax.ppermute(value, axis, pairs)


def spot():
    index = lax.axis_index("ctx")
    return index & 1, lax.shift_right_logical(index, 1) & 1, index & (ROW - 1), index // ROW


ALL_VMEM = 67043328


def limits(mib):
    return pltpu.CompilerParams(vmem_limit_bytes=mib << 20)


def cost(flops, moved, exps=0):
    return pl.CostEstimate(flops=flops, bytes_accessed=moved, transcendentals=exps)


VMEM = pl.BlockSpec(memory_space=pltpu.VMEM)
SMEM = pl.BlockSpec(memory_space=pltpu.SMEM)
ANY = pl.BlockSpec(memory_space=pl.ANY)
HBM = pl.BlockSpec(memory_space=pltpu.HBM)


def same_filter(modes, width, terms, lanes):
    row_at = lax.broadcasted_iota(jnp.int32, (terms, lanes), 0)
    lane_at = lax.broadcasted_iota(jnp.int32, (terms, lanes), 1)
    kept = None
    for g in range(terms // modes):
        both = (
            (row_at >= g * modes)
            & (row_at < (g + 1) * modes)
            & (lane_at >= g * width)
            & (lane_at < (g + 1) * width)
        )
        kept = both if kept is None else kept | both
    return kept


def feature(x, halo, w_ref, stream, at):
    here = x.astype(F32)
    halo = halo.astype(F32)
    edge = halo.shape[0]
    row_at = lax.broadcasted_iota(jnp.int32, here.shape, 0)
    one = jnp.where(row_at == 0, halo[edge - 1 :], pltpu.roll(here, 1, 0))
    two = jnp.where(row_at == 1, halo[edge - 1 :], pltpu.roll(here, 2, 0))
    two = jnp.where(row_at == 0, halo[edge - 2 : edge - 1], two)
    tap = [w_ref[n, stream : stream + 1, at] for n in range(3)]
    return tap[0] * here + tap[1] * one + tap[2] * two


def of_step(table_ref):
    groups = table_ref.shape[1]
    return pltpu.roll(table_ref[...], groups - pl.program_id(0) * (groups // STEPS), 1)


def down(table, part, filters, lanes):
    columns = [table[:, part * filters + g : part * filters + g + 1] for g in range(filters)]
    return jnp.concatenate([jnp.broadcast_to(c, (c.shape[0], lanes)) for c in columns], axis=0)


def hyena_ends_body(
    filters, x_ref, halo_ref, w_ref, rate_ref, res_ref, mixed_ref, keep_ref, away_ref, wide_ref, gain_ref
):
    rows = x_ref.shape[1]
    modes, groups = rate_ref.shape
    parts = groups // STEPS // filters
    terms = filters * modes
    lanes = x_ref.shape[2] // parts
    width = lanes // filters
    rates = of_step(rate_ref)
    coeffs = of_step(res_ref) * jnp.sqrt(2.0 * rates / modes)
    lag = (rows - 1 - lax.broadcasted_iota(jnp.int32, (terms, rows), 1)).astype(F32)
    own = same_filter(modes, width, terms, lanes)
    pick = lambda matrix: jnp.sum(jnp.where(own, matrix, 0.0).reshape(filters, modes, lanes), axis=0)
    step = pl.program_id(0)
    mine = step // (STEPS // 2) == spot()[0]
    for part in range(parts):
        at = slice(part * lanes, (part + 1) * lanes)
        there = pl.ds(pl.multiple_of((step % (STEPS // 2)) * (parts * lanes) + part * lanes, lanes), lanes)
        key, value = (feature(x_ref[n, :, at], halo_ref[n, :, at], w_ref, n, at) for n in (1, 2))
        mixed = (key * value).astype(BF16)
        mixed_ref[:, at] = mixed
        rate = down(rates, part, filters, rows)
        powers = jnp.exp(-rate * lag)
        high = powers.astype(BF16)
        low = (powers - high.astype(F32)).astype(BF16)
        ends = pick(
            jnp.dot(high, mixed, preferred_element_type=F32)
            + jnp.dot(low, mixed, preferred_element_type=F32)
        )

        @pl.when(mine)
        def _():
            keep_ref[:, there] = ends
            wide_ref[:, there] = pick(rate)
            gain_ref[:, there] = pick(down(coeffs, part, filters, rows))

        @pl.when(jnp.logical_not(mine))
        def _():
            away_ref[:, there] = ends


STEPS = 4


def hyena_ends(streams, halo, short_weight, rates, residues):
    _, rows, channels = streams.shape
    edge = halo.shape[1]
    modes, groups = rates.shape
    filters = groups * LANES // channels
    terms = filters * modes
    wide = channels // STEPS
    lead = lambda n: (0, 0, n)
    whole = lambda n: (0, 0)
    half = (modes, channels // 2)
    return pl.pallas_call(
        functools.partial(hyena_ends_body, filters),
        grid=(STEPS,),
        in_specs=[
            pl.BlockSpec((3, rows, wide), lead),
            pl.BlockSpec((3, edge, wide), lead),
            pl.BlockSpec((3, 3, wide), lead),
            pl.BlockSpec((modes, groups), whole),
            pl.BlockSpec((modes, groups), whole),
        ],
        out_specs=[pl.BlockSpec((rows, wide), lambda n: (0, n))] + [pl.BlockSpec(half, whole)] * 4,
        out_shape=[jax.ShapeDtypeStruct((rows, channels), BF16)] + [jax.ShapeDtypeStruct(half, F32)] * 4,
        compiler_params=limits(16),
        cost_estimate=cost(4 * rows * terms * channels, 8 * rows * channels),
        name="hyena_ends",
    )(streams, halo, short_weight, rates, residues)


def hyena_near_body(filters, mixed_ref, rate_ref, res_ref, near_ref, taps_s, u_s):
    rows = mixed_ref.shape[0]
    modes, groups = rate_ref.shape
    parts = groups // STEPS // filters
    terms = filters * modes
    lanes = mixed_ref.shape[1] // parts
    width = lanes // filters
    rates = of_step(rate_ref)
    coeffs = of_step(res_ref) * jnp.sqrt(2.0 * rates / modes)
    row_at = lax.broadcasted_iota(jnp.int32, (rows, lanes), 0)
    lane_at = lax.broadcasted_iota(jnp.int32, (rows, lanes), 1)
    lag = (rows - 1 - lax.broadcasted_iota(jnp.int32, (terms, rows), 1)).astype(F32)
    zero = jnp.zeros((rows, lanes), BF16)
    for part in range(parts):
        at = slice(part * lanes, (part + 1) * lanes)
        mixed = mixed_ref[:, at]
        rate = down(rates, part, filters, rows)
        powers = down(coeffs, part, filters, rows) * jnp.exp(-rate * lag)
        backward = jnp.sum(powers.reshape(filters, modes, rows), axis=1)
        for g in range(filters):
            spread = jnp.broadcast_to(backward[g : g + 1], (rows, rows))
            shifted = pltpu.roll(spread, 1, 1, stride=1, stride_axis=0)
            kept = jnp.where(lane_at <= row_at, shifted, 0.0)
            taps_s[part, :, g * rows : (g + 1) * rows] = kept.astype(BF16)
            mine = (lane_at >= g * width) & (lane_at < (g + 1) * width)
            u_s[part, g * rows : (g + 1) * rows, :] = jnp.where(mine, mixed, zero)
        near_ref[:, at] = jnp.dot(taps_s[part], u_s[part], preferred_element_type=F32)


def hyena_near(mixed, rates, residues):
    rows, channels = mixed.shape
    modes, groups = rates.shape
    lanes = LANES
    filters = groups * lanes // channels
    parts = groups // STEPS // filters
    wide = channels // STEPS
    by_block = lambda n: (0, n)
    whole = lambda n: (0, 0)
    return pl.pallas_call(
        functools.partial(hyena_near_body, filters),
        grid=(STEPS,),
        in_specs=[
            pl.BlockSpec((rows, wide), by_block),
            pl.BlockSpec((modes, groups), whole),
            pl.BlockSpec((modes, groups), whole),
        ],
        out_specs=pl.BlockSpec((rows, wide), by_block),
        out_shape=jax.ShapeDtypeStruct((rows, channels), F32),
        scratch_shapes=[
            pltpu.VMEM((parts, rows, filters * rows), BF16),
            pltpu.VMEM((parts, filters * rows, lanes), BF16),
        ],
        compiler_params=limits(16),
        cost_estimate=cost(2 * rows * rows * filters * channels, 12 * rows * channels),
        name="hyena_near",
    )(mixed, rates, residues)


def hyena_out_body(filters, near_ref, x_ref, halo_ref, w_ref, keep_ref, back_ref, rate_ref, out_ref):
    rows = near_ref.shape[0]
    modes, groups = rate_ref.shape
    parts = groups // STEPS // filters
    terms = filters * modes
    lanes = near_ref.shape[1] // parts
    width = lanes // filters
    rates = of_step(rate_ref)
    lag = (1 + lax.broadcasted_iota(jnp.int32, (terms, rows), 1)).astype(F32)
    own = same_filter(modes, width, terms, lanes)
    mine = pl.program_id(0) // (STEPS // 2) == spot()[0]
    for part in range(parts):
        at = slice(part * lanes, (part + 1) * lanes)
        powers = jnp.exp(-down(rates, part, filters, rows) * lag).T
        p_high = powers.astype(BF16)
        p_low = (powers - p_high.astype(F32)).astype(BF16)
        carried = jnp.where(mine, keep_ref[:, at], back_ref[:, at])
        carried = jnp.where(own, jnp.concatenate([carried] * filters, axis=0), 0.0)
        c_high = carried.astype(BF16)
        c_low = (carried - c_high.astype(F32)).astype(BF16)
        far = (
            jnp.dot(p_high, c_high, preferred_element_type=F32)
            + jnp.dot(p_low, c_high, preferred_element_type=F32)
            + jnp.dot(p_high, c_low, preferred_element_type=F32)
        )
        query = feature(x_ref[0, :, at], halo_ref[0, :, at], w_ref, 0, at)
        out_ref[:, at] = (query * (near_ref[:, at] + far)).astype(BF16)


def hyena_finish(near, streams, halo, short_weight, keep, back, rates):
    rows, channels = near.shape
    edge = halo.shape[1]
    modes, groups = rates.shape
    filters = groups * LANES // channels
    terms = filters * modes
    wide = channels // STEPS
    by_block = lambda n: (0, n)
    by_half = lambda n: (0, n % (STEPS // 2))
    lead = lambda n: (0, 0, n)
    return pl.pallas_call(
        functools.partial(hyena_out_body, filters),
        grid=(STEPS,),
        in_specs=[
            pl.BlockSpec((rows, wide), by_block),
            pl.BlockSpec((1, rows, wide), lead),
            pl.BlockSpec((1, edge, wide), lead),
            pl.BlockSpec((3, 3, wide), lead),
            pl.BlockSpec((modes, wide), by_half),
            pl.BlockSpec((modes, wide), by_half),
            pl.BlockSpec((modes, groups), lambda n: (0, 0)),
        ],
        out_specs=pl.BlockSpec((rows, wide), by_block),
        out_shape=jax.ShapeDtypeStruct((rows, channels), BF16),
        compiler_params=limits(16),
        cost_estimate=cost(6 * rows * terms * channels, 10 * rows * channels),
        name="hyena_finish",
    )(near, streams, halo, short_weight, keep, back, rates)


def small(body, *operands, outs=1):
    def kernel(*refs):
        made = body(*(ref[...] for ref in refs[: len(operands)]))
        for ref, value in zip(refs[len(operands) :], made if outs > 1 else (made,)):
            ref[...] = value

    shape = pltpu.VMEM(operands[0].shape, operands[0].dtype)
    made = pl.pallas_call(
        kernel,
        in_specs=[VMEM] * len(operands),
        out_specs=[VMEM] * outs,
        out_shape=[shape] * outs,
        compiler_params=limits(4),
        cost_estimate=cost(operands[0].size, 4 * operands[0].size),
    )(*operands)
    return made if outs > 1 else made[0]


def scan_states(keep, away, rate, gain, rows):
    count = lax.axis_size("ctx") // ROW
    decay = lambda blocks, rate: jnp.exp(-rate * float(rows * blocks))

    def both(mine, theirs, rate):
        first = spot()[0] == 0
        even = jnp.where(first, mine, theirs)
        return decay(1, rate) * even + jnp.where(first, theirs, mine), even

    theirs = flip(away, "ctx", 1)
    chip, even = small(both, keep, theirs, rate, outs=2)

    def whole(mine, other, rate):
        first = spot()[1] == 0
        left = jnp.where(first, mine, other)
        return decay(2, rate) * left + jnp.where(first, other, mine), left

    other = flip(chip, "ctx", 2)
    total, left = small(whole, chip, other, rate, outs=2)
    before = ahead(total, "ctx", ROW)
    reach = 2
    while reach < count:
        upto = small(lambda total, before, rate: total + decay(ROW, rate) * before, total, before, rate)
        earlier = ahead(upto, "ctx", ROW * reach)
        reach *= 2
        if reach < count:
            before = small(
                lambda before, earlier, rate: before + decay(ROW * (reach // 2 - 1), rate) * earlier,
                before,
                earlier,
                rate,
            )

    def last(before, earlier, left, even, rate, gain):
        before = before + decay(ROW * (reach // 2 - 1), rate) * earlier
        core, side, _, _ = spot()
        before = jnp.where(side == 0, before, decay(2, rate) * before + left)
        second = decay(1, rate) * before + even
        return (
            gain * jnp.where(core == 0, before, second),
            gain * jnp.where(core == 0, second, before),
        )

    if count == 2:
        earlier = jnp.zeros_like(before)
    if count > 1:
        mine, away = small(last, before, earlier, left, even, rate, gain, outs=2)
    return mine, flip(away, "ctx", 1)


def lanes_from(start, size):
    return pl.ds(pl.multiple_of(start * size, size), size)


def front_body(attn, hyena, theirs_ref, edge_ref, sems):
    rows, half = theirs_ref.shape[1:]
    away = attn.at[:, :, lanes_from(1 - spot()[0], half)]
    edge = hyena.at[:, rows - EDGE : rows, :]
    copies = [
        pltpu.make_async_copy(away, theirs_ref, sems.at[0]),
        pltpu.make_async_copy(edge, edge_ref, sems.at[1]),
    ]
    for copy in copies:
        copy.start()
    for copy in copies:
        copy.wait()


def front(attn, hyena):
    count, rows, channels = attn.shape
    return pl.pallas_call(
        front_body,
        in_specs=[HBM, HBM],
        out_specs=[VMEM, VMEM],
        out_shape=[
            pltpu.VMEM((count, rows, channels // 2), attn.dtype),
            pltpu.VMEM((count, EDGE, channels), hyena.dtype),
        ],
        scratch_shapes=[pltpu.SemaphoreType.DMA((2,))],
        compiler_params=pltpu.CompilerParams(vmem_limit_bytes=ALL_VMEM - (26 << 17)),
        cost_estimate=cost(0, 4 * count * rows * channels // 2),
        name="front",
    )(attn, hyena)


def pack_body(first, streams_ref, theirs_ref, *outs):
    core, side, _, _ = spot()
    slots = (0, 1) if first == 0 else (1 - core, core)
    quarter = theirs_ref.shape[2] // 2
    for out, away in zip(outs, (0, 1)[-len(outs) :]):
        to = 1 - side if away else side
        for stream in range(first, 3):
            out[slots[0], stream - first] = streams_ref[stream, :, lanes_from(2 * core + to, quarter)]
            out[slots[1], stream - first] = theirs_ref[stream, :, lanes_from(to, quarter)]


def pack(streams, theirs, first, amount):
    _, rows, half = theirs.shape
    shape = pltpu.VMEM((2, 3 - first, rows, half // 2), BF16)
    return pl.pallas_call(
        functools.partial(pack_body, first),
        in_specs=[VMEM, VMEM],
        out_specs=[VMEM] * amount,
        out_shape=[shape] * amount,
        compiler_params=limits(10),
        cost_estimate=cost(0, 8 * amount * rows * half),
        name="pack",
    )(streams, theirs)


def odd_body(wanted, pairs, out_ref, sem):
    @pl.when(spot()[1] == wanted)
    def _():
        copy = pltpu.make_async_copy(pairs.at[0:1], out_ref, sem)
        copy.start()
        copy.wait()


def odd(pairs, wanted):
    return pl.pallas_call(
        functools.partial(odd_body, wanted),
        in_specs=[ANY],
        out_specs=VMEM,
        out_shape=pltpu.VMEM((1,) + pairs.shape[1:], pairs.dtype),
        scratch_shapes=[pltpu.SemaphoreType.DMA],
        compiler_params=limits(4),
        cost_estimate=cost(0, pairs.size * 2),
        name="odd",
    )(pairs)


def contig_start(docs_ref, position):
    first = jnp.zeros_like(position)
    bound = jnp.int32(0)
    for n in range(docs_ref.shape[0]):
        bound = bound + docs_ref[n]
        first = jnp.where(position >= bound, bound, first)
    return first


def row_part(streams, theirs, swap, slot, stream, quarter):
    core, side, _, _ = spot()
    if slot == 0:
        return streams.at[stream, :, lanes_from(2 * core + side, quarter)]
    if slot == 1:
        return theirs.at[stream, :, lanes_from(side, quarter)]
    return swap.at[slot - 2, stream]


SCALE = math.log2(math.e) / math.sqrt(HEAD)


KEYS = 256
GROUP = 2
CHUNK = 32


def attend_body(docs_ref, streams, theirs, swap, own, cross, acc_ref, m_ref, l_ref, q_s, k_s, v_s, bias_s, s_s, p_s, sems):
    _, side, place, row = spot()
    rows, quarter = q_s.shape[0] // ROW, q_s.shape[1]
    base = row * (ROW * rows)
    copies = []

    def bring(source, target):
        copies.append(pltpu.make_async_copy(source, target, sems.at[len(copies)]))
        copies[-1].start()

    for n in range(2):
        for old, which in ((own, side), (cross, 1 - side)):
            older = lanes_from(2 * which + 1 - n, rows)
            bring(old.at[n, 0], k_s.at[older])
            bring(old.at[n, 1], v_s.at[older])
    for slot in range(ROW):
        part = lambda stream: row_part(streams, theirs, swap, slot, stream, quarter)
        block = place ^ slot
        newer = lanes_from(ROW + block, rows)
        bring(part(0), q_s.at[lanes_from(block, rows)])
        bring(part(1), k_s.at[newer])
        bring(part(2), v_s.at[newer])
    for copy in copies:
        copy.wait()

    for group in range(ROW // GROUP):
        tall = GROUP * rows
        width = (ROW + GROUP * (group + 1)) * rows
        here = slice(group * tall, (group + 1) * tall)
        for block in range(GROUP):
            position = base + (group * GROUP + block) * rows + lax.broadcasted_iota(jnp.int32, (rows, 1), 0)
            first = contig_start(docs_ref, position)
            at = base - ROW * rows + lax.broadcasted_iota(jnp.int32, (rows, width), 1)
            bias_s[block * rows : (block + 1) * rows, 0:width] = jnp.where(
                (at >= first) & (at <= position), 0.0, -jnp.inf
            )
        for head in range(quarter // HEAD):
            lanes = slice(head * HEAD, (head + 1) * HEAD)
            turn = head % 2
            for n in range(0, width, KEYS):
                tile = slice(n, n + KEYS)
                s_s[turn, :, tile] = lax.dot_general(
                    q_s[here, lanes],
                    k_s[tile, lanes],
                    (((1,), (1,)), ((), ())),
                    preferred_element_type=F32,
                )
            for m in range(0, tall, CHUNK):
                some = slice(m, m + CHUNK)
                out = slice(group * tall + m, group * tall + m + CHUNK)
                top = None
                parts = []
                for n in range(0, width, LANES):
                    part = s_s[turn, some, n : n + LANES] + bias_s[some, n : n + LANES]
                    parts.append(part)
                    top = part if top is None else jnp.maximum(top, part)
                top = jnp.broadcast_to(jnp.max(top, axis=1, keepdims=True), (CHUNK, LANES))
                m_ref[out, lanes] = top
                below = jnp.zeros((CHUNK, LANES), F32)
                for n, part in enumerate(parts):
                    weight = jnp.exp2((part - top) * SCALE)
                    below = below + weight
                    p_s[turn, some, n * LANES : (n + 1) * LANES] = weight.astype(BF16)
                l_ref[out, lanes] = jnp.broadcast_to(jnp.sum(below, axis=1, keepdims=True), (CHUNK, LANES))
            acc_ref[here, lanes] = jnp.dot(
                p_s[turn, :, 0:width], v_s[0:width, lanes], preferred_element_type=F32
            )


def attend(doc_lengths, streams, theirs, swap, own, cross):
    _, _, rows, quarter = own.shape
    heads = quarter // HEAD
    return pl.pallas_call(
        attend_body,
        in_specs=[SMEM] + [ANY] * 5,
        out_specs=[VMEM] * 3,
        out_shape=[
            jax.ShapeDtypeStruct((ROW * rows, quarter), F32),
        ]
        * 3,
        scratch_shapes=[
            pltpu.VMEM((ROW * rows, quarter), BF16),
            pltpu.VMEM((2 * ROW * rows, quarter), BF16),
            pltpu.VMEM((2 * ROW * rows, quarter), BF16),
            pltpu.VMEM((GROUP * rows, 2 * ROW * rows), F32),
            pltpu.VMEM((2, GROUP * rows, 2 * ROW * rows), F32),
            pltpu.VMEM((2, GROUP * rows, 2 * ROW * rows), BF16),
            pltpu.SemaphoreType.DMA((5 * ROW,)),
        ],
        compiler_params=limits(20),
        cost_estimate=cost(26 * 4 * rows * rows * quarter, 14 * ROW * rows * quarter, 26 * heads * rows * rows),
        name="attend",
    )(doc_lengths, streams, theirs, swap, own, cross)


def attend_last_body(docs_ref, streams, theirs, swap, *refs):
    olds, (acc_ref, m_ref, l_ref), outs, (q_s, kv_s, o_s, sems) = refs[:4], refs[4:7], refs[7:11], refs[11:]
    _, side, place, row = spot()
    rows, quarter = q_s.shape[1:]
    base = row * (ROW * rows)
    copies = []

    def copy_of(source, target, n):
        return pltpu.make_async_copy(source, target, sems.at[n])

    for slot in range(ROW):
        copies.append(copy_of(row_part(streams, theirs, swap, slot, 0, quarter), q_s.at[place ^ slot], slot))
        copies[-1].start()
    for which in range(2):
        large, small = olds[2 * which : 2 * which + 2]
        arrived = [
            copy_of(small.at[0], kv_s.at[0], ROW),
            copy_of(large.at[1], kv_s.at[1], ROW + 1),
            copy_of(large.at[0], kv_s.at[2], ROW + 2),
        ]

        @pl.when(side == which)
        def _():
            for copy in arrived:
                copy.start()

    for copy in copies + arrived:
        copy.wait()
    heads = [slice(n, n + HEAD) for n in range(0, quarter, HEAD)]
    for block in range(ROW):
        slot = place ^ block
        here = slice(block * rows, (block + 1) * rows)
        seen = ROW - 1 - block
        width = seen * rows
        if not seen:
            for lanes in heads:
                o_s[slot, :, lanes] = (acc_ref[here, lanes] * (1.0 / l_ref[here, lanes])).astype(BF16)
            continue
        position = base + block * rows + lax.broadcasted_iota(jnp.int32, (rows, 1), 0)
        first = contig_start(docs_ref, position)
        at = base - (ROW + seen) * rows + lax.broadcasted_iota(jnp.int32, (rows, width), 1)
        allowed = at >= first
        scores = [
            lax.dot_general(
                q_s[block, :, lanes],
                kv_s[block : ROW - 1, 0, :, lanes].reshape(width, HEAD),
                (((1,), (1,)), ((), ())),
                preferred_element_type=F32,
            )
            for lanes in heads
        ]
        scores = [jnp.where(allowed, score, -jnp.inf) for score in scores]
        tops = [
            jnp.maximum(m_ref[here, lanes], jnp.max(score, axis=1, keepdims=True))
            for lanes, score in zip(heads, scores)
        ]
        weights = [
            jnp.exp2((score - jnp.concatenate([top] * seen, axis=1)) * SCALE)
            for score, top in zip(scores, tops)
        ]
        for lanes, top, weight in zip(heads, tops, weights):
            fade = jnp.exp2((m_ref[here, lanes] - top) * SCALE)
            share = 1.0 / (l_ref[here, lanes] * fade + jnp.sum(weight, axis=1, keepdims=True))
            more = jnp.dot(
                weight.astype(BF16),
                kv_s[block : ROW - 1, 1, :, lanes].reshape(width, HEAD),
                preferred_element_type=F32,
            )
            o_s[slot, :, lanes] = ((acc_ref[here, lanes] * fade + more) * share).astype(BF16)
    for slot, out in enumerate(outs):
        out[...] = o_s[slot]


def attend_last(doc_lengths, streams, theirs, swap, olds, acc, top, below):
    rows, quarter = acc.shape[0] // ROW, acc.shape[1]
    heads = quarter // HEAD
    return pl.pallas_call(
        attend_last_body,
        in_specs=[SMEM] + [ANY] * 7 + [VMEM] * 3,
        out_specs=[VMEM] * ROW,
        out_shape=[jax.ShapeDtypeStruct((rows, quarter), BF16)] * ROW,
        scratch_shapes=[
            pltpu.VMEM((ROW, rows, quarter), BF16),
            pltpu.VMEM((ROW - 1, 2, rows, quarter), BF16),
            pltpu.VMEM((ROW, rows, quarter), BF16),
            pltpu.SemaphoreType.DMA((2 * ROW,)),
        ],
        compiler_params=limits(16),
        cost_estimate=cost(6 * 4 * rows * rows * quarter, 12 * ROW * rows * quarter, 6 * heads * rows * rows),
        name="attend_last",
    )(doc_lengths, streams, theirs, swap, *olds, acc, top, below)


def assemble_body(*refs):
    place = spot()[2]
    *pieces, out_ref = refs
    quarter = pieces[0].shape[1]
    for slot, piece in enumerate(pieces):
        maker = place ^ slot
        which = 2 * (maker & 1) + lax.shift_right_logical(maker, 1)
        out_ref[:, lanes_from(which, quarter)] = piece[...]


def assemble(pieces):
    rows, quarter = pieces[0].shape
    return pl.pallas_call(
        assemble_body,
        in_specs=[VMEM] * ROW,
        out_specs=VMEM,
        out_shape=jax.ShapeDtypeStruct((rows, ROW * quarter), BF16),
        compiler_params=limits(6),
        cost_estimate=cost(0, 16 * rows * quarter),
        name="assemble",
    )(*pieces)


def on_device(hyena_qkv, short_weight, filter_rate, filter_residue, attn_qkv, doc_lengths):
    rows = attn_qkv.shape[0]
    inner = hyena_qkv.transpose(1, 0, 2)
    streams = attn_qkv.transpose(1, 0, 2)
    rates, residues = filter_rate.T, filter_residue.T
    theirs, edge = front(streams, inner)

    theirs = flip(theirs, "ctx", 1)
    edge = ahead(edge, "ctx", 1)
    own, cross = pack(streams, theirs, 1, 2)
    cross = ahead(cross, "ctx", ROW, 2)
    own = ahead(own, "ctx", ROW)
    (swap,) = pack(streams, theirs, 0, 1)
    swap = flip(swap, "ctx", 2)
    olds = (
        ahead(cross, "ctx", ROW, 0, ROW, 0),
        ahead(odd(own, 0), "ctx", ROW, 0, ROW, 0),
        ahead(own, "ctx", ROW, 0, ROW, 1),
        ahead(odd(cross, 1), "ctx", ROW, 0, ROW, 1),
    )

    mixed, keep, away, wide, gain = hyena_ends(inner, edge, short_weight, rates, residues)
    near = hyena_near(mixed, rates, residues)
    keep, back = scan_states(keep, away, wide, gain, rows)
    hyena_out = hyena_finish(near, inner, edge, short_weight, keep, back, rates)

    acc, top, below = attend(doc_lengths, streams, theirs, swap, own, cross)
    made = attend_last(doc_lengths, streams, theirs, swap, olds, acc, top, below)
    pieces = [made[0]] + [flip(made[n], "ctx", n) for n in range(1, ROW)]
    attn_out = assemble(pieces)
    return (hyena_out, attn_out)


def solution(mesh):
    in_specs = (
        P(("group", "ctx"), None, None),
        P(),
        P(),
        P(),
        P(("group", "ctx"), None, None),
        P("group"),
    )
    out_specs = (P(("group", "ctx"), None), P(("group", "ctx"), None))
    return jax.shard_map(on_device, mesh=mesh, in_specs=in_specs, out_specs=out_specs, check_vma=False)
```

```python
import functools
import math

import jax
import jax.numpy as jnp
from jax import lax
from jax.experimental import pallas as pl
from jax.experimental.pallas import tpu as pltpu
from jax.sharding import PartitionSpec as P


HEAD = 128
LANES = 128
EDGE = 8
ROW = 4

F32 = jnp.float32
BF16 = jnp.bfloat16


def flip(value, axis, bit):
    count = lax.axis_size(axis)
    return lax.ppermute(value, axis, [(at, at ^ bit) for at in range(count)])


def side_of(at):
    return at // 2 % 2


def ahead(value, axis, steps, bit=0, first=0, side=None):
    count = lax.axis_size(axis)
    pairs = [
        (at, (at + steps) ^ bit)
        for at in range(first, count - steps)
        if side is None or side_of(at) == side
    ]
    return lax.ppermute(value, axis, pairs)


def spot():
    index = lax.axis_index("ctx")
    return index & 1, lax.shift_right_logical(index, 1) & 1, index & (ROW - 1), index // ROW


ALL_VMEM = 67043328


def limits(mib):
    return pltpu.CompilerParams(vmem_limit_bytes=mib << 20)


def cost(flops, moved, exps=0):
    return pl.CostEstimate(flops=flops, bytes_accessed=moved, transcendentals=exps)


VMEM = pl.BlockSpec(memory_space=pltpu.VMEM)
SMEM = pl.BlockSpec(memory_space=pltpu.SMEM)
ANY = pl.BlockSpec(memory_space=pl.ANY)
HBM = pl.BlockSpec(memory_space=pltpu.HBM)


def same_filter(modes, width, terms, lanes):
    row_at = lax.broadcasted_iota(jnp.int32, (terms, lanes), 0)
    lane_at = lax.broadcasted_iota(jnp.int32, (terms, lanes), 1)
    kept = None
    for g in range(terms // modes):
        both = (
            (row_at >= g * modes)
            & (row_at < (g + 1) * modes)
            & (lane_at >= g * width)
            & (lane_at < (g + 1) * width)
        )
        kept = both if kept is None else kept | both
    return kept


def feature(x, halo, w_ref, stream, at):
    here = x.astype(F32)
    halo = halo.astype(F32)
    edge = halo.shape[0]
    row_at = lax.broadcasted_iota(jnp.int32, here.shape, 0)
    one = jnp.where(row_at == 0, halo[edge - 1 :], pltpu.roll(here, 1, 0))
    two = jnp.where(row_at == 1, halo[edge - 1 :], pltpu.roll(here, 2, 0))
    two = jnp.where(row_at == 0, halo[edge - 2 : edge - 1], two)
    tap = [w_ref[n, stream : stream + 1, at] for n in range(3)]
    return tap[0] * here + tap[1] * one + tap[2] * two


def of_step(table_ref):
    groups = table_ref.shape[1]
    return pltpu.roll(table_ref[...], groups - pl.program_id(0) * (groups // STEPS), 1)


def down(table, part, filters, lanes):
    columns = [table[:, part * filters + g : part * filters + g + 1] for g in range(filters)]
    return jnp.concatenate([jnp.broadcast_to(c, (c.shape[0], lanes)) for c in columns], axis=0)


def hyena_ends_body(
    filters, x_ref, halo_ref, w_ref, rate_ref, res_ref, mixed_ref, keep_ref, away_ref, wide_ref, gain_ref, all_s
):
    rows = x_ref.shape[1]
    modes, groups = rate_ref.shape
    parts = groups // STEPS // filters
    terms = filters * modes
    lanes = x_ref.shape[2] // parts
    width = lanes // filters
    rates = of_step(rate_ref)
    coeffs = of_step(res_ref) * jnp.sqrt(2.0 * rates / modes)
    lag = (rows - 1 - lax.broadcasted_iota(jnp.int32, (terms, rows), 1)).astype(F32)
    own = same_filter(modes, width, terms, lanes)
    pick = lambda matrix: jnp.sum(jnp.where(own, matrix, 0.0).reshape(filters, modes, lanes), axis=0)
    step = pl.program_id(0)
    for part in range(parts):
        at = slice(part * lanes, (part + 1) * lanes)
        key, value = (feature(x_ref[n, :, at], halo_ref[n, :, at], w_ref, n, at) for n in (1, 2))
        mixed = (key * value).astype(BF16)
        mixed_ref[:, at] = mixed
        rate = down(rates, part, filters, rows)
        powers = jnp.exp(-rate * lag)
        high = powers.astype(BF16)
        low = (powers - high.astype(F32)).astype(BF16)
        ends = jnp.dot(high, mixed, preferred_element_type=F32) + jnp.dot(
            low, mixed, preferred_element_type=F32
        )
        all_s[0, step, :, at] = pick(ends)
        all_s[1, step, :, at] = pick(rate)
        all_s[2, step, :, at] = pick(down(coeffs, part, filters, rows))

    @pl.when(step == STEPS - 1)
    def _():
        core = spot()[0]
        half = STEPS // 2
        for n in range(half):
            at = slice(n * parts * lanes, (n + 1) * parts * lanes)
            away_ref[:, at] = all_s[0, (1 - core) * half + n]
            for table, out in enumerate((keep_ref, wide_ref, gain_ref)):
                out[:, at] = all_s[table, core * half + n]


STEPS = 4


def hyena_ends(streams, halo, short_weight, rates, residues):
    _, rows, channels = streams.shape
    edge = halo.shape[1]
    modes, groups = rates.shape
    filters = groups * LANES // channels
    terms = filters * modes
    wide = channels // STEPS
    lead = lambda n: (0, 0, n)
    whole = lambda n: (0, 0)
    half = (modes, channels // 2)
    return pl.pallas_call(
        functools.partial(hyena_ends_body, filters),
        grid=(STEPS,),
        in_specs=[
            pl.BlockSpec((3, rows, wide), lead),
            pl.BlockSpec((3, edge, wide), lead),
            pl.BlockSpec((3, 3, wide), lead),
            pl.BlockSpec((modes, groups), whole),
            pl.BlockSpec((modes, groups), whole),
        ],
        out_specs=[pl.BlockSpec((rows, wide), lambda n: (0, n))] + [pl.BlockSpec(half, whole)] * 4,
        out_shape=[jax.ShapeDtypeStruct((rows, channels), BF16)] + [jax.ShapeDtypeStruct(half, F32)] * 4,
        scratch_shapes=[pltpu.VMEM((3, STEPS, modes, wide), F32)],
        compiler_params=limits(16),
        cost_estimate=cost(4 * rows * terms * channels, 8 * rows * channels),
        name="hyena_ends",
    )(streams, halo, short_weight, rates, residues)


def hyena_near_body(filters, mixed_ref, rate_ref, res_ref, near_ref, taps_s, u_s):
    rows = mixed_ref.shape[0]
    modes, groups = rate_ref.shape
    parts = groups // STEPS // filters
    terms = filters * modes
    lanes = mixed_ref.shape[1] // parts
    width = lanes // filters
    rates = of_step(rate_ref)
    coeffs = of_step(res_ref) * jnp.sqrt(2.0 * rates / modes)
    row_at = lax.broadcasted_iota(jnp.int32, (rows, lanes), 0)
    lane_at = lax.broadcasted_iota(jnp.int32, (rows, lanes), 1)
    lag = (rows - 1 - lax.broadcasted_iota(jnp.int32, (terms, rows), 1)).astype(F32)
    zero = jnp.zeros((rows, lanes), BF16)
    for part in range(parts):
        at = slice(part * lanes, (part + 1) * lanes)
        mixed = mixed_ref[:, at]
        rate = down(rates, part, filters, rows)
        powers = down(coeffs, part, filters, rows) * jnp.exp(-rate * lag)
        backward = jnp.sum(powers.reshape(filters, modes, rows), axis=1)
        for g in range(filters):
            spread = jnp.broadcast_to(backward[g : g + 1], (rows, rows))
            shifted = pltpu.roll(spread, 1, 1, stride=1, stride_axis=0)
            kept = jnp.where(lane_at <= row_at, shifted, 0.0)
            taps_s[part, :, g * rows : (g + 1) * rows] = kept.astype(BF16)
            mine = (lane_at >= g * width) & (lane_at < (g + 1) * width)
            u_s[part, g * rows : (g + 1) * rows, :] = jnp.where(mine, mixed, zero)
        near_ref[:, at] = jnp.dot(taps_s[part], u_s[part], preferred_element_type=F32)


def hyena_near(mixed, rates, residues):
    rows, channels = mixed.shape
    modes, groups = rates.shape
    lanes = LANES
    filters = groups * lanes // channels
    parts = groups // STEPS // filters
    wide = channels // STEPS
    by_block = lambda n: (0, n)
    whole = lambda n: (0, 0)
    return pl.pallas_call(
        functools.partial(hyena_near_body, filters),
        grid=(STEPS,),
        in_specs=[
            pl.BlockSpec((rows, wide), by_block),
            pl.BlockSpec((modes, groups), whole),
            pl.BlockSpec((modes, groups), whole),
        ],
        out_specs=pl.BlockSpec((rows, wide), by_block),
        out_shape=jax.ShapeDtypeStruct((rows, channels), F32),
        scratch_shapes=[
            pltpu.VMEM((parts, rows, filters * rows), BF16),
            pltpu.VMEM((parts, filters * rows, lanes), BF16),
        ],
        compiler_params=limits(16),
        cost_estimate=cost(2 * rows * rows * filters * channels, 12 * rows * channels),
        name="hyena_near",
    )(mixed, rates, residues)


def hyena_out_body(filters, near_ref, x_ref, halo_ref, w_ref, keep_ref, back_ref, rate_ref, out_ref):
    rows = near_ref.shape[0]
    modes, groups = rate_ref.shape
    parts = groups // STEPS // filters
    terms = filters * modes
    lanes = near_ref.shape[1] // parts
    width = lanes // filters
    rates = of_step(rate_ref)
    lag = (1 + lax.broadcasted_iota(jnp.int32, (terms, rows), 1)).astype(F32)
    own = same_filter(modes, width, terms, lanes)
    mine = pl.program_id(0) // (STEPS // 2) == spot()[0]
    for part in range(parts):
        at = slice(part * lanes, (part + 1) * lanes)
        powers = jnp.exp(-down(rates, part, filters, rows) * lag).T
        p_high = powers.astype(BF16)
        p_low = (powers - p_high.astype(F32)).astype(BF16)
        carried = jnp.where(mine, keep_ref[:, at], back_ref[:, at])
        carried = jnp.where(own, jnp.concatenate([carried] * filters, axis=0), 0.0)
        c_high = carried.astype(BF16)
        c_low = (carried - c_high.astype(F32)).astype(BF16)
        far = (
            jnp.dot(p_high, c_high, preferred_element_type=F32)
            + jnp.dot(p_low, c_high, preferred_element_type=F32)
            + jnp.dot(p_high, c_low, preferred_element_type=F32)
        )
        query = feature(x_ref[0, :, at], halo_ref[0, :, at], w_ref, 0, at)
        out_ref[:, at] = (query * (near_ref[:, at] + far)).astype(BF16)


def hyena_finish(near, streams, halo, short_weight, keep, back, rates):
    rows, channels = near.shape
    edge = halo.shape[1]
    modes, groups = rates.shape
    filters = groups * LANES // channels
    terms = filters * modes
    wide = channels // STEPS
    by_block = lambda n: (0, n)
    by_half = lambda n: (0, n % (STEPS // 2))
    lead = lambda n: (0, 0, n)
    return pl.pallas_call(
        functools.partial(hyena_out_body, filters),
        grid=(STEPS,),
        in_specs=[
            pl.BlockSpec((rows, wide), by_block),
            pl.BlockSpec((1, rows, wide), lead),
            pl.BlockSpec((1, edge, wide), lead),
            pl.BlockSpec((3, 3, wide), lead),
            pl.BlockSpec((modes, wide), by_half),
            pl.BlockSpec((modes, wide), by_half),
            pl.BlockSpec((modes, groups), lambda n: (0, 0)),
        ],
        out_specs=pl.BlockSpec((rows, wide), by_block),
        out_shape=jax.ShapeDtypeStruct((rows, channels), BF16),
        compiler_params=limits(16),
        cost_estimate=cost(6 * rows * terms * channels, 10 * rows * channels),
        name="hyena_finish",
    )(near, streams, halo, short_weight, keep, back, rates)


def small(body, *operands, outs=1):
    def kernel(*refs):
        made = body(*(ref[...] for ref in refs[: len(operands)]))
        for ref, value in zip(refs[len(operands) :], made if outs > 1 else (made,)):
            ref[...] = value

    shape = pltpu.VMEM(operands[0].shape, operands[0].dtype)
    made = pl.pallas_call(
        kernel,
        in_specs=[VMEM] * len(operands),
        out_specs=[VMEM] * outs,
        out_shape=[shape] * outs,
        compiler_params=limits(4),
        cost_estimate=cost(operands[0].size, 4 * operands[0].size),
    )(*operands)
    return made if outs > 1 else made[0]


def scan_states(keep, away, rate, gain, rows):
    count = lax.axis_size("ctx") // ROW
    decay = lambda blocks, rate: jnp.exp(-rate * float(rows * blocks))

    def both(mine, theirs, rate):
        first = spot()[0] == 0
        even = jnp.where(first, mine, theirs)
        return decay(1, rate) * even + jnp.where(first, theirs, mine), even

    theirs = flip(away, "ctx", 1)
    chip, even = small(both, keep, theirs, rate, outs=2)

    def whole(mine, other, rate):
        first = spot()[1] == 0
        left = jnp.where(first, mine, other)
        return decay(2, rate) * left + jnp.where(first, other, mine), left

    other = flip(chip, "ctx", 2)
    total, left = small(whole, chip, other, rate, outs=2)
    before = ahead(total, "ctx", ROW)
    reach = 2
    while reach < count:
        upto = small(lambda total, before, rate: total + decay(ROW, rate) * before, total, before, rate)
        earlier = ahead(upto, "ctx", ROW * reach)
        reach *= 2
        if reach < count:
            before = small(
                lambda before, earlier, rate: before + decay(ROW * (reach // 2 - 1), rate) * earlier,
                before,
                earlier,
                rate,
            )

    def last(before, earlier, left, even, rate, gain):
        before = before + decay(ROW * (reach // 2 - 1), rate) * earlier
        core, side, _, _ = spot()
        before = jnp.where(side == 0, before, decay(2, rate) * before + left)
        second = decay(1, rate) * before + even
        return (
            gain * jnp.where(core == 0, before, second),
            gain * jnp.where(core == 0, second, before),
        )

    if count == 2:
        earlier = jnp.zeros_like(before)
    if count > 1:
        mine, away = small(last, before, earlier, left, even, rate, gain, outs=2)
    return mine, flip(away, "ctx", 1)


def lanes_from(start, size):
    return pl.ds(pl.multiple_of(start * size, size), size)


def front_body(attn, hyena, theirs_ref, edge_ref, sems):
    rows, half = theirs_ref.shape[1:]
    away = attn.at[:, :, lanes_from(1 - spot()[0], half)]
    edge = hyena.at[:, rows - EDGE : rows, :]
    copies = [
        pltpu.make_async_copy(away, theirs_ref, sems.at[0]),
        pltpu.make_async_copy(edge, edge_ref, sems.at[1]),
    ]
    for copy in copies:
        copy.start()
    for copy in copies:
        copy.wait()


def front(attn, hyena):
    count, rows, channels = attn.shape
    return pl.pallas_call(
        front_body,
        in_specs=[HBM, HBM],
        out_specs=[VMEM, VMEM],
        out_shape=[
            pltpu.VMEM((count, rows, channels // 2), attn.dtype),
            pltpu.VMEM((count, EDGE, channels), hyena.dtype),
        ],
        scratch_shapes=[pltpu.SemaphoreType.DMA((2,))],
        compiler_params=pltpu.CompilerParams(vmem_limit_bytes=ALL_VMEM - (26 << 17)),
        cost_estimate=cost(0, 4 * count * rows * channels // 2),
        name="front",
    )(attn, hyena)


def pack_body(first, streams_ref, theirs_ref, *outs):
    core, side, _, _ = spot()
    slots = (0, 1) if first == 0 else (1 - core, core)
    quarter = theirs_ref.shape[2] // 2
    for out, away in zip(outs, (0, 1)[-len(outs) :]):
        to = 1 - side if away else side
        for stream in range(first, 3):
            out[slots[0], stream - first] = streams_ref[stream, :, lanes_from(2 * core + to, quarter)]
            out[slots[1], stream - first] = theirs_ref[stream, :, lanes_from(to, quarter)]


def pack(streams, theirs, first, amount):
    _, rows, half = theirs.shape
    shape = pltpu.VMEM((2, 3 - first, rows, half // 2), BF16)
    return pl.pallas_call(
        functools.partial(pack_body, first),
        in_specs=[VMEM, VMEM],
        out_specs=[VMEM] * amount,
        out_shape=[shape] * amount,
        compiler_params=limits(10),
        cost_estimate=cost(0, 8 * amount * rows * half),
        name="pack",
    )(streams, theirs)


def odd_body(wanted, pairs, out_ref, sem):
    @pl.when(spot()[1] == wanted)
    def _():
        copy = pltpu.make_async_copy(pairs.at[0:1], out_ref, sem)
        copy.start()
        copy.wait()


def odd(pairs, wanted):
    return pl.pallas_call(
        functools.partial(odd_body, wanted),
        in_specs=[ANY],
        out_specs=VMEM,
        out_shape=pltpu.VMEM((1,) + pairs.shape[1:], pairs.dtype),
        scratch_shapes=[pltpu.SemaphoreType.DMA],
        compiler_params=limits(4),
        cost_estimate=cost(0, pairs.size * 2),
        name="odd",
    )(pairs)


def contig_start(docs_ref, position):
    first = jnp.zeros_like(position)
    bound = jnp.int32(0)
    for n in range(docs_ref.shape[0]):
        bound = bound + docs_ref[n]
        first = jnp.where(position >= bound, bound, first)
    return first


def row_part(streams, theirs, swap, slot, stream, head, quarter):
    core, side, _, _ = spot()
    if slot < 2:
        start = (side if slot else 2 * core + side) * quarter + head * HEAD
        lanes = pl.ds(pl.multiple_of(start, HEAD), HEAD)
        return theirs[stream, :, lanes] if slot else streams[stream, :, lanes]
    return swap[slot - 2, stream, :, head * HEAD : (head + 1) * HEAD]


SCALE = math.log2(math.e) / math.sqrt(HEAD)


CHUNK = 32


def softmax_group(queries, keys, values, bias, turn, s_s, p_s, keep):
    tall, rows = queries.shape[0], keys[0].shape[0]
    width = len(keys) * rows
    for n in range(0, len(keys), 2):
        s_s[turn, 0:tall, n * rows : (n + 2) * rows] = lax.dot_general(
            queries,
            jnp.concatenate(keys[n : n + 2], axis=0),
            (((1,), (1,)), ((), ())),
            preferred_element_type=F32,
        )
    for m in range(0, tall, CHUNK):
        some = slice(m, m + CHUNK)
        top = None
        parts = []
        for n in range(0, width, LANES):
            part = s_s[turn, some, n : n + LANES] + bias[some, n : n + LANES]
            parts.append(part)
            top = part if top is None else jnp.maximum(top, part)
        top = jnp.broadcast_to(jnp.max(top, axis=1, keepdims=True), (CHUNK, LANES))
        below = jnp.zeros((CHUNK, LANES), F32)
        for n, part in enumerate(parts):
            weight = jnp.exp2((part - top) * SCALE)
            below = below + weight
            p_s[turn, some, n * LANES : (n + 1) * LANES] = weight.astype(BF16)
        keep(m, top, jnp.broadcast_to(jnp.sum(below, axis=1, keepdims=True), (CHUNK, LANES)))
    return jnp.dot(
        p_s[turn, 0:tall, 0:width], jnp.concatenate(values, axis=0), preferred_element_type=F32
    )


def attend_body(docs_ref, streams, theirs, swap, own, cross, acc_ref, m_ref, l_ref, bias_s, s_s, p_s):
    _, side, place, row = spot()
    rows, quarter = own.shape[2:]
    base = row * (ROW * rows)
    part = functools.partial(row_part, streams, theirs, swap, quarter=quarter)

    def run(first_pair, second_pair):
        for group, (asking, seen) in enumerate(((first_pair, first_pair), (second_pair, (0, 1, 2, 3)))):
            starts = [base + (2 * (side if old else 1 - side) + 1 - n - ROW) * rows for old in (1, 0) for n in (0, 1)]
            starts += [base + (place ^ slot) * rows for slot in seen]
            for at, slot in enumerate(asking):
                position = base + (place ^ slot) * rows + lax.broadcasted_iota(jnp.int32, (rows, 1), 0)
                first = contig_start(docs_ref, position)
                for n, start in enumerate(starts):
                    token = start + lax.broadcasted_iota(jnp.int32, (rows, rows), 1)
                    bias_s[group, at * rows : (at + 1) * rows, n * rows : (n + 1) * rows] = jnp.where(
                        (token >= first) & (token <= position), 0.0, -jnp.inf
                    )
            for head in range(quarter // HEAD):
                lanes = slice(head * HEAD, (head + 1) * HEAD)
                olds = lambda kind: [old[n, kind, :, lanes] for old in (own, cross) for n in (0, 1)]

                def keep(m, top, below):
                    out = slice(asking[0] * rows + m, asking[0] * rows + m + CHUNK)
                    m_ref[out, lanes] = top
                    l_ref[out, lanes] = below

                acc_ref[asking[0] * rows : (asking[1] + 1) * rows, lanes] = softmax_group(
                    jnp.concatenate([part(slot, 0, head) for slot in asking], axis=0),
                    olds(0) + [part(slot, 1, head) for slot in seen],
                    olds(1) + [part(slot, 2, head) for slot in seen],
                    bias_s.at[group],
                    head % 2,
                    s_s,
                    p_s,
                    keep,
                )

    @pl.when(side == 0)
    def _():
        run((0, 1), (2, 3))

    @pl.when(side == 1)
    def _():
        run((2, 3), (0, 1))


def attend(doc_lengths, streams, theirs, swap, own, cross):
    _, _, rows, quarter = own.shape
    heads = quarter // HEAD
    return pl.pallas_call(
        attend_body,
        in_specs=[SMEM] + [VMEM] * 5,
        out_specs=[VMEM] * 3,
        out_shape=[
            jax.ShapeDtypeStruct((ROW * rows, quarter), F32),
        ]
        * 3,
        scratch_shapes=[
            pltpu.VMEM((2, 2 * rows, 2 * ROW * rows), F32),
            pltpu.VMEM((2, 2 * rows, 2 * ROW * rows), F32),
            pltpu.VMEM((2, 2 * rows, 2 * ROW * rows), BF16),
        ],
        compiler_params=limits(20),
        cost_estimate=cost(26 * 4 * rows * rows * quarter, 14 * ROW * rows * quarter, 26 * heads * rows * rows),
        name="attend",
    )(doc_lengths, streams, theirs, swap, own, cross)


def attend_last_body(docs_ref, streams, theirs, swap, *refs):
    cross_l, own_s, own_l, cross_s, acc_ref, m_ref, l_ref = refs[:7]
    outs = refs[7:]
    _, side, place, row = spot()
    rows, quarter = acc_ref.shape[0] // ROW, acc_ref.shape[1]
    base = row * (ROW * rows)
    heads = range(quarter // HEAD)

    def run(early, late, large, small):
        for asking, blocks in ((early, ((small, 0), (large, 1), (large, 0))), (late, ((large, 0),))):
            width = len(blocks) * rows
            here = slice(asking[0] * rows, (asking[1] + 1) * rows)
            token = base - (ROW + len(blocks)) * rows + lax.broadcasted_iota(jnp.int32, (rows, width), 1)
            allowed = []
            for slot in asking:
                position = base + (place ^ slot) * rows + lax.broadcasted_iota(jnp.int32, (rows, 1), 0)
                allowed.append((token >= contig_start(docs_ref, position)).astype(jnp.int32))
            allowed = jnp.concatenate(allowed, axis=0) != 0
            lanes_of = [slice(head * HEAD, (head + 1) * HEAD) for head in heads]
            stack = lambda kind, lanes: jnp.concatenate([ref[n, kind, :, lanes] for ref, n in blocks], axis=0)
            scores = [
                lax.dot_general(
                    jnp.concatenate(
                        [row_part(streams, theirs, swap, slot, 0, head, quarter) for slot in asking], axis=0
                    ),
                    stack(0, lanes_of[head]),
                    (((1,), (1,)), ((), ())),
                    preferred_element_type=F32,
                )
                for head in heads
            ]
            scores = [jnp.where(allowed, score, -jnp.inf) for score in scores]
            tops = [
                jnp.maximum(m_ref[here, lanes], jnp.max(score, axis=1, keepdims=True))
                for lanes, score in zip(lanes_of, scores)
            ]
            weights = [
                jnp.exp2((score - jnp.concatenate([top] * len(blocks), axis=1)) * SCALE)
                for score, top in zip(scores, tops)
            ]
            for lanes, top, weight in zip(lanes_of, tops, weights):
                fade = jnp.exp2((m_ref[here, lanes] - top) * SCALE)
                share = 1.0 / (l_ref[here, lanes] * fade + jnp.sum(weight, axis=1, keepdims=True))
                more = jnp.dot(weight.astype(BF16), stack(1, lanes), preferred_element_type=F32)
                made = ((acc_ref[here, lanes] * fade + more) * share).astype(BF16)
                for n, slot in enumerate(asking):
                    outs[slot][:, lanes] = made[n * rows : (n + 1) * rows]

    @pl.when(side == 0)
    def _():
        run((0, 1), (2, 3), cross_l, own_s)

    @pl.when(side == 1)
    def _():
        run((2, 3), (0, 1), own_l, cross_s)


def attend_last(doc_lengths, streams, theirs, swap, olds, acc, top, below):
    rows, quarter = acc.shape[0] // ROW, acc.shape[1]
    heads = quarter // HEAD
    return pl.pallas_call(
        attend_last_body,
        in_specs=[SMEM] + [VMEM] * 10,
        out_specs=[VMEM] * ROW,
        out_shape=[jax.ShapeDtypeStruct((rows, quarter), BF16)] * ROW,
        compiler_params=limits(16),
        cost_estimate=cost(6 * 4 * rows * rows * quarter, 12 * ROW * rows * quarter, 6 * heads * rows * rows),
        name="attend_last",
    )(doc_lengths, streams, theirs, swap, *olds, acc, top, below)


def assemble_body(*refs):
    place = spot()[2]
    *pieces, out_ref = refs
    quarter = pieces[0].shape[1]
    for slot, piece in enumerate(pieces):
        maker = place ^ slot
        which = 2 * (maker & 1) + lax.shift_right_logical(maker, 1)
        out_ref[:, lanes_from(which, quarter)] = piece[...]


def assemble(pieces):
    rows, quarter = pieces[0].shape
    return pl.pallas_call(
        assemble_body,
        in_specs=[VMEM] * ROW,
        out_specs=VMEM,
        out_shape=jax.ShapeDtypeStruct((rows, ROW * quarter), BF16),
        compiler_params=limits(6),
        cost_estimate=cost(0, 16 * rows * quarter),
        name="assemble",
    )(*pieces)


def on_device(hyena_qkv, short_weight, filter_rate, filter_residue, attn_qkv, doc_lengths):
    rows = attn_qkv.shape[0]
    inner = hyena_qkv.transpose(1, 0, 2)
    streams = attn_qkv.transpose(1, 0, 2)
    rates, residues = filter_rate.T, filter_residue.T
    theirs, edge = front(streams, inner)

    theirs = flip(theirs, "ctx", 1)
    edge = ahead(edge, "ctx", 1)
    own, cross = pack(streams, theirs, 1, 2)
    cross = ahead(cross, "ctx", ROW, 2)
    own = ahead(own, "ctx", ROW)
    (swap,) = pack(streams, theirs, 0, 1)
    swap = flip(swap, "ctx", 2)
    olds = (
        ahead(cross, "ctx", ROW, 0, ROW, 0),
        ahead(odd(own, 0), "ctx", ROW, 0, ROW, 0),
        ahead(own, "ctx", ROW, 0, ROW, 1),
        ahead(odd(cross, 1), "ctx", ROW, 0, ROW, 1),
    )

    mixed, keep, away, wide, gain = hyena_ends(inner, edge, short_weight, rates, residues)
    near = hyena_near(mixed, rates, residues)
    keep, back = scan_states(keep, away, wide, gain, rows)
    hyena_out = hyena_finish(near, inner, edge, short_weight, keep, back, rates)

    acc, top, below = attend(doc_lengths, streams, theirs, swap, own, cross)
    made = attend_last(doc_lengths, streams, theirs, swap, olds, acc, top, below)
    pieces = [made[0]] + [flip(made[n], "ctx", n) for n in range(1, ROW)]
    attn_out = assemble(pieces)
    return (hyena_out, attn_out)


def solution(mesh):
    in_specs = (
        P(("group", "ctx"), None, None),
        P(),
        P(),
        P(),
        P(("group", "ctx"), None, None),
        P("group"),
    )
    out_specs = (P(("group", "ctx"), None), P(("group", "ctx"), None))
    return jax.shard_map(on_device, mesh=mesh, in_specs=in_specs, out_specs=out_specs, check_vma=False)
```

```python
import functools
import math

import jax
import jax.numpy as jnp
from jax import lax
from jax.experimental import pallas as pl
from jax.experimental.pallas import tpu as pltpu
from jax.sharding import PartitionSpec as P


HEAD = 128
LANES = 128
TURNS = 1
EDGE = 8
ROW = 4


F32 = jnp.float32
BF16 = jnp.bfloat16


def flip(value, axis, bit):
    count = lax.axis_size(axis)
    return lax.ppermute(value, axis, [(at, at ^ bit) for at in range(count)])


def side_of(at):
    return at // 2 % 2


def ahead(value, axis, steps, bit=0, first=0, side=None):
    count = lax.axis_size(axis)
    pairs = [
        (at, (at + steps) ^ bit)
        for at in range(first, count - steps)
        if side is None or side_of(at) == side
    ]
    return lax.ppermute(value, axis, pairs)


def spot():
    index = lax.axis_index("ctx")
    return index & 1, lax.shift_right_logical(index, 1) & 1, index & (ROW - 1), index // ROW


ALL_VMEM = 67043328


def limits(mib):
    return pltpu.CompilerParams(vmem_limit_bytes=mib << 20)


def cost(flops, moved, exps=0):
    return pl.CostEstimate(flops=flops, bytes_accessed=moved, transcendentals=exps)


VMEM = pl.BlockSpec(memory_space=pltpu.VMEM)
SMEM = pl.BlockSpec(memory_space=pltpu.SMEM)
ANY = pl.BlockSpec(memory_space=pl.ANY)
HBM = pl.BlockSpec(memory_space=pltpu.HBM)


def same_filter(modes, width, terms, lanes):
    row_at = lax.broadcasted_iota(jnp.int32, (terms, lanes), 0)
    lane_at = lax.broadcasted_iota(jnp.int32, (terms, lanes), 1)
    kept = None
    for g in range(terms // modes):
        both = (
            (row_at >= g * modes)
            & (row_at < (g + 1) * modes)
            & (lane_at >= g * width)
            & (lane_at < (g + 1) * width)
        )
        kept = both if kept is None else kept | both
    return kept


def feature(x, halo, w_ref, stream, at):
    here = x.astype(F32)
    halo = halo.astype(F32)
    edge = halo.shape[0]
    row_at = lax.broadcasted_iota(jnp.int32, here.shape, 0)
    one = jnp.where(row_at == 0, halo[edge - 1 :], pltpu.roll(here, 1, 0))
    two = jnp.where(row_at == 1, halo[edge - 1 :], pltpu.roll(here, 2, 0))
    two = jnp.where(row_at == 0, halo[edge - 2 : edge - 1], two)
    tap = [w_ref[n, stream : stream + 1, at] for n in range(3)]
    return tap[0] * here + tap[1] * one + tap[2] * two


def of_step(table_ref):
    groups = table_ref.shape[1]
    return pltpu.roll(table_ref[...], groups - pl.program_id(0) * (groups // STEPS), 1)


def down(table, part, filters, lanes):
    columns = [table[:, part * filters + g : part * filters + g + 1] for g in range(filters)]
    return jnp.concatenate([jnp.broadcast_to(c, (c.shape[0], lanes)) for c in columns], axis=0)


def hyena_ends_body(
    filters, x_ref, halo_ref, w_ref, rate_ref, res_ref, mixed_ref, keep_ref, away_ref, wide_ref, gain_ref, all_s
):
    rows = x_ref.shape[1]
    modes, groups = rate_ref.shape
    parts = groups // STEPS // filters
    terms = filters * modes
    lanes = x_ref.shape[2] // parts
    width = lanes // filters
    rates = of_step(rate_ref)
    coeffs = of_step(res_ref) * jnp.sqrt(2.0 * rates / modes)
    lag = (rows - 1 - lax.broadcasted_iota(jnp.int32, (terms, rows), 1)).astype(F32)
    own = same_filter(modes, width, terms, lanes)
    pick = lambda matrix: jnp.sum(jnp.where(own, matrix, 0.0).reshape(filters, modes, lanes), axis=0)
    step = pl.program_id(0)
    for part in range(parts):
        at = slice(part * lanes, (part + 1) * lanes)
        key, value = (feature(x_ref[n, :, at], halo_ref[n, :, at], w_ref, n, at) for n in (1, 2))
        mixed = (key * value).astype(BF16)
        mixed_ref[:, at] = mixed
        rate = down(rates, part, filters, rows)
        powers = jnp.exp(-rate * lag)
        high = powers.astype(BF16)
        low = (powers - high.astype(F32)).astype(BF16)
        ends = jnp.dot(high, mixed, preferred_element_type=F32) + jnp.dot(
            low, mixed, preferred_element_type=F32
        )
        all_s[0, step, :, at] = pick(ends)
        all_s[1, step, :, at] = pick(rate)
        all_s[2, step, :, at] = pick(down(coeffs, part, filters, rows))

    @pl.when(step == STEPS - 1)
    def _():
        core = spot()[0]
        half = STEPS // 2
        for n in range(half):
            at = slice(n * parts * lanes, (n + 1) * parts * lanes)
            away_ref[:, at] = all_s[0, (1 - core) * half + n]
            for table, out in enumerate((keep_ref, wide_ref, gain_ref)):
                out[:, at] = all_s[table, core * half + n]


STEPS = 4


def hyena_ends(streams, halo, short_weight, rates, residues):
    _, rows, channels = streams.shape
    edge = halo.shape[1]
    modes, groups = rates.shape
    filters = groups * LANES // channels
    terms = filters * modes
    wide = channels // STEPS
    lead = lambda n: (0, 0, n)
    whole = lambda n: (0, 0)
    half = (modes, channels // 2)
    return pl.pallas_call(
        functools.partial(hyena_ends_body, filters),
        grid=(STEPS,),
        in_specs=[
            pl.BlockSpec((3, rows, wide), lead),
            pl.BlockSpec((3, edge, wide), lead),
            pl.BlockSpec((3, 3, wide), lead),
            pl.BlockSpec((modes, groups), whole),
            pl.BlockSpec((modes, groups), whole),
        ],
        out_specs=[pl.BlockSpec((rows, wide), lambda n: (0, n))] + [pl.BlockSpec(half, whole)] * 4,
        out_shape=[jax.ShapeDtypeStruct((rows, channels), BF16)] + [jax.ShapeDtypeStruct(half, F32)] * 4,
        scratch_shapes=[pltpu.VMEM((3, STEPS, modes, wide), F32)],
        compiler_params=limits(16),
        cost_estimate=cost(4 * rows * terms * channels, 8 * rows * channels),
        name="hyena_ends",
    )(streams, halo, short_weight, rates, residues)


def hyena_near_body(
    filters, x_ref, halo_ref, w_ref, mixed_ref, rate_ref, res_ref, near_ref, q_ref, high_ref, low_ref, taps_s, u_s
):
    rows = mixed_ref.shape[0]
    modes, groups = rate_ref.shape
    parts = groups // STEPS // filters
    terms = filters * modes
    lanes = mixed_ref.shape[1] // parts
    width = lanes // filters
    rates = of_step(rate_ref)
    coeffs = of_step(res_ref) * jnp.sqrt(2.0 * rates / modes)
    row_at = lax.broadcasted_iota(jnp.int32, (rows, lanes), 0)
    lane_at = lax.broadcasted_iota(jnp.int32, (rows, lanes), 1)
    lag = (rows - 1 - lax.broadcasted_iota(jnp.int32, (terms, rows), 1)).astype(F32)
    ahead_lag = (1 + lax.broadcasted_iota(jnp.int32, (terms, rows), 1)).astype(F32)
    zero = jnp.zeros((rows, lanes), BF16)
    for part in range(parts):
        at = slice(part * lanes, (part + 1) * lanes)
        mixed = mixed_ref[:, at]
        rate = down(rates, part, filters, rows)
        powers = down(coeffs, part, filters, rows) * jnp.exp(-rate * lag)
        backward = jnp.sum(powers.reshape(filters, modes, rows), axis=1)
        for g in range(filters):
            spread = jnp.broadcast_to(backward[g : g + 1], (rows, rows))
            shifted = pltpu.roll(spread, 1, 1, stride=1, stride_axis=0)
            kept = jnp.where(lane_at <= row_at, shifted, 0.0)
            taps_s[part, :, g * rows : (g + 1) * rows] = kept.astype(BF16)
            mine = (lane_at >= g * width) & (lane_at < (g + 1) * width)
            u_s[part, g * rows : (g + 1) * rows, :] = jnp.where(mine, mixed, zero)
        near_ref[:, at] = jnp.dot(taps_s[part], u_s[part], preferred_element_type=F32)
        q_ref[:, at] = feature(x_ref[0, :, at], halo_ref[0, :, at], w_ref, 0, at)
        decays = jnp.exp(-rate * ahead_lag).T
        here = slice(part * terms, (part + 1) * terms)
        high = decays.astype(BF16)
        high_ref[:, here] = high
        low_ref[:, here] = (decays - high.astype(F32)).astype(BF16)


def hyena_near(streams, halo, short_weight, mixed, rates, residues):
    rows, channels = mixed.shape
    edge = halo.shape[1]
    modes, groups = rates.shape
    lanes = LANES
    filters = groups * lanes // channels
    terms = filters * modes
    parts = groups // STEPS // filters
    wide = channels // STEPS
    by_block = lambda n: (0, n)
    lead = lambda n: (0, 0, n)
    whole = lambda n: (0, 0)
    return pl.pallas_call(
        functools.partial(hyena_near_body, filters),
        grid=(STEPS,),
        in_specs=[
            pl.BlockSpec((1, rows, wide), lead),
            pl.BlockSpec((1, edge, wide), lead),
            pl.BlockSpec((3, 3, wide), lead),
            pl.BlockSpec((rows, wide), by_block),
            pl.BlockSpec((modes, groups), whole),
            pl.BlockSpec((modes, groups), whole),
        ],
        out_specs=[pl.BlockSpec((rows, wide), by_block)] * 2 + [pl.BlockSpec((rows, parts * terms), by_block)] * 2,
        out_shape=[jax.ShapeDtypeStruct((rows, channels), F32)] * 2
        + [jax.ShapeDtypeStruct((rows, groups * modes), BF16)] * 2,
        scratch_shapes=[
            pltpu.VMEM((parts, rows, filters * rows), BF16),
            pltpu.VMEM((parts, filters * rows, lanes), BF16),
        ],
        compiler_params=limits(16),
        cost_estimate=cost(2 * rows * rows * filters * channels, 12 * rows * channels),
        name="hyena_near",
    )(streams, halo, short_weight, mixed, rates, residues)


def hyena_out_body(modes, near_ref, q_ref, high_ref, low_ref, keep_ref, back_ref, out_ref):
    wide = near_ref.shape[1]
    terms = high_ref.shape[1] * LANES // wide
    filters = terms // modes
    own = same_filter(modes, LANES // filters, terms, LANES)
    mine = pl.program_id(0) // (STEPS // 2) == spot()[0]
    for part in range(wide // LANES):
        at = slice(part * LANES, (part + 1) * LANES)
        here = slice(part * terms, (part + 1) * terms)
        carried = jnp.where(mine, keep_ref[:, at], back_ref[:, at])
        carried = jnp.where(own, jnp.concatenate([carried] * filters, axis=0), 0.0)
        c_high = carried.astype(BF16)
        c_low = (carried - c_high.astype(F32)).astype(BF16)
        high, low = high_ref[:, here], low_ref[:, here]
        far = (
            jnp.dot(high, c_high, preferred_element_type=F32)
            + jnp.dot(low, c_high, preferred_element_type=F32)
            + jnp.dot(high, c_low, preferred_element_type=F32)
        )
        out_ref[:, at] = (q_ref[:, at] * (near_ref[:, at] + far)).astype(BF16)


def hyena_finish(near, query, high, low, keep, back):
    rows, channels = near.shape
    modes = keep.shape[0]
    wide = channels // STEPS
    by_block = lambda n: (0, n)
    by_half = lambda n: (0, n % (STEPS // 2))
    return pl.pallas_call(
        functools.partial(hyena_out_body, modes),
        grid=(STEPS,),
        in_specs=[
            pl.BlockSpec((rows, wide), by_block),
            pl.BlockSpec((rows, wide), by_block),
            pl.BlockSpec((rows, high.shape[1] // STEPS), by_block),
            pl.BlockSpec((rows, high.shape[1] // STEPS), by_block),
            pl.BlockSpec((modes, wide), by_half),
            pl.BlockSpec((modes, wide), by_half),
        ],
        out_specs=pl.BlockSpec((rows, wide), by_block),
        out_shape=jax.ShapeDtypeStruct((rows, channels), BF16),
        compiler_params=limits(16),
        cost_estimate=cost(6 * rows * high.size, 10 * rows * channels),
        name="hyena_finish",
    )(near, query, high, low, keep, back)


def small(body, *operands, outs=1):
    def kernel(*refs):
        made = body(*(ref[...] for ref in refs[: len(operands)]))
        for ref, value in zip(refs[len(operands) :], made if outs > 1 else (made,)):
            ref[...] = value

    shape = pltpu.VMEM(operands[0].shape, operands[0].dtype)
    made = pl.pallas_call(
        kernel,
        in_specs=[VMEM] * len(operands),
        out_specs=[VMEM] * outs,
        out_shape=[shape] * outs,
        compiler_params=limits(4),
        cost_estimate=cost(operands[0].size, 4 * operands[0].size),
    )(*operands)
    return made if outs > 1 else made[0]


def scan_states(keep, away, rate, gain, rows):
    count = lax.axis_size("ctx") // ROW
    decay = lambda blocks, rate: jnp.exp(-rate * float(rows * blocks))

    def both(mine, theirs, rate):
        first = spot()[0] == 0
        even = jnp.where(first, mine, theirs)
        return decay(1, rate) * even + jnp.where(first, theirs, mine), even

    theirs = flip(away, "ctx", 1)
    chip, even = small(both, keep, theirs, rate, outs=2)

    def whole(mine, other, rate):
        first = spot()[1] == 0
        left = jnp.where(first, mine, other)
        return decay(2, rate) * left + jnp.where(first, other, mine), left

    other = flip(chip, "ctx", 2)
    total, left = small(whole, chip, other, rate, outs=2)
    before = ahead(total, "ctx", ROW)
    reach = 2
    while reach < count:
        upto = small(lambda total, before, rate: total + decay(ROW, rate) * before, total, before, rate)
        earlier = ahead(upto, "ctx", ROW * reach)
        reach *= 2
        if reach < count:
            before = small(
                lambda before, earlier, rate: before + decay(ROW * (reach // 2 - 1), rate) * earlier,
                before,
                earlier,
                rate,
            )

    def last(before, earlier, left, even, rate, gain):
        before = before + decay(ROW * (reach // 2 - 1), rate) * earlier
        core, side, _, _ = spot()
        before = jnp.where(side == 0, before, decay(2, rate) * before + left)
        second = decay(1, rate) * before + even
        return (
            gain * jnp.where(core == 0, before, second),
            gain * jnp.where(core == 0, second, before),
        )

    if count == 2:
        earlier = jnp.zeros_like(before)
    if count > 1:
        mine, away = small(last, before, earlier, left, even, rate, gain, outs=2)
    return mine, flip(away, "ctx", 1)


def lanes_from(start, size):
    return pl.ds(pl.multiple_of(start * size, size), size)


def front_body(attn, hyena, theirs_ref, edge_ref, sems):
    rows, half = theirs_ref.shape[1:]
    away = attn.at[:, :, lanes_from(1 - spot()[0], half)]
    edge = hyena.at[:, rows - EDGE : rows, :]
    copies = [
        pltpu.make_async_copy(away, theirs_ref, sems.at[0]),
        pltpu.make_async_copy(edge, edge_ref, sems.at[1]),
    ]
    for copy in copies:
        copy.start()
    for copy in copies:
        copy.wait()


def front(attn, hyena):
    count, rows, channels = attn.shape
    return pl.pallas_call(
        front_body,
        in_specs=[HBM, HBM],
        out_specs=[VMEM, VMEM],
        out_shape=[
            pltpu.VMEM((count, rows, channels // 2), attn.dtype),
            pltpu.VMEM((count, EDGE, channels), hyena.dtype),
        ],
        scratch_shapes=[pltpu.SemaphoreType.DMA((2,))],
        compiler_params=pltpu.CompilerParams(vmem_limit_bytes=ALL_VMEM - (26 << 17)),
        cost_estimate=cost(0, 4 * count * rows * channels // 2),
        name="front",
    )(attn, hyena)


def pack_body(first, streams_ref, theirs_ref, *outs):
    core, side, _, _ = spot()
    slots = (0, 1) if first == 0 else (1 - core, core)
    quarter = theirs_ref.shape[2] // 2
    for out, away in zip(outs, (0, 1)[-len(outs) :]):
        to = 1 - side if away else side
        for stream in range(first, 3):
            out[slots[0], stream - first] = streams_ref[stream, :, lanes_from(2 * core + to, quarter)]
            out[slots[1], stream - first] = theirs_ref[stream, :, lanes_from(to, quarter)]


def pack(streams, theirs, first, amount):
    _, rows, half = theirs.shape
    shape = pltpu.VMEM((2, 3 - first, rows, half // 2), BF16)
    return pl.pallas_call(
        functools.partial(pack_body, first),
        in_specs=[VMEM, VMEM],
        out_specs=[VMEM] * amount,
        out_shape=[shape] * amount,
        compiler_params=limits(10),
        cost_estimate=cost(0, 8 * amount * rows * half),
        name="pack",
    )(streams, theirs)


def odd_body(wanted, pairs, out_ref, sem):
    @pl.when(spot()[1] == wanted)
    def _():
        copy = pltpu.make_async_copy(pairs.at[0:1], out_ref, sem)
        copy.start()
        copy.wait()


def odd(pairs, wanted):
    return pl.pallas_call(
        functools.partial(odd_body, wanted),
        in_specs=[ANY],
        out_specs=VMEM,
        out_shape=pltpu.VMEM((1,) + pairs.shape[1:], pairs.dtype),
        scratch_shapes=[pltpu.SemaphoreType.DMA],
        compiler_params=limits(4),
        cost_estimate=cost(0, pairs.size * 2),
        name="odd",
    )(pairs)


def contig_start(docs_ref, position):
    first = jnp.zeros_like(position)
    bound = jnp.int32(0)
    for n in range(docs_ref.shape[0]):
        bound = bound + docs_ref[n]
        first = jnp.where(position >= bound, bound, first)
    return first


def row_part(streams, theirs, swap, slot, stream, head, quarter):
    core, side, _, _ = spot()
    if slot < 2:
        start = (side if slot else 2 * core + side) * quarter + head * HEAD
        lanes = pl.ds(pl.multiple_of(start, HEAD), HEAD)
        return theirs[stream, :, lanes] if slot else streams[stream, :, lanes]
    return swap[slot - 2, stream, :, head * HEAD : (head + 1) * HEAD]


SCALE = math.log2(math.e) / math.sqrt(HEAD)


CHUNK = 32


def softmax_group(queries, keys, values, bias, turn, s_s, p_s, keep):
    tall, rows = queries.shape[0], keys[0].shape[0]
    width = len(keys) * rows
    for n in range(0, len(keys), 2):
        s_s[turn, 0:tall, n * rows : (n + 2) * rows] = lax.dot_general(
            queries,
            jnp.concatenate(keys[n : n + 2], axis=0),
            (((1,), (1,)), ((), ())),
            preferred_element_type=F32,
        )
    for m in range(0, tall, CHUNK):
        some = slice(m, m + CHUNK)
        top = None
        parts = []
        for n in range(0, width, LANES):
            part = s_s[turn, some, n : n + LANES] + bias[some, n : n + LANES]
            parts.append(part)
            top = part if top is None else jnp.maximum(top, part)
        top = jnp.broadcast_to(jnp.max(top, axis=1, keepdims=True), (CHUNK, LANES))
        below = jnp.zeros((CHUNK, LANES), F32)
        for n, part in enumerate(parts):
            weight = jnp.exp2((part - top) * SCALE)
            below = below + weight
            p_s[turn, some, n * LANES : (n + 1) * LANES] = weight.astype(BF16)
        keep(m, top, jnp.broadcast_to(jnp.sum(below, axis=1, keepdims=True), (CHUNK, LANES)))
    return jnp.dot(
        p_s[turn, 0:tall, 0:width], jnp.concatenate(values, axis=0), preferred_element_type=F32
    )


def attend_body(docs_ref, streams, theirs, swap, own, cross, acc_ref, m_ref, l_ref, bias_s, s_s, p_s):
    _, side, place, row = spot()
    rows, quarter = own.shape[2:]
    base = row * (ROW * rows)
    part = functools.partial(row_part, streams, theirs, swap, quarter=quarter)

    def run(first_pair, second_pair):
        for group, (asking, seen) in enumerate(((first_pair, first_pair), (second_pair, (0, 1, 2, 3)))):
            starts = [base + (2 * (side if old else 1 - side) + 1 - n - ROW) * rows for old in (1, 0) for n in (0, 1)]
            starts += [base + (place ^ slot) * rows for slot in seen]
            for at, slot in enumerate(asking):
                position = base + (place ^ slot) * rows + lax.broadcasted_iota(jnp.int32, (rows, 1), 0)
                first = contig_start(docs_ref, position)
                for n, start in enumerate(starts):
                    token = start + lax.broadcasted_iota(jnp.int32, (rows, rows), 1)
                    bias_s[group, at * rows : (at + 1) * rows, n * rows : (n + 1) * rows] = jnp.where(
                        (token >= first) & (token <= position), 0.0, -jnp.inf
                    )
            for head in range(quarter // HEAD):
                lanes = slice(head * HEAD, (head + 1) * HEAD)
                olds = lambda kind: [old[n, kind, :, lanes] for old in (own, cross) for n in (0, 1)]

                def keep(m, top, below):
                    out = slice(asking[0] * rows + m, asking[0] * rows + m + CHUNK)
                    m_ref[out, lanes] = top
                    l_ref[out, lanes] = below

                acc_ref[asking[0] * rows : (asking[1] + 1) * rows, lanes] = softmax_group(
                    jnp.concatenate([part(slot, 0, head) for slot in asking], axis=0),
                    olds(0) + [part(slot, 1, head) for slot in seen],
                    olds(1) + [part(slot, 2, head) for slot in seen],
                    bias_s.at[group],
                    head % 2,
                    s_s,
                    p_s,
                    keep,
                )

    @pl.when(side == 0)
    def _():
        run((0, 1), (2, 3))

    @pl.when(side == 1)
    def _():
        run((2, 3), (0, 1))


def attend(doc_lengths, streams, theirs, swap, own, cross):
    _, _, rows, quarter = own.shape
    heads = quarter // HEAD
    return pl.pallas_call(
        attend_body,
        in_specs=[SMEM] + [VMEM] * 5,
        out_specs=[VMEM] * 3,
        out_shape=[
            jax.ShapeDtypeStruct((ROW * rows, quarter), F32),
        ]
        * 3,
        scratch_shapes=[
            pltpu.VMEM((2, 2 * rows, 2 * ROW * rows), F32),
            pltpu.VMEM((2, 2 * rows, 2 * ROW * rows), F32),
            pltpu.VMEM((2, 2 * rows, 2 * ROW * rows), BF16),
        ],
        compiler_params=limits(20),
        cost_estimate=cost(26 * 4 * rows * rows * quarter, 14 * ROW * rows * quarter, 26 * heads * rows * rows),
        name="attend",
    )(doc_lengths, streams, theirs, swap, own, cross)


def attend_last_body(heads, docs_ref, streams, theirs, swap, *refs):
    cross_l, own_s, own_l, cross_s, acc_ref, m_ref, l_ref = refs[:7]
    outs = refs[7:]
    _, side, place, row = spot()
    rows, quarter = acc_ref.shape[0] // ROW, acc_ref.shape[1]
    base = row * (ROW * rows)

    def run(early, late, large, small):
        for asking, blocks in ((early, ((small, 0), (large, 1), (large, 0))), (late, ((large, 0),))):
            width = len(blocks) * rows
            here = slice(asking[0] * rows, (asking[1] + 1) * rows)
            token = base - (ROW + len(blocks)) * rows + lax.broadcasted_iota(jnp.int32, (rows, width), 1)
            allowed = []
            for slot in asking:
                position = base + (place ^ slot) * rows + lax.broadcasted_iota(jnp.int32, (rows, 1), 0)
                allowed.append((token >= contig_start(docs_ref, position)).astype(jnp.int32))
            allowed = jnp.concatenate(allowed, axis=0) != 0
            lanes_of = [slice(head * HEAD, (head + 1) * HEAD) for head in heads]
            stack = lambda kind, lanes: jnp.concatenate([ref[n, kind, :, lanes] for ref, n in blocks], axis=0)
            scores = [
                lax.dot_general(
                    jnp.concatenate(
                        [row_part(streams, theirs, swap, slot, 0, head, quarter) for slot in asking], axis=0
                    ),
                    stack(0, lanes_of[head - heads[0]]),
                    (((1,), (1,)), ((), ())),
                    preferred_element_type=F32,
                )
                for head in heads
            ]
            scores = [jnp.where(allowed, score, -jnp.inf) for score in scores]
            tops = [
                jnp.maximum(m_ref[here, lanes], jnp.max(score, axis=1, keepdims=True))
                for lanes, score in zip(lanes_of, scores)
            ]
            weights = [
                jnp.exp2((score - jnp.concatenate([top] * len(blocks), axis=1)) * SCALE)
                for score, top in zip(scores, tops)
            ]
            for lanes, top, weight in zip(lanes_of, tops, weights):
                fade = jnp.exp2((m_ref[here, lanes] - top) * SCALE)
                share = 1.0 / (l_ref[here, lanes] * fade + jnp.sum(weight, axis=1, keepdims=True))
                more = jnp.dot(weight.astype(BF16), stack(1, lanes), preferred_element_type=F32)
                made = ((acc_ref[here, lanes] * fade + more) * share).astype(BF16)
                put = slice(lanes.start - heads[0] * HEAD, lanes.stop - heads[0] * HEAD)
                for n, slot in enumerate(asking):
                    outs[slot][:, put] = made[n * rows : (n + 1) * rows]

    @pl.when(side == 0)
    def _():
        run((0, 1), (2, 3), cross_l, own_s)

    @pl.when(side == 1)
    def _():
        run((2, 3), (0, 1), own_l, cross_s)


def attend_last(heads, doc_lengths, streams, theirs, swap, olds, acc, top, below):
    rows = acc.shape[0] // ROW
    lanes = len(heads) * HEAD
    return pl.pallas_call(
        functools.partial(attend_last_body, heads),
        in_specs=[SMEM] + [VMEM] * 10,
        out_specs=[VMEM] * ROW,
        out_shape=[jax.ShapeDtypeStruct((rows, lanes), BF16)] * ROW,
        compiler_params=limits(16),
        cost_estimate=cost(32 * rows * rows * lanes, 48 * rows * lanes, 8 * len(heads) * rows * rows),
        name="attend_last",
    )(doc_lengths, streams, theirs, swap, *olds, acc, top, below)


def assemble_body(*refs):
    place = spot()[2]
    *pieces, out_ref = refs
    turns = len(pieces) // ROW
    lanes = pieces[0].shape[1]
    for n, piece in enumerate(pieces):
        maker = place ^ (n % ROW)
        which = 2 * (maker & 1) + lax.shift_right_logical(maker, 1)
        out_ref[:, lanes_from(which * turns + n // ROW, lanes)] = piece[...]


def assemble(pieces):
    rows, lanes = pieces[0].shape
    return pl.pallas_call(
        assemble_body,
        in_specs=[VMEM] * len(pieces),
        out_specs=VMEM,
        out_shape=jax.ShapeDtypeStruct((rows, len(pieces) * lanes), BF16),
        compiler_params=limits(6),
        cost_estimate=cost(0, 4 * rows * lanes * len(pieces)),
        name="assemble",
    )(*pieces)


def on_device(hyena_qkv, short_weight, filter_rate, filter_residue, attn_qkv, doc_lengths):
    rows = attn_qkv.shape[0]
    inner = hyena_qkv.transpose(1, 0, 2)
    streams = attn_qkv.transpose(1, 0, 2)
    rates, residues = filter_rate.T, filter_residue.T
    theirs, edge = front(streams, inner)

    theirs = flip(theirs, "ctx", 1)
    edge = ahead(edge, "ctx", 1)
    own, cross = pack(streams, theirs, 1, 2)
    cross = ahead(cross, "ctx", ROW, 2)
    own = ahead(own, "ctx", ROW)
    (swap,) = pack(streams, theirs, 0, 1)
    swap = flip(swap, "ctx", 2)
    olds = (
        ahead(cross, "ctx", ROW, 0, ROW, 0),
        ahead(odd(own, 0), "ctx", ROW, 0, ROW, 0),
        ahead(own, "ctx", ROW, 0, ROW, 1),
        ahead(odd(cross, 1), "ctx", ROW, 0, ROW, 1),
    )

    mixed, keep, away, wide, gain = hyena_ends(inner, edge, short_weight, rates, residues)
    near, query, high, low = hyena_near(inner, edge, short_weight, mixed, rates, residues)
    keep, back = scan_states(keep, away, wide, gain, rows)
    hyena_out = hyena_finish(near, query, high, low, keep, back)

    acc, top, below = attend(doc_lengths, streams, theirs, swap, own, cross)
    pieces = []
    heads = acc.shape[1] // HEAD
    for turn in range(TURNS):
        these = range(turn * heads // TURNS, (turn + 1) * heads // TURNS)
        made = attend_last(these, doc_lengths, streams, theirs, swap, olds, acc, top, below)
        pieces.append(made[0])
        pieces += [flip(made[n], "ctx", n) for n in range(1, ROW)]
    attn_out = assemble(pieces)
    return (hyena_out, attn_out)


def solution(mesh):
    in_specs = (
        P(("group", "ctx"), None, None),
        P(),
        P(),
        P(),
        P(("group", "ctx"), None, None),
        P("group"),
    )
    out_specs = (P(("group", "ctx"), None), P(("group", "ctx"), None))
    return jax.shard_map(on_device, mesh=mesh, in_specs=in_specs, out_specs=out_specs, check_vma=False)
```

```python
import functools
import math

import jax
import jax.numpy as jnp
from jax import lax
from jax.experimental import pallas as pl
from jax.experimental.pallas import tpu as pltpu
from jax.sharding import PartitionSpec as P


HEAD = 128
LANES = 128
EDGE = 8
ROW = 4


F32 = jnp.float32
BF16 = jnp.bfloat16


def flip(value, axis, bit):
    count = lax.axis_size(axis)
    return lax.ppermute(value, axis, [(at, at ^ bit) for at in range(count)])


def side_of(at):
    return at // 2 % 2


def ahead(value, axis, steps, bit=0, first=0, side=None):
    count = lax.axis_size(axis)
    pairs = [
        (at, (at + steps) ^ bit)
        for at in range(first, count - steps)
        if side is None or side_of(at) == side
    ]
    return lax.ppermute(value, axis, pairs)


def spot():
    index = lax.axis_index("ctx")
    return index & 1, lax.shift_right_logical(index, 1) & 1, index & (ROW - 1), index // ROW


ALL_VMEM = 67043328


def limits(mib):
    return pltpu.CompilerParams(vmem_limit_bytes=mib << 20)


def cost(flops, moved, exps=0):
    return pl.CostEstimate(flops=flops, bytes_accessed=moved, transcendentals=exps)


VMEM = pl.BlockSpec(memory_space=pltpu.VMEM)
SMEM = pl.BlockSpec(memory_space=pltpu.SMEM)
ANY = pl.BlockSpec(memory_space=pl.ANY)
HBM = pl.BlockSpec(memory_space=pltpu.HBM)


def same_filter(modes, width, terms, lanes):
    row_at = lax.broadcasted_iota(jnp.int32, (terms, lanes), 0)
    lane_at = lax.broadcasted_iota(jnp.int32, (terms, lanes), 1)
    kept = None
    for g in range(terms // modes):
        both = (
            (row_at >= g * modes)
            & (row_at < (g + 1) * modes)
            & (lane_at >= g * width)
            & (lane_at < (g + 1) * width)
        )
        kept = both if kept is None else kept | both
    return kept


def feature(x, halo, w_ref, stream, at):
    here = x.astype(F32)
    halo = halo.astype(F32)
    edge = halo.shape[0]
    row_at = lax.broadcasted_iota(jnp.int32, here.shape, 0)
    one = jnp.where(row_at == 0, halo[edge - 1 :], pltpu.roll(here, 1, 0))
    two = jnp.where(row_at == 1, halo[edge - 1 :], pltpu.roll(here, 2, 0))
    two = jnp.where(row_at == 0, halo[edge - 2 : edge - 1], two)
    tap = [w_ref[n, stream : stream + 1, at] for n in range(3)]
    return tap[0] * here + tap[1] * one + tap[2] * two


def of_step(table_ref):
    groups = table_ref.shape[1]
    return pltpu.roll(table_ref[...], groups - pl.program_id(0) * (groups // STEPS), 1)


def down(table, part, filters, lanes):
    columns = [table[:, part * filters + g : part * filters + g + 1] for g in range(filters)]
    return jnp.concatenate([jnp.broadcast_to(c, (c.shape[0], lanes)) for c in columns], axis=0)


def hyena_ends_body(
    filters, x_ref, halo_ref, w_ref, rate_ref, res_ref, mixed_ref, keep_ref, away_ref, wide_ref, gain_ref, all_s
):
    rows = x_ref.shape[1]
    modes, groups = rate_ref.shape
    parts = groups // STEPS // filters
    terms = filters * modes
    lanes = x_ref.shape[2] // parts
    width = lanes // filters
    rates = of_step(rate_ref)
    coeffs = of_step(res_ref) * jnp.sqrt(2.0 * rates / modes)
    lag = (rows - 1 - lax.broadcasted_iota(jnp.int32, (terms, rows), 1)).astype(F32)
    own = same_filter(modes, width, terms, lanes)
    pick = lambda matrix: jnp.sum(jnp.where(own, matrix, 0.0).reshape(filters, modes, lanes), axis=0)
    step = pl.program_id(0)
    for part in range(parts):
        at = slice(part * lanes, (part + 1) * lanes)
        key, value = (feature(x_ref[n, :, at], halo_ref[n, :, at], w_ref, n, at) for n in (1, 2))
        mixed = (key * value).astype(BF16)
        mixed_ref[:, at] = mixed
        rate = down(rates, part, filters, rows)
        powers = jnp.exp(-rate * lag)
        high = powers.astype(BF16)
        low = (powers - high.astype(F32)).astype(BF16)
        ends = jnp.dot(high, mixed, preferred_element_type=F32) + jnp.dot(
            low, mixed, preferred_element_type=F32
        )
        all_s[0, step, :, at] = pick(ends)
        all_s[1, step, :, at] = pick(rate)
        all_s[2, step, :, at] = pick(down(coeffs, part, filters, rows))

    @pl.when(step == STEPS - 1)
    def _():
        core = spot()[0]
        half = STEPS // 2
        for n in range(half):
            at = slice(n * parts * lanes, (n + 1) * parts * lanes)
            away_ref[:, at] = all_s[0, (1 - core) * half + n]
            for table, out in enumerate((keep_ref, wide_ref, gain_ref)):
                out[:, at] = all_s[table, core * half + n]


STEPS = 4


def hyena_ends(streams, halo, short_weight, rates, residues):
    _, rows, channels = streams.shape
    edge = halo.shape[1]
    modes, groups = rates.shape
    filters = groups * LANES // channels
    terms = filters * modes
    wide = channels // STEPS
    lead = lambda n: (0, 0, n)
    whole = lambda n: (0, 0)
    half = (modes, channels // 2)
    return pl.pallas_call(
        functools.partial(hyena_ends_body, filters),
        grid=(STEPS,),
        in_specs=[
            pl.BlockSpec((3, rows, wide), lead),
            pl.BlockSpec((3, edge, wide), lead),
            pl.BlockSpec((3, 3, wide), lead),
            pl.BlockSpec((modes, groups), whole),
            pl.BlockSpec((modes, groups), whole),
        ],
        out_specs=[pl.BlockSpec((rows, wide), lambda n: (0, n))] + [pl.BlockSpec(half, whole)] * 4,
        out_shape=[jax.ShapeDtypeStruct((rows, channels), BF16)] + [jax.ShapeDtypeStruct(half, F32)] * 4,
        scratch_shapes=[pltpu.VMEM((3, STEPS, modes, wide), F32)],
        compiler_params=limits(16),
        cost_estimate=cost(4 * rows * terms * channels, 8 * rows * channels),
        name="hyena_ends",
    )(streams, halo, short_weight, rates, residues)


def hyena_near_body(
    filters, x_ref, halo_ref, w_ref, mixed_ref, rate_ref, res_ref, near_ref, q_ref, high_ref, low_ref, taps_s, u_s
):
    rows = mixed_ref.shape[0]
    modes, groups = rate_ref.shape
    parts = groups // STEPS // filters
    terms = filters * modes
    lanes = mixed_ref.shape[1] // parts
    width = lanes // filters
    rates = of_step(rate_ref)
    coeffs = of_step(res_ref) * jnp.sqrt(2.0 * rates / modes)
    row_at = lax.broadcasted_iota(jnp.int32, (rows, lanes), 0)
    lane_at = lax.broadcasted_iota(jnp.int32, (rows, lanes), 1)
    lag = (rows - 1 - lax.broadcasted_iota(jnp.int32, (terms, rows), 1)).astype(F32)
    ahead_lag = (1 + lax.broadcasted_iota(jnp.int32, (terms, rows), 1)).astype(F32)
    zero = jnp.zeros((rows, lanes), BF16)
    for part in range(parts):
        at = slice(part * lanes, (part + 1) * lanes)
        mixed = mixed_ref[:, at]
        rate = down(rates, part, filters, rows)
        powers = down(coeffs, part, filters, rows) * jnp.exp(-rate * lag)
        backward = jnp.sum(powers.reshape(filters, modes, rows), axis=1)
        for g in range(filters):
            spread = jnp.broadcast_to(backward[g : g + 1], (rows, rows))
            shifted = pltpu.roll(spread, 1, 1, stride=1, stride_axis=0)
            kept = jnp.where(lane_at <= row_at, shifted, 0.0)
            taps_s[part, :, g * rows : (g + 1) * rows] = kept.astype(BF16)
            mine = (lane_at >= g * width) & (lane_at < (g + 1) * width)
            u_s[part, g * rows : (g + 1) * rows, :] = jnp.where(mine, mixed, zero)
        near_ref[:, at] = jnp.dot(taps_s[part], u_s[part], preferred_element_type=F32)
        q_ref[:, at] = feature(x_ref[0, :, at], halo_ref[0, :, at], w_ref, 0, at)
        decays = jnp.exp(-rate * ahead_lag).T
        here = slice(part * terms, (part + 1) * terms)
        high = decays.astype(BF16)
        high_ref[:, here] = high
        low_ref[:, here] = (decays - high.astype(F32)).astype(BF16)


def hyena_near(streams, halo, short_weight, mixed, rates, residues):
    rows, channels = mixed.shape
    edge = halo.shape[1]
    modes, groups = rates.shape
    lanes = LANES
    filters = groups * lanes // channels
    terms = filters * modes
    parts = groups // STEPS // filters
    wide = channels // STEPS
    by_block = lambda n: (0, n)
    lead = lambda n: (0, 0, n)
    whole = lambda n: (0, 0)
    return pl.pallas_call(
        functools.partial(hyena_near_body, filters),
        grid=(STEPS,),
        in_specs=[
            pl.BlockSpec((1, rows, wide), lead),
            pl.BlockSpec((1, edge, wide), lead),
            pl.BlockSpec((3, 3, wide), lead),
            pl.BlockSpec((rows, wide), by_block),
            pl.BlockSpec((modes, groups), whole),
            pl.BlockSpec((modes, groups), whole),
        ],
        out_specs=[pl.BlockSpec((rows, wide), by_block)] * 2 + [pl.BlockSpec((rows, parts * terms), by_block)] * 2,
        out_shape=[jax.ShapeDtypeStruct((rows, channels), F32)] * 2
        + [jax.ShapeDtypeStruct((rows, groups * modes), BF16)] * 2,
        scratch_shapes=[
            pltpu.VMEM((parts, rows, filters * rows), BF16),
            pltpu.VMEM((parts, filters * rows, lanes), BF16),
        ],
        compiler_params=limits(16),
        cost_estimate=cost(2 * rows * rows * filters * channels, 12 * rows * channels),
        name="hyena_near",
    )(streams, halo, short_weight, mixed, rates, residues)


def hyena_out_body(modes, near_ref, q_ref, high_ref, low_ref, keep_ref, back_ref, out_ref):
    wide = near_ref.shape[1]
    terms = high_ref.shape[1] * LANES // wide
    filters = terms // modes
    own = same_filter(modes, LANES // filters, terms, LANES)
    mine = pl.program_id(0) // (STEPS // 2) == spot()[0]
    for part in range(wide // LANES):
        at = slice(part * LANES, (part + 1) * LANES)
        here = slice(part * terms, (part + 1) * terms)
        carried = jnp.where(mine, keep_ref[:, at], back_ref[:, at])
        carried = jnp.where(own, jnp.concatenate([carried] * filters, axis=0), 0.0)
        c_high = carried.astype(BF16)
        c_low = (carried - c_high.astype(F32)).astype(BF16)
        high, low = high_ref[:, here], low_ref[:, here]
        far = (
            jnp.dot(high, c_high, preferred_element_type=F32)
            + jnp.dot(low, c_high, preferred_element_type=F32)
            + jnp.dot(high, c_low, preferred_element_type=F32)
        )
        out_ref[:, at] = (q_ref[:, at] * (near_ref[:, at] + far)).astype(BF16)


def hyena_finish(near, query, high, low, keep, back):
    rows, channels = near.shape
    modes = keep.shape[0]
    wide = channels // STEPS
    by_block = lambda n: (0, n)
    by_half = lambda n: (0, n % (STEPS // 2))
    return pl.pallas_call(
        functools.partial(hyena_out_body, modes),
        grid=(STEPS,),
        in_specs=[
            pl.BlockSpec((rows, wide), by_block),
            pl.BlockSpec((rows, wide), by_block),
            pl.BlockSpec((rows, high.shape[1] // STEPS), by_block),
            pl.BlockSpec((rows, high.shape[1] // STEPS), by_block),
            pl.BlockSpec((modes, wide), by_half),
            pl.BlockSpec((modes, wide), by_half),
        ],
        out_specs=pl.BlockSpec((rows, wide), by_block),
        out_shape=jax.ShapeDtypeStruct((rows, channels), BF16),
        compiler_params=limits(16),
        cost_estimate=cost(6 * rows * high.size, 10 * rows * channels),
        name="hyena_finish",
    )(near, query, high, low, keep, back)


def small(body, *operands, outs=1):
    def kernel(*refs):
        made = body(*(ref[...] for ref in refs[: len(operands)]))
        for ref, value in zip(refs[len(operands) :], made if outs > 1 else (made,)):
            ref[...] = value

    shape = pltpu.VMEM(operands[0].shape, operands[0].dtype)
    made = pl.pallas_call(
        kernel,
        in_specs=[VMEM] * len(operands),
        out_specs=[VMEM] * outs,
        out_shape=[shape] * outs,
        compiler_params=limits(4),
        cost_estimate=cost(operands[0].size, 4 * operands[0].size),
    )(*operands)
    return made if outs > 1 else made[0]


def scan_states(keep, away, rate, gain, rows):
    count = lax.axis_size("ctx") // ROW
    decay = lambda blocks, rate: jnp.exp(-rate * float(rows * blocks))

    def both(mine, theirs, rate):
        first = spot()[0] == 0
        even = jnp.where(first, mine, theirs)
        return decay(1, rate) * even + jnp.where(first, theirs, mine), even

    theirs = flip(away, "ctx", 1)
    chip, even = small(both, keep, theirs, rate, outs=2)

    def whole(mine, other, rate):
        first = spot()[1] == 0
        left = jnp.where(first, mine, other)
        return decay(2, rate) * left + jnp.where(first, other, mine), left

    other = flip(chip, "ctx", 2)
    total, left = small(whole, chip, other, rate, outs=2)
    before = ahead(total, "ctx", ROW)
    reach = 2
    while reach < count:
        upto = small(lambda total, before, rate: total + decay(ROW, rate) * before, total, before, rate)
        earlier = ahead(upto, "ctx", ROW * reach)
        reach *= 2
        if reach < count:
            before = small(
                lambda before, earlier, rate: before + decay(ROW * (reach // 2 - 1), rate) * earlier,
                before,
                earlier,
                rate,
            )

    def last(before, earlier, left, even, rate, gain):
        before = before + decay(ROW * (reach // 2 - 1), rate) * earlier
        core, side, _, _ = spot()
        before = jnp.where(side == 0, before, decay(2, rate) * before + left)
        second = decay(1, rate) * before + even
        return (
            gain * jnp.where(core == 0, before, second),
            gain * jnp.where(core == 0, second, before),
        )

    if count == 2:
        earlier = jnp.zeros_like(before)
    if count > 1:
        mine, away = small(last, before, earlier, left, even, rate, gain, outs=2)
    return mine, flip(away, "ctx", 1)


def lanes_from(start, size):
    return pl.ds(pl.multiple_of(start * size, size), size)


def front_body(attn, hyena, theirs_ref, edge_ref, sems):
    rows, half = theirs_ref.shape[1:]
    away = attn.at[:, :, lanes_from(1 - spot()[0], half)]
    edge = hyena.at[:, rows - EDGE : rows, :]
    copies = [
        pltpu.make_async_copy(away, theirs_ref, sems.at[0]),
        pltpu.make_async_copy(edge, edge_ref, sems.at[1]),
    ]
    for copy in copies:
        copy.start()
    for copy in copies:
        copy.wait()


def front(attn, hyena):
    count, rows, channels = attn.shape
    return pl.pallas_call(
        front_body,
        in_specs=[HBM, HBM],
        out_specs=[VMEM, VMEM],
        out_shape=[
            pltpu.VMEM((count, rows, channels // 2), attn.dtype),
            pltpu.VMEM((count, EDGE, channels), hyena.dtype),
        ],
        scratch_shapes=[pltpu.SemaphoreType.DMA((2,))],
        compiler_params=pltpu.CompilerParams(vmem_limit_bytes=ALL_VMEM - (26 << 17)),
        cost_estimate=cost(0, 4 * count * rows * channels // 2),
        name="front",
    )(attn, hyena)


def pack_body(first, streams_ref, theirs_ref, *outs):
    core, side, _, _ = spot()
    slots = (0, 1) if first == 0 else (1 - core, core)
    quarter = theirs_ref.shape[2] // 2
    for out, away in zip(outs, (0, 1)[-len(outs) :]):
        to = 1 - side if away else side
        for stream in range(first, 3):
            out[slots[0], stream - first] = streams_ref[stream, :, lanes_from(2 * core + to, quarter)]
            out[slots[1], stream - first] = theirs_ref[stream, :, lanes_from(to, quarter)]


def pack(streams, theirs, first, amount):
    _, rows, half = theirs.shape
    shape = pltpu.VMEM((2, 3 - first, rows, half // 2), BF16)
    return pl.pallas_call(
        functools.partial(pack_body, first),
        in_specs=[VMEM, VMEM],
        out_specs=[VMEM] * amount,
        out_shape=[shape] * amount,
        compiler_params=limits(10),
        cost_estimate=cost(0, 8 * amount * rows * half),
        name="pack",
    )(streams, theirs)


def odd_body(wanted, pairs, out_ref, sem):
    @pl.when(spot()[1] == wanted)
    def _():
        copy = pltpu.make_async_copy(pairs.at[0:1], out_ref, sem)
        copy.start()
        copy.wait()


def odd(pairs, wanted):
    return pl.pallas_call(
        functools.partial(odd_body, wanted),
        in_specs=[ANY],
        out_specs=VMEM,
        out_shape=pltpu.VMEM((1,) + pairs.shape[1:], pairs.dtype),
        scratch_shapes=[pltpu.SemaphoreType.DMA],
        compiler_params=limits(4),
        cost_estimate=cost(0, pairs.size * 2),
        name="odd",
    )(pairs)


def contig_start(docs_ref, position):
    first = jnp.zeros_like(position)
    bound = jnp.int32(0)
    for n in range(docs_ref.shape[0]):
        bound = bound + docs_ref[n]
        first = jnp.where(position >= bound, bound, first)
    return first


def row_part(streams, theirs, swap, slot, stream, head, quarter):
    core, side, _, _ = spot()
    if slot < 2:
        start = (side if slot else 2 * core + side) * quarter + head * HEAD
        lanes = pl.ds(pl.multiple_of(start, HEAD), HEAD)
        return theirs[stream, :, lanes] if slot else streams[stream, :, lanes]
    return swap[slot - 2, stream, :, head * HEAD : (head + 1) * HEAD]


SCALE = math.log2(math.e) / math.sqrt(HEAD)


CHUNK = 32


def softmax_group(queries, keys, values, bias, turn, s_s, p_s, keep):
    tall, rows = queries.shape[0], keys[0].shape[0]
    width = len(keys) * rows
    for n in range(0, len(keys), 2):
        s_s[turn, 0:tall, n * rows : (n + 2) * rows] = lax.dot_general(
            queries,
            jnp.concatenate(keys[n : n + 2], axis=0),
            (((1,), (1,)), ((), ())),
            preferred_element_type=F32,
        )
    for m in range(0, tall, CHUNK):
        some = slice(m, m + CHUNK)
        top = None
        parts = []
        for n in range(0, width, LANES):
            part = s_s[turn, some, n : n + LANES] + bias[some, n : n + LANES]
            parts.append(part)
            top = part if top is None else jnp.maximum(top, part)
        top = jnp.broadcast_to(jnp.max(top, axis=1, keepdims=True), (CHUNK, LANES))
        below = jnp.zeros((CHUNK, LANES), F32)
        for n, part in enumerate(parts):
            weight = jnp.exp2((part - top) * SCALE)
            below = below + weight
            p_s[turn, some, n * LANES : (n + 1) * LANES] = weight.astype(BF16)
        keep(m, top, jnp.broadcast_to(jnp.sum(below, axis=1, keepdims=True), (CHUNK, LANES)))
    return jnp.dot(
        p_s[turn, 0:tall, 0:width], jnp.concatenate(values, axis=0), preferred_element_type=F32
    )


def attend_body(docs_ref, streams, theirs, swap, own, cross, acc_ref, m_ref, l_ref, bias_s, s_s, p_s):
    _, side, place, row = spot()
    rows, quarter = own.shape[2:]
    base = row * (ROW * rows)
    part = functools.partial(row_part, streams, theirs, swap, quarter=quarter)

    def run(first_pair, second_pair):
        for group, (asking, seen) in enumerate(((first_pair, first_pair), (second_pair, (0, 1, 2, 3)))):
            starts = [base + (2 * (side if old else 1 - side) + 1 - n - ROW) * rows for old in (1, 0) for n in (0, 1)]
            starts += [base + (place ^ slot) * rows for slot in seen]
            for at, slot in enumerate(asking):
                position = base + (place ^ slot) * rows + lax.broadcasted_iota(jnp.int32, (rows, 1), 0)
                first = contig_start(docs_ref, position)
                for n, start in enumerate(starts):
                    token = start + lax.broadcasted_iota(jnp.int32, (rows, rows), 1)
                    bias_s[group, at * rows : (at + 1) * rows, n * rows : (n + 1) * rows] = jnp.where(
                        (token >= first) & (token <= position), 0.0, -jnp.inf
                    )
            for head in range(quarter // HEAD):
                lanes = slice(head * HEAD, (head + 1) * HEAD)
                olds = lambda kind: [old[n, kind, :, lanes] for old in (own, cross) for n in (0, 1)]

                def keep(m, top, below):
                    out = slice(asking[0] * rows + m, asking[0] * rows + m + CHUNK)
                    m_ref[out, lanes] = top
                    l_ref[out, lanes] = below

                acc_ref[asking[0] * rows : (asking[1] + 1) * rows, lanes] = softmax_group(
                    jnp.concatenate([part(slot, 0, head) for slot in asking], axis=0),
                    olds(0) + [part(slot, 1, head) for slot in seen],
                    olds(1) + [part(slot, 2, head) for slot in seen],
                    bias_s.at[group],
                    head % 2,
                    s_s,
                    p_s,
                    keep,
                )

    @pl.when(side == 0)
    def _():
        run((0, 1), (2, 3))

    @pl.when(side == 1)
    def _():
        run((2, 3), (0, 1))


def attend(doc_lengths, streams, theirs, swap, own, cross):
    _, _, rows, quarter = own.shape
    heads = quarter // HEAD
    return pl.pallas_call(
        attend_body,
        in_specs=[SMEM] + [VMEM] * 5,
        out_specs=[VMEM] * 3,
        out_shape=[
            jax.ShapeDtypeStruct((ROW * rows, quarter), F32),
        ]
        * 3,
        scratch_shapes=[
            pltpu.VMEM((2, 2 * rows, 2 * ROW * rows), F32),
            pltpu.VMEM((2, 2 * rows, 2 * ROW * rows), F32),
            pltpu.VMEM((2, 2 * rows, 2 * ROW * rows), BF16),
        ],
        compiler_params=limits(20),
        cost_estimate=cost(26 * 4 * rows * rows * quarter, 14 * ROW * rows * quarter, 26 * heads * rows * rows),
        name="attend",
    )(doc_lengths, streams, theirs, swap, own, cross)


def merge(scores, values, past, below, total):
    top = jnp.maximum(past, jnp.max(scores, axis=1, keepdims=True))
    fade = jnp.exp2((past - top) * SCALE)
    weight = jnp.exp2((scores - jnp.concatenate([top] * (scores.shape[1] // LANES), axis=1)) * SCALE)
    below = below * fade + jnp.sum(weight, axis=1, keepdims=True)
    total = total * fade + jnp.dot(weight.astype(BF16), values, preferred_element_type=F32)
    return top, below, total


def product(queries, keys):
    return lax.dot_general(queries, keys, (((1,), (1,)), ((), ())), preferred_element_type=F32)


def attend_mid_body(docs_ref, streams, theirs, swap, cross_l, own_l, acc_ref, m_ref, l_ref, *refs):
    outs, (acc_out, m_out, l_out, q_out) = refs[:ROW], refs[ROW:]
    _, side, place, row = spot()
    rows, quarter = acc_ref.shape[0] // ROW, acc_ref.shape[1]
    base = row * (ROW * rows)
    all_lanes = [slice(n, n + HEAD) for n in range(0, quarter, HEAD)]

    def run(early, late, large):
        for asking, blocks in ((early, (1, 0)), (late, (0,))):
            width = len(blocks) * rows
            here = slice(asking[0] * rows, (asking[1] + 1) * rows)
            token = base - (ROW + len(blocks)) * rows + lax.broadcasted_iota(jnp.int32, (rows, width), 1)
            allowed = []
            for slot in asking:
                position = base + (place ^ slot) * rows + lax.broadcasted_iota(jnp.int32, (rows, 1), 0)
                allowed.append((token >= contig_start(docs_ref, position)).astype(jnp.int32))
            allowed = jnp.concatenate(allowed, axis=0) != 0
            stack = lambda kind, lanes: jnp.concatenate([large[n, kind, :, lanes] for n in blocks], axis=0)
            queries = [
                jnp.concatenate([row_part(streams, theirs, swap, slot, 0, head, quarter) for slot in asking], axis=0)
                for head in range(len(all_lanes))
            ]
            scores = [product(query, stack(0, lanes)) for query, lanes in zip(queries, all_lanes)]
            scores = [jnp.where(allowed, score, -jnp.inf) for score in scores]
            for lanes, query, score in zip(all_lanes, queries, scores):
                top, below, total = merge(
                    score, stack(1, lanes), m_ref[here, lanes], l_ref[here, lanes], acc_ref[here, lanes]
                )
                made = (total * (1.0 / below)).astype(BF16)
                for n, slot in enumerate(asking):
                    outs[slot][:, lanes] = made[n * rows : (n + 1) * rows]
                if asking is early:
                    m_out[:, lanes], l_out[:, lanes], acc_out[:, lanes] = top, below, total
                    q_out[:, lanes] = query

    @pl.when(side == 0)
    def _():
        run((0, 1), (2, 3), cross_l)

    @pl.when(side == 1)
    def _():
        run((2, 3), (0, 1), own_l)


def attend_mid(doc_lengths, streams, theirs, swap, cross_l, own_l, acc, top, below):
    rows, quarter = acc.shape[0] // ROW, acc.shape[1]
    pair = jax.ShapeDtypeStruct((2 * rows, quarter), F32)
    return pl.pallas_call(
        attend_mid_body,
        in_specs=[SMEM] + [VMEM] * 8,
        out_specs=[VMEM] * (ROW + 4),
        out_shape=[jax.ShapeDtypeStruct((rows, quarter), BF16)] * ROW
        + [pair] * 3
        + [jax.ShapeDtypeStruct((2 * rows, quarter), BF16)],
        compiler_params=limits(16),
        cost_estimate=cost(24 * rows * rows * quarter, 48 * rows * quarter, 24 * rows * rows),
        name="attend_mid",
    )(doc_lengths, streams, theirs, swap, cross_l, own_l, acc, top, below)


def attend_last_body(docs_ref, own_s, cross_s, acc_ref, m_ref, l_ref, q_ref, out_ref):
    core, side, _, row = spot()
    rows, quarter = out_ref.shape
    base = row * (ROW * rows)
    here = pl.ds(pl.multiple_of(core * rows, rows), rows)
    position = base + lax.broadcasted_iota(jnp.int32, (rows, 1), 0)
    token = base - (2 * ROW - 1) * rows + lax.broadcasted_iota(jnp.int32, (rows, rows), 1)
    allowed = token >= contig_start(docs_ref, position)

    def run(odd_block):
        all_lanes = [slice(n, n + HEAD) for n in range(0, quarter, HEAD)]
        scores = [product(q_ref[here, lanes], odd_block[0, 0, :, lanes]) for lanes in all_lanes]
        for lanes, score in zip(all_lanes, scores):
            _, below, total = merge(
                jnp.where(allowed, score, -jnp.inf),
                odd_block[0, 1, :, lanes],
                m_ref[here, lanes],
                l_ref[here, lanes],
                acc_ref[here, lanes],
            )
            out_ref[:, lanes] = (total * (1.0 / below)).astype(BF16)

    @pl.when(side == 0)
    def _():
        run(own_s)

    @pl.when(side == 1)
    def _():
        run(cross_s)


def attend_last(doc_lengths, own_s, cross_s, acc, top, below, queries):
    rows, quarter = acc.shape[0] // 2, acc.shape[1]
    return pl.pallas_call(
        attend_last_body,
        in_specs=[SMEM] + [VMEM] * 6,
        out_specs=VMEM,
        out_shape=jax.ShapeDtypeStruct((rows, quarter), BF16),
        compiler_params=limits(16),
        cost_estimate=cost(4 * rows * rows * quarter, 16 * rows * quarter, 4 * rows * rows),
        name="attend_last",
    )(doc_lengths, own_s, cross_s, acc, top, below, queries)


def assemble_body(*refs):
    place = spot()[2]
    *pieces, out_ref = refs
    quarter = pieces[0].shape[1]

    def run(chosen):
        for slot, piece in enumerate(chosen):
            maker = place ^ slot
            which = 2 * (maker & 1) + lax.shift_right_logical(maker, 1)
            out_ref[:, lanes_from(which, quarter)] = piece[...]

    @pl.when(place == 0)
    def _():
        run(pieces[ROW:])

    @pl.when(place != 0)
    def _():
        run(pieces[:ROW])


def assemble(soon, late):
    rows, quarter = soon[0].shape
    return pl.pallas_call(
        assemble_body,
        in_specs=[VMEM] * (2 * ROW),
        out_specs=VMEM,
        out_shape=jax.ShapeDtypeStruct((rows, ROW * quarter), BF16),
        compiler_params=limits(6),
        cost_estimate=cost(0, 16 * rows * quarter),
        name="assemble",
    )(*soon, *late)


def to_first(value, axis, place):
    count = lax.axis_size(axis)
    return lax.ppermute(value, axis, [(at, at - place) for at in range(place, count, ROW)])


def on_device(hyena_qkv, short_weight, filter_rate, filter_residue, attn_qkv, doc_lengths):
    rows = attn_qkv.shape[0]
    inner = hyena_qkv.transpose(1, 0, 2)
    streams = attn_qkv.transpose(1, 0, 2)
    rates, residues = filter_rate.T, filter_residue.T
    theirs, edge = front(streams, inner)

    theirs = flip(theirs, "ctx", 1)
    edge = ahead(edge, "ctx", 1)
    own, cross = pack(streams, theirs, 1, 2)
    cross = ahead(cross, "ctx", ROW, 2)
    own = ahead(own, "ctx", ROW)
    (swap,) = pack(streams, theirs, 0, 1)
    swap = flip(swap, "ctx", 2)
    olds = (
        ahead(cross, "ctx", ROW, 0, ROW, 0),
        ahead(odd(own, 0), "ctx", ROW, 0, ROW, 0),
        ahead(own, "ctx", ROW, 0, ROW, 1),
        ahead(odd(cross, 1), "ctx", ROW, 0, ROW, 1),
    )

    mixed, keep, away, wide, gain = hyena_ends(inner, edge, short_weight, rates, residues)
    near, query, high, low = hyena_near(inner, edge, short_weight, mixed, rates, residues)
    keep, back = scan_states(keep, away, wide, gain, rows)
    hyena_out = hyena_finish(near, query, high, low, keep, back)

    acc, top, below = attend(doc_lengths, streams, theirs, swap, own, cross)
    cross_l, own_s, own_l, cross_s = olds
    *made, acc, top, below, queries = attend_mid(doc_lengths, streams, theirs, swap, cross_l, own_l, acc, top, below)
    soon = [made[0]] + [flip(made[n], "ctx", n) for n in range(1, ROW)]
    first = attend_last(doc_lengths, own_s, cross_s, acc, top, below, queries)
    late = [first] + [to_first(first, "ctx", n) for n in range(1, ROW)]
    attn_out = assemble(soon, late)
    return (hyena_out, attn_out)


def solution(mesh):
    in_specs = (
        P(("group", "ctx"), None, None),
        P(),
        P(),
        P(),
        P(("group", "ctx"), None, None),
        P("group"),
    )
    out_specs = (P(("group", "ctx"), None), P(("group", "ctx"), None))
    return jax.shard_map(on_device, mesh=mesh, in_specs=in_specs, out_specs=out_specs, check_vma=False)
```

```python
import functools
import math

import jax
import jax.numpy as jnp
from jax import lax
from jax.experimental import pallas as pl
from jax.experimental.pallas import tpu as pltpu
from jax.sharding import PartitionSpec as P


HEAD = 128
LANES = 128
EDGE = 8
ROW = 4


F32 = jnp.float32
BF16 = jnp.bfloat16


def flip(value, axis, bit):
    count = lax.axis_size(axis)
    return lax.ppermute(value, axis, [(at, at ^ bit) for at in range(count)])


def side_of(at):
    return at // 2 % 2


def ahead(value, axis, steps, bit=0, first=0, side=None):
    count = lax.axis_size(axis)
    pairs = [
        (at, (at + steps) ^ bit)
        for at in range(first, count - steps)
        if side is None or side_of(at) == side
    ]
    return lax.ppermute(value, axis, pairs)


def spot():
    index = lax.axis_index("ctx")
    return index & 1, lax.shift_right_logical(index, 1) & 1, index & (ROW - 1), index // ROW


ALL_VMEM = 67043328


def limits(mib):
    return pltpu.CompilerParams(vmem_limit_bytes=mib << 20)


def cost(flops, moved, exps=0):
    return pl.CostEstimate(flops=flops, bytes_accessed=moved, transcendentals=exps)


VMEM = pl.BlockSpec(memory_space=pltpu.VMEM)
SMEM = pl.BlockSpec(memory_space=pltpu.SMEM)
ANY = pl.BlockSpec(memory_space=pl.ANY)
HBM = pl.BlockSpec(memory_space=pltpu.HBM)


def same_filter(modes, width, terms, lanes):
    row_at = lax.broadcasted_iota(jnp.int32, (terms, lanes), 0)
    lane_at = lax.broadcasted_iota(jnp.int32, (terms, lanes), 1)
    kept = None
    for g in range(terms // modes):
        both = (
            (row_at >= g * modes)
            & (row_at < (g + 1) * modes)
            & (lane_at >= g * width)
            & (lane_at < (g + 1) * width)
        )
        kept = both if kept is None else kept | both
    return kept


def feature(x, halo, w_ref, stream, at):
    here = x.astype(F32)
    halo = halo.astype(F32)
    edge = halo.shape[0]
    row_at = lax.broadcasted_iota(jnp.int32, here.shape, 0)
    one = jnp.where(row_at == 0, halo[edge - 1 :], pltpu.roll(here, 1, 0))
    two = jnp.where(row_at == 1, halo[edge - 1 :], pltpu.roll(here, 2, 0))
    two = jnp.where(row_at == 0, halo[edge - 2 : edge - 1], two)
    tap = [w_ref[n, stream : stream + 1, at] for n in range(3)]
    return tap[0] * here + tap[1] * one + tap[2] * two


def of_step(table_ref):
    groups = table_ref.shape[1]
    return pltpu.roll(table_ref[...], groups - pl.program_id(0) * (groups // STEPS), 1)


def down(table, part, filters, lanes):
    columns = [table[:, part * filters + g : part * filters + g + 1] for g in range(filters)]
    return jnp.concatenate([jnp.broadcast_to(c, (c.shape[0], lanes)) for c in columns], axis=0)


def hyena_ends_body(
    filters, x_ref, halo_ref, w_ref, rate_ref, res_ref, mixed_ref, keep_ref, away_ref, wide_ref, gain_ref, all_s
):
    rows = x_ref.shape[1]
    modes, groups = rate_ref.shape
    parts = groups // STEPS // filters
    terms = filters * modes
    lanes = x_ref.shape[2] // parts
    width = lanes // filters
    rates = of_step(rate_ref)
    coeffs = of_step(res_ref) * jnp.sqrt(2.0 * rates / modes)
    lag = (rows - 1 - lax.broadcasted_iota(jnp.int32, (terms, rows), 1)).astype(F32)
    own = same_filter(modes, width, terms, lanes)
    pick = lambda matrix: jnp.sum(jnp.where(own, matrix, 0.0).reshape(filters, modes, lanes), axis=0)
    step = pl.program_id(0)
    for part in range(parts):
        at = slice(part * lanes, (part + 1) * lanes)
        key, value = (feature(x_ref[n, :, at], halo_ref[n, :, at], w_ref, n, at) for n in (1, 2))
        mixed = (key * value).astype(BF16)
        mixed_ref[:, at] = mixed
        rate = down(rates, part, filters, rows)
        powers = jnp.exp(-rate * lag)
        high = powers.astype(BF16)
        low = (powers - high.astype(F32)).astype(BF16)
        ends = jnp.dot(high, mixed, preferred_element_type=F32) + jnp.dot(
            low, mixed, preferred_element_type=F32
        )
        all_s[0, step, :, at] = pick(ends)
        all_s[1, step, :, at] = pick(rate)
        all_s[2, step, :, at] = pick(down(coeffs, part, filters, rows))

    @pl.when(step == STEPS - 1)
    def _():
        core = spot()[0]
        half = STEPS // 2
        for n in range(half):
            at = slice(n * parts * lanes, (n + 1) * parts * lanes)
            away_ref[:, at] = all_s[0, (1 - core) * half + n]
            for table, out in enumerate((keep_ref, wide_ref, gain_ref)):
                out[:, at] = all_s[table, core * half + n]


STEPS = 4


def hyena_ends(streams, halo, short_weight, rates, residues):
    _, rows, channels = streams.shape
    edge = halo.shape[1]
    modes, groups = rates.shape
    filters = groups * LANES // channels
    terms = filters * modes
    wide = channels // STEPS
    lead = lambda n: (0, 0, n)
    whole = lambda n: (0, 0)
    half = (modes, channels // 2)
    return pl.pallas_call(
        functools.partial(hyena_ends_body, filters),
        grid=(STEPS,),
        in_specs=[
            pl.BlockSpec((3, rows, wide), lead),
            pl.BlockSpec((3, edge, wide), lead),
            pl.BlockSpec((3, 3, wide), lead),
            pl.BlockSpec((modes, groups), whole),
            pl.BlockSpec((modes, groups), whole),
        ],
        out_specs=[pl.BlockSpec((rows, wide), lambda n: (0, n))] + [pl.BlockSpec(half, whole)] * 4,
        out_shape=[jax.ShapeDtypeStruct((rows, channels), BF16)] + [jax.ShapeDtypeStruct(half, F32)] * 4,
        scratch_shapes=[pltpu.VMEM((3, STEPS, modes, wide), F32)],
        compiler_params=limits(16),
        cost_estimate=cost(4 * rows * terms * channels, 8 * rows * channels),
        name="hyena_ends",
    )(streams, halo, short_weight, rates, residues)


def hyena_near_body(
    filters, x_ref, halo_ref, w_ref, mixed_ref, rate_ref, res_ref, near_ref, q_ref, high_ref, low_ref, taps_s, u_s
):
    rows = mixed_ref.shape[0]
    modes, groups = rate_ref.shape
    parts = groups // STEPS // filters
    terms = filters * modes
    lanes = mixed_ref.shape[1] // parts
    width = lanes // filters
    rates = of_step(rate_ref)
    coeffs = of_step(res_ref) * jnp.sqrt(2.0 * rates / modes)
    row_at = lax.broadcasted_iota(jnp.int32, (rows, lanes), 0)
    lane_at = lax.broadcasted_iota(jnp.int32, (rows, lanes), 1)
    lag = (rows - 1 - lax.broadcasted_iota(jnp.int32, (terms, rows), 1)).astype(F32)
    ahead_lag = (1 + lax.broadcasted_iota(jnp.int32, (terms, rows), 1)).astype(F32)
    zero = jnp.zeros((rows, lanes), BF16)
    for part in range(parts):
        at = slice(part * lanes, (part + 1) * lanes)
        mixed = mixed_ref[:, at]
        rate = down(rates, part, filters, rows)
        powers = down(coeffs, part, filters, rows) * jnp.exp(-rate * lag)
        backward = jnp.sum(powers.reshape(filters, modes, rows), axis=1)
        for g in range(filters):
            spread = jnp.broadcast_to(backward[g : g + 1], (rows, rows))
            shifted = pltpu.roll(spread, 1, 1, stride=1, stride_axis=0)
            kept = jnp.where(lane_at <= row_at, shifted, 0.0)
            taps_s[part, :, g * rows : (g + 1) * rows] = kept.astype(BF16)
            mine = (lane_at >= g * width) & (lane_at < (g + 1) * width)
            u_s[part, g * rows : (g + 1) * rows, :] = jnp.where(mine, mixed, zero)
        near_ref[:, at] = jnp.dot(taps_s[part], u_s[part], preferred_element_type=F32)
        q_ref[:, at] = feature(x_ref[0, :, at], halo_ref[0, :, at], w_ref, 0, at)
        decays = jnp.exp(-rate * ahead_lag).T
        here = slice(part * terms, (part + 1) * terms)
        high = decays.astype(BF16)
        high_ref[:, here] = high
        low_ref[:, here] = (decays - high.astype(F32)).astype(BF16)


def hyena_near(streams, halo, short_weight, mixed, rates, residues):
    rows, channels = mixed.shape
    edge = halo.shape[1]
    modes, groups = rates.shape
    lanes = LANES
    filters = groups * lanes // channels
    terms = filters * modes
    parts = groups // STEPS // filters
    wide = channels // STEPS
    by_block = lambda n: (0, n)
    lead = lambda n: (0, 0, n)
    whole = lambda n: (0, 0)
    return pl.pallas_call(
        functools.partial(hyena_near_body, filters),
        grid=(STEPS,),
        in_specs=[
            pl.BlockSpec((1, rows, wide), lead),
            pl.BlockSpec((1, edge, wide), lead),
            pl.BlockSpec((3, 3, wide), lead),
            pl.BlockSpec((rows, wide), by_block),
            pl.BlockSpec((modes, groups), whole),
            pl.BlockSpec((modes, groups), whole),
        ],
        out_specs=[pl.BlockSpec((rows, wide), by_block)] * 2 + [pl.BlockSpec((rows, parts * terms), by_block)] * 2,
        out_shape=[jax.ShapeDtypeStruct((rows, channels), F32)] * 2
        + [jax.ShapeDtypeStruct((rows, groups * modes), BF16)] * 2,
        scratch_shapes=[
            pltpu.VMEM((parts, rows, filters * rows), BF16),
            pltpu.VMEM((parts, filters * rows, lanes), BF16),
        ],
        compiler_params=limits(16),
        cost_estimate=cost(2 * rows * rows * filters * channels, 12 * rows * channels),
        name="hyena_near",
    )(streams, halo, short_weight, mixed, rates, residues)


def hyena_out_body(modes, near_ref, q_ref, high_ref, low_ref, keep_ref, back_ref, out_ref):
    wide = near_ref.shape[1]
    terms = high_ref.shape[1] * LANES // wide
    filters = terms // modes
    own = same_filter(modes, LANES // filters, terms, LANES)
    mine = pl.program_id(0) // (STEPS // 2) == spot()[0]
    for part in range(wide // LANES):
        at = slice(part * LANES, (part + 1) * LANES)
        here = slice(part * terms, (part + 1) * terms)
        carried = jnp.where(mine, keep_ref[:, at], back_ref[:, at])
        carried = jnp.where(own, jnp.concatenate([carried] * filters, axis=0), 0.0)
        c_high = carried.astype(BF16)
        c_low = (carried - c_high.astype(F32)).astype(BF16)
        high, low = high_ref[:, here], low_ref[:, here]
        far = (
            jnp.dot(high, c_high, preferred_element_type=F32)
            + jnp.dot(low, c_high, preferred_element_type=F32)
            + jnp.dot(high, c_low, preferred_element_type=F32)
        )
        out_ref[:, at] = (q_ref[:, at] * (near_ref[:, at] + far)).astype(BF16)


def hyena_finish(near, query, high, low, keep, back):
    rows, channels = near.shape
    modes = keep.shape[0]
    wide = channels // STEPS
    by_block = lambda n: (0, n)
    by_half = lambda n: (0, n % (STEPS // 2))
    return pl.pallas_call(
        functools.partial(hyena_out_body, modes),
        grid=(STEPS,),
        in_specs=[
            pl.BlockSpec((rows, wide), by_block),
            pl.BlockSpec((rows, wide), by_block),
            pl.BlockSpec((rows, high.shape[1] // STEPS), by_block),
            pl.BlockSpec((rows, high.shape[1] // STEPS), by_block),
            pl.BlockSpec((modes, wide), by_half),
            pl.BlockSpec((modes, wide), by_half),
        ],
        out_specs=pl.BlockSpec((rows, wide), by_block),
        out_shape=jax.ShapeDtypeStruct((rows, channels), BF16),
        compiler_params=limits(16),
        cost_estimate=cost(6 * rows * high.size, 10 * rows * channels),
        name="hyena_finish",
    )(near, query, high, low, keep, back)


def small(body, *operands, outs=1):
    def kernel(*refs):
        made = body(*(ref[...] for ref in refs[: len(operands)]))
        for ref, value in zip(refs[len(operands) :], made if outs > 1 else (made,)):
            ref[...] = value

    shape = pltpu.VMEM(operands[0].shape, operands[0].dtype)
    made = pl.pallas_call(
        kernel,
        in_specs=[VMEM] * len(operands),
        out_specs=[VMEM] * outs,
        out_shape=[shape] * outs,
        compiler_params=limits(4),
        cost_estimate=cost(operands[0].size, 4 * operands[0].size),
    )(*operands)
    return made if outs > 1 else made[0]


def scan_states(keep, away, rate, gain, rows):
    count = lax.axis_size("ctx") // ROW
    decay = lambda blocks, rate: jnp.exp(-rate * float(rows * blocks))

    def both(mine, theirs, rate):
        first = spot()[0] == 0
        even = jnp.where(first, mine, theirs)
        return decay(1, rate) * even + jnp.where(first, theirs, mine), even

    theirs = flip(away, "ctx", 1)
    chip, even = small(both, keep, theirs, rate, outs=2)

    def whole(mine, other, rate):
        first = spot()[1] == 0
        left = jnp.where(first, mine, other)
        return decay(2, rate) * left + jnp.where(first, other, mine), left

    other = flip(chip, "ctx", 2)
    total, left = small(whole, chip, other, rate, outs=2)
    before = ahead(total, "ctx", ROW)
    reach = 2
    while reach < count:
        upto = small(lambda total, before, rate: total + decay(ROW, rate) * before, total, before, rate)
        earlier = ahead(upto, "ctx", ROW * reach)
        reach *= 2
        if reach < count:
            before = small(
                lambda before, earlier, rate: before + decay(ROW * (reach // 2 - 1), rate) * earlier,
                before,
                earlier,
                rate,
            )

    def last(before, earlier, left, even, rate, gain):
        before = before + decay(ROW * (reach // 2 - 1), rate) * earlier
        core, side, _, _ = spot()
        before = jnp.where(side == 0, before, decay(2, rate) * before + left)
        second = decay(1, rate) * before + even
        return (
            gain * jnp.where(core == 0, before, second),
            gain * jnp.where(core == 0, second, before),
        )

    if count == 2:
        earlier = jnp.zeros_like(before)
    if count > 1:
        mine, away = small(last, before, earlier, left, even, rate, gain, outs=2)
    return mine, flip(away, "ctx", 1)


def lanes_from(start, size):
    return pl.ds(pl.multiple_of(start * size, size), size)


def front_body(attn, hyena, theirs_ref, edge_ref, sems):
    rows, half = theirs_ref.shape[1:]
    away = attn.at[:, :, lanes_from(1 - spot()[0], half)]
    edge = hyena.at[:, rows - EDGE : rows, :]
    copies = [
        pltpu.make_async_copy(away, theirs_ref, sems.at[0]),
        pltpu.make_async_copy(edge, edge_ref, sems.at[1]),
    ]
    for copy in copies:
        copy.start()
    for copy in copies:
        copy.wait()


def front(attn, hyena):
    count, rows, channels = attn.shape
    return pl.pallas_call(
        front_body,
        in_specs=[HBM, HBM],
        out_specs=[VMEM, VMEM],
        out_shape=[
            pltpu.VMEM((count, rows, channels // 2), attn.dtype),
            pltpu.VMEM((count, EDGE, channels), hyena.dtype),
        ],
        scratch_shapes=[pltpu.SemaphoreType.DMA((2,))],
        compiler_params=pltpu.CompilerParams(vmem_limit_bytes=ALL_VMEM - (26 << 17)),
        cost_estimate=cost(0, 4 * count * rows * channels // 2),
        name="front",
    )(attn, hyena)


def pack_body(first, streams_ref, theirs_ref, *outs):
    core, side, _, _ = spot()
    slots = (0, 1) if first == 0 else (1 - core, core)
    quarter = theirs_ref.shape[2] // 2
    for out, away in zip(outs, (0, 1)[-len(outs) :]):
        to = 1 - side if away else side
        for stream in range(first, 3):
            out[slots[0], stream - first] = streams_ref[stream, :, lanes_from(2 * core + to, quarter)]
            out[slots[1], stream - first] = theirs_ref[stream, :, lanes_from(to, quarter)]


def pack(streams, theirs, first, amount):
    _, rows, half = theirs.shape
    shape = pltpu.VMEM((2, 3 - first, rows, half // 2), BF16)
    return pl.pallas_call(
        functools.partial(pack_body, first),
        in_specs=[VMEM, VMEM],
        out_specs=[VMEM] * amount,
        out_shape=[shape] * amount,
        compiler_params=limits(10),
        cost_estimate=cost(0, 8 * amount * rows * half),
        name="pack",
    )(streams, theirs)


def odd_body(wanted, pairs, out_ref, sem):
    @pl.when(spot()[1] == wanted)
    def _():
        copy = pltpu.make_async_copy(pairs.at[0:1], out_ref, sem)
        copy.start()
        copy.wait()


def odd(pairs, wanted):
    return pl.pallas_call(
        functools.partial(odd_body, wanted),
        in_specs=[ANY],
        out_specs=VMEM,
        out_shape=pltpu.VMEM((1,) + pairs.shape[1:], pairs.dtype),
        scratch_shapes=[pltpu.SemaphoreType.DMA],
        compiler_params=limits(4),
        cost_estimate=cost(0, pairs.size * 2),
        name="odd",
    )(pairs)


def contig_start(docs_ref, position):
    first = jnp.zeros_like(position)
    bound = jnp.int32(0)
    for n in range(docs_ref.shape[0]):
        bound = bound + docs_ref[n]
        first = jnp.where(position >= bound, bound, first)
    return first


def row_part(streams, theirs, swap, slot, stream, head, quarter):
    core, side, _, _ = spot()
    if slot < 2:
        start = (side if slot else 2 * core + side) * quarter + head * HEAD
        lanes = pl.ds(pl.multiple_of(start, HEAD), HEAD)
        return theirs[stream, :, lanes] if slot else streams[stream, :, lanes]
    return swap[slot - 2, stream, :, head * HEAD : (head + 1) * HEAD]


SCALE = math.log2(math.e) / math.sqrt(HEAD)


CHUNK = 32


def softmax_group(queries, keys, values, bias, turn, s_s, p_s, keep):
    tall, rows = queries.shape[0], keys[0].shape[0]
    width = len(keys) * rows
    for n in range(0, len(keys), 2):
        s_s[turn, 0:tall, n * rows : (n + 2) * rows] = lax.dot_general(
            queries,
            jnp.concatenate(keys[n : n + 2], axis=0),
            (((1,), (1,)), ((), ())),
            preferred_element_type=F32,
        )
    for m in range(0, tall, CHUNK):
        some = slice(m, m + CHUNK)
        top = None
        parts = []
        for n in range(0, width, LANES):
            part = s_s[turn, some, n : n + LANES] + bias[some, n : n + LANES]
            parts.append(part)
            top = part if top is None else jnp.maximum(top, part)
        top = jnp.broadcast_to(jnp.max(top, axis=1, keepdims=True), (CHUNK, LANES))
        below = jnp.zeros((CHUNK, LANES), F32)
        for n, part in enumerate(parts):
            weight = jnp.exp2((part - top) * SCALE)
            below = below + weight
            p_s[turn, some, n * LANES : (n + 1) * LANES] = weight.astype(BF16)
        keep(m, top, jnp.broadcast_to(jnp.sum(below, axis=1, keepdims=True), (CHUNK, LANES)))
    return jnp.dot(
        p_s[turn, 0:tall, 0:width], jnp.concatenate(values, axis=0), preferred_element_type=F32
    )


def attend_body(docs_ref, streams, theirs, swap, own, cross, acc_ref, m_ref, l_ref, bias_s, s_s, p_s):
    _, side, place, row = spot()
    rows, quarter = own.shape[2:]
    base = row * (ROW * rows)
    part = functools.partial(row_part, streams, theirs, swap, quarter=quarter)

    def run(first_pair, second_pair):
        for group, (asking, seen) in enumerate(((first_pair, first_pair), (second_pair, (0, 1, 2, 3)))):
            starts = [base + (2 * (side if old else 1 - side) + 1 - n - ROW) * rows for old in (1, 0) for n in (0, 1)]
            starts += [base + (place ^ slot) * rows for slot in seen]
            for at, slot in enumerate(asking):
                position = base + (place ^ slot) * rows + lax.broadcasted_iota(jnp.int32, (rows, 1), 0)
                first = contig_start(docs_ref, position)
                for n, start in enumerate(starts):
                    token = start + lax.broadcasted_iota(jnp.int32, (rows, rows), 1)
                    bias_s[group, at * rows : (at + 1) * rows, n * rows : (n + 1) * rows] = jnp.where(
                        (token >= first) & (token <= position), 0.0, -jnp.inf
                    )
            for head in range(quarter // HEAD):
                lanes = slice(head * HEAD, (head + 1) * HEAD)
                olds = lambda kind: [old[n, kind, :, lanes] for old in (own, cross) for n in (0, 1)]

                def keep(m, top, below):
                    out = slice(asking[0] * rows + m, asking[0] * rows + m + CHUNK)
                    m_ref[out, lanes] = top
                    l_ref[out, lanes] = below

                acc_ref[asking[0] * rows : (asking[1] + 1) * rows, lanes] = softmax_group(
                    jnp.concatenate([part(slot, 0, head) for slot in asking], axis=0),
                    olds(0) + [part(slot, 1, head) for slot in seen],
                    olds(1) + [part(slot, 2, head) for slot in seen],
                    bias_s.at[group],
                    head % 2,
                    s_s,
                    p_s,
                    keep,
                )

    @pl.when(side == 0)
    def _():
        run((0, 1), (2, 3))

    @pl.when(side == 1)
    def _():
        run((2, 3), (0, 1))


def attend(doc_lengths, streams, theirs, swap, own, cross):
    _, _, rows, quarter = own.shape
    heads = quarter // HEAD
    return pl.pallas_call(
        attend_body,
        in_specs=[SMEM] + [VMEM] * 5,
        out_specs=[VMEM] * 3,
        out_shape=[
            jax.ShapeDtypeStruct((ROW * rows, quarter), F32),
        ]
        * 3,
        scratch_shapes=[
            pltpu.VMEM((2, 2 * rows, 2 * ROW * rows), F32),
            pltpu.VMEM((2, 2 * rows, 2 * ROW * rows), F32),
            pltpu.VMEM((2, 2 * rows, 2 * ROW * rows), BF16),
        ],
        compiler_params=limits(20),
        cost_estimate=cost(26 * 4 * rows * rows * quarter, 14 * ROW * rows * quarter, 26 * heads * rows * rows),
        name="attend",
    )(doc_lengths, streams, theirs, swap, own, cross)


def attend_last_body(pair, docs_ref, streams, theirs, swap, *refs):
    cross_l, own_s, own_l, cross_s, acc_ref, m_ref, l_ref = refs[:7]
    outs = refs[7:]
    _, side, place, row = spot()
    rows, quarter = acc_ref.shape[0] // ROW, acc_ref.shape[1]
    base = row * (ROW * rows)
    heads = range(quarter // HEAD)

    def run(early, late, large, small):
        for asking, blocks in ((early, ((small, 0), (large, 1), (large, 0))), (late, ((large, 0),))):
            if asking != pair:
                continue
            width = len(blocks) * rows
            here = slice(asking[0] * rows, (asking[1] + 1) * rows)
            token = base - (ROW + len(blocks)) * rows + lax.broadcasted_iota(jnp.int32, (rows, width), 1)
            allowed = []
            for slot in asking:
                position = base + (place ^ slot) * rows + lax.broadcasted_iota(jnp.int32, (rows, 1), 0)
                allowed.append((token >= contig_start(docs_ref, position)).astype(jnp.int32))
            allowed = jnp.concatenate(allowed, axis=0) != 0
            lanes_of = [slice(head * HEAD, (head + 1) * HEAD) for head in heads]
            stack = lambda kind, lanes: jnp.concatenate([ref[n, kind, :, lanes] for ref, n in blocks], axis=0)
            scores = [
                lax.dot_general(
                    jnp.concatenate(
                        [row_part(streams, theirs, swap, slot, 0, head, quarter) for slot in asking], axis=0
                    ),
                    stack(0, lanes_of[head]),
                    (((1,), (1,)), ((), ())),
                    preferred_element_type=F32,
                )
                for head in heads
            ]
            scores = [jnp.where(allowed, score, -jnp.inf) for score in scores]
            tops = [
                jnp.maximum(m_ref[here, lanes], jnp.max(score, axis=1, keepdims=True))
                for lanes, score in zip(lanes_of, scores)
            ]
            weights = [
                jnp.exp2((score - jnp.concatenate([top] * len(blocks), axis=1)) * SCALE)
                for score, top in zip(scores, tops)
            ]
            for lanes, top, weight in zip(lanes_of, tops, weights):
                fade = jnp.exp2((m_ref[here, lanes] - top) * SCALE)
                share = 1.0 / (l_ref[here, lanes] * fade + jnp.sum(weight, axis=1, keepdims=True))
                more = jnp.dot(weight.astype(BF16), stack(1, lanes), preferred_element_type=F32)
                made = ((acc_ref[here, lanes] * fade + more) * share).astype(BF16)
                for n, out in enumerate(outs):
                    out[:, lanes] = made[n * rows : (n + 1) * rows]

    @pl.when(side == 0)
    def _():
        run((0, 1), (2, 3), cross_l, own_s)

    @pl.when(side == 1)
    def _():
        run((2, 3), (0, 1), own_l, cross_s)


def attend_last(pair, doc_lengths, streams, theirs, swap, olds, acc, top, below):
    rows, quarter = acc.shape[0] // ROW, acc.shape[1]
    return pl.pallas_call(
        functools.partial(attend_last_body, pair),
        in_specs=[SMEM] + [VMEM] * 10,
        out_specs=[VMEM] * 2,
        out_shape=[jax.ShapeDtypeStruct((rows, quarter), BF16)] * 2,
        compiler_params=limits(16),
        cost_estimate=cost(16 * rows * rows * quarter, 24 * rows * quarter, 16 * rows * rows),
        name="attend_last",
    )(doc_lengths, streams, theirs, swap, *olds, acc, top, below)


def assemble_body(*refs):
    place = spot()[2]
    *pieces, out_ref = refs
    turns = len(pieces) // ROW
    lanes = pieces[0].shape[1]
    for n, piece in enumerate(pieces):
        maker = place ^ (n % ROW)
        which = 2 * (maker & 1) + lax.shift_right_logical(maker, 1)
        out_ref[:, lanes_from(which * turns + n // ROW, lanes)] = piece[...]


def assemble(pieces):
    rows, lanes = pieces[0].shape
    return pl.pallas_call(
        assemble_body,
        in_specs=[VMEM] * len(pieces),
        out_specs=VMEM,
        out_shape=jax.ShapeDtypeStruct((rows, len(pieces) * lanes), BF16),
        compiler_params=limits(6),
        cost_estimate=cost(0, 4 * rows * lanes * len(pieces)),
        name="assemble",
    )(*pieces)


def on_device(hyena_qkv, short_weight, filter_rate, filter_residue, attn_qkv, doc_lengths):
    rows = attn_qkv.shape[0]
    inner = hyena_qkv.transpose(1, 0, 2)
    streams = attn_qkv.transpose(1, 0, 2)
    rates, residues = filter_rate.T, filter_residue.T
    theirs, edge = front(streams, inner)

    theirs = flip(theirs, "ctx", 1)
    edge = ahead(edge, "ctx", 1)
    own, cross = pack(streams, theirs, 1, 2)
    cross = ahead(cross, "ctx", ROW, 2)
    own = ahead(own, "ctx", ROW)
    (swap,) = pack(streams, theirs, 0, 1)
    swap = flip(swap, "ctx", 2)
    olds = (
        ahead(cross, "ctx", ROW, 0, ROW, 0),
        ahead(odd(own, 0), "ctx", ROW, 0, ROW, 0),
        ahead(own, "ctx", ROW, 0, ROW, 1),
        ahead(odd(cross, 1), "ctx", ROW, 0, ROW, 1),
    )

    mixed, keep, away, wide, gain = hyena_ends(inner, edge, short_weight, rates, residues)
    near, query, high, low = hyena_near(inner, edge, short_weight, mixed, rates, residues)
    keep, back = scan_states(keep, away, wide, gain, rows)
    hyena_out = hyena_finish(near, query, high, low, keep, back)

    acc, top, below = attend(doc_lengths, streams, theirs, swap, own, cross)
    last = lambda pair: attend_last(pair, doc_lengths, streams, theirs, swap, olds, acc, top, below)
    far2, far3 = last((2, 3))
    far2 = flip(far2, "ctx", 2)
    far3 = flip(far3, "ctx", 3)
    kept, near1 = last((0, 1))
    near1 = flip(near1, "ctx", 1)
    attn_out = assemble([kept, near1, far2, far3])
    return (hyena_out, attn_out)


def solution(mesh):
    in_specs = (
        P(("group", "ctx"), None, None),
        P(),
        P(),
        P(),
        P(("group", "ctx"), None, None),
        P("group"),
    )
    out_specs = (P(("group", "ctx"), None), P(("group", "ctx"), None))
    return jax.shard_map(on_device, mesh=mesh, in_specs=in_specs, out_specs=out_specs, check_vma=False)
```

```python
import functools
import math

import jax
import jax.numpy as jnp
from jax import lax
from jax.experimental import pallas as pl
from jax.experimental.pallas import tpu as pltpu
from jax.sharding import PartitionSpec as P


HEAD = 128
LANES = 128
EDGE = 8
ROW = 4


F32 = jnp.float32
BF16 = jnp.bfloat16


def flip(value, axis, bit):
    count = lax.axis_size(axis)
    return lax.ppermute(value, axis, [(at, at ^ bit) for at in range(count)])


def side_of(at):
    return at // 2 % 2


def ahead(value, axis, steps, bit=0, first=0, side=None):
    count = lax.axis_size(axis)
    pairs = [
        (at, (at + steps) ^ bit)
        for at in range(first, count - steps)
        if side is None or side_of(at) == side
    ]
    return lax.ppermute(value, axis, pairs)


def spot():
    index = lax.axis_index("ctx")
    return index & 1, lax.shift_right_logical(index, 1) & 1, index & (ROW - 1), index // ROW


def next_block(value, axis, first):
    count = lax.axis_size(axis)
    return lax.ppermute(value, axis, [(at, at + 1) for at in range(first, count - 1, 2)])


ALL_VMEM = 67043328


def limits(mib):
    return pltpu.CompilerParams(vmem_limit_bytes=mib << 20)


def cost(flops, moved, exps=0):
    return pl.CostEstimate(flops=flops, bytes_accessed=moved, transcendentals=exps)


VMEM = pl.BlockSpec(memory_space=pltpu.VMEM)
SMEM = pl.BlockSpec(memory_space=pltpu.SMEM)
ANY = pl.BlockSpec(memory_space=pl.ANY)
HBM = pl.BlockSpec(memory_space=pltpu.HBM)


def same_filter(modes, width, terms, lanes):
    row_at = lax.broadcasted_iota(jnp.int32, (terms, lanes), 0)
    lane_at = lax.broadcasted_iota(jnp.int32, (terms, lanes), 1)
    kept = None
    for g in range(terms // modes):
        both = (
            (row_at >= g * modes)
            & (row_at < (g + 1) * modes)
            & (lane_at >= g * width)
            & (lane_at < (g + 1) * width)
        )
        kept = both if kept is None else kept | both
    return kept


def either(one, other):
    return one.astype(F32) + other.astype(F32)


def feature(x, halo, w_ref, stream, at):
    here = x.astype(F32)
    halo = halo.astype(F32)
    edge = halo.shape[0]
    row_at = lax.broadcasted_iota(jnp.int32, here.shape, 0)
    one = jnp.where(row_at == 0, halo[edge - 1 :], pltpu.roll(here, 1, 0))
    two = jnp.where(row_at == 1, halo[edge - 1 :], pltpu.roll(here, 2, 0))
    two = jnp.where(row_at == 0, halo[edge - 2 : edge - 1], two)
    tap = [w_ref[n, stream : stream + 1, at] for n in range(3)]
    return tap[0] * here + tap[1] * one + tap[2] * two


def of_step(table_ref):
    groups = table_ref.shape[1]
    return pltpu.roll(table_ref[...], groups - pl.program_id(0) * (groups // STEPS), 1)


def down(table, part, filters, lanes):
    columns = [table[:, part * filters + g : part * filters + g + 1] for g in range(filters)]
    return jnp.concatenate([jnp.broadcast_to(c, (c.shape[0], lanes)) for c in columns], axis=0)


def hyena_ends_body(
    filters, x_ref, halo_ref, other_ref, w_ref, rate_ref, res_ref, mixed_ref, keep_ref, away_ref, wide_ref, gain_ref, all_s
):
    rows = x_ref.shape[1]
    modes, groups = rate_ref.shape
    parts = groups // STEPS // filters
    terms = filters * modes
    lanes = x_ref.shape[2] // parts
    width = lanes // filters
    rates = of_step(rate_ref)
    coeffs = of_step(res_ref) * jnp.sqrt(2.0 * rates / modes)
    lag = (rows - 1 - lax.broadcasted_iota(jnp.int32, (terms, rows), 1)).astype(F32)
    own = same_filter(modes, width, terms, lanes)
    pick = lambda matrix: jnp.sum(jnp.where(own, matrix, 0.0).reshape(filters, modes, lanes), axis=0)
    step = pl.program_id(0)
    for part in range(parts):
        at = slice(part * lanes, (part + 1) * lanes)
        key, value = (
            feature(x_ref[n, :, at], either(halo_ref[n, :, at], other_ref[n, :, at]), w_ref, n, at) for n in (1, 2)
        )
        mixed = (key * value).astype(BF16)
        mixed_ref[:, at] = mixed
        rate = down(rates, part, filters, rows)
        powers = jnp.exp(-rate * lag)
        high = powers.astype(BF16)
        low = (powers - high.astype(F32)).astype(BF16)
        ends = jnp.dot(high, mixed, preferred_element_type=F32) + jnp.dot(
            low, mixed, preferred_element_type=F32
        )
        all_s[0, step, :, at] = pick(ends)
        all_s[1, step, :, at] = pick(rate)
        all_s[2, step, :, at] = pick(down(coeffs, part, filters, rows))

    @pl.when(step == STEPS - 1)
    def _():
        core = spot()[0]
        half = STEPS // 2
        for n in range(half):
            at = slice(n * parts * lanes, (n + 1) * parts * lanes)
            away_ref[:, at] = all_s[0, (1 - core) * half + n]
            for table, out in enumerate((keep_ref, wide_ref, gain_ref)):
                out[:, at] = all_s[table, core * half + n]


STEPS = 4


def hyena_ends(streams, halos, short_weight, rates, residues):
    _, rows, channels = streams.shape
    edge = halos[0].shape[1]
    modes, groups = rates.shape
    filters = groups * LANES // channels
    terms = filters * modes
    wide = channels // STEPS
    lead = lambda n: (0, 0, n)
    whole = lambda n: (0, 0)
    half = (modes, channels // 2)
    return pl.pallas_call(
        functools.partial(hyena_ends_body, filters),
        grid=(STEPS,),
        in_specs=[
            pl.BlockSpec((3, rows, wide), lead),
            pl.BlockSpec((3, edge, wide), lead),
            pl.BlockSpec((3, edge, wide), lead),
            pl.BlockSpec((3, 3, wide), lead),
            pl.BlockSpec((modes, groups), whole),
            pl.BlockSpec((modes, groups), whole),
        ],
        out_specs=[pl.BlockSpec((rows, wide), lambda n: (0, n))] + [pl.BlockSpec(half, whole)] * 4,
        out_shape=[jax.ShapeDtypeStruct((rows, channels), BF16)] + [jax.ShapeDtypeStruct(half, F32)] * 4,
        scratch_shapes=[pltpu.VMEM((3, STEPS, modes, wide), F32)],
        compiler_params=limits(16),
        cost_estimate=cost(4 * rows * terms * channels, 8 * rows * channels),
        name="hyena_ends",
    )(streams, *halos, short_weight, rates, residues)


def hyena_near_body(
    filters, x_ref, halo_ref, other_ref, w_ref, mixed_ref, rate_ref, res_ref, near_ref, q_ref, high_ref, low_ref, taps_s, u_s
):
    rows = mixed_ref.shape[0]
    modes, groups = rate_ref.shape
    parts = groups // STEPS // filters
    terms = filters * modes
    lanes = mixed_ref.shape[1] // parts
    width = lanes // filters
    rates = of_step(rate_ref)
    coeffs = of_step(res_ref) * jnp.sqrt(2.0 * rates / modes)
    row_at = lax.broadcasted_iota(jnp.int32, (rows, lanes), 0)
    lane_at = lax.broadcasted_iota(jnp.int32, (rows, lanes), 1)
    lag = (rows - 1 - lax.broadcasted_iota(jnp.int32, (terms, rows), 1)).astype(F32)
    ahead_lag = (1 + lax.broadcasted_iota(jnp.int32, (terms, rows), 1)).astype(F32)
    zero = jnp.zeros((rows, lanes), BF16)
    for part in range(parts):
        at = slice(part * lanes, (part + 1) * lanes)
        mixed = mixed_ref[:, at]
        rate = down(rates, part, filters, rows)
        powers = down(coeffs, part, filters, rows) * jnp.exp(-rate * lag)
        backward = jnp.sum(powers.reshape(filters, modes, rows), axis=1)
        for g in range(filters):
            spread = jnp.broadcast_to(backward[g : g + 1], (rows, rows))
            shifted = pltpu.roll(spread, 1, 1, stride=1, stride_axis=0)
            kept = jnp.where(lane_at <= row_at, shifted, 0.0)
            taps_s[part, :, g * rows : (g + 1) * rows] = kept.astype(BF16)
            mine = (lane_at >= g * width) & (lane_at < (g + 1) * width)
            u_s[part, g * rows : (g + 1) * rows, :] = jnp.where(mine, mixed, zero)
        near_ref[:, at] = jnp.dot(taps_s[part], u_s[part], preferred_element_type=F32)
        q_ref[:, at] = feature(x_ref[0, :, at], either(halo_ref[0, :, at], other_ref[0, :, at]), w_ref, 0, at)
        decays = jnp.exp(-rate * ahead_lag).T
        here = slice(part * terms, (part + 1) * terms)
        high = decays.astype(BF16)
        high_ref[:, here] = high
        low_ref[:, here] = (decays - high.astype(F32)).astype(BF16)


def hyena_near(streams, halos, short_weight, mixed, rates, residues):
    rows, channels = mixed.shape
    edge = halos[0].shape[1]
    modes, groups = rates.shape
    lanes = LANES
    filters = groups * lanes // channels
    terms = filters * modes
    parts = groups // STEPS // filters
    wide = channels // STEPS
    by_block = lambda n: (0, n)
    lead = lambda n: (0, 0, n)
    whole = lambda n: (0, 0)
    return pl.pallas_call(
        functools.partial(hyena_near_body, filters),
        grid=(STEPS,),
        in_specs=[
            pl.BlockSpec((1, rows, wide), lead),
            pl.BlockSpec((1, edge, wide), lead),
            pl.BlockSpec((1, edge, wide), lead),
            pl.BlockSpec((3, 3, wide), lead),
            pl.BlockSpec((rows, wide), by_block),
            pl.BlockSpec((modes, groups), whole),
            pl.BlockSpec((modes, groups), whole),
        ],
        out_specs=[pl.BlockSpec((rows, wide), by_block)] * 2 + [pl.BlockSpec((rows, parts * terms), by_block)] * 2,
        out_shape=[jax.ShapeDtypeStruct((rows, channels), F32)] * 2
        + [jax.ShapeDtypeStruct((rows, groups * modes), BF16)] * 2,
        scratch_shapes=[
            pltpu.VMEM((parts, rows, filters * rows), BF16),
            pltpu.VMEM((parts, filters * rows, lanes), BF16),
        ],
        compiler_params=limits(16),
        cost_estimate=cost(2 * rows * rows * filters * channels, 12 * rows * channels),
        name="hyena_near",
    )(streams, *halos, short_weight, mixed, rates, residues)


def hyena_out_body(modes, near_ref, q_ref, high_ref, low_ref, keep_ref, back_ref, out_ref):
    wide = near_ref.shape[1]
    terms = high_ref.shape[1] * LANES // wide
    filters = terms // modes
    own = same_filter(modes, LANES // filters, terms, LANES)
    mine = pl.program_id(0) // (STEPS // 2) == spot()[0]
    for part in range(wide // LANES):
        at = slice(part * LANES, (part + 1) * LANES)
        here = slice(part * terms, (part + 1) * terms)
        carried = jnp.where(mine, keep_ref[:, at], back_ref[:, at])
        carried = jnp.where(own, jnp.concatenate([carried] * filters, axis=0), 0.0)
        c_high = carried.astype(BF16)
        c_low = (carried - c_high.astype(F32)).astype(BF16)
        high, low = high_ref[:, here], low_ref[:, here]
        far = (
            jnp.dot(high, c_high, preferred_element_type=F32)
            + jnp.dot(low, c_high, preferred_element_type=F32)
            + jnp.dot(high, c_low, preferred_element_type=F32)
        )
        out_ref[:, at] = (q_ref[:, at] * (near_ref[:, at] + far)).astype(BF16)


def hyena_finish(near, query, high, low, keep, back):
    rows, channels = near.shape
    modes = keep.shape[0]
    wide = channels // STEPS
    by_block = lambda n: (0, n)
    by_half = lambda n: (0, n % (STEPS // 2))
    return pl.pallas_call(
        functools.partial(hyena_out_body, modes),
        grid=(STEPS,),
        in_specs=[
            pl.BlockSpec((rows, wide), by_block),
            pl.BlockSpec((rows, wide), by_block),
            pl.BlockSpec((rows, high.shape[1] // STEPS), by_block),
            pl.BlockSpec((rows, high.shape[1] // STEPS), by_block),
            pl.BlockSpec((modes, wide), by_half),
            pl.BlockSpec((modes, wide), by_half),
        ],
        out_specs=pl.BlockSpec((rows, wide), by_block),
        out_shape=jax.ShapeDtypeStruct((rows, channels), BF16),
        compiler_params=limits(16),
        cost_estimate=cost(6 * rows * high.size, 10 * rows * channels),
        name="hyena_finish",
    )(near, query, high, low, keep, back)


def small(body, *operands, outs=1):
    def kernel(*refs):
        made = body(*(ref[...] for ref in refs[: len(operands)]))
        for ref, value in zip(refs[len(operands) :], made if outs > 1 else (made,)):
            ref[...] = value

    shape = pltpu.VMEM(operands[0].shape, operands[0].dtype)
    made = pl.pallas_call(
        kernel,
        in_specs=[VMEM] * len(operands),
        out_specs=[VMEM] * outs,
        out_shape=[shape] * outs,
        compiler_params=limits(4),
        cost_estimate=cost(operands[0].size, 4 * operands[0].size),
    )(*operands)
    return made if outs > 1 else made[0]


def scan_states(keep, away, rate, gain, rows):
    count = lax.axis_size("ctx") // ROW
    decay = lambda blocks, rate: jnp.exp(-rate * float(rows * blocks))

    def both(mine, theirs, rate):
        first = spot()[0] == 0
        even = jnp.where(first, mine, theirs)
        return decay(1, rate) * even + jnp.where(first, theirs, mine), even

    theirs = flip(away, "ctx", 1)
    chip, even = small(both, keep, theirs, rate, outs=2)

    def whole(mine, other, rate):
        first = spot()[1] == 0
        left = jnp.where(first, mine, other)
        return decay(2, rate) * left + jnp.where(first, other, mine), left

    other = flip(chip, "ctx", 2)
    total, left = small(whole, chip, other, rate, outs=2)
    before = ahead(total, "ctx", ROW)
    reach = 2
    while reach < count:
        upto = small(lambda total, before, rate: total + decay(ROW, rate) * before, total, before, rate)
        earlier = ahead(upto, "ctx", ROW * reach)
        reach *= 2
        if reach < count:
            before = small(
                lambda before, earlier, rate: before + decay(ROW * (reach // 2 - 1), rate) * earlier,
                before,
                earlier,
                rate,
            )

    def last(before, earlier, left, even, rate, gain):
        before = before + decay(ROW * (reach // 2 - 1), rate) * earlier
        core, side, _, _ = spot()
        before = jnp.where(side == 0, before, decay(2, rate) * before + left)
        second = decay(1, rate) * before + even
        return (
            gain * jnp.where(core == 0, before, second),
            gain * jnp.where(core == 0, second, before),
        )

    if count == 2:
        earlier = jnp.zeros_like(before)
    if count > 1:
        mine, away = small(last, before, earlier, left, even, rate, gain, outs=2)
    return mine, flip(away, "ctx", 1)


def lanes_from(start, size):
    return pl.ds(pl.multiple_of(start * size, size), size)


def front_body(attn, hyena, theirs_ref, edge_ref, sems):
    rows, half = theirs_ref.shape[1:]
    away = attn.at[:, :, lanes_from(1 - spot()[0], half)]
    edge = hyena.at[:, rows - EDGE : rows, :]
    copies = [
        pltpu.make_async_copy(away, theirs_ref, sems.at[0]),
        pltpu.make_async_copy(edge, edge_ref, sems.at[1]),
    ]
    for copy in copies:
        copy.start()
    for copy in copies:
        copy.wait()


def front(attn, hyena):
    count, rows, channels = attn.shape
    return pl.pallas_call(
        front_body,
        in_specs=[HBM, HBM],
        out_specs=[VMEM, VMEM],
        out_shape=[
            pltpu.VMEM((count, rows, channels // 2), attn.dtype),
            pltpu.VMEM((count, EDGE, channels), hyena.dtype),
        ],
        scratch_shapes=[pltpu.SemaphoreType.DMA((2,))],
        compiler_params=pltpu.CompilerParams(vmem_limit_bytes=ALL_VMEM - (26 << 17)),
        cost_estimate=cost(0, 4 * count * rows * channels // 2),
        name="front",
    )(attn, hyena)


def pack_body(first, streams_ref, theirs_ref, *outs):
    core, side, _, _ = spot()
    slots = (0, 1) if first == 0 else (1 - core, core)
    quarter = theirs_ref.shape[2] // 2
    for out, away in zip(outs, (0, 1)[-len(outs) :]):
        to = 1 - side if away else side
        for stream in range(first, 3):
            out[slots[0], stream - first] = streams_ref[stream, :, lanes_from(2 * core + to, quarter)]
            out[slots[1], stream - first] = theirs_ref[stream, :, lanes_from(to, quarter)]


def pack(streams, theirs, first, amount):
    _, rows, half = theirs.shape
    shape = pltpu.VMEM((2, 3 - first, rows, half // 2), BF16)
    return pl.pallas_call(
        functools.partial(pack_body, first),
        in_specs=[VMEM, VMEM],
        out_specs=[VMEM] * amount,
        out_shape=[shape] * amount,
        compiler_params=limits(10),
        cost_estimate=cost(0, 8 * amount * rows * half),
        name="pack",
    )(streams, theirs)


def odd_body(wanted, pairs, out_ref, sem):
    @pl.when(spot()[1] == wanted)
    def _():
        copy = pltpu.make_async_copy(pairs.at[0:1], out_ref, sem)
        copy.start()
        copy.wait()


def odd(pairs, wanted):
    return pl.pallas_call(
        functools.partial(odd_body, wanted),
        in_specs=[ANY],
        out_specs=VMEM,
        out_shape=pltpu.VMEM((1,) + pairs.shape[1:], pairs.dtype),
        scratch_shapes=[pltpu.SemaphoreType.DMA],
        compiler_params=limits(4),
        cost_estimate=cost(0, pairs.size * 2),
        name="odd",
    )(pairs)


def contig_start(docs_ref, position):
    first = jnp.zeros_like(position)
    bound = jnp.int32(0)
    for n in range(docs_ref.shape[0]):
        bound = bound + docs_ref[n]
        first = jnp.where(position >= bound, bound, first)
    return first


def row_part(streams, theirs, swap, slot, stream, head, quarter):
    core, side, _, _ = spot()
    if slot < 2:
        start = (side if slot else 2 * core + side) * quarter + head * HEAD
        lanes = pl.ds(pl.multiple_of(start, HEAD), HEAD)
        return theirs[stream, :, lanes] if slot else streams[stream, :, lanes]
    return swap[slot - 2, stream, :, head * HEAD : (head + 1) * HEAD]


SCALE = math.log2(math.e) / math.sqrt(HEAD)


CHUNK = 32


def softmax_group(queries, keys, values, bias, turn, s_s, p_s, keep):
    tall, rows = queries.shape[0], keys[0].shape[0]
    width = len(keys) * rows
    for n in range(0, len(keys), 2):
        s_s[turn, 0:tall, n * rows : (n + 2) * rows] = lax.dot_general(
            queries,
            jnp.concatenate(keys[n : n + 2], axis=0),
            (((1,), (1,)), ((), ())),
            preferred_element_type=F32,
        )
    for m in range(0, tall, CHUNK):
        some = slice(m, m + CHUNK)
        top = None
        parts = []
        for n in range(0, width, LANES):
            part = s_s[turn, some, n : n + LANES] + bias[some, n : n + LANES]
            parts.append(part)
            top = part if top is None else jnp.maximum(top, part)
        top = jnp.broadcast_to(jnp.max(top, axis=1, keepdims=True), (CHUNK, LANES))
        below = jnp.zeros((CHUNK, LANES), F32)
        for n, part in enumerate(parts):
            weight = jnp.exp2((part - top) * SCALE)
            below = below + weight
            p_s[turn, some, n * LANES : (n + 1) * LANES] = weight.astype(BF16)
        keep(m, top, jnp.broadcast_to(jnp.sum(below, axis=1, keepdims=True), (CHUNK, LANES)))
    return jnp.dot(
        p_s[turn, 0:tall, 0:width], jnp.concatenate(values, axis=0), preferred_element_type=F32
    )


def attend_body(docs_ref, streams, theirs, swap, own, cross, acc_ref, m_ref, l_ref, bias_s, s_s, p_s):
    _, side, place, row = spot()
    rows, quarter = own.shape[2:]
    base = row * (ROW * rows)
    part = functools.partial(row_part, streams, theirs, swap, quarter=quarter)

    def run(first_pair, second_pair):
        for group, (asking, seen) in enumerate(((first_pair, first_pair), (second_pair, (0, 1, 2, 3)))):
            starts = [base + (2 * (side if old else 1 - side) + 1 - n - ROW) * rows for old in (1, 0) for n in (0, 1)]
            starts += [base + (place ^ slot) * rows for slot in seen]
            for at, slot in enumerate(asking):
                position = base + (place ^ slot) * rows + lax.broadcasted_iota(jnp.int32, (rows, 1), 0)
                first = contig_start(docs_ref, position)
                for n, start in enumerate(starts):
                    token = start + lax.broadcasted_iota(jnp.int32, (rows, rows), 1)
                    bias_s[group, at * rows : (at + 1) * rows, n * rows : (n + 1) * rows] = jnp.where(
                        (token >= first) & (token <= position), 0.0, -jnp.inf
                    )
            for head in range(quarter // HEAD):
                lanes = slice(head * HEAD, (head + 1) * HEAD)
                olds = lambda kind: [old[n, kind, :, lanes] for old in (own, cross) for n in (0, 1)]

                def keep(m, top, below):
                    out = slice(asking[0] * rows + m, asking[0] * rows + m + CHUNK)
                    m_ref[out, lanes] = top
                    l_ref[out, lanes] = below

                acc_ref[asking[0] * rows : (asking[1] + 1) * rows, lanes] = softmax_group(
                    jnp.concatenate([part(slot, 0, head) for slot in asking], axis=0),
                    olds(0) + [part(slot, 1, head) for slot in seen],
                    olds(1) + [part(slot, 2, head) for slot in seen],
                    bias_s.at[group],
                    head % 2,
                    s_s,
                    p_s,
                    keep,
                )

    @pl.when(side == 0)
    def _():
        run((0, 1), (2, 3))

    @pl.when(side == 1)
    def _():
        run((2, 3), (0, 1))


def attend(doc_lengths, streams, theirs, swap, own, cross):
    _, _, rows, quarter = own.shape
    heads = quarter // HEAD
    return pl.pallas_call(
        attend_body,
        in_specs=[SMEM] + [VMEM] * 5,
        out_specs=[VMEM] * 3,
        out_shape=[
            jax.ShapeDtypeStruct((ROW * rows, quarter), F32),
        ]
        * 3,
        scratch_shapes=[
            pltpu.VMEM((2, 2 * rows, 2 * ROW * rows), F32),
            pltpu.VMEM((2, 2 * rows, 2 * ROW * rows), F32),
            pltpu.VMEM((2, 2 * rows, 2 * ROW * rows), BF16),
        ],
        compiler_params=limits(20),
        cost_estimate=cost(26 * 4 * rows * rows * quarter, 14 * ROW * rows * quarter, 26 * heads * rows * rows),
        name="attend",
    )(doc_lengths, streams, theirs, swap, own, cross)


def attend_last_body(pair, docs_ref, streams, theirs, swap, *refs):
    cross_l, own_s, own_l, cross_s, acc_ref, m_ref, l_ref = refs[:7]
    outs = refs[7:]
    _, side, place, row = spot()
    rows, quarter = acc_ref.shape[0] // ROW, acc_ref.shape[1]
    base = row * (ROW * rows)
    heads = range(quarter // HEAD)

    def run(early, late, large, small):
        for asking, blocks in ((early, ((small, 0), (large, 1), (large, 0))), (late, ((large, 0),))):
            if asking != pair:
                continue
            width = len(blocks) * rows
            here = slice(asking[0] * rows, (asking[1] + 1) * rows)
            token = base - (ROW + len(blocks)) * rows + lax.broadcasted_iota(jnp.int32, (rows, width), 1)
            allowed = []
            for slot in asking:
                position = base + (place ^ slot) * rows + lax.broadcasted_iota(jnp.int32, (rows, 1), 0)
                allowed.append((token >= contig_start(docs_ref, position)).astype(jnp.int32))
            allowed = jnp.concatenate(allowed, axis=0) != 0
            lanes_of = [slice(head * HEAD, (head + 1) * HEAD) for head in heads]
            stack = lambda kind, lanes: jnp.concatenate([ref[n, kind, :, lanes] for ref, n in blocks], axis=0)
            scores = [
                lax.dot_general(
                    jnp.concatenate(
                        [row_part(streams, theirs, swap, slot, 0, head, quarter) for slot in asking], axis=0
                    ),
                    stack(0, lanes_of[head]),
                    (((1,), (1,)), ((), ())),
                    preferred_element_type=F32,
                )
                for head in heads
            ]
            scores = [jnp.where(allowed, score, -jnp.inf) for score in scores]
            tops = [
                jnp.maximum(m_ref[here, lanes], jnp.max(score, axis=1, keepdims=True))
                for lanes, score in zip(lanes_of, scores)
            ]
            weights = [
                jnp.exp2((score - jnp.concatenate([top] * len(blocks), axis=1)) * SCALE)
                for score, top in zip(scores, tops)
            ]
            for lanes, top, weight in zip(lanes_of, tops, weights):
                fade = jnp.exp2((m_ref[here, lanes] - top) * SCALE)
                share = 1.0 / (l_ref[here, lanes] * fade + jnp.sum(weight, axis=1, keepdims=True))
                more = jnp.dot(weight.astype(BF16), stack(1, lanes), preferred_element_type=F32)
                made = ((acc_ref[here, lanes] * fade + more) * share).astype(BF16)
                for n, out in enumerate(outs):
                    out[:, lanes] = made[n * rows : (n + 1) * rows]

    @pl.when(side == 0)
    def _():
        run((0, 1), (2, 3), cross_l, own_s)

    @pl.when(side == 1)
    def _():
        run((2, 3), (0, 1), own_l, cross_s)


def attend_last(pair, doc_lengths, streams, theirs, swap, olds, acc, top, below):
    rows, quarter = acc.shape[0] // ROW, acc.shape[1]
    return pl.pallas_call(
        functools.partial(attend_last_body, pair),
        in_specs=[SMEM] + [VMEM] * 10,
        out_specs=[VMEM] * 2,
        out_shape=[jax.ShapeDtypeStruct((rows, quarter), BF16)] * 2,
        compiler_params=limits(16),
        cost_estimate=cost(16 * rows * rows * quarter, 24 * rows * quarter, 16 * rows * rows),
        name="attend_last",
    )(doc_lengths, streams, theirs, swap, *olds, acc, top, below)


def assemble_body(*refs):
    place = spot()[2]
    *pieces, out_ref = refs
    turns = len(pieces) // ROW
    lanes = pieces[0].shape[1]
    for n, piece in enumerate(pieces):
        maker = place ^ (n % ROW)
        which = 2 * (maker & 1) + lax.shift_right_logical(maker, 1)
        out_ref[:, lanes_from(which * turns + n // ROW, lanes)] = piece[...]


def assemble(pieces):
    rows, lanes = pieces[0].shape
    return pl.pallas_call(
        assemble_body,
        in_specs=[VMEM] * len(pieces),
        out_specs=VMEM,
        out_shape=jax.ShapeDtypeStruct((rows, len(pieces) * lanes), BF16),
        compiler_params=limits(6),
        cost_estimate=cost(0, 4 * rows * lanes * len(pieces)),
        name="assemble",
    )(*pieces)


def on_device(hyena_qkv, short_weight, filter_rate, filter_residue, attn_qkv, doc_lengths):
    rows = attn_qkv.shape[0]
    inner = hyena_qkv.transpose(1, 0, 2)
    streams = attn_qkv.transpose(1, 0, 2)
    rates, residues = filter_rate.T, filter_residue.T
    theirs, edge = front(streams, inner)

    theirs = flip(theirs, "ctx", 1)
    edges = (next_block(edge, "ctx", 0), next_block(edge, "ctx", 1))
    own, cross = pack(streams, theirs, 1, 2)
    cross = ahead(cross, "ctx", ROW, 2)
    own = ahead(own, "ctx", ROW)
    (swap,) = pack(streams, theirs, 0, 1)
    swap = flip(swap, "ctx", 2)
    olds = (
        ahead(cross, "ctx", ROW, 0, ROW, 0),
        ahead(odd(own, 0), "ctx", ROW, 0, ROW, 0),
        ahead(own, "ctx", ROW, 0, ROW, 1),
        ahead(odd(cross, 1), "ctx", ROW, 0, ROW, 1),
    )

    mixed, keep, away, wide, gain = hyena_ends(inner, edges, short_weight, rates, residues)
    near, query, high, low = hyena_near(inner, edges, short_weight, mixed, rates, residues)
    keep, back = scan_states(keep, away, wide, gain, rows)
    hyena_out = hyena_finish(near, query, high, low, keep, back)

    acc, top, below = attend(doc_lengths, streams, theirs, swap, own, cross)
    last = lambda pair: attend_last(pair, doc_lengths, streams, theirs, swap, olds, acc, top, below)
    far2, far3 = last((2, 3))
    far2 = flip(far2, "ctx", 2)
    far3 = flip(far3, "ctx", 3)
    kept, near1 = last((0, 1))
    near1 = flip(near1, "ctx", 1)
    attn_out = assemble([kept, near1, far2, far3])
    return (hyena_out, attn_out)


def solution(mesh):
    in_specs = (
        P(("group", "ctx"), None, None),
        P(),
        P(),
        P(),
        P(("group", "ctx"), None, None),
        P("group"),
    )
    out_specs = (P(("group", "ctx"), None), P(("group", "ctx"), None))
    return jax.shard_map(on_device, mesh=mesh, in_specs=in_specs, out_specs=out_specs, check_vma=False)
```

```python
import functools
import math

import jax
import jax.numpy as jnp
from jax import lax
from jax.experimental import pallas as pl
from jax.experimental.pallas import tpu as pltpu
from jax.sharding import PartitionSpec as P


HEAD = 128
LANES = 128
EDGE = 8
ROW = 4


F32 = jnp.float32
BF16 = jnp.bfloat16


def flip(value, axis, bit):
    count = lax.axis_size(axis)
    return lax.ppermute(value, axis, [(at, at ^ bit) for at in range(count)])


def side_of(at):
    return at // 2 % 2


def ahead(value, axis, steps, bit=0, first=0, side=None):
    count = lax.axis_size(axis)
    pairs = [
        (at, (at + steps) ^ bit)
        for at in range(first, count - steps)
        if side is None or side_of(at) == side
    ]
    return lax.ppermute(value, axis, pairs)


def to_side_0(value, axis):
    count = lax.axis_size(axis)
    return lax.ppermute(value, axis, [(at, at ^ 2) for at in range(count) if side_of(at)])


def spot():
    index = lax.axis_index("ctx")
    return index & 1, lax.shift_right_logical(index, 1) & 1, index & (ROW - 1), index // ROW


ALL_VMEM = 67043328


def limits(mib):
    return pltpu.CompilerParams(vmem_limit_bytes=mib << 20)


def cost(flops, moved, exps=0):
    return pl.CostEstimate(flops=flops, bytes_accessed=moved, transcendentals=exps)


VMEM = pl.BlockSpec(memory_space=pltpu.VMEM)
SMEM = pl.BlockSpec(memory_space=pltpu.SMEM)
ANY = pl.BlockSpec(memory_space=pl.ANY)
HBM = pl.BlockSpec(memory_space=pltpu.HBM)


def same_filter(modes, width, terms, lanes):
    row_at = lax.broadcasted_iota(jnp.int32, (terms, lanes), 0)
    lane_at = lax.broadcasted_iota(jnp.int32, (terms, lanes), 1)
    kept = None
    for g in range(terms // modes):
        both = (
            (row_at >= g * modes)
            & (row_at < (g + 1) * modes)
            & (lane_at >= g * width)
            & (lane_at < (g + 1) * width)
        )
        kept = both if kept is None else kept | both
    return kept


def feature(x, halo, w_ref, stream, at):
    here = x.astype(F32)
    halo = halo.astype(F32)
    edge = halo.shape[0]
    row_at = lax.broadcasted_iota(jnp.int32, here.shape, 0)
    one = jnp.where(row_at == 0, halo[edge - 1 :], pltpu.roll(here, 1, 0))
    two = jnp.where(row_at == 1, halo[edge - 1 :], pltpu.roll(here, 2, 0))
    two = jnp.where(row_at == 0, halo[edge - 2 : edge - 1], two)
    tap = [w_ref[n, stream : stream + 1, at] for n in range(3)]
    return tap[0] * here + tap[1] * one + tap[2] * two


def of_step(table_ref):
    groups = table_ref.shape[1]
    return pltpu.roll(table_ref[...], groups - pl.program_id(0) * (groups // STEPS), 1)


def down(table, part, filters, lanes):
    columns = [table[:, part * filters + g : part * filters + g + 1] for g in range(filters)]
    return jnp.concatenate([jnp.broadcast_to(c, (c.shape[0], lanes)) for c in columns], axis=0)


def hyena_ends_body(
    filters, x_ref, halo_ref, w_ref, rate_ref, res_ref, mixed_ref, keep_ref, away_ref, wide_ref, gain_ref, all_s
):
    rows = x_ref.shape[1]
    modes, groups = rate_ref.shape
    parts = groups // STEPS // filters
    terms = filters * modes
    lanes = x_ref.shape[2] // parts
    width = lanes // filters
    rates = of_step(rate_ref)
    coeffs = of_step(res_ref) * jnp.sqrt(2.0 * rates / modes)
    lag = (rows - 1 - lax.broadcasted_iota(jnp.int32, (terms, rows), 1)).astype(F32)
    own = same_filter(modes, width, terms, lanes)
    pick = lambda matrix: jnp.sum(jnp.where(own, matrix, 0.0).reshape(filters, modes, lanes), axis=0)
    step = pl.program_id(0)
    for part in range(parts):
        at = slice(part * lanes, (part + 1) * lanes)
        key, value = (feature(x_ref[n, :, at], halo_ref[n, :, at], w_ref, n, at) for n in (1, 2))
        mixed = (key * value).astype(BF16)
        mixed_ref[:, at] = mixed
        rate = down(rates, part, filters, rows)
        powers = jnp.exp(-rate * lag)
        high = powers.astype(BF16)
        low = (powers - high.astype(F32)).astype(BF16)
        ends = jnp.dot(high, mixed, preferred_element_type=F32) + jnp.dot(
            low, mixed, preferred_element_type=F32
        )
        all_s[0, step, :, at] = pick(ends)
        all_s[1, step, :, at] = pick(rate)
        all_s[2, step, :, at] = pick(down(coeffs, part, filters, rows))

    @pl.when(step == STEPS - 1)
    def _():
        core = spot()[0]
        half = STEPS // 2
        for n in range(half):
            at = slice(n * parts * lanes, (n + 1) * parts * lanes)
            away_ref[:, at] = all_s[0, (1 - core) * half + n]
            for table, out in enumerate((keep_ref, wide_ref, gain_ref)):
                out[:, at] = all_s[table, core * half + n]


STEPS = 4


def hyena_ends(streams, halo, short_weight, rates, residues):
    _, rows, channels = streams.shape
    edge = halo.shape[1]
    modes, groups = rates.shape
    filters = groups * LANES // channels
    terms = filters * modes
    wide = channels // STEPS
    lead = lambda n: (0, 0, n)
    whole = lambda n: (0, 0)
    half = (modes, channels // 2)
    return pl.pallas_call(
        functools.partial(hyena_ends_body, filters),
        grid=(STEPS,),
        in_specs=[
            pl.BlockSpec((3, rows, wide), lead),
            pl.BlockSpec((3, edge, wide), lead),
            pl.BlockSpec((3, 3, wide), lead),
            pl.BlockSpec((modes, groups), whole),
            pl.BlockSpec((modes, groups), whole),
        ],
        out_specs=[pl.BlockSpec((rows, wide), lambda n: (0, n))] + [pl.BlockSpec(half, whole)] * 4,
        out_shape=[jax.ShapeDtypeStruct((rows, channels), BF16)] + [jax.ShapeDtypeStruct(half, F32)] * 4,
        scratch_shapes=[pltpu.VMEM((3, STEPS, modes, wide), F32)],
        compiler_params=limits(16),
        cost_estimate=cost(4 * rows * terms * channels, 8 * rows * channels),
        name="hyena_ends",
    )(streams, halo, short_weight, rates, residues)


def hyena_near_body(
    filters, x_ref, halo_ref, w_ref, mixed_ref, rate_ref, res_ref, near_ref, q_ref, high_ref, low_ref, taps_s, u_s
):
    rows = mixed_ref.shape[0]
    modes, groups = rate_ref.shape
    parts = groups // STEPS // filters
    terms = filters * modes
    lanes = mixed_ref.shape[1] // parts
    width = lanes // filters
    rates = of_step(rate_ref)
    coeffs = of_step(res_ref) * jnp.sqrt(2.0 * rates / modes)
    row_at = lax.broadcasted_iota(jnp.int32, (rows, lanes), 0)
    lane_at = lax.broadcasted_iota(jnp.int32, (rows, lanes), 1)
    lag = (rows - 1 - lax.broadcasted_iota(jnp.int32, (terms, rows), 1)).astype(F32)
    ahead_lag = (1 + lax.broadcasted_iota(jnp.int32, (terms, rows), 1)).astype(F32)
    zero = jnp.zeros((rows, lanes), BF16)
    for part in range(parts):
        at = slice(part * lanes, (part + 1) * lanes)
        mixed = mixed_ref[:, at]
        rate = down(rates, part, filters, rows)
        powers = down(coeffs, part, filters, rows) * jnp.exp(-rate * lag)
        backward = jnp.sum(powers.reshape(filters, modes, rows), axis=1)
        for g in range(filters):
            spread = jnp.broadcast_to(backward[g : g + 1], (rows, rows))
            shifted = pltpu.roll(spread, 1, 1, stride=1, stride_axis=0)
            kept = jnp.where(lane_at <= row_at, shifted, 0.0)
            taps_s[part, :, g * rows : (g + 1) * rows] = kept.astype(BF16)
            mine = (lane_at >= g * width) & (lane_at < (g + 1) * width)
            u_s[part, g * rows : (g + 1) * rows, :] = jnp.where(mine, mixed, zero)
        near_ref[:, at] = jnp.dot(taps_s[part], u_s[part], preferred_element_type=F32)
        q_ref[:, at] = feature(x_ref[0, :, at], halo_ref[0, :, at], w_ref, 0, at)
        decays = jnp.exp(-rate * ahead_lag).T
        here = slice(part * terms, (part + 1) * terms)
        high = decays.astype(BF16)
        high_ref[:, here] = high
        low_ref[:, here] = (decays - high.astype(F32)).astype(BF16)


def hyena_near(streams, halo, short_weight, mixed, rates, residues):
    rows, channels = mixed.shape
    edge = halo.shape[1]
    modes, groups = rates.shape
    lanes = LANES
    filters = groups * lanes // channels
    terms = filters * modes
    parts = groups // STEPS // filters
    wide = channels // STEPS
    by_block = lambda n: (0, n)
    lead = lambda n: (0, 0, n)
    whole = lambda n: (0, 0)
    return pl.pallas_call(
        functools.partial(hyena_near_body, filters),
        grid=(STEPS,),
        in_specs=[
            pl.BlockSpec((1, rows, wide), lead),
            pl.BlockSpec((1, edge, wide), lead),
            pl.BlockSpec((3, 3, wide), lead),
            pl.BlockSpec((rows, wide), by_block),
            pl.BlockSpec((modes, groups), whole),
            pl.BlockSpec((modes, groups), whole),
        ],
        out_specs=[pl.BlockSpec((rows, wide), by_block)] * 2 + [pl.BlockSpec((rows, parts * terms), by_block)] * 2,
        out_shape=[jax.ShapeDtypeStruct((rows, channels), F32)] * 2
        + [jax.ShapeDtypeStruct((rows, groups * modes), BF16)] * 2,
        scratch_shapes=[
            pltpu.VMEM((parts, rows, filters * rows), BF16),
            pltpu.VMEM((parts, filters * rows, lanes), BF16),
        ],
        compiler_params=limits(16),
        cost_estimate=cost(2 * rows * rows * filters * channels, 12 * rows * channels),
        name="hyena_near",
    )(streams, halo, short_weight, mixed, rates, residues)


def hyena_out_body(modes, near_ref, q_ref, high_ref, low_ref, keep_ref, back_ref, out_ref):
    wide = near_ref.shape[1]
    terms = high_ref.shape[1] * LANES // wide
    filters = terms // modes
    own = same_filter(modes, LANES // filters, terms, LANES)
    mine = pl.program_id(0) // (STEPS // 2) == spot()[0]
    for part in range(wide // LANES):
        at = slice(part * LANES, (part + 1) * LANES)
        here = slice(part * terms, (part + 1) * terms)
        carried = jnp.where(mine, keep_ref[:, at], back_ref[:, at])
        carried = jnp.where(own, jnp.concatenate([carried] * filters, axis=0), 0.0)
        c_high = carried.astype(BF16)
        c_low = (carried - c_high.astype(F32)).astype(BF16)
        high, low = high_ref[:, here], low_ref[:, here]
        far = (
            jnp.dot(high, c_high, preferred_element_type=F32)
            + jnp.dot(low, c_high, preferred_element_type=F32)
            + jnp.dot(high, c_low, preferred_element_type=F32)
        )
        out_ref[:, at] = (q_ref[:, at] * (near_ref[:, at] + far)).astype(BF16)


def hyena_finish(near, query, high, low, keep, back):
    rows, channels = near.shape
    modes = keep.shape[0]
    wide = channels // STEPS
    by_block = lambda n: (0, n)
    by_half = lambda n: (0, n % (STEPS // 2))
    return pl.pallas_call(
        functools.partial(hyena_out_body, modes),
        grid=(STEPS,),
        in_specs=[
            pl.BlockSpec((rows, wide), by_block),
            pl.BlockSpec((rows, wide), by_block),
            pl.BlockSpec((rows, high.shape[1] // STEPS), by_block),
            pl.BlockSpec((rows, high.shape[1] // STEPS), by_block),
            pl.BlockSpec((modes, wide), by_half),
            pl.BlockSpec((modes, wide), by_half),
        ],
        out_specs=pl.BlockSpec((rows, wide), by_block),
        out_shape=jax.ShapeDtypeStruct((rows, channels), BF16),
        compiler_params=limits(16),
        cost_estimate=cost(6 * rows * high.size, 10 * rows * channels),
        name="hyena_finish",
    )(near, query, high, low, keep, back)


def small(body, *operands, outs=1):
    def kernel(*refs):
        made = body(*(ref[...] for ref in refs[: len(operands)]))
        for ref, value in zip(refs[len(operands) :], made if outs > 1 else (made,)):
            ref[...] = value

    shape = pltpu.VMEM(operands[0].shape, operands[0].dtype)
    made = pl.pallas_call(
        kernel,
        in_specs=[VMEM] * len(operands),
        out_specs=[VMEM] * outs,
        out_shape=[shape] * outs,
        compiler_params=limits(4),
        cost_estimate=cost(operands[0].size, 4 * operands[0].size),
    )(*operands)
    return made if outs > 1 else made[0]


def scan_states(keep, away, rate, gain, rows):
    count = lax.axis_size("ctx") // ROW
    decay = lambda blocks, rate: jnp.exp(-rate * float(rows * blocks))

    def both(mine, theirs, rate):
        first = spot()[0] == 0
        even = jnp.where(first, mine, theirs)
        return decay(1, rate) * even + jnp.where(first, theirs, mine), even

    theirs = flip(away, "ctx", 1)
    chip, even = small(both, keep, theirs, rate, outs=2)

    def whole(mine, other, rate):
        first = spot()[1] == 0
        left = jnp.where(first, mine, other)
        return decay(2, rate) * left + jnp.where(first, other, mine), left

    other = flip(chip, "ctx", 2)
    total, left = small(whole, chip, other, rate, outs=2)
    direct = ahead(total, "ctx", ROW, 0, 0, 1)
    handed = to_side_0(direct, "ctx")
    before = small(lambda one, other: one + other, direct, handed)
    reach = 2
    while reach < count:
        upto = small(lambda total, before, rate: total + decay(ROW, rate) * before, total, before, rate)
        earlier = ahead(upto, "ctx", ROW * reach)
        reach *= 2
        if reach < count:
            before = small(
                lambda before, earlier, rate: before + decay(ROW * (reach // 2 - 1), rate) * earlier,
                before,
                earlier,
                rate,
            )

    def last(before, earlier, left, even, rate, gain):
        before = before + decay(ROW * (reach // 2 - 1), rate) * earlier
        core, side, _, _ = spot()
        before = jnp.where(side == 0, before, decay(2, rate) * before + left)
        second = decay(1, rate) * before + even
        return (
            gain * jnp.where(core == 0, before, second),
            gain * jnp.where(core == 0, second, before),
        )

    if count == 2:
        earlier = jnp.zeros_like(before)
    if count > 1:
        mine, away = small(last, before, earlier, left, even, rate, gain, outs=2)
    return mine, flip(away, "ctx", 1)


def lanes_from(start, size):
    return pl.ds(pl.multiple_of(start * size, size), size)


def front_body(attn, hyena, theirs_ref, edge_ref, sems):
    rows, half = theirs_ref.shape[1:]
    away = attn.at[:, :, lanes_from(1 - spot()[0], half)]
    edge = hyena.at[:, rows - EDGE : rows, :]
    copies = [
        pltpu.make_async_copy(away, theirs_ref, sems.at[0]),
        pltpu.make_async_copy(edge, edge_ref, sems.at[1]),
    ]
    for copy in copies:
        copy.start()
    for copy in copies:
        copy.wait()


def front(attn, hyena):
    count, rows, channels = attn.shape
    return pl.pallas_call(
        front_body,
        in_specs=[HBM, HBM],
        out_specs=[VMEM, VMEM],
        out_shape=[
            pltpu.VMEM((count, rows, channels // 2), attn.dtype),
            pltpu.VMEM((count, EDGE, channels), hyena.dtype),
        ],
        scratch_shapes=[pltpu.SemaphoreType.DMA((2,))],
        compiler_params=pltpu.CompilerParams(vmem_limit_bytes=ALL_VMEM - (26 << 17)),
        cost_estimate=cost(0, 4 * count * rows * channels // 2),
        name="front",
    )(attn, hyena)


def pack_body(first, streams_ref, theirs_ref, *outs):
    core, side, _, _ = spot()
    slots = (0, 1) if first == 0 else (1 - core, core)
    quarter = theirs_ref.shape[2] // 2
    for out, away in zip(outs, (0, 1)[-len(outs) :]):
        to = 1 - side if away else side
        for stream in range(first, 3):
            out[slots[0], stream - first] = streams_ref[stream, :, lanes_from(2 * core + to, quarter)]
            out[slots[1], stream - first] = theirs_ref[stream, :, lanes_from(to, quarter)]


def pack(streams, theirs, first, amount):
    _, rows, half = theirs.shape
    shape = pltpu.VMEM((2, 3 - first, rows, half // 2), BF16)
    return pl.pallas_call(
        functools.partial(pack_body, first),
        in_specs=[VMEM, VMEM],
        out_specs=[VMEM] * amount,
        out_shape=[shape] * amount,
        compiler_params=limits(10),
        cost_estimate=cost(0, 8 * amount * rows * half),
        name="pack",
    )(streams, theirs)


def odd_body(wanted, pairs, out_ref, sem):
    @pl.when(spot()[1] == wanted)
    def _():
        copy = pltpu.make_async_copy(pairs.at[0:1], out_ref, sem)
        copy.start()
        copy.wait()


def odd(pairs, wanted):
    return pl.pallas_call(
        functools.partial(odd_body, wanted),
        in_specs=[ANY],
        out_specs=VMEM,
        out_shape=pltpu.VMEM((1,) + pairs.shape[1:], pairs.dtype),
        scratch_shapes=[pltpu.SemaphoreType.DMA],
        compiler_params=limits(4),
        cost_estimate=cost(0, pairs.size * 2),
        name="odd",
    )(pairs)


def contig_start(docs_ref, position):
    first = jnp.zeros_like(position)
    bound = jnp.int32(0)
    for n in range(docs_ref.shape[0]):
        bound = bound + docs_ref[n]
        first = jnp.where(position >= bound, bound, first)
    return first


def row_part(streams, theirs, swap, slot, stream, head, quarter):
    core, side, _, _ = spot()
    if slot < 2:
        start = (side if slot else 2 * core + side) * quarter + head * HEAD
        lanes = pl.ds(pl.multiple_of(start, HEAD), HEAD)
        return theirs[stream, :, lanes] if slot else streams[stream, :, lanes]
    return swap[slot - 2, stream, :, head * HEAD : (head + 1) * HEAD]


SCALE = math.log2(math.e) / math.sqrt(HEAD)


CHUNK = 32


def softmax_group(queries, keys, values, bias, turn, s_s, p_s, keep):
    tall, rows = queries.shape[0], keys[0].shape[0]
    width = len(keys) * rows
    for n in range(0, len(keys), 2):
        s_s[turn, 0:tall, n * rows : (n + 2) * rows] = lax.dot_general(
            queries,
            jnp.concatenate(keys[n : n + 2], axis=0),
            (((1,), (1,)), ((), ())),
            preferred_element_type=F32,
        )
    for m in range(0, tall, CHUNK):
        some = slice(m, m + CHUNK)
        top = None
        parts = []
        for n in range(0, width, LANES):
            part = s_s[turn, some, n : n + LANES] + bias[some, n : n + LANES]
            parts.append(part)
            top = part if top is None else jnp.maximum(top, part)
        top = jnp.broadcast_to(jnp.max(top, axis=1, keepdims=True), (CHUNK, LANES))
        below = jnp.zeros((CHUNK, LANES), F32)
        for n, part in enumerate(parts):
            weight = jnp.exp2((part - top) * SCALE)
            below = below + weight
            p_s[turn, some, n * LANES : (n + 1) * LANES] = weight.astype(BF16)
        keep(m, top, jnp.broadcast_to(jnp.sum(below, axis=1, keepdims=True), (CHUNK, LANES)))
    return jnp.dot(
        p_s[turn, 0:tall, 0:width], jnp.concatenate(values, axis=0), preferred_element_type=F32
    )


def attend_body(docs_ref, streams, theirs, swap, own, cross, acc_ref, m_ref, l_ref, bias_s, s_s, p_s):
    _, side, place, row = spot()
    rows, quarter = own.shape[2:]
    base = row * (ROW * rows)
    part = functools.partial(row_part, streams, theirs, swap, quarter=quarter)

    def run(first_pair, second_pair):
        for group, (asking, seen) in enumerate(((first_pair, first_pair), (second_pair, (0, 1, 2, 3)))):
            starts = [base + (2 * (side if old else 1 - side) + 1 - n - ROW) * rows for old in (1, 0) for n in (0, 1)]
            starts += [base + (place ^ slot) * rows for slot in seen]
            for at, slot in enumerate(asking):
                position = base + (place ^ slot) * rows + lax.broadcasted_iota(jnp.int32, (rows, 1), 0)
                first = contig_start(docs_ref, position)
                for n, start in enumerate(starts):
                    token = start + lax.broadcasted_iota(jnp.int32, (rows, rows), 1)
                    bias_s[group, at * rows : (at + 1) * rows, n * rows : (n + 1) * rows] = jnp.where(
                        (token >= first) & (token <= position), 0.0, -jnp.inf
                    )
            for head in range(quarter // HEAD):
                lanes = slice(head * HEAD, (head + 1) * HEAD)
                olds = lambda kind: [old[n, kind, :, lanes] for old in (own, cross) for n in (0, 1)]

                def keep(m, top, below):
                    out = slice(asking[0] * rows + m, asking[0] * rows + m + CHUNK)
                    m_ref[out, lanes] = top
                    l_ref[out, lanes] = below

                acc_ref[asking[0] * rows : (asking[1] + 1) * rows, lanes] = softmax_group(
                    jnp.concatenate([part(slot, 0, head) for slot in asking], axis=0),
                    olds(0) + [part(slot, 1, head) for slot in seen],
                    olds(1) + [part(slot, 2, head) for slot in seen],
                    bias_s.at[group],
                    head % 2,
                    s_s,
                    p_s,
                    keep,
                )

    @pl.when(side == 0)
    def _():
        run((0, 1), (2, 3))

    @pl.when(side == 1)
    def _():
        run((2, 3), (0, 1))


def attend(doc_lengths, streams, theirs, swap, own, cross):
    _, _, rows, quarter = own.shape
    heads = quarter // HEAD
    return pl.pallas_call(
        attend_body,
        in_specs=[SMEM] + [VMEM] * 5,
        out_specs=[VMEM] * 3,
        out_shape=[
            jax.ShapeDtypeStruct((ROW * rows, quarter), F32),
        ]
        * 3,
        scratch_shapes=[
            pltpu.VMEM((2, 2 * rows, 2 * ROW * rows), F32),
            pltpu.VMEM((2, 2 * rows, 2 * ROW * rows), F32),
            pltpu.VMEM((2, 2 * rows, 2 * ROW * rows), BF16),
        ],
        compiler_params=limits(20),
        cost_estimate=cost(26 * 4 * rows * rows * quarter, 14 * ROW * rows * quarter, 26 * heads * rows * rows),
        name="attend",
    )(doc_lengths, streams, theirs, swap, own, cross)


def attend_last_body(pair, docs_ref, streams, theirs, swap, *refs):
    cross_l, own_s, own_l, cross_s, acc_ref, m_ref, l_ref = refs[:7]
    outs = refs[7:]
    _, side, place, row = spot()
    rows, quarter = acc_ref.shape[0] // ROW, acc_ref.shape[1]
    base = row * (ROW * rows)
    heads = range(quarter // HEAD)

    def run(early, late, large, small):
        for asking, blocks in ((early, ((small, 0), (large, 1), (large, 0))), (late, ((large, 0),))):
            if asking != pair:
                continue
            width = len(blocks) * rows
            here = slice(asking[0] * rows, (asking[1] + 1) * rows)
            token = base - (ROW + len(blocks)) * rows + lax.broadcasted_iota(jnp.int32, (rows, width), 1)
            allowed = []
            for slot in asking:
                position = base + (place ^ slot) * rows + lax.broadcasted_iota(jnp.int32, (rows, 1), 0)
                allowed.append((token >= contig_start(docs_ref, position)).astype(jnp.int32))
            allowed = jnp.concatenate(allowed, axis=0) != 0
            lanes_of = [slice(head * HEAD, (head + 1) * HEAD) for head in heads]
            stack = lambda kind, lanes: jnp.concatenate([ref[n, kind, :, lanes] for ref, n in blocks], axis=0)
            scores = [
                lax.dot_general(
                    jnp.concatenate(
                        [row_part(streams, theirs, swap, slot, 0, head, quarter) for slot in asking], axis=0
                    ),
                    stack(0, lanes_of[head]),
                    (((1,), (1,)), ((), ())),
                    preferred_element_type=F32,
                )
                for head in heads
            ]
            scores = [jnp.where(allowed, score, -jnp.inf) for score in scores]
            tops = [
                jnp.maximum(m_ref[here, lanes], jnp.max(score, axis=1, keepdims=True))
                for lanes, score in zip(lanes_of, scores)
            ]
            weights = [
                jnp.exp2((score - jnp.concatenate([top] * len(blocks), axis=1)) * SCALE)
                for score, top in zip(scores, tops)
            ]
            for lanes, top, weight in zip(lanes_of, tops, weights):
                fade = jnp.exp2((m_ref[here, lanes] - top) * SCALE)
                share = 1.0 / (l_ref[here, lanes] * fade + jnp.sum(weight, axis=1, keepdims=True))
                more = jnp.dot(weight.astype(BF16), stack(1, lanes), preferred_element_type=F32)
                made = ((acc_ref[here, lanes] * fade + more) * share).astype(BF16)
                for n, out in enumerate(outs):
                    out[:, lanes] = made[n * rows : (n + 1) * rows]

    @pl.when(side == 0)
    def _():
        run((0, 1), (2, 3), cross_l, own_s)

    @pl.when(side == 1)
    def _():
        run((2, 3), (0, 1), own_l, cross_s)


def attend_last(pair, doc_lengths, streams, theirs, swap, olds, acc, top, below):
    rows, quarter = acc.shape[0] // ROW, acc.shape[1]
    return pl.pallas_call(
        functools.partial(attend_last_body, pair),
        in_specs=[SMEM] + [VMEM] * 10,
        out_specs=[VMEM] * 2,
        out_shape=[jax.ShapeDtypeStruct((rows, quarter), BF16)] * 2,
        compiler_params=limits(16),
        cost_estimate=cost(16 * rows * rows * quarter, 24 * rows * quarter, 16 * rows * rows),
        name="attend_last",
    )(doc_lengths, streams, theirs, swap, *olds, acc, top, below)


def assemble_body(*refs):
    place = spot()[2]
    *pieces, out_ref = refs
    turns = len(pieces) // ROW
    lanes = pieces[0].shape[1]
    for n, piece in enumerate(pieces):
        maker = place ^ (n % ROW)
        which = 2 * (maker & 1) + lax.shift_right_logical(maker, 1)
        out_ref[:, lanes_from(which * turns + n // ROW, lanes)] = piece[...]


def assemble(pieces):
    rows, lanes = pieces[0].shape
    return pl.pallas_call(
        assemble_body,
        in_specs=[VMEM] * len(pieces),
        out_specs=VMEM,
        out_shape=jax.ShapeDtypeStruct((rows, len(pieces) * lanes), BF16),
        compiler_params=limits(6),
        cost_estimate=cost(0, 4 * rows * lanes * len(pieces)),
        name="assemble",
    )(*pieces)


def on_device(hyena_qkv, short_weight, filter_rate, filter_residue, attn_qkv, doc_lengths):
    rows = attn_qkv.shape[0]
    inner = hyena_qkv.transpose(1, 0, 2)
    streams = attn_qkv.transpose(1, 0, 2)
    rates, residues = filter_rate.T, filter_residue.T
    theirs, edge = front(streams, inner)

    theirs = flip(theirs, "ctx", 1)
    edge = ahead(edge, "ctx", 1)
    own, cross = pack(streams, theirs, 1, 2)
    cross = ahead(cross, "ctx", ROW, 2)
    own = ahead(own, "ctx", ROW)
    (swap,) = pack(streams, theirs, 0, 1)
    swap = flip(swap, "ctx", 2)
    olds = (
        ahead(cross, "ctx", ROW, 0, ROW, 0),
        ahead(odd(own, 0), "ctx", ROW, 0, ROW, 0),
        ahead(own, "ctx", ROW, 0, ROW, 1),
        ahead(odd(cross, 1), "ctx", ROW, 0, ROW, 1),
    )

    mixed, keep, away, wide, gain = hyena_ends(inner, edge, short_weight, rates, residues)
    near, query, high, low = hyena_near(inner, edge, short_weight, mixed, rates, residues)
    keep, back = scan_states(keep, away, wide, gain, rows)
    hyena_out = hyena_finish(near, query, high, low, keep, back)

    acc, top, below = attend(doc_lengths, streams, theirs, swap, own, cross)
    last = lambda pair: attend_last(pair, doc_lengths, streams, theirs, swap, olds, acc, top, below)
    far2, far3 = last((2, 3))
    far2 = flip(far2, "ctx", 2)
    far3 = flip(far3, "ctx", 3)
    kept, near1 = last((0, 1))
    near1 = flip(near1, "ctx", 1)
    attn_out = assemble([kept, near1, far2, far3])
    return (hyena_out, attn_out)


def solution(mesh):
    in_specs = (
        P(("group", "ctx"), None, None),
        P(),
        P(),
        P(),
        P(("group", "ctx"), None, None),
        P("group"),
    )
    out_specs = (P(("group", "ctx"), None), P(("group", "ctx"), None))
    return jax.shard_map(on_device, mesh=mesh, in_specs=in_specs, out_specs=out_specs, check_vma=False)
```

```python
import functools
import math

import jax
import jax.numpy as jnp
from jax import lax
from jax.experimental import pallas as pl
from jax.experimental.pallas import tpu as pltpu
from jax.sharding import PartitionSpec as P


HEAD = 128
LANES = 128
EDGE = 8
ROW = 4


F32 = jnp.float32
BF16 = jnp.bfloat16


def flip(value, axis, bit):
    count = lax.axis_size(axis)
    return lax.ppermute(value, axis, [(at, at ^ bit) for at in range(count)])


def side_of(at):
    return at // 2 % 2


def ahead(value, axis, steps, bit=0, first=0, side=None):
    count = lax.axis_size(axis)
    pairs = [
        (at, (at + steps) ^ bit)
        for at in range(first, count - steps)
        if side is None or side_of(at) == side
    ]
    return lax.ppermute(value, axis, pairs)


def to_side_0(value, axis):
    count = lax.axis_size(axis)
    return lax.ppermute(value, axis, [(at, at ^ 2) for at in range(count) if side_of(at)])


def spot():
    index = lax.axis_index("ctx")
    return index & 1, lax.shift_right_logical(index, 1) & 1, index & (ROW - 1), index // ROW


ALL_VMEM = 67043328


def limits(mib):
    return pltpu.CompilerParams(vmem_limit_bytes=mib << 20)


def cost(flops, moved, exps=0):
    return pl.CostEstimate(flops=flops, bytes_accessed=moved, transcendentals=exps)


VMEM = pl.BlockSpec(memory_space=pltpu.VMEM)
SMEM = pl.BlockSpec(memory_space=pltpu.SMEM)
ANY = pl.BlockSpec(memory_space=pl.ANY)
HBM = pl.BlockSpec(memory_space=pltpu.HBM)


def same_filter(modes, width, terms, lanes):
    row_at = lax.broadcasted_iota(jnp.int32, (terms, lanes), 0)
    lane_at = lax.broadcasted_iota(jnp.int32, (terms, lanes), 1)
    kept = None
    for g in range(terms // modes):
        both = (
            (row_at >= g * modes)
            & (row_at < (g + 1) * modes)
            & (lane_at >= g * width)
            & (lane_at < (g + 1) * width)
        )
        kept = both if kept is None else kept | both
    return kept


def feature(x, halo, w_ref, stream, at):
    here = x.astype(F32)
    halo = halo.astype(F32)
    edge = halo.shape[0]
    row_at = lax.broadcasted_iota(jnp.int32, here.shape, 0)
    one = jnp.where(row_at == 0, halo[edge - 1 :], pltpu.roll(here, 1, 0))
    two = jnp.where(row_at == 1, halo[edge - 1 :], pltpu.roll(here, 2, 0))
    two = jnp.where(row_at == 0, halo[edge - 2 : edge - 1], two)
    tap = [w_ref[n, stream : stream + 1, at] for n in range(3)]
    return tap[0] * here + tap[1] * one + tap[2] * two


def of_step(table_ref):
    groups = table_ref.shape[1]
    return pltpu.roll(table_ref[...], groups - pl.program_id(0) * (groups // STEPS), 1)


def down(table, part, filters, lanes):
    columns = [table[:, part * filters + g : part * filters + g + 1] for g in range(filters)]
    return jnp.concatenate([jnp.broadcast_to(c, (c.shape[0], lanes)) for c in columns], axis=0)


def hyena_ends_body(
    filters, x_ref, halo_ref, w_ref, rate_ref, res_ref, mixed_ref, keep_ref, away_ref, wide_ref, gain_ref, all_s
):
    rows = x_ref.shape[1]
    modes, groups = rate_ref.shape
    parts = groups // STEPS // filters
    terms = filters * modes
    lanes = x_ref.shape[2] // parts
    width = lanes // filters
    rates = of_step(rate_ref)
    coeffs = of_step(res_ref) * jnp.sqrt(2.0 * rates / modes)
    lag = (rows - 1 - lax.broadcasted_iota(jnp.int32, (terms, rows), 1)).astype(F32)
    own = same_filter(modes, width, terms, lanes)
    pick = lambda matrix: jnp.sum(jnp.where(own, matrix, 0.0).reshape(filters, modes, lanes), axis=0)
    step = pl.program_id(0)
    for part in range(parts):
        at = slice(part * lanes, (part + 1) * lanes)
        key, value = (feature(x_ref[n, :, at], halo_ref[n, :, at], w_ref, n, at) for n in (1, 2))
        mixed = (key * value).astype(BF16)
        mixed_ref[:, at] = mixed
        rate = down(rates, part, filters, rows)
        powers = jnp.exp(-rate * lag)
        high = powers.astype(BF16)
        low = (powers - high.astype(F32)).astype(BF16)
        ends = jnp.dot(high, mixed, preferred_element_type=F32) + jnp.dot(
            low, mixed, preferred_element_type=F32
        )
        all_s[0, step, :, at] = pick(ends)
        all_s[1, step, :, at] = pick(rate)
        all_s[2, step, :, at] = pick(down(coeffs, part, filters, rows))

    @pl.when(step == STEPS - 1)
    def _():
        core = spot()[0]
        half = STEPS // 2
        for n in range(half):
            at = slice(n * parts * lanes, (n + 1) * parts * lanes)
            away_ref[:, at] = all_s[0, (1 - core) * half + n]
            for table, out in enumerate((keep_ref, wide_ref, gain_ref)):
                out[:, at] = all_s[table, core * half + n]


STEPS = 4


def hyena_ends(streams, halo, short_weight, rates, residues):
    _, rows, channels = streams.shape
    edge = halo.shape[1]
    modes, groups = rates.shape
    filters = groups * LANES // channels
    terms = filters * modes
    wide = channels // STEPS
    lead = lambda n: (0, 0, n)
    whole = lambda n: (0, 0)
    half = (modes, channels // 2)
    return pl.pallas_call(
        functools.partial(hyena_ends_body, filters),
        grid=(STEPS,),
        in_specs=[
            pl.BlockSpec((3, rows, wide), lead),
            pl.BlockSpec((3, edge, wide), lead),
            pl.BlockSpec((3, 3, wide), lead),
            pl.BlockSpec((modes, groups), whole),
            pl.BlockSpec((modes, groups), whole),
        ],
        out_specs=[pl.BlockSpec((rows, wide), lambda n: (0, n))] + [pl.BlockSpec(half, whole)] * 4,
        out_shape=[jax.ShapeDtypeStruct((rows, channels), BF16)] + [jax.ShapeDtypeStruct(half, F32)] * 4,
        scratch_shapes=[pltpu.VMEM((3, STEPS, modes, wide), F32)],
        compiler_params=limits(16),
        cost_estimate=cost(4 * rows * terms * channels, 8 * rows * channels),
        name="hyena_ends",
    )(streams, halo, short_weight, rates, residues)


def hyena_near_body(
    filters, x_ref, halo_ref, w_ref, mixed_ref, rate_ref, res_ref, near_ref, q_ref, high_ref, low_ref, taps_s, u_s
):
    rows = mixed_ref.shape[0]
    modes, groups = rate_ref.shape
    parts = groups // STEPS // filters
    terms = filters * modes
    lanes = mixed_ref.shape[1] // parts
    width = lanes // filters
    rates = of_step(rate_ref)
    coeffs = of_step(res_ref) * jnp.sqrt(2.0 * rates / modes)
    row_at = lax.broadcasted_iota(jnp.int32, (rows, lanes), 0)
    lane_at = lax.broadcasted_iota(jnp.int32, (rows, lanes), 1)
    lag = (rows - 1 - lax.broadcasted_iota(jnp.int32, (terms, rows), 1)).astype(F32)
    ahead_lag = (1 + lax.broadcasted_iota(jnp.int32, (terms, rows), 1)).astype(F32)
    zero = jnp.zeros((rows, lanes), BF16)
    for part in range(parts):
        at = slice(part * lanes, (part + 1) * lanes)
        mixed = mixed_ref[:, at]
        rate = down(rates, part, filters, rows)
        powers = down(coeffs, part, filters, rows) * jnp.exp(-rate * lag)
        backward = jnp.sum(powers.reshape(filters, modes, rows), axis=1)
        for g in range(filters):
            spread = jnp.broadcast_to(backward[g : g + 1], (rows, rows))
            shifted = pltpu.roll(spread, 1, 1, stride=1, stride_axis=0)
            kept = jnp.where(lane_at <= row_at, shifted, 0.0)
            taps_s[part, :, g * rows : (g + 1) * rows] = kept.astype(BF16)
            mine = (lane_at >= g * width) & (lane_at < (g + 1) * width)
            u_s[part, g * rows : (g + 1) * rows, :] = jnp.where(mine, mixed, zero)
        near_ref[:, at] = jnp.dot(taps_s[part], u_s[part], preferred_element_type=F32)
        q_ref[:, at] = feature(x_ref[0, :, at], halo_ref[0, :, at], w_ref, 0, at)
        decays = jnp.exp(-rate * ahead_lag).T
        here = slice(part * terms, (part + 1) * terms)
        high = decays.astype(BF16)
        high_ref[:, here] = high
        low_ref[:, here] = (decays - high.astype(F32)).astype(BF16)


def hyena_near(streams, halo, short_weight, mixed, rates, residues):
    rows, channels = mixed.shape
    edge = halo.shape[1]
    modes, groups = rates.shape
    lanes = LANES
    filters = groups * lanes // channels
    terms = filters * modes
    parts = groups // STEPS // filters
    wide = channels // STEPS
    by_block = lambda n: (0, n)
    lead = lambda n: (0, 0, n)
    whole = lambda n: (0, 0)
    return pl.pallas_call(
        functools.partial(hyena_near_body, filters),
        grid=(STEPS,),
        in_specs=[
            pl.BlockSpec((1, rows, wide), lead),
            pl.BlockSpec((1, edge, wide), lead),
            pl.BlockSpec((3, 3, wide), lead),
            pl.BlockSpec((rows, wide), by_block),
            pl.BlockSpec((modes, groups), whole),
            pl.BlockSpec((modes, groups), whole),
        ],
        out_specs=[pl.BlockSpec((rows, wide), by_block)] * 2 + [pl.BlockSpec((rows, parts * terms), by_block)] * 2,
        out_shape=[jax.ShapeDtypeStruct((rows, channels), F32)] * 2
        + [jax.ShapeDtypeStruct((rows, groups * modes), BF16)] * 2,
        scratch_shapes=[
            pltpu.VMEM((parts, rows, filters * rows), BF16),
            pltpu.VMEM((parts, filters * rows, lanes), BF16),
        ],
        compiler_params=limits(16),
        cost_estimate=cost(2 * rows * rows * filters * channels, 12 * rows * channels),
        name="hyena_near",
    )(streams, halo, short_weight, mixed, rates, residues)


def hyena_out_body(modes, near_ref, q_ref, high_ref, low_ref, keep_ref, back_ref, out_ref):
    wide = near_ref.shape[1]
    terms = high_ref.shape[1] * LANES // wide
    filters = terms // modes
    own = same_filter(modes, LANES // filters, terms, LANES)
    mine = pl.program_id(0) // (STEPS // 2) == spot()[0]
    for part in range(wide // LANES):
        at = slice(part * LANES, (part + 1) * LANES)
        here = slice(part * terms, (part + 1) * terms)
        carried = jnp.where(mine, keep_ref[:, at], back_ref[:, at])
        carried = jnp.where(own, jnp.concatenate([carried] * filters, axis=0), 0.0)
        c_high = carried.astype(BF16)
        c_low = (carried - c_high.astype(F32)).astype(BF16)
        high, low = high_ref[:, here], low_ref[:, here]
        far = (
            jnp.dot(high, c_high, preferred_element_type=F32)
            + jnp.dot(low, c_high, preferred_element_type=F32)
            + jnp.dot(high, c_low, preferred_element_type=F32)
        )
        out_ref[:, at] = (q_ref[:, at] * (near_ref[:, at] + far)).astype(BF16)


def hyena_finish(near, query, high, low, keep, back):
    rows, channels = near.shape
    modes = keep.shape[0]
    wide = channels // STEPS
    by_block = lambda n: (0, n)
    by_half = lambda n: (0, n % (STEPS // 2))
    return pl.pallas_call(
        functools.partial(hyena_out_body, modes),
        grid=(STEPS,),
        in_specs=[
            pl.BlockSpec((rows, wide), by_block),
            pl.BlockSpec((rows, wide), by_block),
            pl.BlockSpec((rows, high.shape[1] // STEPS), by_block),
            pl.BlockSpec((rows, high.shape[1] // STEPS), by_block),
            pl.BlockSpec((modes, wide), by_half),
            pl.BlockSpec((modes, wide), by_half),
        ],
        out_specs=pl.BlockSpec((rows, wide), by_block),
        out_shape=jax.ShapeDtypeStruct((rows, channels), BF16),
        compiler_params=limits(16),
        cost_estimate=cost(6 * rows * high.size, 10 * rows * channels),
        name="hyena_finish",
    )(near, query, high, low, keep, back)


def small(body, *operands, outs=1):
    def kernel(*refs):
        made = body(*(ref[...] for ref in refs[: len(operands)]))
        for ref, value in zip(refs[len(operands) :], made if outs > 1 else (made,)):
            ref[...] = value

    shape = pltpu.VMEM(operands[0].shape, operands[0].dtype)
    made = pl.pallas_call(
        kernel,
        in_specs=[VMEM] * len(operands),
        out_specs=[VMEM] * outs,
        out_shape=[shape] * outs,
        compiler_params=limits(4),
        cost_estimate=cost(operands[0].size, 4 * operands[0].size),
    )(*operands)
    return made if outs > 1 else made[0]


def scan_states(keep, away, rate, gain, rows):
    count = lax.axis_size("ctx") // ROW
    decay = lambda blocks, rate: jnp.exp(-rate * float(rows * blocks))

    def both(mine, theirs, rate):
        first = spot()[0] == 0
        even = jnp.where(first, mine, theirs)
        return decay(1, rate) * even + jnp.where(first, theirs, mine), even

    theirs = flip(away, "ctx", 1)
    chip, even = small(both, keep, theirs, rate, outs=2)

    def whole(mine, other, rate):
        first = spot()[1] == 0
        left = jnp.where(first, mine, other)
        return decay(2, rate) * left + jnp.where(first, other, mine), left

    other = flip(chip, "ctx", 2)
    total, left = small(whole, chip, other, rate, outs=2)
    direct = ahead(total, "ctx", ROW, 0, 0, 1)
    handed = to_side_0(direct, "ctx")
    before = small(lambda one, other: one + other, direct, handed)
    reach = 2
    while reach < count:
        upto = small(lambda total, before, rate: total + decay(ROW, rate) * before, total, before, rate)
        earlier = ahead(upto, "ctx", ROW * reach)
        reach *= 2
        if reach < count:
            before = small(
                lambda before, earlier, rate: before + decay(ROW * (reach // 2 - 1), rate) * earlier,
                before,
                earlier,
                rate,
            )

    def last(before, earlier, left, even, rate, gain):
        before = before + decay(ROW * (reach // 2 - 1), rate) * earlier
        core, side, _, _ = spot()
        before = jnp.where(side == 0, before, decay(2, rate) * before + left)
        second = decay(1, rate) * before + even
        return (
            gain * jnp.where(core == 0, before, second),
            gain * jnp.where(core == 0, second, before),
        )

    if count == 2:
        earlier = jnp.zeros_like(before)
    if count > 1:
        mine, away = small(last, before, earlier, left, even, rate, gain, outs=2)
    return mine, flip(away, "ctx", 1)


def lanes_from(start, size):
    return pl.ds(pl.multiple_of(start * size, size), size)


def front_body(attn, hyena, theirs_ref, edge_ref, sems):
    rows, half = theirs_ref.shape[1:]
    away = attn.at[:, :, lanes_from(1 - spot()[0], half)]
    edge = hyena.at[:, rows - EDGE : rows, :]
    copies = [
        pltpu.make_async_copy(away, theirs_ref, sems.at[0]),
        pltpu.make_async_copy(edge, edge_ref, sems.at[1]),
    ]
    for copy in copies:
        copy.start()
    for copy in copies:
        copy.wait()


def front(attn, hyena):
    count, rows, channels = attn.shape
    return pl.pallas_call(
        front_body,
        in_specs=[HBM, HBM],
        out_specs=[VMEM, VMEM],
        out_shape=[
            pltpu.VMEM((count, rows, channels // 2), attn.dtype),
            pltpu.VMEM((count, EDGE, channels), hyena.dtype),
        ],
        scratch_shapes=[pltpu.SemaphoreType.DMA((2,))],
        compiler_params=pltpu.CompilerParams(vmem_limit_bytes=ALL_VMEM - (26 << 17)),
        cost_estimate=cost(0, 4 * count * rows * channels // 2),
        name="front",
    )(attn, hyena)


def pack_body(first, streams_ref, theirs_ref, *outs):
    core, side, _, _ = spot()
    slots = (0, 1) if first == 0 else (1 - core, core)
    quarter = theirs_ref.shape[2] // 2
    for out, away in zip(outs, (0, 1)[-len(outs) :]):
        to = 1 - side if away else side
        for stream in range(first, 3):
            out[slots[0], stream - first] = streams_ref[stream, :, lanes_from(2 * core + to, quarter)]
            out[slots[1], stream - first] = theirs_ref[stream, :, lanes_from(to, quarter)]


def pack(streams, theirs, first, amount):
    _, rows, half = theirs.shape
    shape = pltpu.VMEM((2, 3 - first, rows, half // 2), BF16)
    return pl.pallas_call(
        functools.partial(pack_body, first),
        in_specs=[VMEM, VMEM],
        out_specs=[VMEM] * amount,
        out_shape=[shape] * amount,
        compiler_params=limits(10),
        cost_estimate=cost(0, 8 * amount * rows * half),
        name="pack",
    )(streams, theirs)


def odd_body(wanted, pairs, out_ref, sem):
    @pl.when(spot()[1] == wanted)
    def _():
        copy = pltpu.make_async_copy(pairs.at[0:1], out_ref, sem)
        copy.start()
        copy.wait()


def odd(pairs, wanted):
    return pl.pallas_call(
        functools.partial(odd_body, wanted),
        in_specs=[ANY],
        out_specs=VMEM,
        out_shape=pltpu.VMEM((1,) + pairs.shape[1:], pairs.dtype),
        scratch_shapes=[pltpu.SemaphoreType.DMA],
        compiler_params=limits(4),
        cost_estimate=cost(0, pairs.size * 2),
        name="odd",
    )(pairs)


def contig_start(docs_ref, position):
    first = jnp.zeros_like(position)
    bound = jnp.int32(0)
    for n in range(docs_ref.shape[0]):
        bound = bound + docs_ref[n]
        first = jnp.where(position >= bound, bound, first)
    return first


def row_part(streams, theirs, swap, slot, stream, head, quarter):
    core, side, _, _ = spot()
    if slot < 2:
        start = (side if slot else 2 * core + side) * quarter + head * HEAD
        lanes = pl.ds(pl.multiple_of(start, HEAD), HEAD)
        return theirs[stream, :, lanes] if slot else streams[stream, :, lanes]
    return swap[slot - 2, stream, :, head * HEAD : (head + 1) * HEAD]


SCALE = math.log2(math.e) / math.sqrt(HEAD)


CHUNK = 32


def softmax_group(queries, keys, values, bias, turn, s_s, p_s, keep):
    tall, rows = queries.shape[0], keys[0].shape[0]
    width = len(keys) * rows
    for n in range(0, len(keys), 2):
        s_s[turn, 0:tall, n * rows : (n + 2) * rows] = lax.dot_general(
            queries,
            jnp.concatenate(keys[n : n + 2], axis=0),
            (((1,), (1,)), ((), ())),
            preferred_element_type=F32,
        )
    for m in range(0, tall, CHUNK):
        some = slice(m, m + CHUNK)
        top = None
        parts = []
        for n in range(0, width, LANES):
            part = s_s[turn, some, n : n + LANES] + bias[some, n : n + LANES]
            parts.append(part)
            top = part if top is None else jnp.maximum(top, part)
        top = jnp.broadcast_to(jnp.max(top, axis=1, keepdims=True), (CHUNK, LANES))
        below = jnp.zeros((CHUNK, LANES), F32)
        for n, part in enumerate(parts):
            weight = jnp.exp2((part - top) * SCALE)
            below = below + weight
            p_s[turn, some, n * LANES : (n + 1) * LANES] = weight.astype(BF16)
        keep(m, top, jnp.broadcast_to(jnp.sum(below, axis=1, keepdims=True), (CHUNK, LANES)))
    return jnp.dot(
        p_s[turn, 0:tall, 0:width], jnp.concatenate(values, axis=0), preferred_element_type=F32
    )


def attend_body(docs_ref, streams, theirs, swap, own, cross, acc_ref, m_ref, l_ref, bias_s, s_s, p_s):
    _, side, place, row = spot()
    rows, quarter = own.shape[2:]
    base = row * (ROW * rows)
    part = functools.partial(row_part, streams, theirs, swap, quarter=quarter)

    def run(first_pair, second_pair):
        for group, (asking, seen) in enumerate(((first_pair, first_pair), (second_pair, (0, 1, 2, 3)))):
            starts = [base + (2 * (side if old else 1 - side) + 1 - n - ROW) * rows for old in (1, 0) for n in (0, 1)]
            starts += [base + (place ^ slot) * rows for slot in seen]
            for at, slot in enumerate(asking):
                position = base + (place ^ slot) * rows + lax.broadcasted_iota(jnp.int32, (rows, 1), 0)
                first = contig_start(docs_ref, position)
                for n, start in enumerate(starts):
                    token = start + lax.broadcasted_iota(jnp.int32, (rows, rows), 1)
                    bias_s[group, at * rows : (at + 1) * rows, n * rows : (n + 1) * rows] = jnp.where(
                        (token >= first) & (token <= position), 0.0, -jnp.inf
                    )
            for head in range(quarter // HEAD):
                lanes = slice(head * HEAD, (head + 1) * HEAD)
                olds = lambda kind: [old[n, kind, :, lanes] for old in (own, cross) for n in (0, 1)]

                def keep(m, top, below):
                    out = slice(asking[0] * rows + m, asking[0] * rows + m + CHUNK)
                    m_ref[out, lanes] = top
                    l_ref[out, lanes] = below

                acc_ref[asking[0] * rows : (asking[1] + 1) * rows, lanes] = softmax_group(
                    jnp.concatenate([part(slot, 0, head) for slot in asking], axis=0),
                    olds(0) + [part(slot, 1, head) for slot in seen],
                    olds(1) + [part(slot, 2, head) for slot in seen],
                    bias_s.at[group],
                    head % 2,
                    s_s,
                    p_s,
                    keep,
                )

    @pl.when(side == 0)
    def _():
        run((0, 1), (2, 3))

    @pl.when(side == 1)
    def _():
        run((2, 3), (0, 1))


def attend(doc_lengths, streams, theirs, swap, own, cross):
    _, _, rows, quarter = own.shape
    heads = quarter // HEAD
    return pl.pallas_call(
        attend_body,
        in_specs=[SMEM] + [VMEM] * 5,
        out_specs=[VMEM] * 3,
        out_shape=[
            jax.ShapeDtypeStruct((ROW * rows, quarter), F32),
        ]
        * 3,
        scratch_shapes=[
            pltpu.VMEM((2, 2 * rows, 2 * ROW * rows), F32),
            pltpu.VMEM((2, 2 * rows, 2 * ROW * rows), F32),
            pltpu.VMEM((2, 2 * rows, 2 * ROW * rows), BF16),
        ],
        compiler_params=limits(20),
        cost_estimate=cost(26 * 4 * rows * rows * quarter, 14 * ROW * rows * quarter, 26 * heads * rows * rows),
        name="attend",
    )(doc_lengths, streams, theirs, swap, own, cross)


def attend_last_body(pair, docs_ref, streams, theirs, swap, *refs):
    cross_l, own_s, own_l, cross_s, acc_ref, m_ref, l_ref = refs[:7]
    outs = refs[7:]
    _, side, place, row = spot()
    rows, quarter = acc_ref.shape[0] // ROW, acc_ref.shape[1]
    base = row * (ROW * rows)
    heads = range(quarter // HEAD)

    def run(early, late, large, small):
        for asking, blocks in ((early, ((small, 0), (large, 1), (large, 0))), (late, ((large, 0),))):
            if asking != pair:
                continue
            width = len(blocks) * rows
            here = slice(asking[0] * rows, (asking[1] + 1) * rows)
            token = base - (ROW + len(blocks)) * rows + lax.broadcasted_iota(jnp.int32, (rows, width), 1)
            allowed = []
            for slot in asking:
                position = base + (place ^ slot) * rows + lax.broadcasted_iota(jnp.int32, (rows, 1), 0)
                allowed.append((token >= contig_start(docs_ref, position)).astype(jnp.int32))
            allowed = jnp.concatenate(allowed, axis=0) != 0
            lanes_of = [slice(head * HEAD, (head + 1) * HEAD) for head in heads]
            stack = lambda kind, lanes: jnp.concatenate([ref[n, kind, :, lanes] for ref, n in blocks], axis=0)
            scores = [
                lax.dot_general(
                    jnp.concatenate(
                        [row_part(streams, theirs, swap, slot, 0, head, quarter) for slot in asking], axis=0
                    ),
                    stack(0, lanes_of[head]),
                    (((1,), (1,)), ((), ())),
                    preferred_element_type=F32,
                )
                for head in heads
            ]
            scores = [jnp.where(allowed, score, -jnp.inf) for score in scores]
            tops = [
                jnp.maximum(m_ref[here, lanes], jnp.max(score, axis=1, keepdims=True))
                for lanes, score in zip(lanes_of, scores)
            ]
            weights = [
                jnp.exp2((score - jnp.concatenate([top] * len(blocks), axis=1)) * SCALE)
                for score, top in zip(scores, tops)
            ]
            for lanes, top, weight in zip(lanes_of, tops, weights):
                fade = jnp.exp2((m_ref[here, lanes] - top) * SCALE)
                share = 1.0 / (l_ref[here, lanes] * fade + jnp.sum(weight, axis=1, keepdims=True))
                more = jnp.dot(weight.astype(BF16), stack(1, lanes), preferred_element_type=F32)
                made = ((acc_ref[here, lanes] * fade + more) * share).astype(BF16)
                for n, out in enumerate(outs):
                    out[:, lanes] = made[n * rows : (n + 1) * rows]

    @pl.when(side == 0)
    def _():
        run((0, 1), (2, 3), cross_l, own_s)

    @pl.when(side == 1)
    def _():
        run((2, 3), (0, 1), own_l, cross_s)


def attend_last(pair, doc_lengths, streams, theirs, swap, olds, acc, top, below):
    rows, quarter = acc.shape[0] // ROW, acc.shape[1]
    return pl.pallas_call(
        functools.partial(attend_last_body, pair),
        in_specs=[SMEM] + [VMEM] * 10,
        out_specs=[VMEM] * 2,
        out_shape=[jax.ShapeDtypeStruct((rows, quarter), BF16)] * 2,
        compiler_params=limits(16),
        cost_estimate=cost(16 * rows * rows * quarter, 24 * rows * quarter, 16 * rows * rows),
        name="attend_last",
    )(doc_lengths, streams, theirs, swap, *olds, acc, top, below)


def assemble_body(*refs):
    place = spot()[2]
    *pieces, out_ref, sems = refs
    lanes = pieces[0].shape[1]
    copies = []
    for n, piece in enumerate(pieces):
        maker = place ^ n
        which = 2 * (maker & 1) + lax.shift_right_logical(maker, 1)
        copies.append(pltpu.make_async_copy(piece, out_ref.at[:, lanes_from(which, lanes)], sems.at[n]))
        copies[-1].start()
    for copy in copies:
        copy.wait()


def assemble(pieces):
    rows, lanes = pieces[0].shape
    return pl.pallas_call(
        assemble_body,
        in_specs=[VMEM] * len(pieces),
        out_specs=ANY,
        scratch_shapes=[pltpu.SemaphoreType.DMA((ROW,))],
        out_shape=jax.ShapeDtypeStruct((rows, len(pieces) * lanes), BF16),
        compiler_params=limits(6),
        cost_estimate=cost(0, 4 * rows * lanes * len(pieces)),
        name="assemble",
    )(*pieces)


def on_device(hyena_qkv, short_weight, filter_rate, filter_residue, attn_qkv, doc_lengths):
    rows = attn_qkv.shape[0]
    inner = hyena_qkv.transpose(1, 0, 2)
    streams = attn_qkv.transpose(1, 0, 2)
    rates, residues = filter_rate.T, filter_residue.T
    theirs, edge = front(streams, inner)

    theirs = flip(theirs, "ctx", 1)
    edge = ahead(edge, "ctx", 1)
    own, cross = pack(streams, theirs, 1, 2)
    cross = ahead(cross, "ctx", ROW, 2)
    own = ahead(own, "ctx", ROW)
    (swap,) = pack(streams, theirs, 0, 1)
    swap = flip(swap, "ctx", 2)
    olds = (
        ahead(cross, "ctx", ROW, 0, ROW, 0),
        ahead(odd(own, 0), "ctx", ROW, 0, ROW, 0),
        ahead(own, "ctx", ROW, 0, ROW, 1),
        ahead(odd(cross, 1), "ctx", ROW, 0, ROW, 1),
    )

    mixed, keep, away, wide, gain = hyena_ends(inner, edge, short_weight, rates, residues)
    near, query, high, low = hyena_near(inner, edge, short_weight, mixed, rates, residues)
    keep, back = scan_states(keep, away, wide, gain, rows)
    hyena_out = hyena_finish(near, query, high, low, keep, back)

    acc, top, below = attend(doc_lengths, streams, theirs, swap, own, cross)
    last = lambda pair: attend_last(pair, doc_lengths, streams, theirs, swap, olds, acc, top, below)
    far2, far3 = last((2, 3))
    far2 = flip(far2, "ctx", 2)
    far3 = flip(far3, "ctx", 3)
    kept, near1 = last((0, 1))
    near1 = flip(near1, "ctx", 1)
    attn_out = assemble([kept, near1, far2, far3])
    return (hyena_out, attn_out)


def solution(mesh):
    in_specs = (
        P(("group", "ctx"), None, None),
        P(),
        P(),
        P(),
        P(("group", "ctx"), None, None),
        P("group"),
    )
    out_specs = (P(("group", "ctx"), None), P(("group", "ctx"), None))
    return jax.shard_map(on_device, mesh=mesh, in_specs=in_specs, out_specs=out_specs, check_vma=False)
```
